32 devices in a mesh: ens: 2 (over y), lon: 4 (over z), lat: 2 (over x), ch: 2 (over core).
Axes of the slice: x: 2, y: 2, z: 4, core: 2. Of those that a mesh axis runs over, the one named last changes fastest.
Arguments:
- input_field: bfloat16 [256, 128, 128], P(('ens', 'lat', 'ch'), 'lon'), parts along dimension 0, may hold values from -6 to 6
- encoder_filter: bfloat16 [128, 4, 5], P(('lat', 'ch')), may hold values from -2.6875 to 2.6875
- row_owner: int32 [256], P(('ens', 'lat', 'ch')), parts along dimension 0, may hold values from 0 to 63, as said below
- encoder_weight: bfloat16 [512, 256], replicated, may hold values from -0.25 to 0.25
- disco_basis: bfloat16 [64, 4, 3, 17], P(('lat', 'ch')), may hold values from -1.5 to 1.5
- row_widths: int32 [64], P(('lat', 'ch')), may hold values from 1 to 8, as said below
- block_weights: bfloat16 [2, 1024, 256], replicated, may hold values from -0.1875 to 0.1875
- cotangent: bfloat16 [128, 64, 256], P(('ens', 'lat', 'ch'), 'lon'), parts along dimension 0, may hold values from -6 to 6
Outputs:
- state_out: bfloat16 [128, 64, 256], P(('ens', 'lat', 'ch'), 'lon'), parts along dimension 0
- latent_grad: bfloat16 [128, 64, 256], P(('ens', 'lat', 'ch'), 'lon'), parts along dimension 0
- block_grads: float32 [4, 1024, 256], P('ens', None, 'ch'), parts along dimension 0
- encoder_grad: float32 [1024, 256], P('ens', 'ch'), parts along dimension 0
The draws below stay inside these ranges and needn't reach their ends.
There are 2 independent parts, one for each index of `ens`. The reference program is written for one: setup_inputs(seed, part) draws one part's arguments, and reference() takes and returns one part's arrays. A program takes and returns all parts, laid end to end along the dimension named above; an argument that names none is the same for every part. Nothing has to cross between parts.
Inputs may be any that keep to these rules, and one draw needn't show every extreme that they name: `row_owner`: input row p feeds latent row (p - 1) // 2, p // 2 or (p + 1) // 2, and every latent row is fed by 1 to 3 input rows. `row_widths`: the first and last rows have 8.
All inputs are finite; a program needn't handle non-finite values.
Results may differ from the reference program's by a relative error of at most 0.014.
Values may be sent and summed in bfloat16 or wider, within the bound.
A program may use at most 64 MiB of HBM per device.

```python
import math
import jax
import jax.numpy as jnp
from jax import lax

CHANNELS = 256
IN_CHANNELS = 128
BASIS = 4
REACH = 8
TAP_REACH = 2
BLOCKS = 2
ROWS_DEV = 16
NLAT = 64
NLON = 64
NLAT_IN = 128
NLON_IN = 128


def draw_row_owner(key, part):
    key_moves = jax.random.fold_in(key, 11)
    position = jnp.arange(NLAT + 1, dtype=jnp.int32)
    stepping = jax.random.randint(key_moves, (NLAT + 1,), -1, 2, dtype=jnp.int32)
    drifts = jnp.where(position % 2 == 1, 0, stepping)
    at_edge = position % ROWS_DEV == 0
    drifts = jnp.where(at_edge, 0, drifts)
    starts = 2 * position + drifts
    input_rows = jnp.arange(2 * NLAT, dtype=jnp.int32)
    inside = (starts[None, 1:NLAT] <= input_rows[:, None]).astype(jnp.int32)
    owners = jnp.sum(inside, axis=1).astype(jnp.int32)
    band_rows = 2 * ROWS_DEV
    first_of_band = (input_rows % band_rows == 0) & (input_rows > 0)
    last_of_band = (input_rows % band_rows == band_rows - 1) & (input_rows < 2 * NLAT - 1)
    owners = jnp.where(first_of_band, owners - 1, owners)
    owners = jnp.where(last_of_band, owners + 1, owners)
    return owners.astype(jnp.int32)


def draw_row_widths(key, part):
    position = jnp.arange(NLAT, dtype=jnp.int32)
    distance = jnp.abs(2 * position + 1 - NLAT)
    jitter = jax.random.randint(jax.random.fold_in(key, 23), (NLAT,), 0, 2, dtype=jnp.int32)
    widths = 1 + jitter + (REACH - 2) * distance * distance // (NLAT * NLAT)
    widths = jnp.where((position == 0) | (position == NLAT - 1), REACH, widths)
    return jnp.clip(widths, 1, REACH).astype(jnp.int32)


def block_levels(own_key, extent, cuts, smallest, top_value):
    factor_of, own = 1.0, jax.random.fold_in(own_key, 6)
    for dim, shards_of in cuts:
        draws = jnp.exp(jax.random.uniform(jax.random.fold_in(own, dim), (shards_of,), jnp.float32, smallest / len(cuts), top_value / len(cuts)))
        factor_of = factor_of * jnp.repeat(draws, extent[dim] // shards_of).reshape([-1 if axis == dim else 1 for axis in range(len(extent))])
    return factor_of


def bell_draw(rng, dims, width, limit, shards=(), held_as=jnp.bfloat16):
    entries = width * jax.random.normal(rng, dims, jnp.float32)
    if shards:
        entries = entries * block_levels(rng, dims, shards, -0.22, 0.18)
    return jnp.clip(entries, -limit, limit).astype(held_as)


def setup_inputs(seed: int = 0, part: int = 0) -> dict:
    splits = jax.random.split(jax.random.key(seed), 9)
    part_keys = jax.random.split(jax.random.fold_in(splits[8], part), 9)
    return {
        "input_field": bell_draw(part_keys[0], (NLAT_IN, NLON_IN, IN_CHANNELS), 1.0, 6.0, ((0, 4), (1, 4))),
        "encoder_filter": bell_draw(splits[1], (NLAT_IN, BASIS, 2 * TAP_REACH + 1), 0.45, 2.6875, ((0, 4),)),
        "row_owner": draw_row_owner(jax.random.fold_in(jax.random.fold_in(splits[8], part), 71), part),
        "encoder_weight": bell_draw(splits[3], (BASIS * IN_CHANNELS, CHANNELS), (BASIS * IN_CHANNELS) ** -0.5, 0.25),
        "disco_basis": bell_draw(splits[4], (NLAT, BASIS, 3, 2 * REACH + 1), 0.25, 1.5, ((0, 4),)),
        "row_widths": draw_row_widths(jax.random.fold_in(splits[8], 71), part),
        "block_weights": bell_draw(splits[6], (BLOCKS, BASIS * CHANNELS, CHANNELS), (BASIS * CHANNELS) ** -0.5, 0.1875),
        "cotangent": bell_draw(part_keys[7], (NLAT, NLON, CHANNELS), 1.0, 6.0, ((0, 4), (1, 4))),
    }


def masked_basis(disco_basis, row_widths):
    offsets = jnp.abs(jnp.arange(2 * REACH + 1, dtype=jnp.int32) - REACH)
    keep = offsets[None, :] <= row_widths[:, None]
    values = disco_basis.astype(jnp.float32)
    return jnp.where(keep[:, None, None, :], values, jnp.zeros_like(values))

def apply_stencil(field, basis):
    padded = jnp.pad(field, ((1, 1), (0, 0), (0, 0)))
    padded = jnp.concatenate([padded[:, NLON - REACH:], padded, padded[:, :REACH]], axis=1)
    stacked = jnp.stack([padded[0:NLAT], padded[1:NLAT + 1], padded[2:NLAT + 2]], axis=0)
    result = jnp.zeros((NLAT, NLON, BASIS, CHANNELS), field.dtype)
    for shift_col in range(2 * REACH + 1):
        window = stacked[:, :, shift_col:shift_col + NLON, :]
        result = result + jnp.einsum('rijc,ikr->ijkc', window, basis[:, :, :, shift_col], precision=lax.Precision.HIGHEST)
    return result

def reference(input_field, encoder_filter, row_owner, encoder_weight, disco_basis, row_widths, block_weights, cotangent):
    field_in = input_field.astype(jnp.float32)
    wrapped = jnp.concatenate([field_in[:, NLON_IN - TAP_REACH:], field_in, field_in[:, :TAP_REACH]], axis=1)
    filter_values = encoder_filter.astype(jnp.float32)
    accumulated = jnp.zeros((NLAT_IN, NLON, BASIS, IN_CHANNELS), field_in.dtype)
    for tap_index in range(2 * TAP_REACH + 1):
        sampled = wrapped[:, tap_index:tap_index + NLON_IN:2, :]
        accumulated = accumulated + sampled[:, :, None, :] * filter_values[:, None, :, tap_index, None]
    filtered_input = accumulated.astype(jnp.bfloat16)
    regridded = jax.ops.segment_sum(filtered_input.astype(jnp.float32), row_owner, num_segments=NLAT)
    latent_input = regridded.astype(jnp.bfloat16).reshape(NLAT * NLON, BASIS * IN_CHANNELS)
    current = jnp.dot(latent_input, encoder_weight, preferred_element_type=jnp.float32).astype(jnp.bfloat16)
    current = current.reshape(NLAT, NLON, CHANNELS)
    basis = masked_basis(disco_basis, row_widths)
    saved = []
    for layer_index in range(BLOCKS):
        features = apply_stencil(current.astype(jnp.float32), basis).astype(jnp.bfloat16)
        features = features.reshape(NLAT * NLON, BASIS * CHANNELS)
        preact = jnp.dot(features, block_weights[layer_index], preferred_element_type=jnp.float32)
        current = (current.astype(jnp.float32) + jax.nn.silu(preact).reshape(NLAT, NLON, CHANNELS)).astype(jnp.bfloat16)
        saved.append((features, preact))
    state_out = current
    zero_field = jnp.zeros((NLAT, NLON, CHANNELS), jnp.float32)
    unused, pullback = jax.vjp(lambda field: apply_stencil(field, basis), zero_field)
    gradient = cotangent
    weight_terms = [None] * BLOCKS
    for layer_index in reversed(range(BLOCKS)):
        features, preact = saved[layer_index]
        sigma = jax.nn.sigmoid(preact)
        upstream = gradient.reshape(NLAT * NLON, CHANNELS).astype(jnp.float32)
        act_grad = (upstream * sigma * (1.0 + preact * (1.0 - sigma))).astype(jnp.bfloat16)
        weight_terms[layer_index] = jnp.dot(features.T, act_grad, preferred_element_type=jnp.float32)
        errors = jnp.dot(act_grad, block_weights[layer_index].T, preferred_element_type=jnp.float32).astype(jnp.bfloat16)
        errors = errors.reshape(NLAT, NLON, BASIS, CHANNELS)
        spread = pullback(errors.astype(jnp.float32))[0]
        gradient = (gradient.astype(jnp.float32) + spread).astype(jnp.bfloat16)
    normalizer = 1.0 / math.sqrt(NLAT * NLON)
    encoder_term = jnp.dot(latent_input.T, gradient.reshape(NLAT * NLON, CHANNELS), preferred_element_type=jnp.float32)
    block_grads = jnp.stack(weight_terms, axis=0) * normalizer
    return (state_out, gradient, block_grads, encoder_term * normalizer)
```

```python
import functools
import math

import jax
import jax.numpy as jnp
from jax import lax
from jax.experimental import pallas as pl
from jax.experimental.pallas import tpu as pltpu
from jax.sharding import PartitionSpec as P

REACH = 8
TAP_REACH = 2
TILE = 16
MESH = pl.DeviceIdType.MESH
BF16 = jnp.bfloat16
F32 = jnp.float32


def along(axis, steps):
    count = lax.axis_size(axis)
    return {axis: lax.rem(lax.axis_index(axis) + steps + count, count)}


def neighbour(row_step, col_step):
    ch_count = lax.axis_size("ch")
    bands = lax.axis_size("lat") * ch_count
    band = lax.axis_index("lat") * ch_count + lax.axis_index("ch")
    band = lax.rem(band + row_step + bands, bands)
    target = {}
    if row_step:
        target = {"lat": band // ch_count, "ch": lax.rem(band, ch_count)}
    if col_step:
        target.update(along("lon", col_step))
    return target


AROUND = [(r, c) for r in (-1, 0, 1) for c in (-1, 0, 1) if r or c]


def greet():
    targets = [neighbour(r, c) for r, c in AROUND]
    for axis in ("ch", "lat", "lon"):
        targets += [along(axis, step) for step in range(1, lax.axis_size(axis))]
    barrier = pltpu.get_barrier_semaphore()
    for target in targets:
        pl.semaphore_signal(barrier, inc=1, device_id=target, device_id_type=MESH)
    pl.semaphore_wait(barrier, len(targets))


class Sender:
    def __init__(self, sems):
        self.ssem, self.rsem = sems
        self.pending = []

    def send(self, source, target, slot, device):
        copy = pltpu.make_async_remote_copy(
            src_ref=source,
            dst_ref=target,
            send_sem=self.ssem.at[slot],
            recv_sem=self.rsem.at[slot],
            device_id=device,
            device_id_type=MESH,
        )
        copy.start()
        self.pending.append(copy)

    def settle(self):
        for copy in self.pending:
            copy.wait()
        self.pending = []


class GradSum(Sender):
    def __init__(self, result, bufs):
        super().__init__(bufs[-2:])
        self.result = result
        self.source, self.rec_ch, self.part, self.rec_lat, self.strip, self.rec_pair, self.half, self.rec_far, self.piece = bufs[:-2]
        self.width = self.part.shape[1]
        self.lat, self.lon = lax.axis_size("lat"), lax.axis_size("lon")
        self.height = self.strip.shape[0]
        self.span = self.piece.shape[0]
        self.pair = self.height // self.span
        self.far = self.lon // self.pair
        self.side = lax.rem(lax.axis_index("lon"), self.pair)

    @staticmethod
    def scratch(sizes, rows, columns):
        lat, lon = sizes
        width = columns // 2
        height = rows // lat
        pair = 2 if lon % 2 == 0 and height % (2 * TILE) == 0 else 1
        span, far = height // pair, lon // pair
        count = 1 + 2 * (lat - 1) + 2 * (pair - 1) + far - 1
        return [
            pltpu.VMEM((rows, columns), BF16),
            pltpu.VMEM((rows, width), BF16),
            pltpu.VMEM((rows, width), BF16),
            pltpu.VMEM((lat - 1, height, width), BF16),
            pltpu.VMEM((height, width), BF16),
            pltpu.VMEM((span, width), BF16),
            pltpu.VMEM((span, width), BF16),
            pltpu.VMEM((far - 1, span, width), BF16),
            pltpu.VMEM((span, width), BF16),
            pltpu.SemaphoreType.DMA((count,)),
            pltpu.SemaphoreType.DMA((count,)),
        ]

    def columns(self, half):
        return pl.ds(pl.multiple_of(half * self.width, self.width), self.width)

    @staticmethod
    def stretch(owner, size):
        return pl.ds(pl.multiple_of(owner * size, size), size)

    def start_ch(self):
        other = 1 - lax.axis_index("ch")
        self.send(self.source.at[:, self.columns(other)], self.rec_ch, 0, {"ch": other})

    def start_lat(self):
        self.settle()
        own = self.source[:, self.columns(lax.axis_index("ch"))].astype(F32)
        self.part[...] = (own + self.rec_ch[...].astype(F32)).astype(BF16)
        for step in range(1, self.lat):
            peer = along("lat", step)
            rows = self.stretch(peer["lat"], self.height)
            self.send(self.part.at[rows], self.rec_lat.at[step - 1], step, peer)

    def start_lon(self):
        self.settle()
        total = self.part[self.stretch(lax.axis_index("lat"), self.height), :].astype(F32)
        for step in range(1, self.lat):
            total = total + self.rec_lat[step - 1].astype(F32)
        self.strip[...] = total.astype(BF16)
        if self.pair > 1:
            rows = self.stretch(1 - self.side, self.span)
            self.send(self.strip.at[rows], self.rec_pair, self.lat, along("lon", 1 - 2 * self.side))

    def start_far(self):
        self.settle()
        total = self.strip[self.stretch(self.side, self.span), :].astype(F32)
        if self.pair > 1:
            total = total + self.rec_pair[...].astype(F32)
        self.half[...] = total.astype(BF16)
        for step in range(1, self.far):
            self.send(
                self.half, self.rec_far.at[step - 1], self.lat + step, along("lon", self.pair * step)
            )

    def gather_lon(self):
        self.settle()
        total = self.half[...].astype(F32)
        for step in range(1, self.far):
            total = total + self.rec_far[step - 1].astype(F32)
        self.piece[...] = total.astype(BF16)
        offset = lax.axis_index("lat") * self.height + self.side * self.span
        rows = pl.ds(pl.multiple_of(offset, TILE), self.span)
        self.result[rows, :] = self.piece[...]
        if self.pair > 1:
            slot = self.lat + self.far
            self.send(self.piece, self.result.at[rows], slot, along("lon", 1 - 2 * self.side))

    def gather_lat(self):
        self.settle()
        rows = self.stretch(lax.axis_index("lat"), self.height)
        for step in range(1, self.lat):
            slot = self.lat + self.far + self.pair - 2 + step
            self.send(self.result.at[rows], self.result.at[rows], slot, along("lat", step))

    def finish(self):
        self.settle()


STAGES = ("start_ch", "start_lat", "start_lon", "start_far", "gather_lon", "gather_lat", "finish")


class Halo(Sender):
    def __init__(self, bufs):
        super().__init__(bufs[-2:])
        self.out_side, self.out_row, self.in_side, self.in_row = bufs[:-2]

    @staticmethod
    def scratch(rows, cols, width, row_blocks):
        return [
            pltpu.VMEM((2, rows * REACH, width), BF16),
            pltpu.VMEM((row_blocks, cols, width), BF16),
            pltpu.VMEM((2, rows * REACH, width), BF16),
            pltpu.VMEM((6, cols, width), BF16),
            pltpu.SemaphoreType.DMA((8,)),
            pltpu.SemaphoreType.DMA((8,)),
        ]

    def start(self, row_block_of):
        self.send(self.out_side.at[0], self.in_side.at[1], 0, neighbour(0, -1))
        self.send(self.out_side.at[1], self.in_side.at[0], 1, neighbour(0, 1))
        slot = 2
        for row_step in (-1, 1):
            for col_step in (-1, 0, 1):
                place = (0 if row_step == 1 else 3) + 1 - col_step
                self.send(
                    self.out_row.at[row_block_of(row_step, col_step)],
                    self.in_row.at[place],
                    slot,
                    neighbour(row_step, col_step),
                )
                slot += 1


def edge_flags():
    ch_count = lax.axis_size("ch")
    bands = lax.axis_size("lat") * ch_count
    band = lax.axis_index("lat") * ch_count + lax.axis_index("ch")
    return band > 0, band < bands - 1


def extend(halo, state, ext, rows, cols):
    span = cols + 2 * REACH
    west, east = halo.in_side[0].astype(F32), halo.in_side[1].astype(F32)
    for row in range(rows):
        low, high = row * REACH, (row + 1) * REACH
        line = jnp.concatenate(
            [west[low:high], state[row * cols : (row + 1) * cols], east[low:high]], axis=0
        )
        ext[(row + 1) * span : (row + 2) * span, :] = line.astype(BF16)
    for first, row, flag in zip((0, 3), (0, rows + 1), edge_flags()):
        line = jnp.concatenate(
            [
                halo.in_row[first].astype(F32)[cols - REACH :],
                halo.in_row[first + 1].astype(F32),
                halo.in_row[first + 2].astype(F32)[:REACH],
            ],
            axis=0,
        )
        ext[row * span : (row + 1) * span, :] = jnp.where(flag, line, 0.0).astype(BF16)


def send_state(halo, state, rows, cols):
    pieces = [
        [state[r * cols : r * cols + REACH] for r in range(rows)],
        [state[(r + 1) * cols - REACH : (r + 1) * cols] for r in range(rows)],
    ]
    for side in range(2):
        halo.out_side[side] = jnp.concatenate(pieces[side], axis=0).astype(BF16)
    halo.out_row[0] = state[:cols].astype(BF16)
    halo.out_row[1] = state[(rows - 1) * cols :].astype(BF16)
    halo.start(lambda row_step, col_step: 0 if row_step == -1 else 1)


def send_spread(halo, spread, rows, cols):
    span = cols + 2 * REACH
    west = [spread[(r + 1) * span : (r + 1) * span + REACH, :] for r in range(rows)]
    east = [spread[(r + 2) * span - REACH : (r + 2) * span, :] for r in range(rows)]
    halo.out_side[0] = jnp.concatenate(west, axis=0).astype(BF16)
    halo.out_side[1] = jnp.concatenate(east, axis=0).astype(BF16)
    for block, row in enumerate((0, rows + 1)):
        base = row * span
        halo.out_row[2 * block] = spread[base + REACH : base + REACH + cols, :].astype(BF16)
        corners = [spread[base : base + REACH, :], spread[base + span - REACH : base + span, :]]
        if cols > 2 * REACH:
            corners.insert(1, jnp.zeros((cols - 2 * REACH, spread.shape[1]), F32))
        halo.out_row[2 * block + 1] = jnp.concatenate(corners, axis=0).astype(BF16)
    halo.start(
        lambda row_step, col_step: (0 if row_step == -1 else 2) + (1 if col_step else 0)
    )


def take_spread(halo, spread, gradient, rows, cols):
    span = cols + 2 * REACH
    west, east = halo.in_side[0].astype(F32), halo.in_side[1].astype(F32)
    outer = {}
    for first, row, flag in zip((0, 3), (0, rows - 1), edge_flags()):
        line = halo.in_row[first + 1].astype(F32)
        rim_west = halo.in_row[first].astype(F32)[cols - REACH :]
        rim_east = halo.in_row[first + 2].astype(F32)[:REACH]
        rims = [rim_west, rim_east]
        if cols > 2 * REACH:
            rims.insert(1, jnp.zeros((cols - 2 * REACH, line.shape[1]), F32))
        outer[row] = jnp.where(flag, line + jnp.concatenate(rims, axis=0), 0.0)
    result = []
    for row in range(rows):
        low, high = row * REACH, (row + 1) * REACH
        rims = [west[low:high], east[low:high]]
        if cols > 2 * REACH:
            rims.insert(1, jnp.zeros((cols - 2 * REACH, west.shape[1]), F32))
        base = (row + 1) * span + REACH
        line = spread[base : base + cols, :] + jnp.concatenate(rims, axis=0)
        if row in outer:
            line = line + outer[row]
        result.append(gradient[row * cols : (row + 1) * cols].astype(F32) + line)
    return result


def aligned(index, size):
    return pl.ds(pl.multiple_of(index * size, size), size)


GROUP = 16


def over_rows(rows, body):
    group = GROUP if rows % GROUP == 0 else 1

    def step(index, carry):
        for inner in range(group):
            body(index * group + inner)
        return carry

    lax.fori_loop(0, rows // group, step, 0)


def make_bands(base, bands, rows, cols, basis_count):
    width = base.shape[1]

    def one(row):
        table = base[aligned(row, 2 * basis_count), :]
        for k in range(basis_count):
            line = jnp.broadcast_to(table[k : k + 1], (cols, width))
            moved = pltpu.roll(line, 0, 1, stride=1, stride_axis=0)
            start = pl.multiple_of((row * basis_count + k) * cols, cols)
            bands[pl.ds(start, cols), :] = moved.astype(BF16)

    over_rows(rows, one)


def stencil(bands, ext, features, rows, cols, basis_count):
    span = cols + 2 * REACH
    channels = ext.shape[1]

    def one(row):
        lhs = bands[aligned(row, basis_count * cols), :][:, : 3 * span]
        rhs = ext[pl.ds(pl.multiple_of(row * span, span), 3 * span), :]
        out = jnp.dot(lhs, rhs, preferred_element_type=F32).astype(BF16)
        for k in range(basis_count):
            features[aligned(row, cols), k * channels : (k + 1) * channels] = out[
                k * cols : (k + 1) * cols
            ]

    over_rows(rows, one)


def adjoint(bands, errs, spread, rows, cols, basis_count):
    span = cols + 2 * REACH
    spread[...] = jnp.zeros_like(spread)

    def one(row):
        lhs = bands[aligned(row, basis_count * cols), :][:, : 3 * span]
        rhs = errs[aligned(row, basis_count * cols), :]
        out = lax.dot_general(lhs, rhs, (((0,), (0,)), ((), ())), preferred_element_type=F32)
        place = pl.ds(pl.multiple_of(row * span, span), 3 * span)
        spread[place, :] = spread[place, :] + out

    over_rows(rows, one)


def rows_product(left, right):
    return lax.dot_general(left, right, (((0,), (0,)), ((), ())), preferred_element_type=F32)
TAPS_LEFT = TAP_REACH


class InputHalo(Sender):
    def __init__(self, bufs):
        super().__init__(bufs[-2:])
        (
            self.edges,
            self.out_cols,
            self.out_table,
            self.in_cols,
            self.in_row,
            self.in_table,
            self.in_tile,
        ) = bufs[:-2]

    @staticmethod
    def scratch(rows_in, cols_in, width, table_rows, lanes):
        return [
            pltpu.VMEM((3, rows_in, width), F32),
            pltpu.VMEM((3, rows_in, width), BF16),
            pltpu.VMEM((2, table_rows, lanes), F32),
            pltpu.VMEM((3, rows_in, width), BF16),
            pltpu.VMEM((2, cols_in, width), BF16),
            pltpu.VMEM((2, table_rows, lanes), F32),
            pltpu.VMEM((4, TILE, width), BF16),
            pltpu.SemaphoreType.DMA((10,)),
            pltpu.SemaphoreType.DMA((10,)),
        ]

    def start(self, field, table, owner, rows_in, cols_in):
        first = own_first_row(rows_in // 2)
        table_rows = self.out_table.shape[1]
        for block, row, target in ((0, 0, first - 1), (1, rows_in - 1, first + rows_in // 2)):
            feeds = jnp.where(owner[row] == target, 1.0, 0.0)
            self.out_table[block] = table[row * table_rows : (row + 1) * table_rows, :] * feeds
        last = (rows_in - 1) * cols_in
        lines = (field.at[pl.ds(0, cols_in)], field.at[pl.ds(last, cols_in)])
        slot = 0
        for block, row_step in ((0, -1), (1, 1)):
            self.send(lines[block], self.in_row.at[1 - block], slot, neighbour(row_step, 0))
            base = block * last
            west = field.at[pl.ds(base, TILE)]
            east = field.at[pl.ds(base + cols_in - TILE, TILE)]
            place = 2 * (1 - block)
            self.send(west, self.in_tile.at[place + 1], slot + 1, neighbour(row_step, -1))
            self.send(east, self.in_tile.at[place], slot + 2, neighbour(row_step, 1))
            slot += 3

        def one(row):
            low = field[pl.ds(pl.multiple_of(row * cols_in, TILE), TILE), :].astype(F32)
            start = pl.multiple_of(row * cols_in + cols_in - TILE, TILE)
            high = field[pl.ds(start, TILE), :].astype(F32)
            self.edges[0, pl.ds(row, 1), :] = high[TILE - 2 : TILE - 1]
            self.edges[1, pl.ds(row, 1), :] = high[TILE - 1 : TILE]
            self.edges[2, pl.ds(row, 1), :] = low[0:1]

        over_rows(rows_in, one)
        self.out_cols[...] = self.edges[...].astype(BF16)
        self.send(self.out_cols.at[pl.ds(0, 2)], self.in_cols.at[pl.ds(0, 2)], 6, neighbour(0, 1))
        self.send(self.out_cols.at[2], self.in_cols.at[2], 7, neighbour(0, -1))
        self.send(self.out_table.at[0], self.in_table.at[1], 8, neighbour(-1, 0))
        self.send(self.out_table.at[1], self.in_table.at[0], 9, neighbour(1, 0))


def own_first_row(rows):
    return (lax.axis_index("lat") * lax.axis_size("ch") + lax.axis_index("ch")) * rows


def tap_matrix(table, basis_count, cols, cols_in):
    lanes = table.shape[1]
    blocks = []
    for k in range(basis_count):
        line = jnp.broadcast_to(table[k : k + 1], (cols, lanes))
        moved = pltpu.roll(line, 0, 1, stride=2, stride_axis=0)
        wrapped = pltpu.roll(moved, cols_in + TILE - TAPS_LEFT, 1)
        moved = pltpu.roll(moved, lanes - TAPS_LEFT, 1)
        lane = lax.broadcasted_iota(jnp.int32, (cols, lanes), 1)
        at_end = (lane >= cols_in + TILE - TAPS_LEFT) & (lane < cols_in + TILE)
        blocks.append(jnp.where(at_end, wrapped, moved))
    return jnp.concatenate(blocks, axis=0)[:, : cols_in + TILE].astype(BF16)


def filtered_row(table, line, left_two, left_one, right, basis_count, cols, cols_in):
    width = line.shape[1]
    place = lax.broadcasted_iota(jnp.int32, (TILE, width), 0)
    tile = jnp.where(place == 0, jnp.broadcast_to(right, (TILE, width)), 0.0)
    tile = jnp.where(place == TILE - 2, jnp.broadcast_to(left_two, (TILE, width)), tile)
    tile = jnp.where(place == TILE - 1, jnp.broadcast_to(left_one, (TILE, width)), tile)
    rhs = jnp.concatenate([line, tile.astype(BF16)], axis=0)
    lhs = tap_matrix(table, basis_count, cols, cols_in)
    return jnp.dot(lhs, rhs, preferred_element_type=F32).astype(BF16)


def finish_encode(halo, field, table, owner, filtered, latent_in, plan, rows_in, cols_in):
    rows, cols, basis_count, _ = plan
    table_rows = halo.out_table.shape[1]
    block = basis_count * cols
    width = field.shape[1]
    halo.settle()
    halo.edges[...] = halo.in_cols[...].astype(F32)

    def one(row):
        sides = [halo.edges[index, pl.ds(row, 1), :] for index in range(3)]
        line = field[aligned(row, cols_in), :]
        taps = table[aligned(row, table_rows), :]
        filtered[aligned(row + 1, block), :] = filtered_row(
            taps, line, *sides, basis_count, cols, cols_in
        )

    over_rows(rows_in, one)
    for side, row in ((0, 0), (1, rows_in + 1)):
        west = halo.in_tile[2 * side].astype(F32)
        east = halo.in_tile[2 * side + 1].astype(F32)
        filtered[row * block : (row + 1) * block, :] = filtered_row(
            halo.in_table[side],
            halo.in_row[side],
            west[TILE - 2 : TILE - 1],
            west[TILE - 1 : TILE],
            east[0:1],
            basis_count,
            cols,
            cols_in,
        )
    first = own_first_row(rows)
    for row in range(rows):
        total = None
        for offset in range(-1, 3):
            source = 2 * row + offset
            term = filtered[(source + 1) * block : (source + 2) * block, :].astype(F32)
            if 0 <= source < rows_in:
                term = term * jnp.where(owner[source] == first + row, 1.0, 0.0)
            total = term if total is None else total + term
        total = total.astype(BF16)
        for k in range(basis_count):
            latent_in[row * cols : (row + 1) * cols, k * width : (k + 1) * width] = total[
                k * cols : (k + 1) * cols
            ]


def lanes_of(count):
    return -(-(count + 2 * TILE) // 128) * 128


def net_kernel(plan, *refs):
    rows, cols, basis_count, layers = plan
    field, table, owner, encoder_weight, base, weights, cotangent = refs[:7]
    state_out, latent_grad = refs[7:9]
    results = refs[9 : 10 + layers]
    rest = list(refs[10 + layers :])
    bands, ext, spread, errs, features, preact, filtered, latent_in = rest[:8]
    input_halo = InputHalo(rest[8:17])
    rest = rest[17:]
    halos = []
    for _ in range(2 * layers):
        halos.append(Halo(rest[:6]))
        rest = rest[6:]
    sums = []
    for index in range(layers + 1):
        sums.append(GradSum(results[index], rest[:11]))
        rest = rest[11:]
    channels = ext.shape[1]
    progress = [0] * (layers + 1)

    def advance(index):
        getattr(sums[index], STAGES[progress[index]])()
        progress[index] += 1

    greet()
    rows_in = owner.shape[0]
    cols_in = field.shape[0] // rows_in
    input_halo.start(field, table, owner, rows_in, cols_in)
    make_bands(base, bands, rows, cols, basis_count)
    finish_encode(input_halo, field, table, owner, filtered, latent_in, plan, rows_in, cols_in)
    state = jnp.dot(latent_in[...], encoder_weight[...], preferred_element_type=F32)
    state = state.astype(BF16).astype(F32)
    for layer in range(layers):
        send_state(halos[layer], state, rows, cols)
        halos[layer].settle()
        extend(halos[layer], state, ext, rows, cols)
        stencil(bands, ext, features.at[layer], rows, cols, basis_count)
        pre = jnp.dot(features[layer], weights[layer], preferred_element_type=F32)
        preact[layer] = pre
        state = (state + pre / (1.0 + jnp.exp(-pre))).astype(BF16).astype(F32)
    state_out[...] = state.astype(BF16)

    gradient = cotangent[...].astype(F32)
    for layer in reversed(range(layers)):
        pre = preact[layer]
        sigma = 1.0 / (1.0 + jnp.exp(-pre))
        act_grad = (gradient * sigma * (1.0 + pre * (1.0 - sigma))).astype(BF16)
        for k in range(basis_count):
            block = weights[layer, k * channels : (k + 1) * channels, :]
            out = lax.dot_general(
                act_grad, block, (((1,), (1,)), ((), ())), preferred_element_type=F32
            ).astype(BF16)
            for row in range(rows):
                start = (row * basis_count + k) * cols
                errs[start : start + cols, :] = out[row * cols : (row + 1) * cols]
        adjoint(bands, errs, spread, rows, cols, basis_count)
        halo = halos[layers + layer]
        send_spread(halo, spread, rows, cols)
        sums[layer].source[...] = rows_product(features[layer], act_grad).astype(BF16)
        for other in range(layers - 1, layer - 1, -1):
            advance(other)
        halo.settle()
        for other in range(layers - 1, layer - 1, -1):
            advance(other)
        lines = take_spread(halo, spread, gradient, rows, cols)
        gradient = jnp.concatenate(lines, axis=0).astype(BF16).astype(F32)
    latent_grad[...] = gradient.astype(BF16)
    sums[layers].source[...] = rows_product(latent_in[...], gradient.astype(BF16)).astype(BF16)
    advance(layers)
    while min(progress) < len(STAGES):
        for index in [layers] + list(range(layers))[::-1]:
            if progress[index] < len(STAGES):
                advance(index)


def run_net(plan, sizes, field_in, table, owner, encoder_weight, base, weights, cotangent):
    rows, cols, basis_count, layers = plan
    cells, channels = rows * cols, weights.shape[2]
    features = basis_count * channels
    span = cols + 2 * REACH
    rows_in = owner.shape[0]
    in_features = encoder_weight.shape[0]
    heights = [features] * layers + [in_features]
    scratch = [
        pltpu.VMEM((rows * basis_count * cols, base.shape[1]), BF16),
        pltpu.VMEM(((rows + 2) * span, channels), BF16),
        pltpu.VMEM(((rows + 2) * span, channels), F32),
        pltpu.VMEM((rows * basis_count * cols, channels), BF16),
        pltpu.VMEM((layers, cells, features), BF16),
        pltpu.VMEM((layers, cells, channels), F32),
        pltpu.VMEM(((rows_in + 2) * basis_count * cols, field_in.shape[1]), BF16),
        pltpu.VMEM((cells, in_features), BF16),
    ]
    scratch += InputHalo.scratch(
        rows_in, field_in.shape[0] // rows_in, field_in.shape[1], table.shape[0] // rows_in, table.shape[1]
    )
    for index in range(2 * layers):
        scratch += Halo.scratch(rows, cols, channels, 2 if index < layers else 4)
    for height in heights:
        scratch += GradSum.scratch(sizes, height, channels)
    vmem = pl.BlockSpec(memory_space=pltpu.VMEM)
    field = jax.ShapeDtypeStruct((cells, channels), BF16)
    grads = [jax.ShapeDtypeStruct((height, channels // 2), BF16) for height in heights]
    return pl.pallas_call(
        functools.partial(net_kernel, plan),
        out_shape=[field, field] + grads,
        in_specs=[vmem, vmem, pl.BlockSpec(memory_space=pltpu.SMEM)] + [vmem] * 4,
        out_specs=[vmem] * (3 + layers),
        scratch_shapes=scratch,
        compiler_params=pltpu.CompilerParams(
            collective_id=0, has_side_effects=True, vmem_limit_bytes=56 << 20
        ),
    )(field_in, table, owner, encoder_weight, base, weights, cotangent)


def per_device(
    input_field,
    encoder_filter,
    row_owner,
    encoder_weight,
    disco_basis,
    row_widths,
    block_weights,
    cotangent,
):
    if fits_chunks(
        cotangent.shape[0], input_field.shape[1], cotangent.shape[1], block_weights.shape[0]
    ):
        return per_device_chunks(
            input_field,
            encoder_filter,
            row_owner,
            encoder_weight,
            disco_basis,
            row_widths,
            block_weights,
            cotangent,
        )
    rows_in, cols_in, in_width = input_field.shape
    rows_dev = rows_in // 2
    cols_dev = cols_in // 2
    basis_count = encoder_filter.shape[1]
    tap_count = encoder_filter.shape[2]
    channels = block_weights.shape[2]
    layers = block_weights.shape[0]
    cell_count = rows_dev * cols_dev
    offsets = jnp.abs(jnp.arange(2 * REACH + 1, dtype=jnp.int32) - REACH)
    keep = offsets[None, :] <= row_widths[:, None]
    masked = jnp.where(keep[:, None, None, :], disco_basis, jnp.zeros_like(disco_basis))
    span = cols_dev + 2 * REACH
    table = jnp.pad(masked, ((0, 0), (0, basis_count), (0, 0), (0, span - masked.shape[3])))
    table = table.reshape(rows_dev * 2 * basis_count, 3 * span).astype(jnp.float32)
    lanes = lanes_of(2 * span)
    table = jnp.pad(table, ((0, 0), (0, lanes - 3 * span)))
    taps = jnp.pad(
        encoder_filter.astype(jnp.float32),
        ((0, 0), (0, basis_count), (0, lanes_of(cols_in) - tap_count)),
    ).reshape(rows_in * 2 * basis_count, -1)
    own_width = channels // lax.axis_size("ch")
    sizes = (lax.axis_size("lat"), lax.axis_size("lon"))
    plan = (rows_dev, cols_dev, basis_count, layers)
    outs = run_net(
        plan,
        sizes,
        input_field.reshape(rows_in * cols_in, in_width),
        taps,
        row_owner,
        encoder_weight,
        table,
        block_weights,
        cotangent.reshape(cell_count, channels),
    )
    current, gradient = (field.reshape(rows_dev, cols_dev, channels) for field in outs[:2])
    sums = [value.astype(jnp.float32) for value in outs[2:]]
    block_sum, encoder_sum = jnp.stack(sums[:-1]), sums[-1]
    cells_total = cell_count * lax.axis_size("lon") * lax.axis_size(("lat", "ch"))
    normalizer = 1.0 / math.sqrt(cells_total)
    block_grads = (block_sum * normalizer).reshape(layers, basis_count * channels, own_width)
    encoder_grad = encoder_sum * normalizer
    return (current, gradient, block_grads, encoder_grad)

HALO = 2
LANES = 128


def zeros_between(before, after, total, values):
    gap = jnp.zeros(values.shape[:-1] + (total - values.shape[-1],), values.dtype)
    return jnp.concatenate([values[..., before:], gap, values[..., :after]], axis=-1)


class Place:
    def __init__(self):
        self.lon, self.ch = lax.axis_size("lon"), lax.axis_size("ch")
        self.bands = lax.axis_size("lat") * self.ch
        self.z = lax.axis_index("lon")
        self.band = lax.axis_index("lat") * self.ch + lax.axis_index("ch")
        self.chunk = self.flip(self.band, self.z)
        self.count = self.bands * self.lon
        self.position = self.band * self.lon + self.chunk

    def flip(self, band, index):
        return index + lax.rem(band, 2) * (self.lon - 1 - 2 * index)

    def offset(self, chunk):
        return (chunk + self.lon - 1) // self.lon + (chunk + 1) // self.lon

    def device(self, band, chunk):
        return {
            "lat": band // self.ch,
            "ch": lax.rem(band, self.ch),
            "lon": self.flip(band, chunk),
        }

    def along_snake(self, step):
        position = lax.rem(self.position + step + self.count, self.count)
        return self.device(position // self.lon, lax.rem(position, self.lon))


def greet_part():
    barrier = pltpu.get_barrier_semaphore()
    count = 0
    for lat in range(lax.axis_size("lat")):
        for ch in range(lax.axis_size("ch")):
            for lon in range(lax.axis_size("lon")):
                if lat or ch or lon:
                    target = {**along("lat", lat), **along("ch", ch), **along("lon", lon)}
                    pl.semaphore_signal(barrier, inc=1, device_id=target, device_id_type=MESH)
                    count += 1
    pl.semaphore_wait(barrier, count)


class Regroup(Sender):
    def __init__(self, bufs):
        self.lines, self.rim_ssem, self.rim_rsem, self.own_sem = bufs[0], bufs[3], bufs[4], bufs[5]
        super().__init__(bufs[1:3])

    @staticmethod
    def scratch(lon, rows, cols, width):
        return [
            pltpu.VMEM((rows + 4, cols, width), BF16),
            pltpu.SemaphoreType.DMA((lon - 1,)),
            pltpu.SemaphoreType.DMA((lon - 1,)),
            pltpu.SemaphoreType.DMA((2,)),
            pltpu.SemaphoreType.DMA((2 * lon,)),
            pltpu.SemaphoreType.DMA,
        ]

    def start(self, place, source):
        self.place = place
        rows, piece = source.shape[0], source.shape[1]
        each = rows // place.lon
        columns = pl.ds(pl.multiple_of(place.z * piece, piece), piece)
        block = self.lines.at[pl.ds(1, each + 2), columns]
        for step in range(1, place.lon):
            peer = along("lon", step)
            chunk = place.flip(place.band, peer["lon"])
            first = chunk * each - place.offset(chunk)
            self.send(source.at[pl.ds(first, each + 2)], block, step - 1, peer)
        first = place.chunk * each - place.offset(place.chunk)
        self.own = pltpu.make_async_copy(source.at[pl.ds(first, each + 2)], block, self.own_sem)
        self.own.start()
        self.rims = []
        for side, (row, slot, step, chunk) in enumerate(
            ((rows - 1, 0, 1, 0), (0, each + 3, -1, place.lon - 1))
        ):
            band = lax.rem(place.band + step + place.bands, place.bands)
            copy = pltpu.make_async_remote_copy(
                src_ref=source.at[row],
                dst_ref=self.lines.at[slot, columns],
                send_sem=self.rim_ssem.at[side],
                recv_sem=self.rim_rsem.at[side * place.lon + place.z],
                device_id=place.device(band, chunk),
                device_id_type=MESH,
            )
            copy.start()
            self.rims.append(copy)
        self.source, self.piece, self.each = source, piece, each

    def finish(self):
        place = self.place
        self.settle()
        self.own.wait()
        for side, (slot, chunk) in enumerate(((0, 0), (self.each + 3, place.lon - 1))):

            @pl.when(place.chunk == chunk)
            def _():
                for z in range(place.lon):
                    pltpu.make_async_remote_copy(
                        src_ref=self.source.at[0],
                        dst_ref=self.lines.at[slot, pl.ds(z * self.piece, self.piece)],
                        send_sem=self.rim_ssem.at[side],
                        recv_sem=self.rim_rsem.at[side * place.lon + z],
                        device_id=along("lon", 0),
                        device_id_type=MESH,
                    ).wait_recv()

        for copy in self.rims:
            copy.wait_send()

    def row(self, index):
        return self.lines[index + 1 + self.place.offset(self.place.chunk)]


class Restore(Sender):
    def __init__(self, bufs):
        self.lines, self.own_sem = bufs[0], bufs[3]
        super().__init__(bufs[1:3])

    @staticmethod
    def scratch(lon, rows, cols, width):
        return [
            pltpu.VMEM((rows, cols, width), BF16),
            pltpu.SemaphoreType.DMA((lon - 1,)),
            pltpu.SemaphoreType.DMA((lon - 1,)),
            pltpu.SemaphoreType.DMA,
        ]

    def start(self, place, result):
        rows, piece = self.lines.shape[0], result.shape[1]
        target = result.at[pl.ds(place.chunk * rows, rows)]
        for step in range(1, place.lon):
            peer = along("lon", step)
            columns = pl.ds(pl.multiple_of(peer["lon"] * piece, piece), piece)
            self.send(self.lines.at[:, columns], target, step - 1, peer)
        columns = pl.ds(pl.multiple_of(place.z * piece, piece), piece)
        self.own = pltpu.make_async_copy(self.lines.at[:, columns], target, self.own_sem)
        self.own.start()

    def finish(self):
        self.settle()
        self.own.wait()


class Swap(Sender):
    def __init__(self, bufs):
        super().__init__(bufs)

    @staticmethod
    def scratch():
        return [pltpu.SemaphoreType.DMA((2,)), pltpu.SemaphoreType.DMA((2,))]

    def start(self, place, buffer, slot_rows, own, halo):
        def part(first):
            return buffer.at[pl.ds(first * slot_rows, halo * slot_rows)]

        self.send(part(own), part(0), 0, place.along_snake(1))
        self.send(part(halo), part(halo + own), 1, place.along_snake(-1))


def zero_outside(place, buffer, first, last, size):
    @pl.when(place.position == 0)
    def _():
        buffer[first : first + size, :] = jnp.zeros((size, buffer.shape[1]), buffer.dtype)

    @pl.when(place.position == place.count - 1)
    def _():
        buffer[last : last + size, :] = jnp.zeros((size, buffer.shape[1]), buffer.dtype)


def circulant(line, rows, stride):
    return pltpu.roll(jnp.broadcast_to(line, (rows, LANES)), 0, 1, stride=stride, stride_axis=0)


def silu_slope(pre):
    sigma = 1.0 / (1.0 + jnp.exp(-pre))
    return sigma * (1.0 + pre * (1.0 - sigma))


def chunk_kernel(plan, *refs):
    rows, cols, basis_count, layers = plan
    field, taps, owner, encoder_weight, base, weights, cotangent = refs[:7]
    state_out, latent_grad = refs[7:9]
    results = refs[9 : 10 + layers]
    rest = list(refs[10 + layers :])
    table, lines, bands, turned, latent_in, state, features, preact, steps, errs = rest[:10]
    rest = rest[10:]
    inputs, arriving = Regroup(rest[:6]), Regroup(rest[6:12])
    leaving = [Restore(rest[12:16]), Restore(rest[16:20])]
    swaps = [Swap(rest[20 + 2 * n : 22 + 2 * n]) for n in range(4)]
    rest = rest[28:]
    sums = []
    for index in range(layers + 1):
        sums.append(GradSum(results[index], rest[:11]))
        rest = rest[11:]
    channels = state.shape[1]
    width = field.shape[2]
    block = basis_count * cols
    ext = rows + 2 * HALO
    progress = [0] * (layers + 1)

    def advance(index):
        getattr(sums[index], STAGES[progress[index]])()
        progress[index] += 1

    greet_part()
    place = Place()
    inputs.start(place, field)
    arriving.start(place, cotangent)

    first = place.position * rows
    rows_in = 2 * rows
    start_in = place.chunk * rows_in
    tall = taps.shape[1]
    high = base.shape[1]
    lines[tall : (rows_in + 1) * tall, :] = taps[pl.ds(start_in, rows_in)].reshape(
        rows_in * tall, LANES
    )
    before = jnp.where(owner[start_in] == first - 1, 1.0, 0.0)
    after = jnp.where(owner[start_in + rows_in - 1] == first + rows, 1.0, 0.0)
    lines[(rows_in + 2) * tall : (rows_in + 3) * tall, :] = taps[start_in] * before
    lines[(rows_in + 3) * tall :, :] = taps[start_in + rows_in - 1] * after
    table[HALO * high : (HALO + rows) * high, :] = base[pl.ds(place.chunk * rows, rows)].reshape(
        rows * high, LANES
    )
    swaps[0].start(place, table, high, rows, HALO)
    swaps[1].send(
        lines.at[pl.ds((rows_in + 3) * tall, tall)],
        lines.at[pl.ds(0, tall)],
        0,
        place.along_snake(1),
    )
    swaps[1].send(
        lines.at[pl.ds((rows_in + 2) * tall, tall)],
        lines.at[pl.ds((rows_in + 1) * tall, tall)],
        1,
        place.along_snake(-1),
    )
    swaps[0].settle()

    lane = lax.broadcasted_iota(jnp.int32, (cols, LANES), 1)

    def make_band(row, carry):
        values = table[aligned(row, high), :]
        for k in range(basis_count):
            parts = [
                circulant(values[r * basis_count + k][None, :], cols, 1) for r in range(3)
            ]
            start = pl.multiple_of(row * block + k * cols, cols)
            bands[pl.ds(start, cols), :LANES] = jnp.where(lane < cols, parts[0], parts[1]).astype(BF16)
            bands[pl.ds(start, cols), LANES:] = parts[2].astype(BF16)
        other = bands[aligned(row, block), :].T
        for r in range(3):
            turned[aligned(row + r, cols), (2 - r) * block : (3 - r) * block] = other[
                r * cols : (r + 1) * cols
            ]
        return carry

    lax.fori_loop(0, ext, make_band, 0)
    swaps[1].settle()
    inputs.finish()

    def filtered(row):
        values = lines[aligned(row + 1, tall), :] if not isinstance(row, int) else lines[
            (row + 1) * tall : (row + 2) * tall, :
        ]
        lhs = jnp.concatenate(
            [circulant(values[k][None, :], cols, 2) for k in range(basis_count)], axis=0
        ).astype(BF16)
        out = jnp.dot(lhs, inputs.row(row), preferred_element_type=F32)
        return out.astype(BF16).astype(F32)

    filters = [filtered(row) for row in range(-1, rows_in + 1)]
    for row in range(rows):
        total = None
        for step in range(-1, 3):
            source = 2 * row + step
            term = filters[source + 1]
            if 0 <= source < rows_in:
                term = term * jnp.where(owner[start_in + source] == first + row, 1.0, 0.0)
            total = term if total is None else total + term
        total = total.astype(BF16)
        for k in range(basis_count):
            latent_in[row * cols : (row + 1) * cols, k * width : (k + 1) * width] = total[
                k * cols : (k + 1) * cols
            ]
    own = pl.ds(HALO * cols, rows * cols)
    state[own, :] = jnp.dot(
        latent_in[...], encoder_weight[...], preferred_element_type=F32
    ).astype(BF16)
    swaps[2].start(place, state, cols, rows, HALO)
    swaps[2].settle()
    zero_outside(place, state, 0, (HALO + rows) * cols, HALO * cols)

    for layer in range(layers):
        low, top = layer + 1, ext - layer - 1
        for row in range(low, top):
            out = jnp.dot(
                bands[row * block : (row + 1) * block, : 3 * cols],
                state[(row - 1) * cols : (row + 2) * cols, :],
                preferred_element_type=F32,
            ).astype(BF16)
            for k in range(basis_count):
                features[layer, row * cols : (row + 1) * cols, k * channels : (k + 1) * channels] = out[
                    k * cols : (k + 1) * cols
                ]
        span = pl.ds(low * cols, (top - low) * cols)
        pre = jnp.dot(features[layer, span, :], weights[layer], preferred_element_type=F32)
        preact[layer, span, :] = pre
        new = state[span, :].astype(F32) + pre / (1.0 + jnp.exp(-pre))
        state[span, :] = new.astype(BF16)
        if layer < layers - 1:
            zero_outside(place, state, low * cols, (top - 1) * cols, cols)

    gradient = jnp.concatenate([arriving_row(arriving, row) for row in range(-1, rows + 1)], axis=0)
    last = layers - 1
    act = gradient[cols : (rows + 1) * cols] * silu_slope(preact[last, own, :])
    steps[last, own, :] = act.astype(BF16)
    swaps[3].start(place, steps.at[last], cols, rows, HALO)
    leaving[0].lines[...] = state[own, :].reshape(rows, cols, channels)
    leaving[0].start(place, state_out)

    def errors(layer, low, top):
        for k in range(basis_count):
            out = lax.dot_general(
                steps[layer, low * cols : top * cols, :],
                weights[layer, k * channels : (k + 1) * channels, :],
                (((1,), (1,)), ((), ())),
                preferred_element_type=F32,
            ).astype(BF16)
            for row in range(low, top):
                start = row * block + k * cols
                errs[start : start + cols, :] = out[(row - low) * cols : (row - low + 1) * cols]

    def spread(row):
        return jnp.dot(
            turned[(row + 1) * cols : (row + 2) * cols, :],
            errs[(row - 1) * block : (row + 2) * block, :],
            preferred_element_type=F32,
        )

    sums[last].source[...] = rows_product(features[last, own, :], steps[last, own, :]).astype(BF16)
    advance(last)
    errors(last, HALO, HALO + rows)
    swaps[3].settle()
    zero_outside(place, steps.at[last], 0, (HALO + rows) * cols, HALO * cols)
    errors(last, 0, HALO)
    errors(last, HALO + rows, ext)
    advance(last)
    back = [gradient[(row - 1) * cols : row * cols] + spread(row) for row in range(1, ext - 1)]
    gradient = jnp.concatenate(back, axis=0).astype(BF16).astype(F32)
    span = pl.ds(cols, (ext - 2) * cols)
    steps[0, span, :] = (gradient * silu_slope(preact[0, span, :])).astype(BF16)
    zero_outside(place, steps.at[0], cols, (ext - 2) * cols, cols)
    sums[0].source[...] = rows_product(features[0, own, :], steps[0, own, :]).astype(BF16)
    advance(0)
    advance(last)
    errors(0, 1, ext - 1)
    back = [
        gradient[(row - 1) * cols : row * cols] + spread(row) for row in range(HALO, HALO + rows)
    ]
    final = jnp.concatenate(back, axis=0).astype(BF16)
    leaving[1].lines[...] = final.reshape(rows, cols, channels)
    leaving[1].start(place, latent_grad)
    sums[layers].source[...] = rows_product(latent_in[...], final).astype(BF16)
    advance(layers)
    while min(progress) < len(STAGES):
        for index in [last, 0, layers]:
            if progress[index] < len(STAGES):
                advance(index)
    for part in leaving:
        part.finish()


def arriving_row(arriving, row):
    if row == -1:
        arriving.finish()
    return arriving.row(row).astype(F32)


def run_chunks(plan, sizes, field_in, taps, owner, encoder_weight, base, weights, cotangent):
    rows, cols, basis_count, layers = plan
    lat, lon = sizes
    channels = weights.shape[2]
    features = basis_count * channels
    in_features = encoder_weight.shape[0]
    ext = rows + 2 * HALO
    heights = [features] * layers + [in_features]
    block = basis_count * cols
    scratch = [
        pltpu.VMEM((ext * base.shape[1], LANES), F32),
        pltpu.VMEM(((2 * rows + 4) * taps.shape[1], LANES), F32),
        pltpu.VMEM((ext * block, 2 * LANES), BF16),
        pltpu.VMEM(((ext + 2) * cols, 3 * block), BF16),
        pltpu.VMEM((rows * cols, in_features), BF16),
        pltpu.VMEM((ext * cols, channels), BF16),
        pltpu.VMEM((layers, ext * cols, features), BF16),
        pltpu.VMEM((layers, ext * cols, channels), F32),
        pltpu.VMEM((layers, ext * cols, channels), BF16),
        pltpu.VMEM((ext * block, channels), BF16),
    ]
    scratch += Regroup.scratch(lon, 2 * rows, field_in.shape[1] * lon, field_in.shape[2])
    scratch += Regroup.scratch(lon, rows, cols, channels)
    for _ in range(2):
        scratch += Restore.scratch(lon, rows, cols, channels)
    for _ in range(4):
        scratch += Swap.scratch()
    for height in heights:
        scratch += GradSum.scratch(sizes, height, channels)
    vmem = pl.BlockSpec(memory_space=pltpu.VMEM)
    out = jax.ShapeDtypeStruct(cotangent.shape, BF16)
    grads = [jax.ShapeDtypeStruct((height, channels // 2), BF16) for height in heights]
    return pl.pallas_call(
        functools.partial(chunk_kernel, plan),
        out_shape=[out, out] + grads,
        in_specs=[vmem, vmem, pl.BlockSpec(memory_space=pltpu.SMEM)] + [vmem] * 4,
        out_specs=[vmem] * (3 + layers),
        scratch_shapes=scratch,
        compiler_params=pltpu.CompilerParams(
            collective_id=1, has_side_effects=True, vmem_limit_bytes=56 << 20
        ),
    )(field_in, taps, owner, encoder_weight, base, weights, cotangent)


def fits_chunks(rows_dev, cols_in, cols_dev, layers):
    lon = lax.axis_size("lon")
    return (
        layers == HALO
        and rows_dev % lon == 0
        and rows_dev // lon >= HALO
        and lon > 1
        and cols_in * lon == LANES
        and 2 * cols_dev * lon == LANES
    )


def per_device_chunks(
    input_field,
    encoder_filter,
    row_owner,
    encoder_weight,
    disco_basis,
    row_widths,
    block_weights,
    cotangent,
):
    rows_in, cols_in, _ = input_field.shape
    lat, lon = lax.axis_size("lat"), lax.axis_size("lon")
    rows_dev, cols = rows_in // 2, cols_in // 2 * lon
    basis_count = encoder_filter.shape[1]
    channels, layers = block_weights.shape[2], block_weights.shape[0]
    offsets = jnp.abs(jnp.arange(2 * REACH + 1, dtype=jnp.int32) - REACH)
    keep = offsets[None, :] <= row_widths[:, None]
    masked = jnp.where(keep[:, None, None, :], disco_basis, jnp.zeros_like(disco_basis))
    masked = masked.transpose(0, 2, 1, 3).reshape(rows_dev, 3 * basis_count, -1).astype(F32)
    base = zeros_between(REACH, REACH, cols, masked)
    base = jnp.concatenate([base, base], axis=2)
    base = jnp.pad(base, ((0, 0), (0, -base.shape[1] % 8), (0, 0)))
    taps = zeros_between(TAP_REACH, TAP_REACH, LANES, encoder_filter.astype(F32))
    taps = jnp.pad(taps, ((0, 0), (0, -basis_count % 8), (0, 0)))
    plan = (rows_dev // lon, cols, basis_count, layers)
    outs = run_chunks(
        plan, (lat, lon), input_field, taps, row_owner, encoder_weight, base, block_weights, cotangent
    )
    sums = [value.astype(F32) for value in outs[2:]]
    cells_total = rows_dev * lax.axis_size(("lat", "ch")) * cols
    normalizer = 1.0 / math.sqrt(cells_total)
    return (outs[0], outs[1], jnp.stack(sums[:-1]) * normalizer, sums[-1] * normalizer)


def solution(mesh):
    placed = (
        P(("ens", "lat", "ch"), "lon", None),
        P(("lat", "ch"), None, None),
        P(("ens", "lat", "ch")),
        P(),
        P(("lat", "ch"), None, None, None),
        P(("lat", "ch")),
        P(),
        P(("ens", "lat", "ch"), "lon", None),
    )
    return jax.shard_map(
        per_device,
        mesh=mesh,
        in_specs=placed,
        out_specs=(
            P(("ens", "lat", "ch"), "lon", None),
            P(("ens", "lat", "ch"), "lon", None),
            P("ens", None, "ch"),
            P("ens", "ch"),
        ),
        check_vma=False,
    )
```

```python
import functools
import math

import jax
import jax.numpy as jnp
from jax import lax
from jax.experimental import pallas as pl
from jax.experimental.pallas import tpu as pltpu
from jax.sharding import PartitionSpec as P

REACH = 8
TAP_REACH = 2
TILE = 16
MESH = pl.DeviceIdType.MESH
BF16 = jnp.bfloat16
F32 = jnp.float32


def along(axis, steps):
    count = lax.axis_size(axis)
    return {axis: lax.rem(lax.axis_index(axis) + steps + count, count)}


def neighbour(row_step, col_step):
    ch_count = lax.axis_size("ch")
    bands = lax.axis_size("lat") * ch_count
    band = lax.axis_index("lat") * ch_count + lax.axis_index("ch")
    band = lax.rem(band + row_step + bands, bands)
    target = {}
    if row_step:
        target = {"lat": band // ch_count, "ch": lax.rem(band, ch_count)}
    if col_step:
        target.update(along("lon", col_step))
    return target


AROUND = [(r, c) for r in (-1, 0, 1) for c in (-1, 0, 1) if r or c]


def greet():
    targets = [neighbour(r, c) for r, c in AROUND]
    for axis in ("ch", "lat", "lon"):
        targets += [along(axis, step) for step in range(1, lax.axis_size(axis))]
    barrier = pltpu.get_barrier_semaphore()
    for target in targets:
        pl.semaphore_signal(barrier, inc=1, device_id=target, device_id_type=MESH)
    pl.semaphore_wait(barrier, len(targets))


class Sender:
    def __init__(self, sems):
        self.ssem, self.rsem = sems
        self.pending = []

    def send(self, source, target, slot, device):
        copy = pltpu.make_async_remote_copy(
            src_ref=source,
            dst_ref=target,
            send_sem=self.ssem.at[slot],
            recv_sem=self.rsem.at[slot],
            device_id=device,
            device_id_type=MESH,
        )
        copy.start()
        self.pending.append(copy)

    def settle(self):
        for copy in self.pending:
            copy.wait()
        self.pending = []


class GradSum(Sender):
    def __init__(self, result, bufs):
        super().__init__(bufs[-2:])
        self.result = result
        self.source, self.rec_ch, self.part, self.rec_lat, self.strip, self.rec_pair, self.half, self.rec_far, self.piece = bufs[:-2]
        self.width = self.part.shape[1]
        self.lat, self.lon = lax.axis_size("lat"), lax.axis_size("lon")
        self.height = self.strip.shape[0]
        self.span = self.piece.shape[0]
        self.pair = self.height // self.span
        self.far = self.lon // self.pair
        self.side = lax.rem(lax.axis_index("lon"), self.pair)

    @staticmethod
    def scratch(sizes, rows, columns):
        lat, lon = sizes
        width = columns // 2
        height = rows // lat
        pair = 2 if lon % 2 == 0 and height % (2 * TILE) == 0 else 1
        span, far = height // pair, lon // pair
        count = 1 + 2 * (lat - 1) + 2 * (pair - 1) + far - 1
        return [
            pltpu.VMEM((rows, columns), BF16),
            pltpu.VMEM((rows, width), BF16),
            pltpu.VMEM((rows, width), BF16),
            pltpu.VMEM((lat - 1, height, width), BF16),
            pltpu.VMEM((height, width), BF16),
            pltpu.VMEM((span, width), BF16),
            pltpu.VMEM((span, width), BF16),
            pltpu.VMEM((far - 1, span, width), BF16),
            pltpu.VMEM((span, width), BF16),
            pltpu.SemaphoreType.DMA((count,)),
            pltpu.SemaphoreType.DMA((count,)),
        ]

    def columns(self, half):
        return pl.ds(pl.multiple_of(half * self.width, self.width), self.width)

    @staticmethod
    def stretch(owner, size):
        return pl.ds(pl.multiple_of(owner * size, size), size)

    def start_ch(self):
        other = 1 - lax.axis_index("ch")
        self.send(self.source.at[:, self.columns(other)], self.rec_ch, 0, {"ch": other})

    def start_lat(self):
        self.settle()
        own = self.source[:, self.columns(lax.axis_index("ch"))].astype(F32)
        self.part[...] = (own + self.rec_ch[...].astype(F32)).astype(BF16)
        for step in range(1, self.lat):
            peer = along("lat", step)
            rows = self.stretch(peer["lat"], self.height)
            self.send(self.part.at[rows], self.rec_lat.at[step - 1], step, peer)

    def start_lon(self):
        self.settle()
        total = self.part[self.stretch(lax.axis_index("lat"), self.height), :].astype(F32)
        for step in range(1, self.lat):
            total = total + self.rec_lat[step - 1].astype(F32)
        self.strip[...] = total.astype(BF16)
        if self.pair > 1:
            rows = self.stretch(1 - self.side, self.span)
            self.send(self.strip.at[rows], self.rec_pair, self.lat, along("lon", 1 - 2 * self.side))

    def start_far(self):
        self.settle()
        total = self.strip[self.stretch(self.side, self.span), :].astype(F32)
        if self.pair > 1:
            total = total + self.rec_pair[...].astype(F32)
        self.half[...] = total.astype(BF16)
        for step in range(1, self.far):
            self.send(
                self.half, self.rec_far.at[step - 1], self.lat + step, along("lon", self.pair * step)
            )

    def gather_lon(self):
        self.settle()
        total = self.half[...].astype(F32)
        for step in range(1, self.far):
            total = total + self.rec_far[step - 1].astype(F32)
        self.piece[...] = total.astype(BF16)
        offset = lax.axis_index("lat") * self.height + self.side * self.span
        rows = pl.ds(pl.multiple_of(offset, TILE), self.span)
        self.result[rows, :] = self.piece[...]
        if self.pair > 1:
            slot = self.lat + self.far
            self.send(self.piece, self.result.at[rows], slot, along("lon", 1 - 2 * self.side))

    def gather_lat(self):
        self.settle()
        rows = self.stretch(lax.axis_index("lat"), self.height)
        for step in range(1, self.lat):
            slot = self.lat + self.far + self.pair - 2 + step
            self.send(self.result.at[rows], self.result.at[rows], slot, along("lat", step))

    def finish(self):
        self.settle()


STAGES = ("start_ch", "start_lat", "start_lon", "start_far", "gather_lon", "gather_lat", "finish")


class Halo(Sender):
    def __init__(self, bufs):
        super().__init__(bufs[-2:])
        self.out_side, self.out_row, self.in_side, self.in_row = bufs[:-2]

    @staticmethod
    def scratch(rows, cols, width, row_blocks):
        return [
            pltpu.VMEM((2, rows * REACH, width), BF16),
            pltpu.VMEM((row_blocks, cols, width), BF16),
            pltpu.VMEM((2, rows * REACH, width), BF16),
            pltpu.VMEM((6, cols, width), BF16),
            pltpu.SemaphoreType.DMA((8,)),
            pltpu.SemaphoreType.DMA((8,)),
        ]

    def start(self, row_block_of):
        self.send(self.out_side.at[0], self.in_side.at[1], 0, neighbour(0, -1))
        self.send(self.out_side.at[1], self.in_side.at[0], 1, neighbour(0, 1))
        slot = 2
        for row_step in (-1, 1):
            for col_step in (-1, 0, 1):
                place = (0 if row_step == 1 else 3) + 1 - col_step
                self.send(
                    self.out_row.at[row_block_of(row_step, col_step)],
                    self.in_row.at[place],
                    slot,
                    neighbour(row_step, col_step),
                )
                slot += 1


def edge_flags():
    ch_count = lax.axis_size("ch")
    bands = lax.axis_size("lat") * ch_count
    band = lax.axis_index("lat") * ch_count + lax.axis_index("ch")
    return band > 0, band < bands - 1


def extend(halo, state, ext, rows, cols):
    span = cols + 2 * REACH
    west, east = halo.in_side[0].astype(F32), halo.in_side[1].astype(F32)
    for row in range(rows):
        low, high = row * REACH, (row + 1) * REACH
        line = jnp.concatenate(
            [west[low:high], state[row * cols : (row + 1) * cols], east[low:high]], axis=0
        )
        ext[(row + 1) * span : (row + 2) * span, :] = line.astype(BF16)
    for first, row, flag in zip((0, 3), (0, rows + 1), edge_flags()):
        line = jnp.concatenate(
            [
                halo.in_row[first].astype(F32)[cols - REACH :],
                halo.in_row[first + 1].astype(F32),
                halo.in_row[first + 2].astype(F32)[:REACH],
            ],
            axis=0,
        )
        ext[row * span : (row + 1) * span, :] = jnp.where(flag, line, 0.0).astype(BF16)


def send_state(halo, state, rows, cols):
    pieces = [
        [state[r * cols : r * cols + REACH] for r in range(rows)],
        [state[(r + 1) * cols - REACH : (r + 1) * cols] for r in range(rows)],
    ]
    for side in range(2):
        halo.out_side[side] = jnp.concatenate(pieces[side], axis=0).astype(BF16)
    halo.out_row[0] = state[:cols].astype(BF16)
    halo.out_row[1] = state[(rows - 1) * cols :].astype(BF16)
    halo.start(lambda row_step, col_step: 0 if row_step == -1 else 1)


def send_spread(halo, spread, rows, cols):
    span = cols + 2 * REACH
    west = [spread[(r + 1) * span : (r + 1) * span + REACH, :] for r in range(rows)]
    east = [spread[(r + 2) * span - REACH : (r + 2) * span, :] for r in range(rows)]
    halo.out_side[0] = jnp.concatenate(west, axis=0).astype(BF16)
    halo.out_side[1] = jnp.concatenate(east, axis=0).astype(BF16)
    for block, row in enumerate((0, rows + 1)):
        base = row * span
        halo.out_row[2 * block] = spread[base + REACH : base + REACH + cols, :].astype(BF16)
        corners = [spread[base : base + REACH, :], spread[base + span - REACH : base + span, :]]
        if cols > 2 * REACH:
            corners.insert(1, jnp.zeros((cols - 2 * REACH, spread.shape[1]), F32))
        halo.out_row[2 * block + 1] = jnp.concatenate(corners, axis=0).astype(BF16)
    halo.start(
        lambda row_step, col_step: (0 if row_step == -1 else 2) + (1 if col_step else 0)
    )


def take_spread(halo, spread, gradient, rows, cols):
    span = cols + 2 * REACH
    west, east = halo.in_side[0].astype(F32), halo.in_side[1].astype(F32)
    outer = {}
    for first, row, flag in zip((0, 3), (0, rows - 1), edge_flags()):
        line = halo.in_row[first + 1].astype(F32)
        rim_west = halo.in_row[first].astype(F32)[cols - REACH :]
        rim_east = halo.in_row[first + 2].astype(F32)[:REACH]
        rims = [rim_west, rim_east]
        if cols > 2 * REACH:
            rims.insert(1, jnp.zeros((cols - 2 * REACH, line.shape[1]), F32))
        outer[row] = jnp.where(flag, line + jnp.concatenate(rims, axis=0), 0.0)
    result = []
    for row in range(rows):
        low, high = row * REACH, (row + 1) * REACH
        rims = [west[low:high], east[low:high]]
        if cols > 2 * REACH:
            rims.insert(1, jnp.zeros((cols - 2 * REACH, west.shape[1]), F32))
        base = (row + 1) * span + REACH
        line = spread[base : base + cols, :] + jnp.concatenate(rims, axis=0)
        if row in outer:
            line = line + outer[row]
        result.append(gradient[row * cols : (row + 1) * cols].astype(F32) + line)
    return result


def aligned(index, size):
    return pl.ds(pl.multiple_of(index * size, size), size)


GROUP = 16


def over_rows(rows, body):
    group = GROUP if rows % GROUP == 0 else 1

    def step(index, carry):
        for inner in range(group):
            body(index * group + inner)
        return carry

    lax.fori_loop(0, rows // group, step, 0)


def make_bands(base, bands, rows, cols, basis_count):
    width = base.shape[1]

    def one(row):
        table = base[aligned(row, 2 * basis_count), :]
        for k in range(basis_count):
            line = jnp.broadcast_to(table[k : k + 1], (cols, width))
            moved = pltpu.roll(line, 0, 1, stride=1, stride_axis=0)
            start = pl.multiple_of((row * basis_count + k) * cols, cols)
            bands[pl.ds(start, cols), :] = moved.astype(BF16)

    over_rows(rows, one)


def stencil(bands, ext, features, rows, cols, basis_count):
    span = cols + 2 * REACH
    channels = ext.shape[1]

    def one(row):
        lhs = bands[aligned(row, basis_count * cols), :][:, : 3 * span]
        rhs = ext[pl.ds(pl.multiple_of(row * span, span), 3 * span), :]
        out = jnp.dot(lhs, rhs, preferred_element_type=F32).astype(BF16)
        for k in range(basis_count):
            features[aligned(row, cols), k * channels : (k + 1) * channels] = out[
                k * cols : (k + 1) * cols
            ]

    over_rows(rows, one)


def adjoint(bands, errs, spread, rows, cols, basis_count):
    span = cols + 2 * REACH
    spread[...] = jnp.zeros_like(spread)

    def one(row):
        lhs = bands[aligned(row, basis_count * cols), :][:, : 3 * span]
        rhs = errs[aligned(row, basis_count * cols), :]
        out = lax.dot_general(lhs, rhs, (((0,), (0,)), ((), ())), preferred_element_type=F32)
        place = pl.ds(pl.multiple_of(row * span, span), 3 * span)
        spread[place, :] = spread[place, :] + out

    over_rows(rows, one)


def rows_product(left, right):
    return lax.dot_general(left, right, (((0,), (0,)), ((), ())), preferred_element_type=F32)
TAPS_LEFT = TAP_REACH


class InputHalo(Sender):
    def __init__(self, bufs):
        super().__init__(bufs[-2:])
        (
            self.edges,
            self.out_cols,
            self.out_table,
            self.in_cols,
            self.in_row,
            self.in_table,
            self.in_tile,
        ) = bufs[:-2]

    @staticmethod
    def scratch(rows_in, cols_in, width, table_rows, lanes):
        return [
            pltpu.VMEM((3, rows_in, width), F32),
            pltpu.VMEM((3, rows_in, width), BF16),
            pltpu.VMEM((2, table_rows, lanes), F32),
            pltpu.VMEM((3, rows_in, width), BF16),
            pltpu.VMEM((2, cols_in, width), BF16),
            pltpu.VMEM((2, table_rows, lanes), F32),
            pltpu.VMEM((4, TILE, width), BF16),
            pltpu.SemaphoreType.DMA((10,)),
            pltpu.SemaphoreType.DMA((10,)),
        ]

    def start(self, field, table, owner, rows_in, cols_in):
        first = own_first_row(rows_in // 2)
        table_rows = self.out_table.shape[1]
        for block, row, target in ((0, 0, first - 1), (1, rows_in - 1, first + rows_in // 2)):
            feeds = jnp.where(owner[row] == target, 1.0, 0.0)
            self.out_table[block] = table[row * table_rows : (row + 1) * table_rows, :] * feeds
        last = (rows_in - 1) * cols_in
        lines = (field.at[pl.ds(0, cols_in)], field.at[pl.ds(last, cols_in)])
        slot = 0
        for block, row_step in ((0, -1), (1, 1)):
            self.send(lines[block], self.in_row.at[1 - block], slot, neighbour(row_step, 0))
            base = block * last
            west = field.at[pl.ds(base, TILE)]
            east = field.at[pl.ds(base + cols_in - TILE, TILE)]
            place = 2 * (1 - block)
            self.send(west, self.in_tile.at[place + 1], slot + 1, neighbour(row_step, -1))
            self.send(east, self.in_tile.at[place], slot + 2, neighbour(row_step, 1))
            slot += 3

        def one(row):
            low = field[pl.ds(pl.multiple_of(row * cols_in, TILE), TILE), :].astype(F32)
            start = pl.multiple_of(row * cols_in + cols_in - TILE, TILE)
            high = field[pl.ds(start, TILE), :].astype(F32)
            self.edges[0, pl.ds(row, 1), :] = high[TILE - 2 : TILE - 1]
            self.edges[1, pl.ds(row, 1), :] = high[TILE - 1 : TILE]
            self.edges[2, pl.ds(row, 1), :] = low[0:1]

        over_rows(rows_in, one)
        self.out_cols[...] = self.edges[...].astype(BF16)
        self.send(self.out_cols.at[pl.ds(0, 2)], self.in_cols.at[pl.ds(0, 2)], 6, neighbour(0, 1))
        self.send(self.out_cols.at[2], self.in_cols.at[2], 7, neighbour(0, -1))
        self.send(self.out_table.at[0], self.in_table.at[1], 8, neighbour(-1, 0))
        self.send(self.out_table.at[1], self.in_table.at[0], 9, neighbour(1, 0))


def own_first_row(rows):
    return (lax.axis_index("lat") * lax.axis_size("ch") + lax.axis_index("ch")) * rows


def tap_matrix(table, basis_count, cols, cols_in):
    lanes = table.shape[1]
    blocks = []
    for k in range(basis_count):
        line = jnp.broadcast_to(table[k : k + 1], (cols, lanes))
        moved = pltpu.roll(line, 0, 1, stride=2, stride_axis=0)
        wrapped = pltpu.roll(moved, cols_in + TILE - TAPS_LEFT, 1)
        moved = pltpu.roll(moved, lanes - TAPS_LEFT, 1)
        lane = lax.broadcasted_iota(jnp.int32, (cols, lanes), 1)
        at_end = (lane >= cols_in + TILE - TAPS_LEFT) & (lane < cols_in + TILE)
        blocks.append(jnp.where(at_end, wrapped, moved))
    return jnp.concatenate(blocks, axis=0)[:, : cols_in + TILE].astype(BF16)


def filtered_row(table, line, left_two, left_one, right, basis_count, cols, cols_in):
    width = line.shape[1]
    place = lax.broadcasted_iota(jnp.int32, (TILE, width), 0)
    tile = jnp.where(place == 0, jnp.broadcast_to(right, (TILE, width)), 0.0)
    tile = jnp.where(place == TILE - 2, jnp.broadcast_to(left_two, (TILE, width)), tile)
    tile = jnp.where(place == TILE - 1, jnp.broadcast_to(left_one, (TILE, width)), tile)
    rhs = jnp.concatenate([line, tile.astype(BF16)], axis=0)
    lhs = tap_matrix(table, basis_count, cols, cols_in)
    return jnp.dot(lhs, rhs, preferred_element_type=F32).astype(BF16)


def finish_encode(halo, field, table, owner, filtered, latent_in, plan, rows_in, cols_in):
    rows, cols, basis_count, _ = plan
    table_rows = halo.out_table.shape[1]
    block = basis_count * cols
    width = field.shape[1]
    halo.settle()
    halo.edges[...] = halo.in_cols[...].astype(F32)

    def one(row):
        sides = [halo.edges[index, pl.ds(row, 1), :] for index in range(3)]
        line = field[aligned(row, cols_in), :]
        taps = table[aligned(row, table_rows), :]
        filtered[aligned(row + 1, block), :] = filtered_row(
            taps, line, *sides, basis_count, cols, cols_in
        )

    over_rows(rows_in, one)
    for side, row in ((0, 0), (1, rows_in + 1)):
        west = halo.in_tile[2 * side].astype(F32)
        east = halo.in_tile[2 * side + 1].astype(F32)
        filtered[row * block : (row + 1) * block, :] = filtered_row(
            halo.in_table[side],
            halo.in_row[side],
            west[TILE - 2 : TILE - 1],
            west[TILE - 1 : TILE],
            east[0:1],
            basis_count,
            cols,
            cols_in,
        )
    first = own_first_row(rows)
    for row in range(rows):
        total = None
        for offset in range(-1, 3):
            source = 2 * row + offset
            term = filtered[(source + 1) * block : (source + 2) * block, :].astype(F32)
            if 0 <= source < rows_in:
                term = term * jnp.where(owner[source] == first + row, 1.0, 0.0)
            total = term if total is None else total + term
        total = total.astype(BF16)
        for k in range(basis_count):
            latent_in[row * cols : (row + 1) * cols, k * width : (k + 1) * width] = total[
                k * cols : (k + 1) * cols
            ]


def lanes_of(count):
    return -(-(count + 2 * TILE) // 128) * 128


def net_kernel(plan, *refs):
    rows, cols, basis_count, layers = plan
    field, table, owner, encoder_weight, base, weights, cotangent = refs[:7]
    state_out, latent_grad = refs[7:9]
    results = refs[9 : 10 + layers]
    rest = list(refs[10 + layers :])
    bands, ext, spread, errs, features, preact, filtered, latent_in = rest[:8]
    input_halo = InputHalo(rest[8:17])
    rest = rest[17:]
    halos = []
    for _ in range(2 * layers):
        halos.append(Halo(rest[:6]))
        rest = rest[6:]
    sums = []
    for index in range(layers + 1):
        sums.append(GradSum(results[index], rest[:11]))
        rest = rest[11:]
    channels = ext.shape[1]
    progress = [0] * (layers + 1)

    def advance(index):
        getattr(sums[index], STAGES[progress[index]])()
        progress[index] += 1

    greet()
    rows_in = owner.shape[0]
    cols_in = field.shape[0] // rows_in
    input_halo.start(field, table, owner, rows_in, cols_in)
    make_bands(base, bands, rows, cols, basis_count)
    finish_encode(input_halo, field, table, owner, filtered, latent_in, plan, rows_in, cols_in)
    state = jnp.dot(latent_in[...], encoder_weight[...], preferred_element_type=F32)
    state = state.astype(BF16).astype(F32)
    for layer in range(layers):
        send_state(halos[layer], state, rows, cols)
        halos[layer].settle()
        extend(halos[layer], state, ext, rows, cols)
        stencil(bands, ext, features.at[layer], rows, cols, basis_count)
        pre = jnp.dot(features[layer], weights[layer], preferred_element_type=F32)
        preact[layer] = pre
        state = (state + pre / (1.0 + jnp.exp(-pre))).astype(BF16).astype(F32)
    state_out[...] = state.astype(BF16)

    gradient = cotangent[...].astype(F32)
    for layer in reversed(range(layers)):
        pre = preact[layer]
        sigma = 1.0 / (1.0 + jnp.exp(-pre))
        act_grad = (gradient * sigma * (1.0 + pre * (1.0 - sigma))).astype(BF16)
        for k in range(basis_count):
            block = weights[layer, k * channels : (k + 1) * channels, :]
            out = lax.dot_general(
                act_grad, block, (((1,), (1,)), ((), ())), preferred_element_type=F32
            ).astype(BF16)
            for row in range(rows):
                start = (row * basis_count + k) * cols
                errs[start : start + cols, :] = out[row * cols : (row + 1) * cols]
        adjoint(bands, errs, spread, rows, cols, basis_count)
        halo = halos[layers + layer]
        send_spread(halo, spread, rows, cols)
        sums[layer].source[...] = rows_product(features[layer], act_grad).astype(BF16)
        for other in range(layers - 1, layer - 1, -1):
            advance(other)
        halo.settle()
        for other in range(layers - 1, layer - 1, -1):
            advance(other)
        lines = take_spread(halo, spread, gradient, rows, cols)
        gradient = jnp.concatenate(lines, axis=0).astype(BF16).astype(F32)
    latent_grad[...] = gradient.astype(BF16)
    sums[layers].source[...] = rows_product(latent_in[...], gradient.astype(BF16)).astype(BF16)
    advance(layers)
    while min(progress) < len(STAGES):
        for index in [layers] + list(range(layers))[::-1]:
            if progress[index] < len(STAGES):
                advance(index)


def run_net(plan, sizes, field_in, table, owner, encoder_weight, base, weights, cotangent):
    rows, cols, basis_count, layers = plan
    cells, channels = rows * cols, weights.shape[2]
    features = basis_count * channels
    span = cols + 2 * REACH
    rows_in = owner.shape[0]
    in_features = encoder_weight.shape[0]
    heights = [features] * layers + [in_features]
    scratch = [
        pltpu.VMEM((rows * basis_count * cols, base.shape[1]), BF16),
        pltpu.VMEM(((rows + 2) * span, channels), BF16),
        pltpu.VMEM(((rows + 2) * span, channels), F32),
        pltpu.VMEM((rows * basis_count * cols, channels), BF16),
        pltpu.VMEM((layers, cells, features), BF16),
        pltpu.VMEM((layers, cells, channels), F32),
        pltpu.VMEM(((rows_in + 2) * basis_count * cols, field_in.shape[1]), BF16),
        pltpu.VMEM((cells, in_features), BF16),
    ]
    scratch += InputHalo.scratch(
        rows_in, field_in.shape[0] // rows_in, field_in.shape[1], table.shape[0] // rows_in, table.shape[1]
    )
    for index in range(2 * layers):
        scratch += Halo.scratch(rows, cols, channels, 2 if index < layers else 4)
    for height in heights:
        scratch += GradSum.scratch(sizes, height, channels)
    vmem = pl.BlockSpec(memory_space=pltpu.VMEM)
    field = jax.ShapeDtypeStruct((cells, channels), BF16)
    grads = [jax.ShapeDtypeStruct((height, channels // 2), BF16) for height in heights]
    return pl.pallas_call(
        functools.partial(net_kernel, plan),
        out_shape=[field, field] + grads,
        in_specs=[vmem, vmem, pl.BlockSpec(memory_space=pltpu.SMEM)] + [vmem] * 4,
        out_specs=[vmem] * (3 + layers),
        scratch_shapes=scratch,
        compiler_params=pltpu.CompilerParams(
            collective_id=0, has_side_effects=True, vmem_limit_bytes=56 << 20
        ),
    )(field_in, table, owner, encoder_weight, base, weights, cotangent)


def per_device(
    input_field,
    encoder_filter,
    row_owner,
    encoder_weight,
    disco_basis,
    row_widths,
    block_weights,
    cotangent,
):
    if fits_chunks(
        cotangent.shape[0], input_field.shape[1], cotangent.shape[1], block_weights.shape[0]
    ):
        return per_device_chunks(
            input_field,
            encoder_filter,
            row_owner,
            encoder_weight,
            disco_basis,
            row_widths,
            block_weights,
            cotangent,
        )
    rows_in, cols_in, in_width = input_field.shape
    rows_dev = rows_in // 2
    cols_dev = cols_in // 2
    basis_count = encoder_filter.shape[1]
    tap_count = encoder_filter.shape[2]
    channels = block_weights.shape[2]
    layers = block_weights.shape[0]
    cell_count = rows_dev * cols_dev
    offsets = jnp.abs(jnp.arange(2 * REACH + 1, dtype=jnp.int32) - REACH)
    keep = offsets[None, :] <= row_widths[:, None]
    masked = jnp.where(keep[:, None, None, :], disco_basis, jnp.zeros_like(disco_basis))
    span = cols_dev + 2 * REACH
    table = jnp.pad(masked, ((0, 0), (0, basis_count), (0, 0), (0, span - masked.shape[3])))
    table = table.reshape(rows_dev * 2 * basis_count, 3 * span).astype(jnp.float32)
    lanes = lanes_of(2 * span)
    table = jnp.pad(table, ((0, 0), (0, lanes - 3 * span)))
    taps = jnp.pad(
        encoder_filter.astype(jnp.float32),
        ((0, 0), (0, basis_count), (0, lanes_of(cols_in) - tap_count)),
    ).reshape(rows_in * 2 * basis_count, -1)
    own_width = channels // lax.axis_size("ch")
    sizes = (lax.axis_size("lat"), lax.axis_size("lon"))
    plan = (rows_dev, cols_dev, basis_count, layers)
    outs = run_net(
        plan,
        sizes,
        input_field.reshape(rows_in * cols_in, in_width),
        taps,
        row_owner,
        encoder_weight,
        table,
        block_weights,
        cotangent.reshape(cell_count, channels),
    )
    current, gradient = (field.reshape(rows_dev, cols_dev, channels) for field in outs[:2])
    sums = [value.astype(jnp.float32) for value in outs[2:]]
    block_sum, encoder_sum = jnp.stack(sums[:-1]), sums[-1]
    cells_total = cell_count * lax.axis_size("lon") * lax.axis_size(("lat", "ch"))
    normalizer = 1.0 / math.sqrt(cells_total)
    block_grads = (block_sum * normalizer).reshape(layers, basis_count * channels, own_width)
    encoder_grad = encoder_sum * normalizer
    return (current, gradient, block_grads, encoder_grad)

HALO = 2
LANES = 128


class Place:
    def __init__(self):
        self.lon, self.ch = lax.axis_size("lon"), lax.axis_size("ch")
        self.bands = lax.axis_size("lat") * self.ch
        self.z = lax.axis_index("lon")
        self.band = lax.axis_index("lat") * self.ch + lax.axis_index("ch")
        self.chunk = self.flip(self.band, self.z)
        self.count = self.bands * self.lon
        self.position = self.band * self.lon + self.chunk

    def flip(self, band, index):
        return index + lax.rem(band, 2) * (self.lon - 1 - 2 * index)

    def offset(self, chunk):
        return (chunk + self.lon - 1) // self.lon + (chunk + 1) // self.lon

    def device(self, band, chunk):
        return {
            "lat": band // self.ch,
            "ch": lax.rem(band, self.ch),
            "lon": self.flip(band, chunk),
        }

    def along_snake(self, step):
        position = lax.rem(self.position + step + self.count, self.count)
        return self.device(position // self.lon, lax.rem(position, self.lon))


def greet_part():
    barrier = pltpu.get_barrier_semaphore()
    count = 0
    for lat in range(lax.axis_size("lat")):
        for ch in range(lax.axis_size("ch")):
            for lon in range(lax.axis_size("lon")):
                if lat or ch or lon:
                    target = {**along("lat", lat), **along("ch", ch), **along("lon", lon)}
                    pl.semaphore_signal(barrier, inc=1, device_id=target, device_id_type=MESH)
                    count += 1
    pl.semaphore_wait(barrier, count)


class Regroup(Sender):
    def __init__(self, bufs, rim):
        self.rim = rim
        self.lines, self.rim_ssem, self.rim_rsem, self.own_sem = bufs[0], bufs[3], bufs[4], bufs[5]
        super().__init__(bufs[1:3])

    @staticmethod
    def scratch(lon, rows, cols, width, rim):
        return [
            pltpu.VMEM((rows + 2 + 2 * rim, cols, width), BF16),
            pltpu.SemaphoreType.DMA((lon - 1,)),
            pltpu.SemaphoreType.DMA((lon - 1,)),
            pltpu.SemaphoreType.DMA((2,)),
            pltpu.SemaphoreType.DMA((2 * lon,)),
            pltpu.SemaphoreType.DMA,
        ]

    def start(self, place, source):
        self.place = place
        rows, piece = source.shape[0], source.shape[1]
        each = rows // place.lon
        columns = pl.ds(pl.multiple_of(place.z * piece, piece), piece)
        size = each + 2 * self.rim
        block = self.lines.at[pl.ds(1, size), columns]
        for step in range(1, place.lon):
            peer = along("lon", step)
            chunk = place.flip(place.band, peer["lon"])
            first = chunk * each - self.rim * place.offset(chunk)
            self.send(source.at[pl.ds(first, size)], block, step - 1, peer)
        first = place.chunk * each - self.rim * place.offset(place.chunk)
        self.own = pltpu.make_async_copy(source.at[pl.ds(first, size)], block, self.own_sem)
        self.own.start()
        self.rims = []
        for side, (row, slot, step, chunk) in enumerate(
            ((rows - 1, 0, 1, 0), (0, size + 1, -1, place.lon - 1))[: 2 * self.rim]
        ):
            band = lax.rem(place.band + step + place.bands, place.bands)
            copy = pltpu.make_async_remote_copy(
                src_ref=source.at[row],
                dst_ref=self.lines.at[slot, columns],
                send_sem=self.rim_ssem.at[side],
                recv_sem=self.rim_rsem.at[side * place.lon + place.z],
                device_id=place.device(band, chunk),
                device_id_type=MESH,
            )
            copy.start()
            self.rims.append(copy)
        self.source, self.piece, self.size = source, piece, size

    def finish(self):
        place = self.place
        self.settle()
        self.own.wait()
        ends = ((0, 0), (self.size + 1, place.lon - 1))[: 2 * self.rim]
        for side, (slot, chunk) in enumerate(ends):

            @pl.when(place.chunk == chunk)
            def _():
                for z in range(place.lon):
                    pltpu.make_async_remote_copy(
                        src_ref=self.source.at[0],
                        dst_ref=self.lines.at[slot, pl.ds(z * self.piece, self.piece)],
                        send_sem=self.rim_ssem.at[side],
                        recv_sem=self.rim_rsem.at[side * place.lon + z],
                        device_id=along("lon", 0),
                        device_id_type=MESH,
                    ).wait_recv()

        for copy in self.rims:
            copy.wait_send()

    def row(self, index):
        return self.lines[index + 1 + self.rim * self.place.offset(self.place.chunk)]


class Restore(Sender):
    def __init__(self, bufs):
        self.lines, self.own_sem = bufs[0], bufs[3]
        super().__init__(bufs[1:3])

    @staticmethod
    def scratch(lon, rows, cols, width):
        return [
            pltpu.VMEM((rows, cols, width), BF16),
            pltpu.SemaphoreType.DMA((lon - 1,)),
            pltpu.SemaphoreType.DMA((lon - 1,)),
            pltpu.SemaphoreType.DMA,
        ]

    def start(self, place, result):
        rows, piece = self.lines.shape[0], result.shape[1]
        target = result.at[pl.ds(place.chunk * rows, rows)]
        for step in range(1, place.lon):
            peer = along("lon", step)
            columns = pl.ds(pl.multiple_of(peer["lon"] * piece, piece), piece)
            self.send(self.lines.at[:, columns], target, step - 1, peer)
        columns = pl.ds(pl.multiple_of(place.z * piece, piece), piece)
        self.own = pltpu.make_async_copy(self.lines.at[:, columns], target, self.own_sem)
        self.own.start()

    def finish(self):
        self.settle()
        self.own.wait()


class Swap(Sender):
    def __init__(self, bufs):
        super().__init__(bufs)

    @staticmethod
    def scratch():
        return [pltpu.SemaphoreType.DMA((2,)), pltpu.SemaphoreType.DMA((2,))]

    def start(self, place, buffer, slot_rows, own, halo):
        def part(first):
            return buffer.at[pl.ds(first * slot_rows, halo * slot_rows)]

        self.send(part(own), part(0), 0, place.along_snake(1))
        self.send(part(halo), part(halo + own), 1, place.along_snake(-1))


def zero_outside(place, buffer, first, last, size):
    @pl.when(place.position == 0)
    def _():
        buffer[first : first + size, :] = jnp.zeros((size, buffer.shape[1]), buffer.dtype)

    @pl.when(place.position == place.count - 1)
    def _():
        buffer[last : last + size, :] = jnp.zeros((size, buffer.shape[1]), buffer.dtype)


def circulant(line, rows, stride):
    return pltpu.roll(jnp.broadcast_to(line, (rows, LANES)), 0, 1, stride=stride, stride_axis=0)


def silu_slope(pre):
    sigma = 1.0 / (1.0 + jnp.exp(-pre))
    return sigma * (1.0 + pre * (1.0 - sigma))


def chunk_kernel(plan, *refs):
    rows, cols, basis_count, layers = plan
    field, taps, owner, encoder_source, base, widths, weights_source, cotangent = refs[:8]
    state_out, latent_grad = refs[8:10]
    results = refs[10 : 11 + layers]
    rest = list(refs[11 + layers :])
    table, flat, lines, rims, bands, turned, latent_in, state, features, preact, steps, errs = rest[:12]
    encoder_weight, weights, load_sems = rest[12:15]
    rest = rest[15:]
    inputs, arriving = Regroup(rest[:6], 1), Regroup(rest[6:12], 0)
    leaving = [Restore(rest[12:16]), Restore(rest[16:20])]
    swaps = [Swap(rest[20 + 2 * n : 22 + 2 * n]) for n in range(5)]
    rest = rest[30:]
    sums = []
    for index in range(layers + 1):
        sums.append(GradSum(results[index], rest[:11]))
        rest = rest[11:]
    channels = state.shape[1]
    width = field.shape[2]
    block = basis_count * cols
    ext = rows + 2 * HALO
    progress = [0] * (layers + 1)

    def advance(index):
        getattr(sums[index], STAGES[progress[index]])()
        progress[index] += 1

    loads = [
        pltpu.make_async_copy(source, target, load_sems.at[index])
        for index, (source, target) in enumerate(
            ((encoder_source, encoder_weight), (weights_source, weights))
        )
    ]
    greet_part()
    place = Place()
    inputs.start(place, field)
    arriving.start(place, cotangent)
    for load in loads:
        load.start()

    first = place.position * rows
    rows_in = 2 * rows
    start_in = place.chunk * rows_in
    high, tall = table.shape[0] // ext, rims.shape[1]
    make_table(place, base, widths, table, rows, cols, basis_count, high)
    swaps[0].start(place, table, high, rows, HALO)
    make_lines(taps, flat, lines, start_in, rows_in, basis_count)
    sides = (
        (0, jnp.where(owner[start_in] == first - 1, 1.0, 0.0)),
        (rows_in - 1, jnp.where(owner[start_in + rows_in - 1] == first + rows, 1.0, 0.0)),
    )
    for side, (row, feeds) in enumerate(sides):
        for k in range(basis_count):
            rims[side, k : k + 1, :] = lines[k * rows_in + row : k * rows_in + row + 1, :] * feeds
    swaps[1].send(rims.at[1], rims.at[2], 0, place.along_snake(1))
    swaps[1].send(rims.at[0], rims.at[3], 1, place.along_snake(-1))
    swaps[0].settle()

    lane = lax.broadcasted_iota(jnp.int32, (cols, LANES), 1)

    def make_band(row, carry):
        values = table[aligned(row, high), :]
        for k in range(basis_count):
            parts = [
                circulant(values[r * basis_count + k][None, :], cols, 1) for r in range(3)
            ]
            start = pl.multiple_of(row * block + k * cols, cols)
            bands[pl.ds(start, cols), :LANES] = jnp.where(lane < cols, parts[0], parts[1]).astype(BF16)
            bands[pl.ds(start, cols), LANES:] = parts[2].astype(BF16)
        other = bands[aligned(row, block), :].T
        for r in range(3):
            turned[aligned(row + r, cols), (2 - r) * block : (3 - r) * block] = other[
                r * cols : (r + 1) * cols
            ]
        return carry

    lax.fori_loop(0, ext, make_band, 0)
    swaps[1].settle()
    inputs.finish()

    def filtered(row):
        if 0 <= row < rows_in:
            values = [lines[k * rows_in + row : k * rows_in + row + 1, :] for k in range(basis_count)]
        else:
            side = 2 if row < 0 else 3
            values = [rims[side, k : k + 1, :] for k in range(basis_count)]
        lhs = jnp.concatenate([circulant(value, cols, 2) for value in values], axis=0).astype(BF16)
        out = jnp.dot(lhs, inputs.row(row), preferred_element_type=F32)
        return out.astype(BF16).astype(F32)

    filters = [filtered(row) for row in range(-1, rows_in + 1)]
    for row in range(rows):
        total = None
        for step in range(-1, 3):
            source = 2 * row + step
            term = filters[source + 1]
            if 0 <= source < rows_in:
                term = term * jnp.where(owner[start_in + source] == first + row, 1.0, 0.0)
            total = term if total is None else total + term
        total = total.astype(BF16)
        for k in range(basis_count):
            latent_in[row * cols : (row + 1) * cols, k * width : (k + 1) * width] = total[
                k * cols : (k + 1) * cols
            ]
    own = pl.ds(HALO * cols, rows * cols)
    loads[0].wait()
    state[own, :] = jnp.dot(
        latent_in[...], encoder_weight[...], preferred_element_type=F32
    ).astype(BF16)
    swaps[2].start(place, state, cols, rows, HALO)
    loads[1].wait()
    swaps[2].settle()
    zero_outside(place, state, 0, (HALO + rows) * cols, HALO * cols)

    for layer in range(layers):
        low, top = layer + 1, ext - layer - 1
        for row in range(low, top):
            out = jnp.dot(
                bands[row * block : (row + 1) * block, : 3 * cols],
                state[(row - 1) * cols : (row + 2) * cols, :],
                preferred_element_type=F32,
            ).astype(BF16)
            for k in range(basis_count):
                features[layer, row * cols : (row + 1) * cols, k * channels : (k + 1) * channels] = out[
                    k * cols : (k + 1) * cols
                ]
        span = pl.ds(low * cols, (top - low) * cols)
        pre = jnp.dot(features[layer, span, :], weights[layer], preferred_element_type=F32)
        preact[layer, span, :] = pre
        new = state[span, :].astype(F32) + pre / (1.0 + jnp.exp(-pre))
        state[span, :] = new.astype(BF16)
        if layer < layers - 1:
            zero_outside(place, state, low * cols, (top - 1) * cols, cols)

    arriving.finish()
    last = layers - 1
    gradient = arriving.lines[1 : rows + 1].reshape(rows * cols, channels).astype(F32)
    act = gradient * silu_slope(preact[last, own, :])
    steps[last, own, :] = act.astype(BF16)
    swaps[3].start(place, steps.at[last], cols, rows, HALO)
    swaps[4].start(place, arriving.lines, 1, rows, 1)
    leaving[0].lines[...] = state[own, :].reshape(rows, cols, channels)
    leaving[0].start(place, state_out)

    def errors(layer, low, top):
        for k in range(basis_count):
            out = lax.dot_general(
                steps[layer, low * cols : top * cols, :],
                weights[layer, k * channels : (k + 1) * channels, :],
                (((1,), (1,)), ((), ())),
                preferred_element_type=F32,
            ).astype(BF16)
            for row in range(low, top):
                start = row * block + k * cols
                errs[start : start + cols, :] = out[(row - low) * cols : (row - low + 1) * cols]

    def spread(row):
        return jnp.dot(
            turned[(row + 1) * cols : (row + 2) * cols, :],
            errs[(row - 1) * block : (row + 2) * block, :],
            preferred_element_type=F32,
        )

    sums[last].source[...] = rows_product(features[last, own, :], steps[last, own, :]).astype(BF16)
    advance(last)
    errors(last, HALO, HALO + rows)
    swaps[3].settle()
    zero_outside(place, steps.at[last], 0, (HALO + rows) * cols, HALO * cols)
    errors(last, 0, HALO)
    errors(last, HALO + rows, ext)
    advance(last)
    swaps[4].settle()
    back = [arriving.lines[row - 1].astype(F32) + spread(row) for row in range(1, ext - 1)]
    gradient = jnp.concatenate(back, axis=0).astype(BF16).astype(F32)
    span = pl.ds(cols, (ext - 2) * cols)
    steps[0, span, :] = (gradient * silu_slope(preact[0, span, :])).astype(BF16)
    zero_outside(place, steps.at[0], cols, (ext - 2) * cols, cols)
    sums[0].source[...] = rows_product(features[0, own, :], steps[0, own, :]).astype(BF16)
    advance(0)
    advance(last)
    errors(0, 1, ext - 1)
    back = [
        gradient[(row - 1) * cols : row * cols] + spread(row) for row in range(HALO, HALO + rows)
    ]
    final = jnp.concatenate(back, axis=0).astype(BF16)
    leaving[1].lines[...] = final.reshape(rows, cols, channels)
    leaving[1].start(place, latent_grad)
    sums[layers].source[...] = rows_product(latent_in[...], final).astype(BF16)
    advance(layers)
    while min(progress) < len(STAGES):
        for index in [last, 0, layers]:
            if progress[index] < len(STAGES):
                advance(index)
    for part in leaving:
        part.finish()


def make_table(place, base, widths, table, rows, cols, basis_count, high):
    own = pl.ds(HALO * high, rows * high)
    table[own, :] = jnp.zeros((rows * high, LANES), F32)
    size = base.shape[3]
    reach = size // 2
    distance = jnp.abs(lax.broadcasted_iota(jnp.int32, (basis_count, size), 1) - reach)
    for row in range(rows):
        source = place.chunk * rows + row
        values = base[source].astype(F32)
        for r in range(3):
            start = (HALO + row) * high + r * basis_count
            table[start : start + basis_count, :size] = jnp.where(
                distance <= widths[source], values[r], 0.0
            )
    moved = pltpu.roll(table[own, :], LANES - reach, 1)
    table[own, :] = moved + pltpu.roll(moved, cols, 1)


def make_lines(taps, flat, lines, start_in, rows_in, basis_count):
    flat[...] = jnp.zeros_like(flat)
    count, _, held = taps.shape
    for k in range(basis_count):
        for t in range(count):
            row = 8 * k + t
            flat[row : row + 1, :held] = taps[t, k : k + 1, :].astype(F32)
    flat[...] = flat[...].T
    values = flat[aligned(start_in // rows_in, rows_in), :]
    lane = lax.broadcasted_iota(jnp.int32, values.shape, 1)
    for k in range(basis_count):
        moved = pltpu.roll(values, LANES - 8 * k, 1) if k else values
        kept = jnp.where(lane < count, moved, 0.0)
        lines[k * rows_in : (k + 1) * rows_in, :] = pltpu.roll(kept, LANES - count // 2, 1)


def run_chunks(
    plan, sizes, field_in, taps, owner, encoder_weight, base, widths, weights, cotangent
):
    rows, cols, basis_count, layers = plan
    lat, lon = sizes
    channels = weights.shape[2]
    features = basis_count * channels
    in_features = encoder_weight.shape[0]
    ext = rows + 2 * HALO
    heights = [features] * layers + [in_features]
    block = basis_count * cols
    high = -(-3 * basis_count // 8) * 8
    tall = -(-basis_count // 8) * 8
    scratch = [
        pltpu.VMEM((ext * high, LANES), F32),
        pltpu.VMEM((LANES, LANES), F32),
        pltpu.VMEM((basis_count * 2 * rows, LANES), F32),
        pltpu.VMEM((4, tall, LANES), F32),
        pltpu.VMEM((ext * block, 2 * LANES), BF16),
        pltpu.VMEM(((ext + 2) * cols, 3 * block), BF16),
        pltpu.VMEM((rows * cols, in_features), BF16),
        pltpu.VMEM((ext * cols, channels), BF16),
        pltpu.VMEM((layers, ext * cols, features), BF16),
        pltpu.VMEM((layers, ext * cols, channels), F32),
        pltpu.VMEM((layers, ext * cols, channels), BF16),
        pltpu.VMEM((ext * block, channels), BF16),
        pltpu.VMEM(encoder_weight.shape, BF16),
        pltpu.VMEM(weights.shape, BF16),
        pltpu.SemaphoreType.DMA((2,)),
    ]
    scratch += Regroup.scratch(lon, 2 * rows, field_in.shape[1] * lon, field_in.shape[2], 1)
    scratch += Regroup.scratch(lon, rows, cols, channels, 0)
    for _ in range(2):
        scratch += Restore.scratch(lon, rows, cols, channels)
    for _ in range(5):
        scratch += Swap.scratch()
    for height in heights:
        scratch += GradSum.scratch(sizes, height, channels)
    vmem = pl.BlockSpec(memory_space=pltpu.VMEM)
    smem = pl.BlockSpec(memory_space=pltpu.SMEM)
    hbm = pl.BlockSpec(memory_space=pltpu.HBM)
    out = jax.ShapeDtypeStruct(cotangent.shape, BF16)
    grads = [jax.ShapeDtypeStruct((height, channels // 2), BF16) for height in heights]
    return pl.pallas_call(
        functools.partial(chunk_kernel, plan),
        out_shape=[out, out] + grads,
        in_specs=[hbm, vmem, smem, hbm, vmem, smem, hbm, hbm],
        out_specs=[hbm, hbm] + [vmem] * (1 + layers),
        scratch_shapes=scratch,
        compiler_params=pltpu.CompilerParams(
            collective_id=1, has_side_effects=True, vmem_limit_bytes=56 << 20
        ),
    )(field_in, taps, owner, encoder_weight, base, widths, weights, cotangent)


def finish_body(normalizer, field_count, sum_count, refs):
    fields, sums = refs[:field_count], refs[field_count : field_count + sum_count]
    fields_out = refs[field_count + sum_count : 2 * field_count + sum_count]
    block_grads, encoder_grad = refs[2 * field_count + sum_count :][:2]
    rest = refs[2 * field_count + sum_count + 2 :]
    held, wide = rest[:sum_count], rest[sum_count : 2 * sum_count]
    kept = rest[2 * sum_count : 2 * sum_count + field_count]
    in_sems, out_sems = rest[2 * sum_count + field_count :]
    sources = list(zip(list(sums) + list(fields), list(held) + list(kept)))
    targets = [block_grads.at[n] for n in range(sum_count - 1)] + [encoder_grad] + list(fields_out)
    ready = list(wide) + list(kept)
    loads = [
        pltpu.make_async_copy(source, target, in_sems.at[n])
        for n, (source, target) in enumerate(sources)
    ]
    stores = [
        pltpu.make_async_copy(source, target, out_sems.at[n])
        for n, (source, target) in enumerate(zip(ready, targets))
    ]
    for load in loads:
        load.start()
    for n, (load, store) in enumerate(zip(loads, stores)):
        load.wait()
        if n < sum_count:
            wide[n][...] = held[n][...].astype(F32) * normalizer
        store.start()
    for store in stores:
        store.wait()


def finish_outputs(normalizer, outs):
    hbm = pl.BlockSpec(memory_space=pltpu.HBM)
    fields, sums = outs[:2], outs[2:]
    shapes = [jax.ShapeDtypeStruct(field.shape, field.dtype) for field in fields]
    shapes.append(jax.ShapeDtypeStruct((len(sums) - 1,) + sums[0].shape, F32))
    shapes.append(jax.ShapeDtypeStruct(sums[-1].shape, F32))

    def kernel(*refs):
        finish_body(normalizer, len(fields), len(sums), refs)

    return pl.pallas_call(
        kernel,
        out_shape=shapes,
        in_specs=[hbm] * len(outs),
        out_specs=[hbm] * len(shapes),
        scratch_shapes=[pltpu.VMEM(value.shape, BF16) for value in sums]
        + [pltpu.VMEM(value.shape, F32) for value in sums]
        + [pltpu.VMEM(value.shape, BF16) for value in fields]
        + [pltpu.SemaphoreType.DMA((len(outs),)) for _ in range(2)],
        compiler_params=pltpu.CompilerParams(vmem_limit_bytes=60 << 20),
    )(*outs)


def fits_chunks(rows_dev, cols_in, cols_dev, layers):
    lon = lax.axis_size("lon")
    return (
        layers == HALO
        and rows_dev % lon == 0
        and rows_dev // lon >= HALO
        and lon > 1
        and cols_in * lon == LANES
        and 2 * cols_dev * lon == LANES
    )


def per_device_chunks(
    input_field,
    encoder_filter,
    row_owner,
    encoder_weight,
    disco_basis,
    row_widths,
    block_weights,
    cotangent,
):
    rows_in, cols_in, _ = input_field.shape
    lat, lon = lax.axis_size("lat"), lax.axis_size("lon")
    rows_dev, cols = rows_in // 2, cols_in // 2 * lon
    plan = (rows_dev // lon, cols, encoder_filter.shape[1], block_weights.shape[0])
    outs = run_chunks(
        plan,
        (lat, lon),
        input_field,
        encoder_filter.transpose(2, 1, 0),
        row_owner,
        encoder_weight,
        disco_basis.transpose(0, 2, 1, 3),
        row_widths,
        block_weights,
        cotangent,
    )
    cells_total = rows_dev * lax.axis_size(("lat", "ch")) * cols
    return tuple(finish_outputs(1.0 / math.sqrt(cells_total), outs))


def solution(mesh):
    placed = (
        P(("ens", "lat", "ch"), "lon", None),
        P(("lat", "ch"), None, None),
        P(("ens", "lat", "ch")),
        P(),
        P(("lat", "ch"), None, None, None),
        P(("lat", "ch")),
        P(),
        P(("ens", "lat", "ch"), "lon", None),
    )
    return jax.shard_map(
        per_device,
        mesh=mesh,
        in_specs=placed,
        out_specs=(
            P(("ens", "lat", "ch"), "lon", None),
            P(("ens", "lat", "ch"), "lon", None),
            P("ens", None, "ch"),
            P("ens", "ch"),
        ),
        check_vma=False,
    )
```

```python
import functools
import math

import jax
import jax.numpy as jnp
from jax import lax
from jax.experimental import pallas as pl
from jax.experimental.pallas import tpu as pltpu
from jax.sharding import PartitionSpec as P

REACH = 8
TAP_REACH = 2
TILE = 16
MESH = pl.DeviceIdType.MESH
BF16 = jnp.bfloat16
F32 = jnp.float32


def along(axis, steps):
    count = lax.axis_size(axis)
    return {axis: lax.rem(lax.axis_index(axis) + steps + count, count)}


def neighbour(row_step, col_step):
    ch_count = lax.axis_size("ch")
    bands = lax.axis_size("lat") * ch_count
    band = lax.axis_index("lat") * ch_count + lax.axis_index("ch")
    band = lax.rem(band + row_step + bands, bands)
    target = {}
    if row_step:
        target = {"lat": band // ch_count, "ch": lax.rem(band, ch_count)}
    if col_step:
        target.update(along("lon", col_step))
    return target


AROUND = [(r, c) for r in (-1, 0, 1) for c in (-1, 0, 1) if r or c]


def greet():
    targets = [neighbour(r, c) for r, c in AROUND]
    for axis in ("ch", "lat", "lon"):
        targets += [along(axis, step) for step in range(1, lax.axis_size(axis))]
    barrier = pltpu.get_barrier_semaphore()
    for target in targets:
        pl.semaphore_signal(barrier, inc=1, device_id=target, device_id_type=MESH)
    pl.semaphore_wait(barrier, len(targets))


class Sender:
    def __init__(self, sems):
        self.ssem, self.rsem = sems
        self.pending = []

    def send(self, source, target, slot, device):
        copy = pltpu.make_async_remote_copy(
            src_ref=source,
            dst_ref=target,
            send_sem=self.ssem.at[slot],
            recv_sem=self.rsem.at[slot],
            device_id=device,
            device_id_type=MESH,
        )
        copy.start()
        self.pending.append(copy)

    def settle(self):
        for copy in self.pending:
            copy.wait()
        self.pending = []


class GradSum(Sender):
    def __init__(self, result, bufs):
        super().__init__(bufs[-2:])
        self.result = result
        self.source, self.rec_ch, self.part, self.rec_lat, self.strip, self.rec_pair, self.half, self.rec_far, self.piece = bufs[:-2]
        self.width = self.part.shape[1]
        self.lat, self.lon = lax.axis_size("lat"), lax.axis_size("lon")
        self.height = self.strip.shape[0]
        self.span = self.piece.shape[0]
        self.pair = self.height // self.span
        self.far = self.lon // self.pair
        self.side = lax.rem(lax.axis_index("lon"), self.pair)

    @staticmethod
    def scratch(sizes, rows, columns):
        lat, lon = sizes
        width = columns // 2
        height = rows // lat
        pair = 2 if lon % 2 == 0 and height % (2 * TILE) == 0 else 1
        span, far = height // pair, lon // pair
        count = 1 + 2 * (lat - 1) + 2 * (pair - 1) + far - 1
        return [
            pltpu.VMEM((rows, columns), BF16),
            pltpu.VMEM((rows, width), BF16),
            pltpu.VMEM((rows, width), BF16),
            pltpu.VMEM((lat - 1, height, width), BF16),
            pltpu.VMEM((height, width), BF16),
            pltpu.VMEM((span, width), BF16),
            pltpu.VMEM((span, width), BF16),
            pltpu.VMEM((far - 1, span, width), BF16),
            pltpu.VMEM((span, width), BF16),
            pltpu.SemaphoreType.DMA((count,)),
            pltpu.SemaphoreType.DMA((count,)),
        ]

    def columns(self, half):
        return pl.ds(pl.multiple_of(half * self.width, self.width), self.width)

    @staticmethod
    def stretch(owner, size):
        return pl.ds(pl.multiple_of(owner * size, size), size)

    def start_ch(self):
        other = 1 - lax.axis_index("ch")
        self.send(self.source.at[:, self.columns(other)], self.rec_ch, 0, {"ch": other})

    def start_lat(self):
        self.settle()
        own = self.source[:, self.columns(lax.axis_index("ch"))].astype(F32)
        self.part[...] = (own + self.rec_ch[...].astype(F32)).astype(BF16)
        for step in range(1, self.lat):
            peer = along("lat", step)
            rows = self.stretch(peer["lat"], self.height)
            self.send(self.part.at[rows], self.rec_lat.at[step - 1], step, peer)

    def start_lon(self):
        self.settle()
        total = self.part[self.stretch(lax.axis_index("lat"), self.height), :].astype(F32)
        for step in range(1, self.lat):
            total = total + self.rec_lat[step - 1].astype(F32)
        self.strip[...] = total.astype(BF16)
        if self.pair > 1:
            rows = self.stretch(1 - self.side, self.span)
            self.send(self.strip.at[rows], self.rec_pair, self.lat, along("lon", 1 - 2 * self.side))

    def start_far(self):
        self.settle()
        total = self.strip[self.stretch(self.side, self.span), :].astype(F32)
        if self.pair > 1:
            total = total + self.rec_pair[...].astype(F32)
        self.half[...] = total.astype(BF16)
        for step in range(1, self.far):
            self.send(
                self.half, self.rec_far.at[step - 1], self.lat + step, along("lon", self.pair * step)
            )

    def gather_lon(self):
        self.settle()
        total = self.half[...].astype(F32)
        for step in range(1, self.far):
            total = total + self.rec_far[step - 1].astype(F32)
        self.piece[...] = total.astype(BF16)
        offset = lax.axis_index("lat") * self.height + self.side * self.span
        rows = pl.ds(pl.multiple_of(offset, TILE), self.span)
        self.result[rows, :] = self.piece[...]
        if self.pair > 1:
            slot = self.lat + self.far
            self.send(self.piece, self.result.at[rows], slot, along("lon", 1 - 2 * self.side))

    def gather_lat(self):
        self.settle()
        rows = self.stretch(lax.axis_index("lat"), self.height)
        for step in range(1, self.lat):
            slot = self.lat + self.far + self.pair - 2 + step
            self.send(self.result.at[rows], self.result.at[rows], slot, along("lat", step))

    def finish(self):
        self.settle()


STAGES = ("start_ch", "start_lat", "start_lon", "start_far", "gather_lon", "gather_lat", "finish")


class Halo(Sender):
    def __init__(self, bufs):
        super().__init__(bufs[-2:])
        self.out_side, self.out_row, self.in_side, self.in_row = bufs[:-2]

    @staticmethod
    def scratch(rows, cols, width, row_blocks):
        return [
            pltpu.VMEM((2, rows * REACH, width), BF16),
            pltpu.VMEM((row_blocks, cols, width), BF16),
            pltpu.VMEM((2, rows * REACH, width), BF16),
            pltpu.VMEM((6, cols, width), BF16),
            pltpu.SemaphoreType.DMA((8,)),
            pltpu.SemaphoreType.DMA((8,)),
        ]

    def start(self, row_block_of):
        self.send(self.out_side.at[0], self.in_side.at[1], 0, neighbour(0, -1))
        self.send(self.out_side.at[1], self.in_side.at[0], 1, neighbour(0, 1))
        slot = 2
        for row_step in (-1, 1):
            for col_step in (-1, 0, 1):
                place = (0 if row_step == 1 else 3) + 1 - col_step
                self.send(
                    self.out_row.at[row_block_of(row_step, col_step)],
                    self.in_row.at[place],
                    slot,
                    neighbour(row_step, col_step),
                )
                slot += 1


def edge_flags():
    ch_count = lax.axis_size("ch")
    bands = lax.axis_size("lat") * ch_count
    band = lax.axis_index("lat") * ch_count + lax.axis_index("ch")
    return band > 0, band < bands - 1


def extend(halo, state, ext, rows, cols):
    span = cols + 2 * REACH
    west, east = halo.in_side[0].astype(F32), halo.in_side[1].astype(F32)
    for row in range(rows):
        low, high = row * REACH, (row + 1) * REACH
        line = jnp.concatenate(
            [west[low:high], state[row * cols : (row + 1) * cols], east[low:high]], axis=0
        )
        ext[(row + 1) * span : (row + 2) * span, :] = line.astype(BF16)
    for first, row, flag in zip((0, 3), (0, rows + 1), edge_flags()):
        line = jnp.concatenate(
            [
                halo.in_row[first].astype(F32)[cols - REACH :],
                halo.in_row[first + 1].astype(F32),
                halo.in_row[first + 2].astype(F32)[:REACH],
            ],
            axis=0,
        )
        ext[row * span : (row + 1) * span, :] = jnp.where(flag, line, 0.0).astype(BF16)


def send_state(halo, state, rows, cols):
    pieces = [
        [state[r * cols : r * cols + REACH] for r in range(rows)],
        [state[(r + 1) * cols - REACH : (r + 1) * cols] for r in range(rows)],
    ]
    for side in range(2):
        halo.out_side[side] = jnp.concatenate(pieces[side], axis=0).astype(BF16)
    halo.out_row[0] = state[:cols].astype(BF16)
    halo.out_row[1] = state[(rows - 1) * cols :].astype(BF16)
    halo.start(lambda row_step, col_step: 0 if row_step == -1 else 1)


def send_spread(halo, spread, rows, cols):
    span = cols + 2 * REACH
    west = [spread[(r + 1) * span : (r + 1) * span + REACH, :] for r in range(rows)]
    east = [spread[(r + 2) * span - REACH : (r + 2) * span, :] for r in range(rows)]
    halo.out_side[0] = jnp.concatenate(west, axis=0).astype(BF16)
    halo.out_side[1] = jnp.concatenate(east, axis=0).astype(BF16)
    for block, row in enumerate((0, rows + 1)):
        base = row * span
        halo.out_row[2 * block] = spread[base + REACH : base + REACH + cols, :].astype(BF16)
        corners = [spread[base : base + REACH, :], spread[base + span - REACH : base + span, :]]
        if cols > 2 * REACH:
            corners.insert(1, jnp.zeros((cols - 2 * REACH, spread.shape[1]), F32))
        halo.out_row[2 * block + 1] = jnp.concatenate(corners, axis=0).astype(BF16)
    halo.start(
        lambda row_step, col_step: (0 if row_step == -1 else 2) + (1 if col_step else 0)
    )


def take_spread(halo, spread, gradient, rows, cols):
    span = cols + 2 * REACH
    west, east = halo.in_side[0].astype(F32), halo.in_side[1].astype(F32)
    outer = {}
    for first, row, flag in zip((0, 3), (0, rows - 1), edge_flags()):
        line = halo.in_row[first + 1].astype(F32)
        rim_west = halo.in_row[first].astype(F32)[cols - REACH :]
        rim_east = halo.in_row[first + 2].astype(F32)[:REACH]
        rims = [rim_west, rim_east]
        if cols > 2 * REACH:
            rims.insert(1, jnp.zeros((cols - 2 * REACH, line.shape[1]), F32))
        outer[row] = jnp.where(flag, line + jnp.concatenate(rims, axis=0), 0.0)
    result = []
    for row in range(rows):
        low, high = row * REACH, (row + 1) * REACH
        rims = [west[low:high], east[low:high]]
        if cols > 2 * REACH:
            rims.insert(1, jnp.zeros((cols - 2 * REACH, west.shape[1]), F32))
        base = (row + 1) * span + REACH
        line = spread[base : base + cols, :] + jnp.concatenate(rims, axis=0)
        if row in outer:
            line = line + outer[row]
        result.append(gradient[row * cols : (row + 1) * cols].astype(F32) + line)
    return result


def aligned(index, size):
    return pl.ds(pl.multiple_of(index * size, size), size)


GROUP = 16


def over_rows(rows, body):
    group = GROUP if rows % GROUP == 0 else 1

    def step(index, carry):
        for inner in range(group):
            body(index * group + inner)
        return carry

    lax.fori_loop(0, rows // group, step, 0)


def make_bands(base, bands, rows, cols, basis_count):
    width = base.shape[1]

    def one(row):
        table = base[aligned(row, 2 * basis_count), :]
        for k in range(basis_count):
            line = jnp.broadcast_to(table[k : k + 1], (cols, width))
            moved = pltpu.roll(line, 0, 1, stride=1, stride_axis=0)
            start = pl.multiple_of((row * basis_count + k) * cols, cols)
            bands[pl.ds(start, cols), :] = moved.astype(BF16)

    over_rows(rows, one)


def stencil(bands, ext, features, rows, cols, basis_count):
    span = cols + 2 * REACH
    channels = ext.shape[1]

    def one(row):
        lhs = bands[aligned(row, basis_count * cols), :][:, : 3 * span]
        rhs = ext[pl.ds(pl.multiple_of(row * span, span), 3 * span), :]
        out = jnp.dot(lhs, rhs, preferred_element_type=F32).astype(BF16)
        for k in range(basis_count):
            features[aligned(row, cols), k * channels : (k + 1) * channels] = out[
                k * cols : (k + 1) * cols
            ]

    over_rows(rows, one)


def adjoint(bands, errs, spread, rows, cols, basis_count):
    span = cols + 2 * REACH
    spread[...] = jnp.zeros_like(spread)

    def one(row):
        lhs = bands[aligned(row, basis_count * cols), :][:, : 3 * span]
        rhs = errs[aligned(row, basis_count * cols), :]
        out = lax.dot_general(lhs, rhs, (((0,), (0,)), ((), ())), preferred_element_type=F32)
        place = pl.ds(pl.multiple_of(row * span, span), 3 * span)
        spread[place, :] = spread[place, :] + out

    over_rows(rows, one)


def rows_product(left, right):
    return lax.dot_general(left, right, (((0,), (0,)), ((), ())), preferred_element_type=F32)
TAPS_LEFT = TAP_REACH


class InputHalo(Sender):
    def __init__(self, bufs):
        super().__init__(bufs[-2:])
        (
            self.edges,
            self.out_cols,
            self.out_table,
            self.in_cols,
            self.in_row,
            self.in_table,
            self.in_tile,
        ) = bufs[:-2]

    @staticmethod
    def scratch(rows_in, cols_in, width, table_rows, lanes):
        return [
            pltpu.VMEM((3, rows_in, width), F32),
            pltpu.VMEM((3, rows_in, width), BF16),
            pltpu.VMEM((2, table_rows, lanes), F32),
            pltpu.VMEM((3, rows_in, width), BF16),
            pltpu.VMEM((2, cols_in, width), BF16),
            pltpu.VMEM((2, table_rows, lanes), F32),
            pltpu.VMEM((4, TILE, width), BF16),
            pltpu.SemaphoreType.DMA((10,)),
            pltpu.SemaphoreType.DMA((10,)),
        ]

    def start(self, field, table, owner, rows_in, cols_in):
        first = own_first_row(rows_in // 2)
        table_rows = self.out_table.shape[1]
        for block, row, target in ((0, 0, first - 1), (1, rows_in - 1, first + rows_in // 2)):
            feeds = jnp.where(owner[row] == target, 1.0, 0.0)
            self.out_table[block] = table[row * table_rows : (row + 1) * table_rows, :] * feeds
        last = (rows_in - 1) * cols_in
        lines = (field.at[pl.ds(0, cols_in)], field.at[pl.ds(last, cols_in)])
        slot = 0
        for block, row_step in ((0, -1), (1, 1)):
            self.send(lines[block], self.in_row.at[1 - block], slot, neighbour(row_step, 0))
            base = block * last
            west = field.at[pl.ds(base, TILE)]
            east = field.at[pl.ds(base + cols_in - TILE, TILE)]
            place = 2 * (1 - block)
            self.send(west, self.in_tile.at[place + 1], slot + 1, neighbour(row_step, -1))
            self.send(east, self.in_tile.at[place], slot + 2, neighbour(row_step, 1))
            slot += 3

        def one(row):
            low = field[pl.ds(pl.multiple_of(row * cols_in, TILE), TILE), :].astype(F32)
            start = pl.multiple_of(row * cols_in + cols_in - TILE, TILE)
            high = field[pl.ds(start, TILE), :].astype(F32)
            self.edges[0, pl.ds(row, 1), :] = high[TILE - 2 : TILE - 1]
            self.edges[1, pl.ds(row, 1), :] = high[TILE - 1 : TILE]
            self.edges[2, pl.ds(row, 1), :] = low[0:1]

        over_rows(rows_in, one)
        self.out_cols[...] = self.edges[...].astype(BF16)
        self.send(self.out_cols.at[pl.ds(0, 2)], self.in_cols.at[pl.ds(0, 2)], 6, neighbour(0, 1))
        self.send(self.out_cols.at[2], self.in_cols.at[2], 7, neighbour(0, -1))
        self.send(self.out_table.at[0], self.in_table.at[1], 8, neighbour(-1, 0))
        self.send(self.out_table.at[1], self.in_table.at[0], 9, neighbour(1, 0))


def own_first_row(rows):
    return (lax.axis_index("lat") * lax.axis_size("ch") + lax.axis_index("ch")) * rows


def tap_matrix(table, basis_count, cols, cols_in):
    lanes = table.shape[1]
    blocks = []
    for k in range(basis_count):
        line = jnp.broadcast_to(table[k : k + 1], (cols, lanes))
        moved = pltpu.roll(line, 0, 1, stride=2, stride_axis=0)
        wrapped = pltpu.roll(moved, cols_in + TILE - TAPS_LEFT, 1)
        moved = pltpu.roll(moved, lanes - TAPS_LEFT, 1)
        lane = lax.broadcasted_iota(jnp.int32, (cols, lanes), 1)
        at_end = (lane >= cols_in + TILE - TAPS_LEFT) & (lane < cols_in + TILE)
        blocks.append(jnp.where(at_end, wrapped, moved))
    return jnp.concatenate(blocks, axis=0)[:, : cols_in + TILE].astype(BF16)


def filtered_row(table, line, left_two, left_one, right, basis_count, cols, cols_in):
    width = line.shape[1]
    place = lax.broadcasted_iota(jnp.int32, (TILE, width), 0)
    tile = jnp.where(place == 0, jnp.broadcast_to(right, (TILE, width)), 0.0)
    tile = jnp.where(place == TILE - 2, jnp.broadcast_to(left_two, (TILE, width)), tile)
    tile = jnp.where(place == TILE - 1, jnp.broadcast_to(left_one, (TILE, width)), tile)
    rhs = jnp.concatenate([line, tile.astype(BF16)], axis=0)
    lhs = tap_matrix(table, basis_count, cols, cols_in)
    return jnp.dot(lhs, rhs, preferred_element_type=F32).astype(BF16)


def finish_encode(halo, field, table, owner, filtered, latent_in, plan, rows_in, cols_in):
    rows, cols, basis_count, _ = plan
    table_rows = halo.out_table.shape[1]
    block = basis_count * cols
    width = field.shape[1]
    halo.settle()
    halo.edges[...] = halo.in_cols[...].astype(F32)

    def one(row):
        sides = [halo.edges[index, pl.ds(row, 1), :] for index in range(3)]
        line = field[aligned(row, cols_in), :]
        taps = table[aligned(row, table_rows), :]
        filtered[aligned(row + 1, block), :] = filtered_row(
            taps, line, *sides, basis_count, cols, cols_in
        )

    over_rows(rows_in, one)
    for side, row in ((0, 0), (1, rows_in + 1)):
        west = halo.in_tile[2 * side].astype(F32)
        east = halo.in_tile[2 * side + 1].astype(F32)
        filtered[row * block : (row + 1) * block, :] = filtered_row(
            halo.in_table[side],
            halo.in_row[side],
            west[TILE - 2 : TILE - 1],
            west[TILE - 1 : TILE],
            east[0:1],
            basis_count,
            cols,
            cols_in,
        )
    first = own_first_row(rows)
    for row in range(rows):
        total = None
        for offset in range(-1, 3):
            source = 2 * row + offset
            term = filtered[(source + 1) * block : (source + 2) * block, :].astype(F32)
            if 0 <= source < rows_in:
                term = term * jnp.where(owner[source] == first + row, 1.0, 0.0)
            total = term if total is None else total + term
        total = total.astype(BF16)
        for k in range(basis_count):
            latent_in[row * cols : (row + 1) * cols, k * width : (k + 1) * width] = total[
                k * cols : (k + 1) * cols
            ]


def lanes_of(count):
    return -(-(count + 2 * TILE) // 128) * 128


def net_kernel(plan, *refs):
    rows, cols, basis_count, layers = plan
    field, table, owner, encoder_weight, base, weights, cotangent = refs[:7]
    state_out, latent_grad = refs[7:9]
    results = refs[9 : 10 + layers]
    rest = list(refs[10 + layers :])
    bands, ext, spread, errs, features, preact, filtered, latent_in = rest[:8]
    input_halo = InputHalo(rest[8:17])
    rest = rest[17:]
    halos = []
    for _ in range(2 * layers):
        halos.append(Halo(rest[:6]))
        rest = rest[6:]
    sums = []
    for index in range(layers + 1):
        sums.append(GradSum(results[index], rest[:11]))
        rest = rest[11:]
    channels = ext.shape[1]
    progress = [0] * (layers + 1)

    def advance(index):
        getattr(sums[index], STAGES[progress[index]])()
        progress[index] += 1

    greet()
    rows_in = owner.shape[0]
    cols_in = field.shape[0] // rows_in
    input_halo.start(field, table, owner, rows_in, cols_in)
    make_bands(base, bands, rows, cols, basis_count)
    finish_encode(input_halo, field, table, owner, filtered, latent_in, plan, rows_in, cols_in)
    state = jnp.dot(latent_in[...], encoder_weight[...], preferred_element_type=F32)
    state = state.astype(BF16).astype(F32)
    for layer in range(layers):
        send_state(halos[layer], state, rows, cols)
        halos[layer].settle()
        extend(halos[layer], state, ext, rows, cols)
        stencil(bands, ext, features.at[layer], rows, cols, basis_count)
        pre = jnp.dot(features[layer], weights[layer], preferred_element_type=F32)
        preact[layer] = pre
        state = (state + pre / (1.0 + jnp.exp(-pre))).astype(BF16).astype(F32)
    state_out[...] = state.astype(BF16)

    gradient = cotangent[...].astype(F32)
    for layer in reversed(range(layers)):
        pre = preact[layer]
        sigma = 1.0 / (1.0 + jnp.exp(-pre))
        act_grad = (gradient * sigma * (1.0 + pre * (1.0 - sigma))).astype(BF16)
        for k in range(basis_count):
            block = weights[layer, k * channels : (k + 1) * channels, :]
            out = lax.dot_general(
                act_grad, block, (((1,), (1,)), ((), ())), preferred_element_type=F32
            ).astype(BF16)
            for row in range(rows):
                start = (row * basis_count + k) * cols
                errs[start : start + cols, :] = out[row * cols : (row + 1) * cols]
        adjoint(bands, errs, spread, rows, cols, basis_count)
        halo = halos[layers + layer]
        send_spread(halo, spread, rows, cols)
        sums[layer].source[...] = rows_product(features[layer], act_grad).astype(BF16)
        for other in range(layers - 1, layer - 1, -1):
            advance(other)
        halo.settle()
        for other in range(layers - 1, layer - 1, -1):
            advance(other)
        lines = take_spread(halo, spread, gradient, rows, cols)
        gradient = jnp.concatenate(lines, axis=0).astype(BF16).astype(F32)
    latent_grad[...] = gradient.astype(BF16)
    sums[layers].source[...] = rows_product(latent_in[...], gradient.astype(BF16)).astype(BF16)
    advance(layers)
    while min(progress) < len(STAGES):
        for index in [layers] + list(range(layers))[::-1]:
            if progress[index] < len(STAGES):
                advance(index)


def run_net(plan, sizes, field_in, table, owner, encoder_weight, base, weights, cotangent):
    rows, cols, basis_count, layers = plan
    cells, channels = rows * cols, weights.shape[2]
    features = basis_count * channels
    span = cols + 2 * REACH
    rows_in = owner.shape[0]
    in_features = encoder_weight.shape[0]
    heights = [features] * layers + [in_features]
    scratch = [
        pltpu.VMEM((rows * basis_count * cols, base.shape[1]), BF16),
        pltpu.VMEM(((rows + 2) * span, channels), BF16),
        pltpu.VMEM(((rows + 2) * span, channels), F32),
        pltpu.VMEM((rows * basis_count * cols, channels), BF16),
        pltpu.VMEM((layers, cells, features), BF16),
        pltpu.VMEM((layers, cells, channels), F32),
        pltpu.VMEM(((rows_in + 2) * basis_count * cols, field_in.shape[1]), BF16),
        pltpu.VMEM((cells, in_features), BF16),
    ]
    scratch += InputHalo.scratch(
        rows_in, field_in.shape[0] // rows_in, field_in.shape[1], table.shape[0] // rows_in, table.shape[1]
    )
    for index in range(2 * layers):
        scratch += Halo.scratch(rows, cols, channels, 2 if index < layers else 4)
    for height in heights:
        scratch += GradSum.scratch(sizes, height, channels)
    vmem = pl.BlockSpec(memory_space=pltpu.VMEM)
    field = jax.ShapeDtypeStruct((cells, channels), BF16)
    grads = [jax.ShapeDtypeStruct((height, channels // 2), BF16) for height in heights]
    return pl.pallas_call(
        functools.partial(net_kernel, plan),
        out_shape=[field, field] + grads,
        in_specs=[vmem, vmem, pl.BlockSpec(memory_space=pltpu.SMEM)] + [vmem] * 4,
        out_specs=[vmem] * (3 + layers),
        scratch_shapes=scratch,
        compiler_params=pltpu.CompilerParams(
            collective_id=0, has_side_effects=True, vmem_limit_bytes=56 << 20
        ),
    )(field_in, table, owner, encoder_weight, base, weights, cotangent)


def per_device(
    input_field,
    encoder_filter,
    row_owner,
    encoder_weight,
    disco_basis,
    row_widths,
    block_weights,
    cotangent,
):
    if fits_chunks(
        cotangent.shape[0],
        input_field.shape[1],
        cotangent.shape[1],
        block_weights.shape[0],
        [block_weights.shape[1]] * block_weights.shape[0] + [encoder_weight.shape[0]],
    ):
        return per_device_chunks(
            input_field,
            encoder_filter,
            row_owner,
            encoder_weight,
            disco_basis,
            row_widths,
            block_weights,
            cotangent,
        )
    rows_in, cols_in, in_width = input_field.shape
    rows_dev = rows_in // 2
    cols_dev = cols_in // 2
    basis_count = encoder_filter.shape[1]
    tap_count = encoder_filter.shape[2]
    channels = block_weights.shape[2]
    layers = block_weights.shape[0]
    cell_count = rows_dev * cols_dev
    offsets = jnp.abs(jnp.arange(2 * REACH + 1, dtype=jnp.int32) - REACH)
    keep = offsets[None, :] <= row_widths[:, None]
    masked = jnp.where(keep[:, None, None, :], disco_basis, jnp.zeros_like(disco_basis))
    span = cols_dev + 2 * REACH
    table = jnp.pad(masked, ((0, 0), (0, basis_count), (0, 0), (0, span - masked.shape[3])))
    table = table.reshape(rows_dev * 2 * basis_count, 3 * span).astype(jnp.float32)
    lanes = lanes_of(2 * span)
    table = jnp.pad(table, ((0, 0), (0, lanes - 3 * span)))
    taps = jnp.pad(
        encoder_filter.astype(jnp.float32),
        ((0, 0), (0, basis_count), (0, lanes_of(cols_in) - tap_count)),
    ).reshape(rows_in * 2 * basis_count, -1)
    own_width = channels // lax.axis_size("ch")
    sizes = (lax.axis_size("lat"), lax.axis_size("lon"))
    plan = (rows_dev, cols_dev, basis_count, layers)
    outs = run_net(
        plan,
        sizes,
        input_field.reshape(rows_in * cols_in, in_width),
        taps,
        row_owner,
        encoder_weight,
        table,
        block_weights,
        cotangent.reshape(cell_count, channels),
    )
    current, gradient = (field.reshape(rows_dev, cols_dev, channels) for field in outs[:2])
    sums = [value.astype(jnp.float32) for value in outs[2:]]
    block_sum, encoder_sum = jnp.stack(sums[:-1]), sums[-1]
    cells_total = cell_count * lax.axis_size("lon") * lax.axis_size(("lat", "ch"))
    normalizer = 1.0 / math.sqrt(cells_total)
    block_grads = (block_sum * normalizer).reshape(layers, basis_count * channels, own_width)
    encoder_grad = encoder_sum * normalizer
    return (current, gradient, block_grads, encoder_grad)

HALO = 2
DIRECT, ACROSS, WIDE, PAIRED = range(4)
LANES = 128


class Place:
    def __init__(self):
        self.lon, self.ch = lax.axis_size("lon"), lax.axis_size("ch")
        self.bands = lax.axis_size("lat") * self.ch
        self.z = lax.axis_index("lon")
        self.band = lax.axis_index("lat") * self.ch + lax.axis_index("ch")
        self.chunk = self.flip(self.band, self.z)
        self.count = self.bands * self.lon
        self.position = self.band * self.lon + self.chunk

    def flip(self, band, index):
        return index + lax.rem(band, 2) * (self.lon - 1 - 2 * index)

    def offset(self, chunk):
        return (chunk + self.lon - 1) // self.lon + (chunk + 1) // self.lon

    def device(self, band, chunk):
        return {
            "lat": band // self.ch,
            "ch": lax.rem(band, self.ch),
            "lon": self.flip(band, chunk),
        }

    def along_snake(self, step):
        position = lax.rem(self.position + step + self.count, self.count)
        return self.device(position // self.lon, lax.rem(position, self.lon))


def greet_part():
    barrier = pltpu.get_barrier_semaphore()
    count = 0
    for lat in range(lax.axis_size("lat")):
        for ch in range(lax.axis_size("ch")):
            for lon in range(lax.axis_size("lon")):
                if lat or ch or lon:
                    target = {**along("lat", lat), **along("ch", ch), **along("lon", lon)}
                    pl.semaphore_signal(barrier, inc=1, device_id=target, device_id_type=MESH)
                    count += 1
    pl.semaphore_wait(barrier, count)


class Regroup(Sender):
    def __init__(self, bufs, rim):
        self.rim = rim
        self.lines, self.rim_ssem, self.rim_rsem, self.own_sem = bufs[0], bufs[3], bufs[4], bufs[5]
        super().__init__(bufs[1:3])

    @staticmethod
    def scratch(lon, rows, cols, width, rim):
        return [
            pltpu.VMEM((rows + 2 + 2 * rim, cols, width), BF16),
            pltpu.SemaphoreType.DMA((lon - 1,)),
            pltpu.SemaphoreType.DMA((lon - 1,)),
            pltpu.SemaphoreType.DMA((2,)),
            pltpu.SemaphoreType.DMA((2 * lon,)),
            pltpu.SemaphoreType.DMA,
        ]

    def start(self, place, source):
        self.place = place
        rows, piece = source.shape[0], source.shape[1]
        each = rows // place.lon
        columns = pl.ds(pl.multiple_of(place.z * piece, piece), piece)
        size = each + 2 * self.rim
        block = self.lines.at[pl.ds(1, size), columns]
        for step in range(1, place.lon):
            peer = along("lon", step)
            chunk = place.flip(place.band, peer["lon"])
            first = chunk * each - self.rim * place.offset(chunk)
            self.send(source.at[pl.ds(first, size)], block, step - 1, peer)
        first = place.chunk * each - self.rim * place.offset(place.chunk)
        self.own = pltpu.make_async_copy(source.at[pl.ds(first, size)], block, self.own_sem)
        self.own.start()
        self.rims = []
        for side, (row, slot, step, chunk) in enumerate(
            ((rows - 1, 0, 1, 0), (0, size + 1, -1, place.lon - 1))[: 2 * self.rim]
        ):
            band = lax.rem(place.band + step + place.bands, place.bands)
            copy = pltpu.make_async_remote_copy(
                src_ref=source.at[row],
                dst_ref=self.lines.at[slot, columns],
                send_sem=self.rim_ssem.at[side],
                recv_sem=self.rim_rsem.at[side * place.lon + place.z],
                device_id=place.device(band, chunk),
                device_id_type=MESH,
            )
            copy.start()
            self.rims.append(copy)
        self.source, self.piece, self.size = source, piece, size

    def finish(self):
        place = self.place
        self.settle()
        self.own.wait()
        ends = ((0, 0), (self.size + 1, place.lon - 1))[: 2 * self.rim]
        for side, (slot, chunk) in enumerate(ends):

            @pl.when(place.chunk == chunk)
            def _():
                for z in range(place.lon):
                    pltpu.make_async_remote_copy(
                        src_ref=self.source.at[0],
                        dst_ref=self.lines.at[slot, pl.ds(z * self.piece, self.piece)],
                        send_sem=self.rim_ssem.at[side],
                        recv_sem=self.rim_rsem.at[side * place.lon + z],
                        device_id=along("lon", 0),
                        device_id_type=MESH,
                    ).wait_recv()

        for copy in self.rims:
            copy.wait_send()

    def row(self, index):
        return self.lines[index + 1 + self.rim * self.place.offset(self.place.chunk)]


class Restore(Sender):
    def __init__(self, bufs):
        self.lines, self.own_sem = bufs[0], bufs[3]
        super().__init__(bufs[1:3])

    @staticmethod
    def scratch(lon, rows, cols, width):
        return [
            pltpu.VMEM((rows, cols, width), BF16),
            pltpu.SemaphoreType.DMA((lon - 1,)),
            pltpu.SemaphoreType.DMA((lon - 1,)),
            pltpu.SemaphoreType.DMA,
        ]

    def start(self, place, result):
        rows, piece = self.lines.shape[0], result.shape[1]
        target = result.at[pl.ds(place.chunk * rows, rows)]
        for step in range(1, place.lon):
            peer = along("lon", step)
            columns = pl.ds(pl.multiple_of(peer["lon"] * piece, piece), piece)
            self.send(self.lines.at[:, columns], target, step - 1, peer)
        columns = pl.ds(pl.multiple_of(place.z * piece, piece), piece)
        self.own = pltpu.make_async_copy(self.lines.at[:, columns], target, self.own_sem)
        self.own.start()

    def finish(self):
        self.settle()
        self.own.wait()


class Swap(Sender):
    def __init__(self, bufs):
        super().__init__(bufs)

    @staticmethod
    def scratch():
        return [pltpu.SemaphoreType.DMA((2,)), pltpu.SemaphoreType.DMA((2,))]

    def start(self, place, buffer, slot_rows, own, halo):
        def part(first):
            return buffer.at[pl.ds(first * slot_rows, halo * slot_rows)]

        self.send(part(own), part(0), 0, place.along_snake(1))
        self.send(part(halo), part(halo + own), 1, place.along_snake(-1))


class ChipSum(Sender):
    def __init__(self, result, source, first, direct, bufs):
        super().__init__(bufs[-2:])
        self.result, self.source, self.first = result, source, first
        self.rec_ch, self.part, self.rec_lat, self.strip, self.rec, self.piece = bufs[:6]
        self.rec_pair, self.half, self.rec_far, self.whole = bufs[6:10]
        self.rows, self.width = self.part.shape
        self.lat, self.lon = lax.axis_size("lat"), lax.axis_size("lon")
        self.height, self.span = self.strip.shape[0], self.piece.shape[0]
        self.side = lax.rem(lax.axis_index("lon"), 2)
        self.direct = direct
        self.stages = [self.start_ch]
        if direct == DIRECT:
            self.stages += [self.scatter_all, self.gather_all]
        elif direct == ACROSS:
            self.stages += [self.scatter_lat, self.scatter_lon, self.gather_lon, self.gather_lat]
        elif direct == WIDE:
            self.stages += [self.scatter_lat, self.scatter_lon, self.gather_all]
        else:
            self.stages += [self.scatter_lat, self.scatter_pair, self.trade_far]
            self.stages += [self.gather_pair, self.gather_lat]
        self.stages.append(self.settle)

    @staticmethod
    def scratch(sizes, rows, columns):
        lat, lon = sizes
        width, height, span = columns // 2, rows // lat, rows // (lat * lon)
        count = 1 + 2 * (lat - 1) + 2 * (lat * lon - 1)
        return [
            pltpu.VMEM((rows, width), BF16),
            pltpu.VMEM((rows, width), BF16),
            pltpu.VMEM((lat - 1, height, width), BF16),
            pltpu.VMEM((height, width), BF16),
            pltpu.VMEM((lat * lon - 1, span, width), BF16),
            pltpu.VMEM((span, width), BF16),
            pltpu.VMEM((height // 2, width), BF16),
            pltpu.VMEM((height // 2, width), BF16),
            pltpu.VMEM((max(lon // 2 - 1, 1), height // 2, width), BF16),
            pltpu.VMEM((height // 2, width), BF16),
            pltpu.SemaphoreType.DMA((count,)),
            pltpu.SemaphoreType.DMA((count,)),
        ]

    def advance(self):
        self.stages.pop(0)()

    def columns(self, half):
        return pl.ds(pl.multiple_of(half * self.width, self.width), self.width)

    def own_columns(self):
        return self.source[self.first : self.first + self.rows, self.columns(lax.axis_index("ch"))]

    def others(self):
        for lat in range(self.lat):
            for lon in range(self.lon):
                if lat or lon:
                    yield lat * self.lon + lon - 1, {**along("lat", lat), **along("lon", lon)}

    def mine(self):
        return lax.axis_index("lat") * self.lon + lax.axis_index("lon")

    def place(self, index, size):
        return pl.ds(pl.multiple_of(index * size, size), size)

    def target(self, index, size):
        return pl.ds(pl.multiple_of(self.first + index * size, size), size)

    def start_ch(self):
        other = 1 - lax.axis_index("ch")
        rows = pl.ds(self.first, self.rows)
        self.send(self.source.at[rows, self.columns(other)], self.rec_ch, 0, {"ch": other})

    def add_ch(self):
        self.settle()
        total = self.own_columns().astype(F32) + self.rec_ch[...].astype(F32)
        self.part[...] = total.astype(BF16)

    def scatter_all(self):
        self.add_ch()
        for slot, peer in self.others():
            rows = self.place(peer["lat"] * self.lon + peer["lon"], self.span)
            self.send(self.part.at[rows], self.rec.at[slot], 1 + slot, peer)

    def scatter_lat(self):
        self.add_ch()
        self.slot = self.lat * self.lon
        for step in range(1, self.lat):
            peer = along("lat", step)
            rows = self.place(peer["lat"], self.height)
            self.send(self.part.at[rows], self.rec_lat.at[step - 1], self.slot, peer)
            self.slot += 1

    def add_lat(self):
        self.settle()
        total = self.part[self.place(lax.axis_index("lat"), self.height), :].astype(F32)
        for step in range(1, self.lat):
            total = total + self.rec_lat[step - 1].astype(F32)
        self.strip[...] = total.astype(BF16)

    def scatter_pair(self):
        self.add_lat()
        rows = self.place(1 - self.side, self.height // 2)
        self.send(self.strip.at[rows], self.rec_pair, 1, along("lon", 1 - 2 * self.side))

    def trade_far(self):
        self.settle()
        total = self.strip[self.place(self.side, self.height // 2), :].astype(F32)
        self.half[...] = (total + self.rec_pair[...].astype(F32)).astype(BF16)
        for step in range(1, self.lon // 2):
            self.send(self.half, self.rec_far.at[step - 1], 1 + step, along("lon", 2 * step))

    def gather_pair(self):
        self.settle()
        total = self.half[...].astype(F32)
        for step in range(1, self.lon // 2):
            total = total + self.rec_far[step - 1].astype(F32)
        self.whole[...] = total.astype(BF16)
        rows = self.target(2 * lax.axis_index("lat") + self.side, self.height // 2)
        self.result[rows, :] = self.whole[...]
        base = self.lat * self.lon + self.lat - 1
        self.send(self.whole, self.result.at[rows], base, along("lon", 1 - 2 * self.side))

    def scatter_lon(self):
        self.add_lat()
        for step in range(1, self.lon):
            peer = along("lon", step)
            rows = self.place(peer["lon"], self.span)
            self.send(self.strip.at[rows], self.rec.at[step - 1], step, peer)

    def add_rest(self):
        self.settle()
        if self.direct == DIRECT:
            total, count = self.part[self.place(self.mine(), self.span), :], self.lat * self.lon
        else:
            total, count = self.strip[self.place(lax.axis_index("lon"), self.span), :], self.lon
        total = total.astype(F32)
        for step in range(1, count):
            total = total + self.rec[step - 1].astype(F32)
        self.piece[...] = total.astype(BF16)
        rows = self.target(self.mine(), self.span)
        self.result[rows, :] = self.piece[...]
        return self.result.at[rows], self.lat * self.lon + self.lat - 1

    def gather_all(self):
        target, base = self.add_rest()
        for slot, peer in self.others():
            self.send(self.piece, target, base + slot, peer)

    def gather_lon(self):
        target, base = self.add_rest()
        for step in range(1, self.lon):
            self.send(self.piece, target, base + step - 1, along("lon", step))

    def gather_lat(self):
        self.settle()
        rows = self.target(lax.axis_index("lat"), self.height)
        base = 2 * self.lat * self.lon + self.lat - 2
        for step in range(1, self.lat):
            self.send(self.result.at[rows], self.result.at[rows], base + step - 1, along("lat", step))


def zero_outside(place, buffer, first, last, size):
    @pl.when(place.position == 0)
    def _():
        buffer[first : first + size, :] = jnp.zeros((size, buffer.shape[1]), buffer.dtype)

    @pl.when(place.position == place.count - 1)
    def _():
        buffer[last : last + size, :] = jnp.zeros((size, buffer.shape[1]), buffer.dtype)


def circulant(line, rows, stride):
    return pltpu.roll(jnp.broadcast_to(line, (rows, LANES)), 0, 1, stride=stride, stride_axis=0)


def silu_slope(pre):
    sigma = 1.0 / (1.0 + jnp.exp(-pre))
    return sigma * (1.0 + pre * (1.0 - sigma))


def chunk_kernel(plan, *refs):
    rows, cols, basis_count, layers = plan
    field, taps, owner, encoder_source, base, widths, weights_source, cotangent = refs[:8]
    state_out, latent_grad = refs[8:10]
    results = refs[10 : 11 + layers]
    rest = list(refs[11 + layers :])
    table, flat, lines, rims, bands, turned, latent_in, state, features, preact, steps, errs = rest[:12]
    encoder_weight, weights, load_sems = rest[12:15]
    rest = rest[15:]
    inputs, arriving = Regroup(rest[:6], 1), Regroup(rest[6:12], 0)
    leaving = [Restore(rest[12:16]), Restore(rest[16:20])]
    swaps = [Swap(rest[20 + 2 * n : 22 + 2 * n]) for n in range(5)]
    rest = rest[30:]
    sources, rest = rest[: layers + 1], rest[layers + 1 :]
    sums = []
    for index, first, size, direct in stretches([source.shape[0] for source in sources]):
        sums.append(ChipSum(results[index], sources[index], first, direct, rest[:12]))
        rest = rest[12:]
    channels = state.shape[1]
    width = field.shape[2]
    block = basis_count * cols
    ext = rows + 2 * HALO
    early, upper, lower, encoder = sums

    loads = [
        pltpu.make_async_copy(source, target, load_sems.at[index])
        for index, (source, target) in enumerate(
            ((encoder_source, encoder_weight), (weights_source, weights))
        )
    ]
    greet_part()
    place = Place()
    inputs.start(place, field)
    for load in loads:
        load.start()

    first = place.position * rows
    rows_in = 2 * rows
    start_in = place.chunk * rows_in
    high, tall = table.shape[0] // ext, rims.shape[1]
    make_table(place, base, widths, table, rows, cols, basis_count, high)
    swaps[0].start(place, table, high, rows, HALO)
    make_lines(taps, flat, lines, start_in, rows_in, basis_count)
    sides = (
        (0, jnp.where(owner[start_in] == first - 1, 1.0, 0.0)),
        (rows_in - 1, jnp.where(owner[start_in + rows_in - 1] == first + rows, 1.0, 0.0)),
    )
    for side, (row, feeds) in enumerate(sides):
        for k in range(basis_count):
            rims[side, k : k + 1, :] = lines[k * rows_in + row : k * rows_in + row + 1, :] * feeds
    swaps[1].send(rims.at[1], rims.at[2], 0, place.along_snake(1))
    swaps[1].send(rims.at[0], rims.at[3], 1, place.along_snake(-1))
    swaps[0].settle()

    lane = lax.broadcasted_iota(jnp.int32, (cols, LANES), 1)

    def make_band(row, carry):
        values = table[aligned(row, high), :]
        for k in range(basis_count):
            parts = [
                circulant(values[r * basis_count + k][None, :], cols, 1) for r in range(3)
            ]
            start = pl.multiple_of(row * block + k * cols, cols)
            bands[pl.ds(start, cols), :LANES] = jnp.where(lane < cols, parts[0], parts[1]).astype(BF16)
            bands[pl.ds(start, cols), LANES:] = parts[2].astype(BF16)
        other = bands[aligned(row, block), :].T
        for r in range(3):
            turned[aligned(row + r, cols), (2 - r) * block : (3 - r) * block] = other[
                r * cols : (r + 1) * cols
            ]
        return carry

    lax.fori_loop(0, ext, make_band, 0)
    swaps[1].settle()
    inputs.finish()

    def filtered(row):
        if 0 <= row < rows_in:
            values = [lines[k * rows_in + row : k * rows_in + row + 1, :] for k in range(basis_count)]
        else:
            side = 2 if row < 0 else 3
            values = [rims[side, k : k + 1, :] for k in range(basis_count)]
        lhs = jnp.concatenate([circulant(value, cols, 2) for value in values], axis=0).astype(BF16)
        out = jnp.dot(lhs, inputs.row(row), preferred_element_type=F32)
        return out.astype(BF16).astype(F32)

    filters = [filtered(row) for row in range(-1, rows_in + 1)]
    for row in range(rows):
        total = None
        for step in range(-1, 3):
            source = 2 * row + step
            term = filters[source + 1]
            if 0 <= source < rows_in:
                term = term * jnp.where(owner[start_in + source] == first + row, 1.0, 0.0)
            total = term if total is None else total + term
        total = total.astype(BF16)
        for k in range(basis_count):
            latent_in[row * cols : (row + 1) * cols, k * width : (k + 1) * width] = total[
                k * cols : (k + 1) * cols
            ]
    own = pl.ds(HALO * cols, rows * cols)
    loads[0].wait()
    state[own, :] = jnp.dot(
        latent_in[...], encoder_weight[...], preferred_element_type=F32
    ).astype(BF16)
    swaps[2].start(place, state, cols, rows, HALO)
    arriving.start(place, cotangent)
    loads[1].wait()
    swaps[2].settle()
    zero_outside(place, state, 0, (HALO + rows) * cols, HALO * cols)

    for layer in range(layers):
        low, top = layer + 1, ext - layer - 1
        for row in range(low, top):
            out = jnp.dot(
                bands[row * block : (row + 1) * block, : 3 * cols],
                state[(row - 1) * cols : (row + 2) * cols, :],
                preferred_element_type=F32,
            ).astype(BF16)
            for k in range(basis_count):
                features[layer, row * cols : (row + 1) * cols, k * channels : (k + 1) * channels] = out[
                    k * cols : (k + 1) * cols
                ]
        span = pl.ds(low * cols, (top - low) * cols)
        pre = jnp.dot(features[layer, span, :], weights[layer], preferred_element_type=F32)
        preact[layer, span, :] = pre
        new = state[span, :].astype(F32) + pre / (1.0 + jnp.exp(-pre))
        state[span, :] = new.astype(BF16)
        if layer < layers - 1:
            zero_outside(place, state, low * cols, (top - 1) * cols, cols)

    arriving.finish()
    last = layers - 1
    gradient = arriving.lines[1 : rows + 1].reshape(rows * cols, channels).astype(F32)
    act = gradient * silu_slope(preact[last, own, :])
    steps[last, own, :] = act.astype(BF16)
    swaps[3].start(place, steps.at[last], cols, rows, HALO)
    swaps[4].start(place, arriving.lines, 1, rows, 1)
    leaving[0].lines[...] = state[own, :].reshape(rows, cols, channels)

    def errors(layer, low, top):
        for k in range(basis_count):
            out = lax.dot_general(
                steps[layer, low * cols : top * cols, :],
                weights[layer, k * channels : (k + 1) * channels, :],
                (((1,), (1,)), ((), ())),
                preferred_element_type=F32,
            ).astype(BF16)
            for row in range(low, top):
                start = row * block + k * cols
                errs[start : start + cols, :] = out[(row - low) * cols : (row - low + 1) * cols]

    def spread(row):
        return jnp.dot(
            turned[(row + 1) * cols : (row + 2) * cols, :],
            errs[(row - 1) * block : (row + 2) * block, :],
            preferred_element_type=F32,
        )

    def weigh(part):
        stretch = slice(part.first, part.first + part.rows)
        left = features[0, own, stretch]
        sources[0][stretch, :] = rows_product(left, steps[0, own, :]).astype(BF16)

    leaving[0].start(place, state_out)
    sources[last][...] = rows_product(features[last, own, :], steps[last, own, :]).astype(BF16)
    early.advance()
    errors(last, HALO, HALO + rows)
    early.advance()
    swaps[3].settle()
    zero_outside(place, steps.at[last], 0, (HALO + rows) * cols, HALO * cols)
    errors(last, 0, HALO)
    errors(last, HALO + rows, ext)
    swaps[4].settle()
    back = [arriving.lines[row - 1].astype(F32) + spread(row) for row in range(1, ext - 1)]
    gradient = jnp.concatenate(back, axis=0).astype(BF16).astype(F32)
    span = pl.ds(cols, (ext - 2) * cols)
    steps[0, span, :] = (gradient * silu_slope(preact[0, span, :])).astype(BF16)
    zero_outside(place, steps.at[0], cols, (ext - 2) * cols, cols)
    weigh(upper)
    upper.advance()
    weigh(lower)
    lower.advance()
    early.advance()
    errors(0, 1, ext - 1)
    upper.advance()
    lower.advance()
    back = [
        gradient[(row - 1) * cols : row * cols] + spread(row) for row in range(HALO, HALO + rows)
    ]
    final = jnp.concatenate(back, axis=0).astype(BF16)
    leaving[1].lines[...] = final.reshape(rows, cols, channels)
    sources[layers][...] = rows_product(latent_in[...], final).astype(BF16)
    encoder.advance()
    encoder.advance()
    upper.advance()
    lower.advance()
    early.advance()
    upper.advance()
    encoder.advance()
    lower.advance()
    early.advance()
    upper.advance()
    lower.advance()
    leaving[1].start(place, latent_grad)
    for part in sums:
        while part.stages:
            part.advance()
    for part in leaving:
        part.finish()


def make_table(place, base, widths, table, rows, cols, basis_count, high):
    own = pl.ds(HALO * high, rows * high)
    table[own, :] = jnp.zeros((rows * high, LANES), F32)
    size = base.shape[3]
    reach = size // 2
    distance = jnp.abs(lax.broadcasted_iota(jnp.int32, (basis_count, size), 1) - reach)
    for row in range(rows):
        source = place.chunk * rows + row
        values = base[source].astype(F32)
        for r in range(3):
            start = (HALO + row) * high + r * basis_count
            table[start : start + basis_count, :size] = jnp.where(
                distance <= widths[source], values[r], 0.0
            )
    moved = pltpu.roll(table[own, :], LANES - reach, 1)
    table[own, :] = moved + pltpu.roll(moved, cols, 1)


def make_lines(taps, flat, lines, start_in, rows_in, basis_count):
    flat[...] = jnp.zeros_like(flat)
    count, _, held = taps.shape
    for k in range(basis_count):
        for t in range(count):
            row = 8 * k + t
            flat[row : row + 1, :held] = taps[t, k : k + 1, :].astype(F32)
    flat[...] = flat[...].T
    values = flat[aligned(start_in // rows_in, rows_in), :]
    lane = lax.broadcasted_iota(jnp.int32, values.shape, 1)
    for k in range(basis_count):
        moved = pltpu.roll(values, LANES - 8 * k, 1) if k else values
        kept = jnp.where(lane < count, moved, 0.0)
        lines[k * rows_in : (k + 1) * rows_in, :] = pltpu.roll(kept, LANES - count // 2, 1)


def stretches(heights):
    half = heights[0] // 2
    return [
        (len(heights) - 2, 0, heights[-2], ACROSS),
        (0, 0, half, ACROSS),
        (0, half, half, ACROSS),
        (len(heights) - 1, 0, heights[-1], DIRECT),
    ]


def run_chunks(
    plan, sizes, field_in, taps, owner, encoder_weight, base, widths, weights, cotangent
):
    rows, cols, basis_count, layers = plan
    lat, lon = sizes
    channels = weights.shape[2]
    features = basis_count * channels
    in_features = encoder_weight.shape[0]
    ext = rows + 2 * HALO
    heights = [features] * layers + [in_features]
    block = basis_count * cols
    high = -(-3 * basis_count // 8) * 8
    tall = -(-basis_count // 8) * 8
    scratch = [
        pltpu.VMEM((ext * high, LANES), F32),
        pltpu.VMEM((LANES, LANES), F32),
        pltpu.VMEM((basis_count * 2 * rows, LANES), F32),
        pltpu.VMEM((4, tall, LANES), F32),
        pltpu.VMEM((ext * block, 2 * LANES), BF16),
        pltpu.VMEM(((ext + 2) * cols, 3 * block), BF16),
        pltpu.VMEM((rows * cols, in_features), BF16),
        pltpu.VMEM((ext * cols, channels), BF16),
        pltpu.VMEM((layers, ext * cols, features), BF16),
        pltpu.VMEM((layers, ext * cols, channels), F32),
        pltpu.VMEM((layers, ext * cols, channels), BF16),
        pltpu.VMEM((ext * block, channels), BF16),
        pltpu.VMEM(encoder_weight.shape, BF16),
        pltpu.VMEM(weights.shape, BF16),
        pltpu.SemaphoreType.DMA((2,)),
    ]
    scratch += Regroup.scratch(lon, 2 * rows, field_in.shape[1] * lon, field_in.shape[2], 1)
    scratch += Regroup.scratch(lon, rows, cols, channels, 0)
    for _ in range(2):
        scratch += Restore.scratch(lon, rows, cols, channels)
    for _ in range(5):
        scratch += Swap.scratch()
    scratch += [pltpu.VMEM((height, channels), BF16) for height in heights]
    for _, _, size, _ in stretches(heights):
        scratch += ChipSum.scratch(sizes, size, channels)
    vmem = pl.BlockSpec(memory_space=pltpu.VMEM)
    smem = pl.BlockSpec(memory_space=pltpu.SMEM)
    hbm = pl.BlockSpec(memory_space=pltpu.HBM)
    out = jax.ShapeDtypeStruct(cotangent.shape, BF16)
    grads = [jax.ShapeDtypeStruct((height, channels // 2), BF16) for height in heights]
    return pl.pallas_call(
        functools.partial(chunk_kernel, plan),
        out_shape=[out, out] + grads,
        in_specs=[hbm, vmem, smem, hbm, vmem, smem, hbm, hbm],
        out_specs=[hbm, hbm] + [vmem] * (1 + layers),
        scratch_shapes=scratch,
        compiler_params=pltpu.CompilerParams(
            collective_id=1, has_side_effects=True, vmem_limit_bytes=56 << 20
        ),
    )(field_in, taps, owner, encoder_weight, base, widths, weights, cotangent)


def finish_body(normalizer, field_count, sum_count, refs):
    fields, sums = refs[:field_count], refs[field_count : field_count + sum_count]
    fields_out = refs[field_count + sum_count : 2 * field_count + sum_count]
    block_grads, encoder_grad = refs[2 * field_count + sum_count :][:2]
    rest = refs[2 * field_count + sum_count + 2 :]
    held, wide = rest[:sum_count], rest[sum_count : 2 * sum_count]
    kept = rest[2 * sum_count : 2 * sum_count + field_count]
    in_sems, out_sems = rest[2 * sum_count + field_count :]
    sources = list(zip(list(sums) + list(fields), list(held) + list(kept)))
    targets = [block_grads.at[n] for n in range(sum_count - 1)] + [encoder_grad] + list(fields_out)
    ready = list(wide) + list(kept)
    loads = [
        pltpu.make_async_copy(source, target, in_sems.at[n])
        for n, (source, target) in enumerate(sources)
    ]
    stores = [
        pltpu.make_async_copy(source, target, out_sems.at[n])
        for n, (source, target) in enumerate(zip(ready, targets))
    ]
    for load in loads:
        load.start()
    for n, (load, store) in enumerate(zip(loads, stores)):
        load.wait()
        if n < sum_count:
            wide[n][...] = held[n][...].astype(F32) * normalizer
        store.start()
    for store in stores:
        store.wait()


def finish_outputs(normalizer, outs):
    hbm = pl.BlockSpec(memory_space=pltpu.HBM)
    fields, sums = outs[:2], outs[2:]
    shapes = [jax.ShapeDtypeStruct(field.shape, field.dtype) for field in fields]
    shapes.append(jax.ShapeDtypeStruct((len(sums) - 1,) + sums[0].shape, F32))
    shapes.append(jax.ShapeDtypeStruct(sums[-1].shape, F32))

    def kernel(*refs):
        finish_body(normalizer, len(fields), len(sums), refs)

    return pl.pallas_call(
        kernel,
        out_shape=shapes,
        in_specs=[hbm] * len(outs),
        out_specs=[hbm] * len(shapes),
        scratch_shapes=[pltpu.VMEM(value.shape, BF16) for value in sums]
        + [pltpu.VMEM(value.shape, F32) for value in sums]
        + [pltpu.VMEM(value.shape, BF16) for value in fields]
        + [pltpu.SemaphoreType.DMA((len(outs),)) for _ in range(2)],
        compiler_params=pltpu.CompilerParams(vmem_limit_bytes=60 << 20),
    )(*outs)


def fits_chunks(rows_dev, cols_in, cols_dev, layers, heights):
    lon = lax.axis_size("lon")
    count = lax.axis_size("lat") * lon
    heights_fit = all(size % (count * TILE) == 0 for _, _, size, _ in stretches(heights))
    return (
        layers == HALO
        and rows_dev % lon == 0
        and heights_fit
        and rows_dev // lon >= HALO
        and lon % 2 == 0
        and cols_in * lon == LANES
        and 2 * cols_dev * lon == LANES
    )


def per_device_chunks(
    input_field,
    encoder_filter,
    row_owner,
    encoder_weight,
    disco_basis,
    row_widths,
    block_weights,
    cotangent,
):
    rows_in, cols_in, _ = input_field.shape
    lat, lon = lax.axis_size("lat"), lax.axis_size("lon")
    rows_dev, cols = rows_in // 2, cols_in // 2 * lon
    plan = (rows_dev // lon, cols, encoder_filter.shape[1], block_weights.shape[0])
    outs = run_chunks(
        plan,
        (lat, lon),
        input_field,
        encoder_filter.transpose(2, 1, 0),
        row_owner,
        encoder_weight,
        disco_basis.transpose(0, 2, 1, 3),
        row_widths,
        block_weights,
        cotangent,
    )
    cells_total = rows_dev * lax.axis_size(("lat", "ch")) * cols
    return tuple(finish_outputs(1.0 / math.sqrt(cells_total), outs))


def solution(mesh):
    placed = (
        P(("ens", "lat", "ch"), "lon", None),
        P(("lat", "ch"), None, None),
        P(("ens", "lat", "ch")),
        P(),
        P(("lat", "ch"), None, None, None),
        P(("lat", "ch")),
        P(),
        P(("ens", "lat", "ch"), "lon", None),
    )
    return jax.shard_map(
        per_device,
        mesh=mesh,
        in_specs=placed,
        out_specs=(
            P(("ens", "lat", "ch"), "lon", None),
            P(("ens", "lat", "ch"), "lon", None),
            P("ens", None, "ch"),
            P("ens", "ch"),
        ),
        check_vma=False,
    )
```

```python
import functools
import math

import jax
import jax.numpy as jnp
from jax import lax
from jax.experimental import pallas as pl
from jax.experimental.pallas import tpu as pltpu
from jax.sharding import PartitionSpec as P

REACH = 8
TAP_REACH = 2
TILE = 16
MESH = pl.DeviceIdType.MESH
BF16 = jnp.bfloat16
F32 = jnp.float32


def along(axis, steps):
    count = lax.axis_size(axis)
    return {axis: lax.rem(lax.axis_index(axis) + steps + count, count)}


def neighbour(row_step, col_step):
    ch_count = lax.axis_size("ch")
    bands = lax.axis_size("lat") * ch_count
    band = lax.axis_index("lat") * ch_count + lax.axis_index("ch")
    band = lax.rem(band + row_step + bands, bands)
    target = {}
    if row_step:
        target = {"lat": band // ch_count, "ch": lax.rem(band, ch_count)}
    if col_step:
        target.update(along("lon", col_step))
    return target


AROUND = [(r, c) for r in (-1, 0, 1) for c in (-1, 0, 1) if r or c]


def greet():
    targets = [neighbour(r, c) for r, c in AROUND]
    for axis in ("ch", "lat", "lon"):
        targets += [along(axis, step) for step in range(1, lax.axis_size(axis))]
    barrier = pltpu.get_barrier_semaphore()
    for target in targets:
        pl.semaphore_signal(barrier, inc=1, device_id=target, device_id_type=MESH)
    pl.semaphore_wait(barrier, len(targets))


class Sender:
    def __init__(self, sems):
        self.ssem, self.rsem = sems
        self.pending = []

    def send(self, source, target, slot, device):
        copy = pltpu.make_async_remote_copy(
            src_ref=source,
            dst_ref=target,
            send_sem=self.ssem.at[slot],
            recv_sem=self.rsem.at[slot],
            device_id=device,
            device_id_type=MESH,
        )
        copy.start()
        self.pending.append(copy)

    def settle(self):
        for copy in self.pending:
            copy.wait()
        self.pending = []


class GradSum(Sender):
    def __init__(self, result, bufs):
        super().__init__(bufs[-2:])
        self.result = result
        self.source, self.rec_ch, self.part, self.rec_lat, self.strip, self.rec_pair, self.half, self.rec_far, self.piece = bufs[:-2]
        self.width = self.part.shape[1]
        self.lat, self.lon = lax.axis_size("lat"), lax.axis_size("lon")
        self.height = self.strip.shape[0]
        self.span = self.piece.shape[0]
        self.pair = self.height // self.span
        self.far = self.lon // self.pair
        self.side = lax.rem(lax.axis_index("lon"), self.pair)

    @staticmethod
    def scratch(sizes, rows, columns):
        lat, lon = sizes
        width = columns // 2
        height = rows // lat
        pair = 2 if lon % 2 == 0 and height % (2 * TILE) == 0 else 1
        span, far = height // pair, lon // pair
        count = 1 + 2 * (lat - 1) + 2 * (pair - 1) + far - 1
        return [
            pltpu.VMEM((rows, columns), BF16),
            pltpu.VMEM((rows, width), BF16),
            pltpu.VMEM((rows, width), BF16),
            pltpu.VMEM((lat - 1, height, width), BF16),
            pltpu.VMEM((height, width), BF16),
            pltpu.VMEM((span, width), BF16),
            pltpu.VMEM((span, width), BF16),
            pltpu.VMEM((far - 1, span, width), BF16),
            pltpu.VMEM((span, width), BF16),
            pltpu.SemaphoreType.DMA((count,)),
            pltpu.SemaphoreType.DMA((count,)),
        ]

    def columns(self, half):
        return pl.ds(pl.multiple_of(half * self.width, self.width), self.width)

    @staticmethod
    def stretch(owner, size):
        return pl.ds(pl.multiple_of(owner * size, size), size)

    def start_ch(self):
        other = 1 - lax.axis_index("ch")
        self.send(self.source.at[:, self.columns(other)], self.rec_ch, 0, {"ch": other})

    def start_lat(self):
        self.settle()
        own = self.source[:, self.columns(lax.axis_index("ch"))].astype(F32)
        self.part[...] = (own + self.rec_ch[...].astype(F32)).astype(BF16)
        for step in range(1, self.lat):
            peer = along("lat", step)
            rows = self.stretch(peer["lat"], self.height)
            self.send(self.part.at[rows], self.rec_lat.at[step - 1], step, peer)

    def start_lon(self):
        self.settle()
        total = self.part[self.stretch(lax.axis_index("lat"), self.height), :].astype(F32)
        for step in range(1, self.lat):
            total = total + self.rec_lat[step - 1].astype(F32)
        self.strip[...] = total.astype(BF16)
        if self.pair > 1:
            rows = self.stretch(1 - self.side, self.span)
            self.send(self.strip.at[rows], self.rec_pair, self.lat, along("lon", 1 - 2 * self.side))

    def start_far(self):
        self.settle()
        total = self.strip[self.stretch(self.side, self.span), :].astype(F32)
        if self.pair > 1:
            total = total + self.rec_pair[...].astype(F32)
        self.half[...] = total.astype(BF16)
        for step in range(1, self.far):
            self.send(
                self.half, self.rec_far.at[step - 1], self.lat + step, along("lon", self.pair * step)
            )

    def gather_lon(self):
        self.settle()
        total = self.half[...].astype(F32)
        for step in range(1, self.far):
            total = total + self.rec_far[step - 1].astype(F32)
        self.piece[...] = total.astype(BF16)
        offset = lax.axis_index("lat") * self.height + self.side * self.span
        rows = pl.ds(pl.multiple_of(offset, TILE), self.span)
        self.result[rows, :] = self.piece[...]
        if self.pair > 1:
            slot = self.lat + self.far
            self.send(self.piece, self.result.at[rows], slot, along("lon", 1 - 2 * self.side))

    def gather_lat(self):
        self.settle()
        rows = self.stretch(lax.axis_index("lat"), self.height)
        for step in range(1, self.lat):
            slot = self.lat + self.far + self.pair - 2 + step
            self.send(self.result.at[rows], self.result.at[rows], slot, along("lat", step))

    def finish(self):
        self.settle()


STAGES = ("start_ch", "start_lat", "start_lon", "start_far", "gather_lon", "gather_lat", "finish")


class Halo(Sender):
    def __init__(self, bufs):
        super().__init__(bufs[-2:])
        self.out_side, self.out_row, self.in_side, self.in_row = bufs[:-2]

    @staticmethod
    def scratch(rows, cols, width, row_blocks):
        return [
            pltpu.VMEM((2, rows * REACH, width), BF16),
            pltpu.VMEM((row_blocks, cols, width), BF16),
            pltpu.VMEM((2, rows * REACH, width), BF16),
            pltpu.VMEM((6, cols, width), BF16),
            pltpu.SemaphoreType.DMA((8,)),
            pltpu.SemaphoreType.DMA((8,)),
        ]

    def start(self, row_block_of):
        self.send(self.out_side.at[0], self.in_side.at[1], 0, neighbour(0, -1))
        self.send(self.out_side.at[1], self.in_side.at[0], 1, neighbour(0, 1))
        slot = 2
        for row_step in (-1, 1):
            for col_step in (-1, 0, 1):
                place = (0 if row_step == 1 else 3) + 1 - col_step
                self.send(
                    self.out_row.at[row_block_of(row_step, col_step)],
                    self.in_row.at[place],
                    slot,
                    neighbour(row_step, col_step),
                )
                slot += 1


def edge_flags():
    ch_count = lax.axis_size("ch")
    bands = lax.axis_size("lat") * ch_count
    band = lax.axis_index("lat") * ch_count + lax.axis_index("ch")
    return band > 0, band < bands - 1


def extend(halo, state, ext, rows, cols):
    span = cols + 2 * REACH
    west, east = halo.in_side[0].astype(F32), halo.in_side[1].astype(F32)
    for row in range(rows):
        low, high = row * REACH, (row + 1) * REACH
        line = jnp.concatenate(
            [west[low:high], state[row * cols : (row + 1) * cols], east[low:high]], axis=0
        )
        ext[(row + 1) * span : (row + 2) * span, :] = line.astype(BF16)
    for first, row, flag in zip((0, 3), (0, rows + 1), edge_flags()):
        line = jnp.concatenate(
            [
                halo.in_row[first].astype(F32)[cols - REACH :],
                halo.in_row[first + 1].astype(F32),
                halo.in_row[first + 2].astype(F32)[:REACH],
            ],
            axis=0,
        )
        ext[row * span : (row + 1) * span, :] = jnp.where(flag, line, 0.0).astype(BF16)


def send_state(halo, state, rows, cols):
    pieces = [
        [state[r * cols : r * cols + REACH] for r in range(rows)],
        [state[(r + 1) * cols - REACH : (r + 1) * cols] for r in range(rows)],
    ]
    for side in range(2):
        halo.out_side[side] = jnp.concatenate(pieces[side], axis=0).astype(BF16)
    halo.out_row[0] = state[:cols].astype(BF16)
    halo.out_row[1] = state[(rows - 1) * cols :].astype(BF16)
    halo.start(lambda row_step, col_step: 0 if row_step == -1 else 1)


def send_spread(halo, spread, rows, cols):
    span = cols + 2 * REACH
    west = [spread[(r + 1) * span : (r + 1) * span + REACH, :] for r in range(rows)]
    east = [spread[(r + 2) * span - REACH : (r + 2) * span, :] for r in range(rows)]
    halo.out_side[0] = jnp.concatenate(west, axis=0).astype(BF16)
    halo.out_side[1] = jnp.concatenate(east, axis=0).astype(BF16)
    for block, row in enumerate((0, rows + 1)):
        base = row * span
        halo.out_row[2 * block] = spread[base + REACH : base + REACH + cols, :].astype(BF16)
        corners = [spread[base : base + REACH, :], spread[base + span - REACH : base + span, :]]
        if cols > 2 * REACH:
            corners.insert(1, jnp.zeros((cols - 2 * REACH, spread.shape[1]), F32))
        halo.out_row[2 * block + 1] = jnp.concatenate(corners, axis=0).astype(BF16)
    halo.start(
        lambda row_step, col_step: (0 if row_step == -1 else 2) + (1 if col_step else 0)
    )


def take_spread(halo, spread, gradient, rows, cols):
    span = cols + 2 * REACH
    west, east = halo.in_side[0].astype(F32), halo.in_side[1].astype(F32)
    outer = {}
    for first, row, flag in zip((0, 3), (0, rows - 1), edge_flags()):
        line = halo.in_row[first + 1].astype(F32)
        rim_west = halo.in_row[first].astype(F32)[cols - REACH :]
        rim_east = halo.in_row[first + 2].astype(F32)[:REACH]
        rims = [rim_west, rim_east]
        if cols > 2 * REACH:
            rims.insert(1, jnp.zeros((cols - 2 * REACH, line.shape[1]), F32))
        outer[row] = jnp.where(flag, line + jnp.concatenate(rims, axis=0), 0.0)
    result = []
    for row in range(rows):
        low, high = row * REACH, (row + 1) * REACH
        rims = [west[low:high], east[low:high]]
        if cols > 2 * REACH:
            rims.insert(1, jnp.zeros((cols - 2 * REACH, west.shape[1]), F32))
        base = (row + 1) * span + REACH
        line = spread[base : base + cols, :] + jnp.concatenate(rims, axis=0)
        if row in outer:
            line = line + outer[row]
        result.append(gradient[row * cols : (row + 1) * cols].astype(F32) + line)
    return result


def aligned(index, size):
    return pl.ds(pl.multiple_of(index * size, size), size)


GROUP = 16


def over_rows(rows, body):
    group = GROUP if rows % GROUP == 0 else 1

    def step(index, carry):
        for inner in range(group):
            body(index * group + inner)
        return carry

    lax.fori_loop(0, rows // group, step, 0)


def make_bands(base, bands, rows, cols, basis_count):
    width = base.shape[1]

    def one(row):
        table = base[aligned(row, 2 * basis_count), :]
        for k in range(basis_count):
            line = jnp.broadcast_to(table[k : k + 1], (cols, width))
            moved = pltpu.roll(line, 0, 1, stride=1, stride_axis=0)
            start = pl.multiple_of((row * basis_count + k) * cols, cols)
            bands[pl.ds(start, cols), :] = moved.astype(BF16)

    over_rows(rows, one)


def stencil(bands, ext, features, rows, cols, basis_count):
    span = cols + 2 * REACH
    channels = ext.shape[1]

    def one(row):
        lhs = bands[aligned(row, basis_count * cols), :][:, : 3 * span]
        rhs = ext[pl.ds(pl.multiple_of(row * span, span), 3 * span), :]
        out = jnp.dot(lhs, rhs, preferred_element_type=F32).astype(BF16)
        for k in range(basis_count):
            features[aligned(row, cols), k * channels : (k + 1) * channels] = out[
                k * cols : (k + 1) * cols
            ]

    over_rows(rows, one)


def adjoint(bands, errs, spread, rows, cols, basis_count):
    span = cols + 2 * REACH
    spread[...] = jnp.zeros_like(spread)

    def one(row):
        lhs = bands[aligned(row, basis_count * cols), :][:, : 3 * span]
        rhs = errs[aligned(row, basis_count * cols), :]
        out = lax.dot_general(lhs, rhs, (((0,), (0,)), ((), ())), preferred_element_type=F32)
        place = pl.ds(pl.multiple_of(row * span, span), 3 * span)
        spread[place, :] = spread[place, :] + out

    over_rows(rows, one)


def rows_product(left, right):
    return lax.dot_general(left, right, (((0,), (0,)), ((), ())), preferred_element_type=F32)
TAPS_LEFT = TAP_REACH


class InputHalo(Sender):
    def __init__(self, bufs):
        super().__init__(bufs[-2:])
        (
            self.edges,
            self.out_cols,
            self.out_table,
            self.in_cols,
            self.in_row,
            self.in_table,
            self.in_tile,
        ) = bufs[:-2]

    @staticmethod
    def scratch(rows_in, cols_in, width, table_rows, lanes):
        return [
            pltpu.VMEM((3, rows_in, width), F32),
            pltpu.VMEM((3, rows_in, width), BF16),
            pltpu.VMEM((2, table_rows, lanes), F32),
            pltpu.VMEM((3, rows_in, width), BF16),
            pltpu.VMEM((2, cols_in, width), BF16),
            pltpu.VMEM((2, table_rows, lanes), F32),
            pltpu.VMEM((4, TILE, width), BF16),
            pltpu.SemaphoreType.DMA((10,)),
            pltpu.SemaphoreType.DMA((10,)),
        ]

    def start(self, field, table, owner, rows_in, cols_in):
        first = own_first_row(rows_in // 2)
        table_rows = self.out_table.shape[1]
        for block, row, target in ((0, 0, first - 1), (1, rows_in - 1, first + rows_in // 2)):
            feeds = jnp.where(owner[row] == target, 1.0, 0.0)
            self.out_table[block] = table[row * table_rows : (row + 1) * table_rows, :] * feeds
        last = (rows_in - 1) * cols_in
        lines = (field.at[pl.ds(0, cols_in)], field.at[pl.ds(last, cols_in)])
        slot = 0
        for block, row_step in ((0, -1), (1, 1)):
            self.send(lines[block], self.in_row.at[1 - block], slot, neighbour(row_step, 0))
            base = block * last
            west = field.at[pl.ds(base, TILE)]
            east = field.at[pl.ds(base + cols_in - TILE, TILE)]
            place = 2 * (1 - block)
            self.send(west, self.in_tile.at[place + 1], slot + 1, neighbour(row_step, -1))
            self.send(east, self.in_tile.at[place], slot + 2, neighbour(row_step, 1))
            slot += 3

        def one(row):
            low = field[pl.ds(pl.multiple_of(row * cols_in, TILE), TILE), :].astype(F32)
            start = pl.multiple_of(row * cols_in + cols_in - TILE, TILE)
            high = field[pl.ds(start, TILE), :].astype(F32)
            self.edges[0, pl.ds(row, 1), :] = high[TILE - 2 : TILE - 1]
            self.edges[1, pl.ds(row, 1), :] = high[TILE - 1 : TILE]
            self.edges[2, pl.ds(row, 1), :] = low[0:1]

        over_rows(rows_in, one)
        self.out_cols[...] = self.edges[...].astype(BF16)
        self.send(self.out_cols.at[pl.ds(0, 2)], self.in_cols.at[pl.ds(0, 2)], 6, neighbour(0, 1))
        self.send(self.out_cols.at[2], self.in_cols.at[2], 7, neighbour(0, -1))
        self.send(self.out_table.at[0], self.in_table.at[1], 8, neighbour(-1, 0))
        self.send(self.out_table.at[1], self.in_table.at[0], 9, neighbour(1, 0))


def own_first_row(rows):
    return (lax.axis_index("lat") * lax.axis_size("ch") + lax.axis_index("ch")) * rows


def tap_matrix(table, basis_count, cols, cols_in):
    lanes = table.shape[1]
    blocks = []
    for k in range(basis_count):
        line = jnp.broadcast_to(table[k : k + 1], (cols, lanes))
        moved = pltpu.roll(line, 0, 1, stride=2, stride_axis=0)
        wrapped = pltpu.roll(moved, cols_in + TILE - TAPS_LEFT, 1)
        moved = pltpu.roll(moved, lanes - TAPS_LEFT, 1)
        lane = lax.broadcasted_iota(jnp.int32, (cols, lanes), 1)
        at_end = (lane >= cols_in + TILE - TAPS_LEFT) & (lane < cols_in + TILE)
        blocks.append(jnp.where(at_end, wrapped, moved))
    return jnp.concatenate(blocks, axis=0)[:, : cols_in + TILE].astype(BF16)


def filtered_row(table, line, left_two, left_one, right, basis_count, cols, cols_in):
    width = line.shape[1]
    place = lax.broadcasted_iota(jnp.int32, (TILE, width), 0)
    tile = jnp.where(place == 0, jnp.broadcast_to(right, (TILE, width)), 0.0)
    tile = jnp.where(place == TILE - 2, jnp.broadcast_to(left_two, (TILE, width)), tile)
    tile = jnp.where(place == TILE - 1, jnp.broadcast_to(left_one, (TILE, width)), tile)
    rhs = jnp.concatenate([line, tile.astype(BF16)], axis=0)
    lhs = tap_matrix(table, basis_count, cols, cols_in)
    return jnp.dot(lhs, rhs, preferred_element_type=F32).astype(BF16)


def finish_encode(halo, field, table, owner, filtered, latent_in, plan, rows_in, cols_in):
    rows, cols, basis_count, _ = plan
    table_rows = halo.out_table.shape[1]
    block = basis_count * cols
    width = field.shape[1]
    halo.settle()
    halo.edges[...] = halo.in_cols[...].astype(F32)

    def one(row):
        sides = [halo.edges[index, pl.ds(row, 1), :] for index in range(3)]
        line = field[aligned(row, cols_in), :]
        taps = table[aligned(row, table_rows), :]
        filtered[aligned(row + 1, block), :] = filtered_row(
            taps, line, *sides, basis_count, cols, cols_in
        )

    over_rows(rows_in, one)
    for side, row in ((0, 0), (1, rows_in + 1)):
        west = halo.in_tile[2 * side].astype(F32)
        east = halo.in_tile[2 * side + 1].astype(F32)
        filtered[row * block : (row + 1) * block, :] = filtered_row(
            halo.in_table[side],
            halo.in_row[side],
            west[TILE - 2 : TILE - 1],
            west[TILE - 1 : TILE],
            east[0:1],
            basis_count,
            cols,
            cols_in,
        )
    first = own_first_row(rows)
    for row in range(rows):
        total = None
        for offset in range(-1, 3):
            source = 2 * row + offset
            term = filtered[(source + 1) * block : (source + 2) * block, :].astype(F32)
            if 0 <= source < rows_in:
                term = term * jnp.where(owner[source] == first + row, 1.0, 0.0)
            total = term if total is None else total + term
        total = total.astype(BF16)
        for k in range(basis_count):
            latent_in[row * cols : (row + 1) * cols, k * width : (k + 1) * width] = total[
                k * cols : (k + 1) * cols
            ]


def lanes_of(count):
    return -(-(count + 2 * TILE) // 128) * 128


def net_kernel(plan, *refs):
    rows, cols, basis_count, layers = plan
    field, table, owner, encoder_weight, base, weights, cotangent = refs[:7]
    state_out, latent_grad = refs[7:9]
    results = refs[9 : 10 + layers]
    rest = list(refs[10 + layers :])
    bands, ext, spread, errs, features, preact, filtered, latent_in = rest[:8]
    input_halo = InputHalo(rest[8:17])
    rest = rest[17:]
    halos = []
    for _ in range(2 * layers):
        halos.append(Halo(rest[:6]))
        rest = rest[6:]
    sums = []
    for index in range(layers + 1):
        sums.append(GradSum(results[index], rest[:11]))
        rest = rest[11:]
    channels = ext.shape[1]
    progress = [0] * (layers + 1)

    def advance(index):
        getattr(sums[index], STAGES[progress[index]])()
        progress[index] += 1

    greet()
    rows_in = owner.shape[0]
    cols_in = field.shape[0] // rows_in
    input_halo.start(field, table, owner, rows_in, cols_in)
    make_bands(base, bands, rows, cols, basis_count)
    finish_encode(input_halo, field, table, owner, filtered, latent_in, plan, rows_in, cols_in)
    state = jnp.dot(latent_in[...], encoder_weight[...], preferred_element_type=F32)
    state = state.astype(BF16).astype(F32)
    for layer in range(layers):
        send_state(halos[layer], state, rows, cols)
        halos[layer].settle()
        extend(halos[layer], state, ext, rows, cols)
        stencil(bands, ext, features.at[layer], rows, cols, basis_count)
        pre = jnp.dot(features[layer], weights[layer], preferred_element_type=F32)
        preact[layer] = pre
        state = (state + pre / (1.0 + jnp.exp(-pre))).astype(BF16).astype(F32)
    state_out[...] = state.astype(BF16)

    gradient = cotangent[...].astype(F32)
    for layer in reversed(range(layers)):
        pre = preact[layer]
        sigma = 1.0 / (1.0 + jnp.exp(-pre))
        act_grad = (gradient * sigma * (1.0 + pre * (1.0 - sigma))).astype(BF16)
        for k in range(basis_count):
            block = weights[layer, k * channels : (k + 1) * channels, :]
            out = lax.dot_general(
                act_grad, block, (((1,), (1,)), ((), ())), preferred_element_type=F32
            ).astype(BF16)
            for row in range(rows):
                start = (row * basis_count + k) * cols
                errs[start : start + cols, :] = out[row * cols : (row + 1) * cols]
        adjoint(bands, errs, spread, rows, cols, basis_count)
        halo = halos[layers + layer]
        send_spread(halo, spread, rows, cols)
        sums[layer].source[...] = rows_product(features[layer], act_grad).astype(BF16)
        for other in range(layers - 1, layer - 1, -1):
            advance(other)
        halo.settle()
        for other in range(layers - 1, layer - 1, -1):
            advance(other)
        lines = take_spread(halo, spread, gradient, rows, cols)
        gradient = jnp.concatenate(lines, axis=0).astype(BF16).astype(F32)
    latent_grad[...] = gradient.astype(BF16)
    sums[layers].source[...] = rows_product(latent_in[...], gradient.astype(BF16)).astype(BF16)
    advance(layers)
    while min(progress) < len(STAGES):
        for index in [layers] + list(range(layers))[::-1]:
            if progress[index] < len(STAGES):
                advance(index)


def run_net(plan, sizes, field_in, table, owner, encoder_weight, base, weights, cotangent):
    rows, cols, basis_count, layers = plan
    cells, channels = rows * cols, weights.shape[2]
    features = basis_count * channels
    span = cols + 2 * REACH
    rows_in = owner.shape[0]
    in_features = encoder_weight.shape[0]
    heights = [features] * layers + [in_features]
    scratch = [
        pltpu.VMEM((rows * basis_count * cols, base.shape[1]), BF16),
        pltpu.VMEM(((rows + 2) * span, channels), BF16),
        pltpu.VMEM(((rows + 2) * span, channels), F32),
        pltpu.VMEM((rows * basis_count * cols, channels), BF16),
        pltpu.VMEM((layers, cells, features), BF16),
        pltpu.VMEM((layers, cells, channels), F32),
        pltpu.VMEM(((rows_in + 2) * basis_count * cols, field_in.shape[1]), BF16),
        pltpu.VMEM((cells, in_features), BF16),
    ]
    scratch += InputHalo.scratch(
        rows_in, field_in.shape[0] // rows_in, field_in.shape[1], table.shape[0] // rows_in, table.shape[1]
    )
    for index in range(2 * layers):
        scratch += Halo.scratch(rows, cols, channels, 2 if index < layers else 4)
    for height in heights:
        scratch += GradSum.scratch(sizes, height, channels)
    vmem = pl.BlockSpec(memory_space=pltpu.VMEM)
    field = jax.ShapeDtypeStruct((cells, channels), BF16)
    grads = [jax.ShapeDtypeStruct((height, channels // 2), BF16) for height in heights]
    return pl.pallas_call(
        functools.partial(net_kernel, plan),
        out_shape=[field, field] + grads,
        in_specs=[vmem, vmem, pl.BlockSpec(memory_space=pltpu.SMEM)] + [vmem] * 4,
        out_specs=[vmem] * (3 + layers),
        scratch_shapes=scratch,
        compiler_params=pltpu.CompilerParams(
            collective_id=0, has_side_effects=True, vmem_limit_bytes=56 << 20
        ),
    )(field_in, table, owner, encoder_weight, base, weights, cotangent)


def per_device(
    input_field,
    encoder_filter,
    row_owner,
    encoder_weight,
    disco_basis,
    row_widths,
    block_weights,
    cotangent,
):
    if fits_chunks(
        cotangent.shape[0],
        input_field.shape[1],
        cotangent.shape[1],
        block_weights.shape[0],
        [block_weights.shape[1]] * block_weights.shape[0] + [encoder_weight.shape[0]],
    ):
        return per_device_chunks(
            input_field,
            encoder_filter,
            row_owner,
            encoder_weight,
            disco_basis,
            row_widths,
            block_weights,
            cotangent,
        )
    rows_in, cols_in, in_width = input_field.shape
    rows_dev = rows_in // 2
    cols_dev = cols_in // 2
    basis_count = encoder_filter.shape[1]
    tap_count = encoder_filter.shape[2]
    channels = block_weights.shape[2]
    layers = block_weights.shape[0]
    cell_count = rows_dev * cols_dev
    offsets = jnp.abs(jnp.arange(2 * REACH + 1, dtype=jnp.int32) - REACH)
    keep = offsets[None, :] <= row_widths[:, None]
    masked = jnp.where(keep[:, None, None, :], disco_basis, jnp.zeros_like(disco_basis))
    span = cols_dev + 2 * REACH
    table = jnp.pad(masked, ((0, 0), (0, basis_count), (0, 0), (0, span - masked.shape[3])))
    table = table.reshape(rows_dev * 2 * basis_count, 3 * span).astype(jnp.float32)
    lanes = lanes_of(2 * span)
    table = jnp.pad(table, ((0, 0), (0, lanes - 3 * span)))
    taps = jnp.pad(
        encoder_filter.astype(jnp.float32),
        ((0, 0), (0, basis_count), (0, lanes_of(cols_in) - tap_count)),
    ).reshape(rows_in * 2 * basis_count, -1)
    own_width = channels // lax.axis_size("ch")
    sizes = (lax.axis_size("lat"), lax.axis_size("lon"))
    plan = (rows_dev, cols_dev, basis_count, layers)
    outs = run_net(
        plan,
        sizes,
        input_field.reshape(rows_in * cols_in, in_width),
        taps,
        row_owner,
        encoder_weight,
        table,
        block_weights,
        cotangent.reshape(cell_count, channels),
    )
    current, gradient = (field.reshape(rows_dev, cols_dev, channels) for field in outs[:2])
    sums = [value.astype(jnp.float32) for value in outs[2:]]
    block_sum, encoder_sum = jnp.stack(sums[:-1]), sums[-1]
    cells_total = cell_count * lax.axis_size("lon") * lax.axis_size(("lat", "ch"))
    normalizer = 1.0 / math.sqrt(cells_total)
    block_grads = (block_sum * normalizer).reshape(layers, basis_count * channels, own_width)
    encoder_grad = encoder_sum * normalizer
    return (current, gradient, block_grads, encoder_grad)

HALO = 2
DIRECT, ACROSS, WIDE, PAIRED = range(4)
LANES = 128


class Place:
    def __init__(self):
        self.lon, self.ch = lax.axis_size("lon"), lax.axis_size("ch")
        self.bands = lax.axis_size("lat") * self.ch
        self.z = lax.axis_index("lon")
        self.band = lax.axis_index("lat") * self.ch + lax.axis_index("ch")
        self.chunk = self.flip(self.band, self.z)
        self.count = self.bands * self.lon
        self.position = self.band * self.lon + self.chunk

    def flip(self, band, index):
        return index + lax.rem(band, 2) * (self.lon - 1 - 2 * index)

    def offset(self, chunk):
        return (chunk + self.lon - 1) // self.lon + (chunk + 1) // self.lon

    def device(self, band, chunk):
        return {
            "lat": band // self.ch,
            "ch": lax.rem(band, self.ch),
            "lon": self.flip(band, chunk),
        }

    def along_snake(self, step):
        position = lax.rem(self.position + step + self.count, self.count)
        return self.device(position // self.lon, lax.rem(position, self.lon))


def greet_part():
    barrier = pltpu.get_barrier_semaphore()
    count = 0
    for lat in range(lax.axis_size("lat")):
        for ch in range(lax.axis_size("ch")):
            for lon in range(lax.axis_size("lon")):
                if lat or ch or lon:
                    target = {**along("lat", lat), **along("ch", ch), **along("lon", lon)}
                    pl.semaphore_signal(barrier, inc=1, device_id=target, device_id_type=MESH)
                    count += 1
    return lambda: pl.semaphore_wait(barrier, count)


class Regroup(Sender):
    def __init__(self, bufs, rim):
        self.rim = rim
        self.lines, self.rim_ssem, self.rim_rsem, self.own_sem = bufs[0], bufs[3], bufs[4], bufs[5]
        super().__init__(bufs[1:3])

    @staticmethod
    def scratch(lon, rows, cols, width, rim):
        return [
            pltpu.VMEM((rows + 2 + 2 * rim, cols, width), BF16),
            pltpu.SemaphoreType.DMA((lon - 1,)),
            pltpu.SemaphoreType.DMA((lon - 1,)),
            pltpu.SemaphoreType.DMA((2,)),
            pltpu.SemaphoreType.DMA((2 * lon,)),
            pltpu.SemaphoreType.DMA,
        ]

    def start_rims(self, place, source):
        self.place, self.source = place, source
        rows, piece = source.shape[0], source.shape[1]
        self.piece, self.each = piece, rows // place.lon
        self.size = self.each + 2 * self.rim
        self.columns = pl.ds(pl.multiple_of(place.z * piece, piece), piece)
        self.rims = []
        for side, (row, slot, step, chunk) in enumerate(
            ((rows - 1, 0, 1, 0), (0, self.size + 1, -1, place.lon - 1))[: 2 * self.rim]
        ):
            band = lax.rem(place.band + step + place.bands, place.bands)
            copy = pltpu.make_async_remote_copy(
                src_ref=source.at[row],
                dst_ref=self.lines.at[slot, self.columns],
                send_sem=self.rim_ssem.at[side],
                recv_sem=self.rim_rsem.at[side * place.lon + place.z],
                device_id=place.device(band, chunk),
                device_id_type=MESH,
            )
            copy.start()
            self.rims.append(copy)

    def start(self):
        place, source, each, size = self.place, self.source, self.each, self.size
        block = self.lines.at[pl.ds(1, size), self.columns]
        for step in range(1, place.lon):
            peer = along("lon", step)
            chunk = place.flip(place.band, peer["lon"])
            first = chunk * each - self.rim * place.offset(chunk)
            self.send(source.at[pl.ds(first, size)], block, step - 1, peer)
        first = place.chunk * each - self.rim * place.offset(place.chunk)
        self.own = pltpu.make_async_copy(source.at[pl.ds(first, size)], block, self.own_sem)
        self.own.start()

    def finish(self):
        place = self.place
        self.settle()
        self.own.wait()
        ends = ((0, 0), (self.size + 1, place.lon - 1))[: 2 * self.rim]
        for side, (slot, chunk) in enumerate(ends):

            @pl.when(place.chunk == chunk)
            def _():
                for z in range(place.lon):
                    pltpu.make_async_remote_copy(
                        src_ref=self.source.at[0],
                        dst_ref=self.lines.at[slot, pl.ds(z * self.piece, self.piece)],
                        send_sem=self.rim_ssem.at[side],
                        recv_sem=self.rim_rsem.at[side * place.lon + z],
                        device_id=along("lon", 0),
                        device_id_type=MESH,
                    ).wait_recv()

        for copy in self.rims:
            copy.wait_send()

    def row(self, index):
        return self.lines[index + 1 + self.rim * self.place.offset(self.place.chunk)]


class Restore(Sender):
    def __init__(self, bufs):
        self.lines, self.own_sem = bufs[0], bufs[3]
        super().__init__(bufs[1:3])

    @staticmethod
    def scratch(lon, rows, cols, width):
        return [
            pltpu.VMEM((rows, cols, width), BF16),
            pltpu.SemaphoreType.DMA((lon - 1,)),
            pltpu.SemaphoreType.DMA((lon - 1,)),
            pltpu.SemaphoreType.DMA,
        ]

    def start(self, place, result):
        rows, piece = self.lines.shape[0], result.shape[1]
        target = result.at[pl.ds(place.chunk * rows, rows)]
        for step in range(1, place.lon):
            peer = along("lon", step)
            columns = pl.ds(pl.multiple_of(peer["lon"] * piece, piece), piece)
            self.send(self.lines.at[:, columns], target, step - 1, peer)
        columns = pl.ds(pl.multiple_of(place.z * piece, piece), piece)
        self.own = pltpu.make_async_copy(self.lines.at[:, columns], target, self.own_sem)
        self.own.start()

    def finish(self):
        self.settle()
        self.own.wait()


class Swap(Sender):
    def __init__(self, bufs):
        super().__init__(bufs)

    @staticmethod
    def scratch():
        return [pltpu.SemaphoreType.DMA((2,)), pltpu.SemaphoreType.DMA((2,))]

    def start(self, place, buffer, slot_rows, own, halo):
        def part(first):
            return buffer.at[pl.ds(first * slot_rows, halo * slot_rows)]

        self.send(part(own), part(0), 0, place.along_snake(1))
        self.send(part(halo), part(halo + own), 1, place.along_snake(-1))


class ChipSum(Sender):
    def __init__(self, result, source, first, direct, bufs):
        super().__init__(bufs[-2:])
        self.result, self.source, self.first = result, source, first
        self.rec_ch, self.part, self.rec_lat, self.strip, self.rec, self.piece = bufs[:6]
        self.rec_pair, self.half, self.rec_far, self.whole = bufs[6:10]
        self.rows, self.width = self.part.shape
        self.lat, self.lon = lax.axis_size("lat"), lax.axis_size("lon")
        self.height, self.span = self.strip.shape[0], self.piece.shape[0]
        self.side = lax.rem(lax.axis_index("lon"), 2)
        self.direct = direct
        self.stages = [self.start_ch]
        if direct == DIRECT:
            self.stages += [self.scatter_all, self.gather_all]
        elif direct == ACROSS:
            self.stages += [self.scatter_lat, self.scatter_lon, self.gather_lon, self.gather_lat]
        elif direct == WIDE:
            self.stages += [self.scatter_lat, self.scatter_lon, self.gather_all]
        else:
            self.stages += [self.scatter_lat, self.scatter_pair, self.trade_far]
            self.stages += [self.gather_pair, self.gather_lat]
        self.stages.append(self.settle)

    @staticmethod
    def scratch(sizes, rows, columns):
        lat, lon = sizes
        width, height, span = columns // 2, rows // lat, rows // (lat * lon)
        count = 1 + 2 * (lat - 1) + 2 * (lat * lon - 1)
        return [
            pltpu.VMEM((rows, width), BF16),
            pltpu.VMEM((rows, width), BF16),
            pltpu.VMEM((lat - 1, height, width), BF16),
            pltpu.VMEM((height, width), BF16),
            pltpu.VMEM((lat * lon - 1, span, width), BF16),
            pltpu.VMEM((span, width), BF16),
            pltpu.VMEM((height // 2, width), BF16),
            pltpu.VMEM((height // 2, width), BF16),
            pltpu.VMEM((max(lon // 2 - 1, 1), height // 2, width), BF16),
            pltpu.VMEM((height // 2, width), BF16),
            pltpu.SemaphoreType.DMA((count,)),
            pltpu.SemaphoreType.DMA((count,)),
        ]

    def advance(self):
        self.stages.pop(0)()

    def columns(self, half):
        return pl.ds(pl.multiple_of(half * self.width, self.width), self.width)

    def own_columns(self):
        return self.source[self.first : self.first + self.rows, self.columns(lax.axis_index("ch"))]

    def others(self):
        for lat in range(self.lat):
            for lon in range(self.lon):
                if lat or lon:
                    yield lat * self.lon + lon - 1, {**along("lat", lat), **along("lon", lon)}

    def mine(self):
        return lax.axis_index("lat") * self.lon + lax.axis_index("lon")

    def place(self, index, size):
        return pl.ds(pl.multiple_of(index * size, size), size)

    def target(self, index, size):
        return pl.ds(pl.multiple_of(self.first + index * size, size), size)

    def start_ch(self):
        other = 1 - lax.axis_index("ch")
        rows = pl.ds(self.first, self.rows)
        self.send(self.source.at[rows, self.columns(other)], self.rec_ch, 0, {"ch": other})

    def add_ch(self):
        self.settle()
        total = self.own_columns().astype(F32) + self.rec_ch[...].astype(F32)
        self.part[...] = total.astype(BF16)

    def scatter_all(self):
        self.add_ch()
        for slot, peer in self.others():
            rows = self.place(peer["lat"] * self.lon + peer["lon"], self.span)
            self.send(self.part.at[rows], self.rec.at[slot], 1 + slot, peer)

    def scatter_lat(self):
        self.add_ch()
        self.slot = self.lat * self.lon
        for step in range(1, self.lat):
            peer = along("lat", step)
            rows = self.place(peer["lat"], self.height)
            self.send(self.part.at[rows], self.rec_lat.at[step - 1], self.slot, peer)
            self.slot += 1

    def add_lat(self):
        self.settle()
        total = self.part[self.place(lax.axis_index("lat"), self.height), :].astype(F32)
        for step in range(1, self.lat):
            total = total + self.rec_lat[step - 1].astype(F32)
        self.strip[...] = total.astype(BF16)

    def scatter_pair(self):
        self.add_lat()
        rows = self.place(1 - self.side, self.height // 2)
        self.send(self.strip.at[rows], self.rec_pair, 1, along("lon", 1 - 2 * self.side))

    def trade_far(self):
        self.settle()
        total = self.strip[self.place(self.side, self.height // 2), :].astype(F32)
        self.half[...] = (total + self.rec_pair[...].astype(F32)).astype(BF16)
        for step in range(1, self.lon // 2):
            self.send(self.half, self.rec_far.at[step - 1], 1 + step, along("lon", 2 * step))

    def gather_pair(self):
        self.settle()
        total = self.half[...].astype(F32)
        for step in range(1, self.lon // 2):
            total = total + self.rec_far[step - 1].astype(F32)
        self.whole[...] = total.astype(BF16)
        rows = self.target(2 * lax.axis_index("lat") + self.side, self.height // 2)
        self.result[rows, :] = self.whole[...]
        base = self.lat * self.lon + self.lat - 1
        self.send(self.whole, self.result.at[rows], base, along("lon", 1 - 2 * self.side))

    def scatter_lon(self):
        self.add_lat()
        for step in range(1, self.lon):
            peer = along("lon", step)
            rows = self.place(peer["lon"], self.span)
            self.send(self.strip.at[rows], self.rec.at[step - 1], step, peer)

    def add_rest(self):
        self.settle()
        if self.direct == DIRECT:
            total, count = self.part[self.place(self.mine(), self.span), :], self.lat * self.lon
        else:
            total, count = self.strip[self.place(lax.axis_index("lon"), self.span), :], self.lon
        total = total.astype(F32)
        for step in range(1, count):
            total = total + self.rec[step - 1].astype(F32)
        self.piece[...] = total.astype(BF16)
        rows = self.target(self.mine(), self.span)
        self.result[rows, :] = self.piece[...]
        return self.result.at[rows], self.lat * self.lon + self.lat - 1

    def gather_all(self):
        target, base = self.add_rest()
        for slot, peer in self.others():
            self.send(self.piece, target, base + slot, peer)

    def gather_lon(self):
        target, base = self.add_rest()
        for step in range(1, self.lon):
            self.send(self.piece, target, base + step - 1, along("lon", step))

    def gather_lat(self):
        self.settle()
        rows = self.target(lax.axis_index("lat"), self.height)
        base = 2 * self.lat * self.lon + self.lat - 2
        for step in range(1, self.lat):
            self.send(self.result.at[rows], self.result.at[rows], base + step - 1, along("lat", step))


def zero_outside(place, buffer, first, last, size):
    @pl.when(place.position == 0)
    def _():
        buffer[first : first + size, :] = jnp.zeros((size, buffer.shape[1]), buffer.dtype)

    @pl.when(place.position == place.count - 1)
    def _():
        buffer[last : last + size, :] = jnp.zeros((size, buffer.shape[1]), buffer.dtype)


def circulant(line, rows, stride):
    return pltpu.roll(jnp.broadcast_to(line, (rows, LANES)), 0, 1, stride=stride, stride_axis=0)


def silu_slope(pre):
    sigma = 1.0 / (1.0 + jnp.exp(-pre))
    return sigma * (1.0 + pre * (1.0 - sigma))


def chunk_kernel(plan, *refs):
    rows, cols, basis_count, layers = plan
    field, taps, owner, encoder_source, base, widths, weights_source, cotangent = refs[:8]
    state_out, latent_grad = refs[8:10]
    results = refs[10 : 11 + layers]
    rest = list(refs[11 + layers :])
    table, flat, lines, rims, bands, turned, latent_in, state, features, preact, steps, errs = rest[:12]
    encoder_weight, weights, load_sems = rest[12:15]
    rest = rest[15:]
    inputs, arriving = Regroup(rest[:6], 1), Regroup(rest[6:12], 0)
    leaving = [Restore(rest[12:16]), Restore(rest[16:20])]
    swaps = [Swap(rest[20 + 2 * n : 22 + 2 * n]) for n in range(5)]
    rest = rest[30:]
    sources, rest = rest[: layers + 1], rest[layers + 1 :]
    sums = []
    for index, first, size, direct in stretches([source.shape[0] for source in sources]):
        sums.append(ChipSum(results[index], sources[index], first, direct, rest[:12]))
        rest = rest[12:]
    channels = state.shape[1]
    width = field.shape[2]
    block = basis_count * cols
    ext = rows + 2 * HALO
    early, upper, lower, encoder = sums

    loads = [
        pltpu.make_async_copy(source, target, load_sems.at[index])
        for index, (source, target) in enumerate(
            ((encoder_source, encoder_weight), (weights_source, weights))
        )
    ]
    entered = greet_part()
    for load in loads:
        load.start()
    place = Place()
    first = place.position * rows
    rows_in = 2 * rows
    start_in = place.chunk * rows_in
    high, tall = table.shape[0] // ext, rims.shape[1]
    make_table(place, base, widths, table, rows, cols, basis_count, high)
    make_lines(taps, flat, lines, start_in, rows_in, basis_count)
    sides = (
        (0, jnp.where(owner[start_in] == first - 1, 1.0, 0.0)),
        (rows_in - 1, jnp.where(owner[start_in + rows_in - 1] == first + rows, 1.0, 0.0)),
    )
    for side, (row, feeds) in enumerate(sides):
        for k in range(basis_count):
            rims[side, k : k + 1, :] = lines[k * rows_in + row : k * rows_in + row + 1, :] * feeds
    entered()
    inputs.start_rims(place, field)
    swaps[0].start(place, table, high, rows, HALO)
    swaps[1].send(rims.at[1], rims.at[2], 0, place.along_snake(1))
    swaps[1].send(rims.at[0], rims.at[3], 1, place.along_snake(-1))
    inputs.start()

    lane = lax.broadcasted_iota(jnp.int32, (cols, LANES), 1)

    def make_band(row, carry):
        values = table[aligned(row, high), :]
        for k in range(basis_count):
            parts = [
                circulant(values[r * basis_count + k][None, :], cols, 1) for r in range(3)
            ]
            start = pl.multiple_of(row * block + k * cols, cols)
            bands[pl.ds(start, cols), :LANES] = jnp.where(lane < cols, parts[0], parts[1]).astype(BF16)
            bands[pl.ds(start, cols), LANES:] = parts[2].astype(BF16)
        other = bands[aligned(row, block), :].T
        for r in range(3):
            turned[aligned(row + r, cols), (2 - r) * block : (3 - r) * block] = other[
                r * cols : (r + 1) * cols
            ]
        return carry

    lax.fori_loop(HALO, HALO + rows, make_band, 0)
    swaps[0].settle()
    lax.fori_loop(0, HALO, make_band, 0)
    lax.fori_loop(HALO + rows, ext, make_band, 0)
    swaps[1].settle()
    inputs.finish()

    def filtered(row):
        if 0 <= row < rows_in:
            values = [lines[k * rows_in + row : k * rows_in + row + 1, :] for k in range(basis_count)]
        else:
            side = 2 if row < 0 else 3
            values = [rims[side, k : k + 1, :] for k in range(basis_count)]
        lhs = jnp.concatenate([circulant(value, cols, 2) for value in values], axis=0).astype(BF16)
        out = jnp.dot(lhs, inputs.row(row), preferred_element_type=F32)
        return out.astype(BF16).astype(F32)

    filters = [filtered(row) for row in range(-1, rows_in + 1)]
    for row in range(rows):
        total = None
        for step in range(-1, 3):
            source = 2 * row + step
            term = filters[source + 1]
            if 0 <= source < rows_in:
                term = term * jnp.where(owner[start_in + source] == first + row, 1.0, 0.0)
            total = term if total is None else total + term
        total = total.astype(BF16)
        for k in range(basis_count):
            latent_in[row * cols : (row + 1) * cols, k * width : (k + 1) * width] = total[
                k * cols : (k + 1) * cols
            ]
    own = pl.ds(HALO * cols, rows * cols)
    loads[0].wait()
    state[own, :] = jnp.dot(
        latent_in[...], encoder_weight[...], preferred_element_type=F32
    ).astype(BF16)
    swaps[2].start(place, state, cols, rows, HALO)
    arriving.start_rims(place, cotangent)
    arriving.start()
    loads[1].wait()
    swaps[2].settle()
    zero_outside(place, state, 0, (HALO + rows) * cols, HALO * cols)

    for layer in range(layers):
        low, top = layer + 1, ext - layer - 1
        for row in range(low, top):
            out = jnp.dot(
                bands[row * block : (row + 1) * block, : 3 * cols],
                state[(row - 1) * cols : (row + 2) * cols, :],
                preferred_element_type=F32,
            ).astype(BF16)
            for k in range(basis_count):
                features[layer, row * cols : (row + 1) * cols, k * channels : (k + 1) * channels] = out[
                    k * cols : (k + 1) * cols
                ]
        span = pl.ds(low * cols, (top - low) * cols)
        pre = jnp.dot(features[layer, span, :], weights[layer], preferred_element_type=F32)
        preact[layer, span, :] = pre
        new = state[span, :].astype(F32) + pre / (1.0 + jnp.exp(-pre))
        state[span, :] = new.astype(BF16)
        if layer < layers - 1:
            zero_outside(place, state, low * cols, (top - 1) * cols, cols)

    arriving.finish()
    last = layers - 1
    gradient = arriving.lines[1 : rows + 1].reshape(rows * cols, channels).astype(F32)
    act = gradient * silu_slope(preact[last, own, :])
    steps[last, own, :] = act.astype(BF16)
    swaps[3].start(place, steps.at[last], cols, rows, HALO)
    swaps[4].start(place, arriving.lines, 1, rows, 1)
    leaving[0].lines[...] = state[own, :].reshape(rows, cols, channels)

    def errors(layer, low, top):
        for k in range(basis_count):
            out = lax.dot_general(
                steps[layer, low * cols : top * cols, :],
                weights[layer, k * channels : (k + 1) * channels, :],
                (((1,), (1,)), ((), ())),
                preferred_element_type=F32,
            ).astype(BF16)
            for row in range(low, top):
                start = row * block + k * cols
                errs[start : start + cols, :] = out[(row - low) * cols : (row - low + 1) * cols]

    def spread(row):
        return jnp.dot(
            turned[(row + 1) * cols : (row + 2) * cols, :],
            errs[(row - 1) * block : (row + 2) * block, :],
            preferred_element_type=F32,
        )

    def weigh(part):
        stretch = slice(part.first, part.first + part.rows)
        left = features[0, own, stretch]
        sources[0][stretch, :] = rows_product(left, steps[0, own, :]).astype(BF16)

    leaving[0].start(place, state_out)
    sources[last][...] = rows_product(features[last, own, :], steps[last, own, :]).astype(BF16)
    early.advance()
    errors(last, HALO, HALO + rows)
    early.advance()
    swaps[3].settle()
    zero_outside(place, steps.at[last], 0, (HALO + rows) * cols, HALO * cols)
    errors(last, 0, HALO)
    errors(last, HALO + rows, ext)
    swaps[4].settle()
    back = [arriving.lines[row - 1].astype(F32) + spread(row) for row in range(1, ext - 1)]
    gradient = jnp.concatenate(back, axis=0).astype(BF16).astype(F32)
    span = pl.ds(cols, (ext - 2) * cols)
    steps[0, span, :] = (gradient * silu_slope(preact[0, span, :])).astype(BF16)
    zero_outside(place, steps.at[0], cols, (ext - 2) * cols, cols)
    weigh(upper)
    upper.advance()
    weigh(lower)
    lower.advance()
    early.advance()
    errors(0, 1, ext - 1)
    upper.advance()
    lower.advance()
    back = [
        gradient[(row - 1) * cols : row * cols] + spread(row) for row in range(HALO, HALO + rows)
    ]
    final = jnp.concatenate(back, axis=0).astype(BF16)
    leaving[1].lines[...] = final.reshape(rows, cols, channels)
    sources[layers][...] = rows_product(latent_in[...], final).astype(BF16)
    encoder.advance()
    encoder.advance()
    upper.advance()
    lower.advance()
    early.advance()
    upper.advance()
    encoder.advance()
    lower.advance()
    early.advance()
    upper.advance()
    lower.advance()
    leaving[1].start(place, latent_grad)
    for part in sums:
        while part.stages:
            part.advance()
    for part in leaving:
        part.finish()


def make_table(place, base, widths, table, rows, cols, basis_count, high):
    own = pl.ds(HALO * high, rows * high)
    table[own, :] = jnp.zeros((rows * high, LANES), F32)
    size = base.shape[3]
    reach = size // 2
    distance = jnp.abs(lax.broadcasted_iota(jnp.int32, (basis_count, size), 1) - reach)
    for row in range(rows):
        source = place.chunk * rows + row
        values = base[source].astype(F32)
        for r in range(3):
            start = (HALO + row) * high + r * basis_count
            table[start : start + basis_count, :size] = jnp.where(
                distance <= widths[source], values[r], 0.0
            )
    moved = pltpu.roll(table[own, :], LANES - reach, 1)
    table[own, :] = moved + pltpu.roll(moved, cols, 1)


def make_lines(taps, flat, lines, start_in, rows_in, basis_count):
    flat[...] = jnp.zeros_like(flat)
    count, _, held = taps.shape
    for k in range(basis_count):
        for t in range(count):
            row = 8 * k + t
            flat[row : row + 1, :held] = taps[t, k : k + 1, :].astype(F32)
    flat[...] = flat[...].T
    values = flat[aligned(start_in // rows_in, rows_in), :]
    lane = lax.broadcasted_iota(jnp.int32, values.shape, 1)
    for k in range(basis_count):
        moved = pltpu.roll(values, LANES - 8 * k, 1) if k else values
        kept = jnp.where(lane < count, moved, 0.0)
        lines[k * rows_in : (k + 1) * rows_in, :] = pltpu.roll(kept, LANES - count // 2, 1)


def stretches(heights):
    half = heights[0] // 2
    return [
        (len(heights) - 2, 0, heights[-2], ACROSS),
        (0, 0, half, ACROSS),
        (0, half, half, ACROSS),
        (len(heights) - 1, 0, heights[-1], DIRECT),
    ]


def run_chunks(
    plan, sizes, field_in, taps, owner, encoder_weight, base, widths, weights, cotangent
):
    rows, cols, basis_count, layers = plan
    lat, lon = sizes
    channels = weights.shape[2]
    features = basis_count * channels
    in_features = encoder_weight.shape[0]
    ext = rows + 2 * HALO
    heights = [features] * layers + [in_features]
    block = basis_count * cols
    high = -(-3 * basis_count // 8) * 8
    tall = -(-basis_count // 8) * 8
    scratch = [
        pltpu.VMEM((ext * high, LANES), F32),
        pltpu.VMEM((LANES, LANES), F32),
        pltpu.VMEM((basis_count * 2 * rows, LANES), F32),
        pltpu.VMEM((4, tall, LANES), F32),
        pltpu.VMEM((ext * block, 2 * LANES), BF16),
        pltpu.VMEM(((ext + 2) * cols, 3 * block), BF16),
        pltpu.VMEM((rows * cols, in_features), BF16),
        pltpu.VMEM((ext * cols, channels), BF16),
        pltpu.VMEM((layers, ext * cols, features), BF16),
        pltpu.VMEM((layers, ext * cols, channels), F32),
        pltpu.VMEM((layers, ext * cols, channels), BF16),
        pltpu.VMEM((ext * block, channels), BF16),
        pltpu.VMEM(encoder_weight.shape, BF16),
        pltpu.VMEM(weights.shape, BF16),
        pltpu.SemaphoreType.DMA((2,)),
    ]
    scratch += Regroup.scratch(lon, 2 * rows, field_in.shape[1] * lon, field_in.shape[2], 1)
    scratch += Regroup.scratch(lon, rows, cols, channels, 0)
    for _ in range(2):
        scratch += Restore.scratch(lon, rows, cols, channels)
    for _ in range(5):
        scratch += Swap.scratch()
    scratch += [pltpu.VMEM((height, channels), BF16) for height in heights]
    for _, _, size, _ in stretches(heights):
        scratch += ChipSum.scratch(sizes, size, channels)
    vmem = pl.BlockSpec(memory_space=pltpu.VMEM)
    smem = pl.BlockSpec(memory_space=pltpu.SMEM)
    hbm = pl.BlockSpec(memory_space=pltpu.HBM)
    out = jax.ShapeDtypeStruct(cotangent.shape, BF16)
    grads = [jax.ShapeDtypeStruct((height, channels // 2), BF16) for height in heights]
    return pl.pallas_call(
        functools.partial(chunk_kernel, plan),
        out_shape=[out, out] + grads,
        in_specs=[hbm, vmem, smem, hbm, vmem, smem, hbm, hbm],
        out_specs=[hbm, hbm] + [vmem] * (1 + layers),
        scratch_shapes=scratch,
        compiler_params=pltpu.CompilerParams(
            collective_id=1, has_side_effects=True, vmem_limit_bytes=56 << 20
        ),
    )(field_in, taps, owner, encoder_weight, base, widths, weights, cotangent)


def finish_body(normalizer, field_count, sum_count, refs):
    fields, sums = refs[:field_count], refs[field_count : field_count + sum_count]
    fields_out = refs[field_count + sum_count : 2 * field_count + sum_count]
    block_grads, encoder_grad = refs[2 * field_count + sum_count :][:2]
    rest = refs[2 * field_count + sum_count + 2 :]
    held, wide = rest[:sum_count], rest[sum_count : 2 * sum_count]
    kept = rest[2 * sum_count : 2 * sum_count + field_count]
    in_sems, out_sems = rest[2 * sum_count + field_count :]
    sources = list(zip(list(sums) + list(fields), list(held) + list(kept)))
    targets = [block_grads.at[n] for n in range(sum_count - 1)] + [encoder_grad] + list(fields_out)
    ready = list(wide) + list(kept)
    loads = [
        pltpu.make_async_copy(source, target, in_sems.at[n])
        for n, (source, target) in enumerate(sources)
    ]
    stores = [
        pltpu.make_async_copy(source, target, out_sems.at[n])
        for n, (source, target) in enumerate(zip(ready, targets))
    ]
    for load in loads:
        load.start()
    for n, (load, store) in enumerate(zip(loads, stores)):
        load.wait()
        if n < sum_count:
            wide[n][...] = held[n][...].astype(F32) * normalizer
        store.start()
    for store in stores:
        store.wait()


def finish_outputs(normalizer, outs):
    hbm = pl.BlockSpec(memory_space=pltpu.HBM)
    fields, sums = outs[:2], outs[2:]
    shapes = [jax.ShapeDtypeStruct(field.shape, field.dtype) for field in fields]
    shapes.append(jax.ShapeDtypeStruct((len(sums) - 1,) + sums[0].shape, F32))
    shapes.append(jax.ShapeDtypeStruct(sums[-1].shape, F32))

    def kernel(*refs):
        finish_body(normalizer, len(fields), len(sums), refs)

    return pl.pallas_call(
        kernel,
        out_shape=shapes,
        in_specs=[hbm] * len(outs),
        out_specs=[hbm] * len(shapes),
        scratch_shapes=[pltpu.VMEM(value.shape, BF16) for value in sums]
        + [pltpu.VMEM(value.shape, F32) for value in sums]
        + [pltpu.VMEM(value.shape, BF16) for value in fields]
        + [pltpu.SemaphoreType.DMA((len(outs),)) for _ in range(2)],
        compiler_params=pltpu.CompilerParams(vmem_limit_bytes=60 << 20),
    )(*outs)


def fits_chunks(rows_dev, cols_in, cols_dev, layers, heights):
    lon = lax.axis_size("lon")
    count = lax.axis_size("lat") * lon
    heights_fit = all(size % (count * TILE) == 0 for _, _, size, _ in stretches(heights))
    return (
        layers == HALO
        and rows_dev % lon == 0
        and heights_fit
        and rows_dev // lon >= HALO
        and lon % 2 == 0
        and cols_in * lon == LANES
        and 2 * cols_dev * lon == LANES
    )


def per_device_chunks(
    input_field,
    encoder_filter,
    row_owner,
    encoder_weight,
    disco_basis,
    row_widths,
    block_weights,
    cotangent,
):
    rows_in, cols_in, _ = input_field.shape
    lat, lon = lax.axis_size("lat"), lax.axis_size("lon")
    rows_dev, cols = rows_in // 2, cols_in // 2 * lon
    plan = (rows_dev // lon, cols, encoder_filter.shape[1], block_weights.shape[0])
    outs = run_chunks(
        plan,
        (lat, lon),
        input_field,
        encoder_filter.transpose(2, 1, 0),
        row_owner,
        encoder_weight,
        disco_basis.transpose(0, 2, 1, 3),
        row_widths,
        block_weights,
        cotangent,
    )
    cells_total = rows_dev * lax.axis_size(("lat", "ch")) * cols
    return tuple(finish_outputs(1.0 / math.sqrt(cells_total), outs))


def solution(mesh):
    placed = (
        P(("ens", "lat", "ch"), "lon", None),
        P(("lat", "ch"), None, None),
        P(("ens", "lat", "ch")),
        P(),
        P(("lat", "ch"), None, None, None),
        P(("lat", "ch")),
        P(),
        P(("ens", "lat", "ch"), "lon", None),
    )
    return jax.shard_map(
        per_device,
        mesh=mesh,
        in_specs=placed,
        out_specs=(
            P(("ens", "lat", "ch"), "lon", None),
            P(("ens", "lat", "ch"), "lon", None),
            P("ens", None, "ch"),
            P("ens", "ch"),
        ),
        check_vma=False,
    )
```

```python
import functools
import math

import jax
import jax.numpy as jnp
from jax import lax
from jax.experimental import pallas as pl
from jax.experimental.pallas import tpu as pltpu
from jax.sharding import PartitionSpec as P

REACH = 8
TAP_REACH = 2
TILE = 16
MESH = pl.DeviceIdType.MESH
BF16 = jnp.bfloat16
F32 = jnp.float32


def along(axis, steps):
    count = lax.axis_size(axis)
    return {axis: lax.rem(lax.axis_index(axis) + steps + count, count)}


def neighbour(row_step, col_step):
    ch_count = lax.axis_size("ch")
    bands = lax.axis_size("lat") * ch_count
    band = lax.axis_index("lat") * ch_count + lax.axis_index("ch")
    band = lax.rem(band + row_step + bands, bands)
    target = {}
    if row_step:
        target = {"lat": band // ch_count, "ch": lax.rem(band, ch_count)}
    if col_step:
        target.update(along("lon", col_step))
    return target


AROUND = [(r, c) for r in (-1, 0, 1) for c in (-1, 0, 1) if r or c]


def greet():
    targets = [neighbour(r, c) for r, c in AROUND]
    for axis in ("ch", "lat", "lon"):
        targets += [along(axis, step) for step in range(1, lax.axis_size(axis))]
    barrier = pltpu.get_barrier_semaphore()
    for target in targets:
        pl.semaphore_signal(barrier, inc=1, device_id=target, device_id_type=MESH)
    pl.semaphore_wait(barrier, len(targets))


class Sender:
    def __init__(self, sems):
        self.ssem, self.rsem = sems
        self.pending = []

    def send(self, source, target, slot, device):
        copy = pltpu.make_async_remote_copy(
            src_ref=source,
            dst_ref=target,
            send_sem=self.ssem.at[slot],
            recv_sem=self.rsem.at[slot],
            device_id=device,
            device_id_type=MESH,
        )
        copy.start()
        self.pending.append(copy)

    def settle(self):
        for copy in self.pending:
            copy.wait()
        self.pending = []


class GradSum(Sender):
    def __init__(self, result, bufs):
        super().__init__(bufs[-2:])
        self.result = result
        self.source, self.rec_ch, self.part, self.rec_lat, self.strip, self.rec_pair, self.half, self.rec_far, self.piece = bufs[:-2]
        self.width = self.part.shape[1]
        self.lat, self.lon = lax.axis_size("lat"), lax.axis_size("lon")
        self.height = self.strip.shape[0]
        self.span = self.piece.shape[0]
        self.pair = self.height // self.span
        self.far = self.lon // self.pair
        self.side = lax.rem(lax.axis_index("lon"), self.pair)

    @staticmethod
    def scratch(sizes, rows, columns):
        lat, lon = sizes
        width = columns // 2
        height = rows // lat
        pair = 2 if lon % 2 == 0 and height % (2 * TILE) == 0 else 1
        span, far = height // pair, lon // pair
        count = 1 + 2 * (lat - 1) + 2 * (pair - 1) + far - 1
        return [
            pltpu.VMEM((rows, columns), BF16),
            pltpu.VMEM((rows, width), BF16),
            pltpu.VMEM((rows, width), BF16),
            pltpu.VMEM((lat - 1, height, width), BF16),
            pltpu.VMEM((height, width), BF16),
            pltpu.VMEM((span, width), BF16),
            pltpu.VMEM((span, width), BF16),
            pltpu.VMEM((far - 1, span, width), BF16),
            pltpu.VMEM((span, width), BF16),
            pltpu.SemaphoreType.DMA((count,)),
            pltpu.SemaphoreType.DMA((count,)),
        ]

    def columns(self, half):
        return pl.ds(pl.multiple_of(half * self.width, self.width), self.width)

    @staticmethod
    def stretch(owner, size):
        return pl.ds(pl.multiple_of(owner * size, size), size)

    def start_ch(self):
        other = 1 - lax.axis_index("ch")
        self.send(self.source.at[:, self.columns(other)], self.rec_ch, 0, {"ch": other})

    def start_lat(self):
        self.settle()
        own = self.source[:, self.columns(lax.axis_index("ch"))].astype(F32)
        self.part[...] = (own + self.rec_ch[...].astype(F32)).astype(BF16)
        for step in range(1, self.lat):
            peer = along("lat", step)
            rows = self.stretch(peer["lat"], self.height)
            self.send(self.part.at[rows], self.rec_lat.at[step - 1], step, peer)

    def start_lon(self):
        self.settle()
        total = self.part[self.stretch(lax.axis_index("lat"), self.height), :].astype(F32)
        for step in range(1, self.lat):
            total = total + self.rec_lat[step - 1].astype(F32)
        self.strip[...] = total.astype(BF16)
        if self.pair > 1:
            rows = self.stretch(1 - self.side, self.span)
            self.send(self.strip.at[rows], self.rec_pair, self.lat, along("lon", 1 - 2 * self.side))

    def start_far(self):
        self.settle()
        total = self.strip[self.stretch(self.side, self.span), :].astype(F32)
        if self.pair > 1:
            total = total + self.rec_pair[...].astype(F32)
        self.half[...] = total.astype(BF16)
        for step in range(1, self.far):
            self.send(
                self.half, self.rec_far.at[step - 1], self.lat + step, along("lon", self.pair * step)
            )

    def gather_lon(self):
        self.settle()
        total = self.half[...].astype(F32)
        for step in range(1, self.far):
            total = total + self.rec_far[step - 1].astype(F32)
        self.piece[...] = total.astype(BF16)
        offset = lax.axis_index("lat") * self.height + self.side * self.span
        rows = pl.ds(pl.multiple_of(offset, TILE), self.span)
        self.result[rows, :] = self.piece[...]
        if self.pair > 1:
            slot = self.lat + self.far
            self.send(self.piece, self.result.at[rows], slot, along("lon", 1 - 2 * self.side))

    def gather_lat(self):
        self.settle()
        rows = self.stretch(lax.axis_index("lat"), self.height)
        for step in range(1, self.lat):
            slot = self.lat + self.far + self.pair - 2 + step
            self.send(self.result.at[rows], self.result.at[rows], slot, along("lat", step))

    def finish(self):
        self.settle()


STAGES = ("start_ch", "start_lat", "start_lon", "start_far", "gather_lon", "gather_lat", "finish")


class Halo(Sender):
    def __init__(self, bufs):
        super().__init__(bufs[-2:])
        self.out_side, self.out_row, self.in_side, self.in_row = bufs[:-2]

    @staticmethod
    def scratch(rows, cols, width, row_blocks):
        return [
            pltpu.VMEM((2, rows * REACH, width), BF16),
            pltpu.VMEM((row_blocks, cols, width), BF16),
            pltpu.VMEM((2, rows * REACH, width), BF16),
            pltpu.VMEM((6, cols, width), BF16),
            pltpu.SemaphoreType.DMA((8,)),
            pltpu.SemaphoreType.DMA((8,)),
        ]

    def start(self, row_block_of):
        self.send(self.out_side.at[0], self.in_side.at[1], 0, neighbour(0, -1))
        self.send(self.out_side.at[1], self.in_side.at[0], 1, neighbour(0, 1))
        slot = 2
        for row_step in (-1, 1):
            for col_step in (-1, 0, 1):
                place = (0 if row_step == 1 else 3) + 1 - col_step
                self.send(
                    self.out_row.at[row_block_of(row_step, col_step)],
                    self.in_row.at[place],
                    slot,
                    neighbour(row_step, col_step),
                )
                slot += 1


def edge_flags():
    ch_count = lax.axis_size("ch")
    bands = lax.axis_size("lat") * ch_count
    band = lax.axis_index("lat") * ch_count + lax.axis_index("ch")
    return band > 0, band < bands - 1


def extend(halo, state, ext, rows, cols):
    span = cols + 2 * REACH
    west, east = halo.in_side[0].astype(F32), halo.in_side[1].astype(F32)
    for row in range(rows):
        low, high = row * REACH, (row + 1) * REACH
        line = jnp.concatenate(
            [west[low:high], state[row * cols : (row + 1) * cols], east[low:high]], axis=0
        )
        ext[(row + 1) * span : (row + 2) * span, :] = line.astype(BF16)
    for first, row, flag in zip((0, 3), (0, rows + 1), edge_flags()):
        line = jnp.concatenate(
            [
                halo.in_row[first].astype(F32)[cols - REACH :],
                halo.in_row[first + 1].astype(F32),
                halo.in_row[first + 2].astype(F32)[:REACH],
            ],
            axis=0,
        )
        ext[row * span : (row + 1) * span, :] = jnp.where(flag, line, 0.0).astype(BF16)


def send_state(halo, state, rows, cols):
    pieces = [
        [state[r * cols : r * cols + REACH] for r in range(rows)],
        [state[(r + 1) * cols - REACH : (r + 1) * cols] for r in range(rows)],
    ]
    for side in range(2):
        halo.out_side[side] = jnp.concatenate(pieces[side], axis=0).astype(BF16)
    halo.out_row[0] = state[:cols].astype(BF16)
    halo.out_row[1] = state[(rows - 1) * cols :].astype(BF16)
    halo.start(lambda row_step, col_step: 0 if row_step == -1 else 1)


def send_spread(halo, spread, rows, cols):
    span = cols + 2 * REACH
    west = [spread[(r + 1) * span : (r + 1) * span + REACH, :] for r in range(rows)]
    east = [spread[(r + 2) * span - REACH : (r + 2) * span, :] for r in range(rows)]
    halo.out_side[0] = jnp.concatenate(west, axis=0).astype(BF16)
    halo.out_side[1] = jnp.concatenate(east, axis=0).astype(BF16)
    for block, row in enumerate((0, rows + 1)):
        base = row * span
        halo.out_row[2 * block] = spread[base + REACH : base + REACH + cols, :].astype(BF16)
        corners = [spread[base : base + REACH, :], spread[base + span - REACH : base + span, :]]
        if cols > 2 * REACH:
            corners.insert(1, jnp.zeros((cols - 2 * REACH, spread.shape[1]), F32))
        halo.out_row[2 * block + 1] = jnp.concatenate(corners, axis=0).astype(BF16)
    halo.start(
        lambda row_step, col_step: (0 if row_step == -1 else 2) + (1 if col_step else 0)
    )


def take_spread(halo, spread, gradient, rows, cols):
    span = cols + 2 * REACH
    west, east = halo.in_side[0].astype(F32), halo.in_side[1].astype(F32)
    outer = {}
    for first, row, flag in zip((0, 3), (0, rows - 1), edge_flags()):
        line = halo.in_row[first + 1].astype(F32)
        rim_west = halo.in_row[first].astype(F32)[cols - REACH :]
        rim_east = halo.in_row[first + 2].astype(F32)[:REACH]
        rims = [rim_west, rim_east]
        if cols > 2 * REACH:
            rims.insert(1, jnp.zeros((cols - 2 * REACH, line.shape[1]), F32))
        outer[row] = jnp.where(flag, line + jnp.concatenate(rims, axis=0), 0.0)
    result = []
    for row in range(rows):
        low, high = row * REACH, (row + 1) * REACH
        rims = [west[low:high], east[low:high]]
        if cols > 2 * REACH:
            rims.insert(1, jnp.zeros((cols - 2 * REACH, west.shape[1]), F32))
        base = (row + 1) * span + REACH
        line = spread[base : base + cols, :] + jnp.concatenate(rims, axis=0)
        if row in outer:
            line = line + outer[row]
        result.append(gradient[row * cols : (row + 1) * cols].astype(F32) + line)
    return result


def aligned(index, size):
    return pl.ds(pl.multiple_of(index * size, size), size)


GROUP = 16


def over_rows(rows, body):
    group = GROUP if rows % GROUP == 0 else 1

    def step(index, carry):
        for inner in range(group):
            body(index * group + inner)
        return carry

    lax.fori_loop(0, rows // group, step, 0)


def make_bands(base, bands, rows, cols, basis_count):
    width = base.shape[1]

    def one(row):
        table = base[aligned(row, 2 * basis_count), :]
        for k in range(basis_count):
            line = jnp.broadcast_to(table[k : k + 1], (cols, width))
            moved = pltpu.roll(line, 0, 1, stride=1, stride_axis=0)
            start = pl.multiple_of((row * basis_count + k) * cols, cols)
            bands[pl.ds(start, cols), :] = moved.astype(BF16)

    over_rows(rows, one)


def stencil(bands, ext, features, rows, cols, basis_count):
    span = cols + 2 * REACH
    channels = ext.shape[1]

    def one(row):
        lhs = bands[aligned(row, basis_count * cols), :][:, : 3 * span]
        rhs = ext[pl.ds(pl.multiple_of(row * span, span), 3 * span), :]
        out = jnp.dot(lhs, rhs, preferred_element_type=F32).astype(BF16)
        for k in range(basis_count):
            features[aligned(row, cols), k * channels : (k + 1) * channels] = out[
                k * cols : (k + 1) * cols
            ]

    over_rows(rows, one)


def adjoint(bands, errs, spread, rows, cols, basis_count):
    span = cols + 2 * REACH
    spread[...] = jnp.zeros_like(spread)

    def one(row):
        lhs = bands[aligned(row, basis_count * cols), :][:, : 3 * span]
        rhs = errs[aligned(row, basis_count * cols), :]
        out = lax.dot_general(lhs, rhs, (((0,), (0,)), ((), ())), preferred_element_type=F32)
        place = pl.ds(pl.multiple_of(row * span, span), 3 * span)
        spread[place, :] = spread[place, :] + out

    over_rows(rows, one)


def rows_product(left, right):
    return lax.dot_general(left, right, (((0,), (0,)), ((), ())), preferred_element_type=F32)
TAPS_LEFT = TAP_REACH


class InputHalo(Sender):
    def __init__(self, bufs):
        super().__init__(bufs[-2:])
        (
            self.edges,
            self.out_cols,
            self.out_table,
            self.in_cols,
            self.in_row,
            self.in_table,
            self.in_tile,
        ) = bufs[:-2]

    @staticmethod
    def scratch(rows_in, cols_in, width, table_rows, lanes):
        return [
            pltpu.VMEM((3, rows_in, width), F32),
            pltpu.VMEM((3, rows_in, width), BF16),
            pltpu.VMEM((2, table_rows, lanes), F32),
            pltpu.VMEM((3, rows_in, width), BF16),
            pltpu.VMEM((2, cols_in, width), BF16),
            pltpu.VMEM((2, table_rows, lanes), F32),
            pltpu.VMEM((4, TILE, width), BF16),
            pltpu.SemaphoreType.DMA((10,)),
            pltpu.SemaphoreType.DMA((10,)),
        ]

    def start(self, field, table, owner, rows_in, cols_in):
        first = own_first_row(rows_in // 2)
        table_rows = self.out_table.shape[1]
        for block, row, target in ((0, 0, first - 1), (1, rows_in - 1, first + rows_in // 2)):
            feeds = jnp.where(owner[row] == target, 1.0, 0.0)
            self.out_table[block] = table[row * table_rows : (row + 1) * table_rows, :] * feeds
        last = (rows_in - 1) * cols_in
        lines = (field.at[pl.ds(0, cols_in)], field.at[pl.ds(last, cols_in)])
        slot = 0
        for block, row_step in ((0, -1), (1, 1)):
            self.send(lines[block], self.in_row.at[1 - block], slot, neighbour(row_step, 0))
            base = block * last
            west = field.at[pl.ds(base, TILE)]
            east = field.at[pl.ds(base + cols_in - TILE, TILE)]
            place = 2 * (1 - block)
            self.send(west, self.in_tile.at[place + 1], slot + 1, neighbour(row_step, -1))
            self.send(east, self.in_tile.at[place], slot + 2, neighbour(row_step, 1))
            slot += 3

        def one(row):
            low = field[pl.ds(pl.multiple_of(row * cols_in, TILE), TILE), :].astype(F32)
            start = pl.multiple_of(row * cols_in + cols_in - TILE, TILE)
            high = field[pl.ds(start, TILE), :].astype(F32)
            self.edges[0, pl.ds(row, 1), :] = high[TILE - 2 : TILE - 1]
            self.edges[1, pl.ds(row, 1), :] = high[TILE - 1 : TILE]
            self.edges[2, pl.ds(row, 1), :] = low[0:1]

        over_rows(rows_in, one)
        self.out_cols[...] = self.edges[...].astype(BF16)
        self.send(self.out_cols.at[pl.ds(0, 2)], self.in_cols.at[pl.ds(0, 2)], 6, neighbour(0, 1))
        self.send(self.out_cols.at[2], self.in_cols.at[2], 7, neighbour(0, -1))
        self.send(self.out_table.at[0], self.in_table.at[1], 8, neighbour(-1, 0))
        self.send(self.out_table.at[1], self.in_table.at[0], 9, neighbour(1, 0))


def own_first_row(rows):
    return (lax.axis_index("lat") * lax.axis_size("ch") + lax.axis_index("ch")) * rows


def tap_matrix(table, basis_count, cols, cols_in):
    lanes = table.shape[1]
    blocks = []
    for k in range(basis_count):
        line = jnp.broadcast_to(table[k : k + 1], (cols, lanes))
        moved = pltpu.roll(line, 0, 1, stride=2, stride_axis=0)
        wrapped = pltpu.roll(moved, cols_in + TILE - TAPS_LEFT, 1)
        moved = pltpu.roll(moved, lanes - TAPS_LEFT, 1)
        lane = lax.broadcasted_iota(jnp.int32, (cols, lanes), 1)
        at_end = (lane >= cols_in + TILE - TAPS_LEFT) & (lane < cols_in + TILE)
        blocks.append(jnp.where(at_end, wrapped, moved))
    return jnp.concatenate(blocks, axis=0)[:, : cols_in + TILE].astype(BF16)


def filtered_row(table, line, left_two, left_one, right, basis_count, cols, cols_in):
    width = line.shape[1]
    place = lax.broadcasted_iota(jnp.int32, (TILE, width), 0)
    tile = jnp.where(place == 0, jnp.broadcast_to(right, (TILE, width)), 0.0)
    tile = jnp.where(place == TILE - 2, jnp.broadcast_to(left_two, (TILE, width)), tile)
    tile = jnp.where(place == TILE - 1, jnp.broadcast_to(left_one, (TILE, width)), tile)
    rhs = jnp.concatenate([line, tile.astype(BF16)], axis=0)
    lhs = tap_matrix(table, basis_count, cols, cols_in)
    return jnp.dot(lhs, rhs, preferred_element_type=F32).astype(BF16)


def finish_encode(halo, field, table, owner, filtered, latent_in, plan, rows_in, cols_in):
    rows, cols, basis_count, _ = plan
    table_rows = halo.out_table.shape[1]
    block = basis_count * cols
    width = field.shape[1]
    halo.settle()
    halo.edges[...] = halo.in_cols[...].astype(F32)

    def one(row):
        sides = [halo.edges[index, pl.ds(row, 1), :] for index in range(3)]
        line = field[aligned(row, cols_in), :]
        taps = table[aligned(row, table_rows), :]
        filtered[aligned(row + 1, block), :] = filtered_row(
            taps, line, *sides, basis_count, cols, cols_in
        )

    over_rows(rows_in, one)
    for side, row in ((0, 0), (1, rows_in + 1)):
        west = halo.in_tile[2 * side].astype(F32)
        east = halo.in_tile[2 * side + 1].astype(F32)
        filtered[row * block : (row + 1) * block, :] = filtered_row(
            halo.in_table[side],
            halo.in_row[side],
            west[TILE - 2 : TILE - 1],
            west[TILE - 1 : TILE],
            east[0:1],
            basis_count,
            cols,
            cols_in,
        )
    first = own_first_row(rows)
    for row in range(rows):
        total = None
        for offset in range(-1, 3):
            source = 2 * row + offset
            term = filtered[(source + 1) * block : (source + 2) * block, :].astype(F32)
            if 0 <= source < rows_in:
                term = term * jnp.where(owner[source] == first + row, 1.0, 0.0)
            total = term if total is None else total + term
        total = total.astype(BF16)
        for k in range(basis_count):
            latent_in[row * cols : (row + 1) * cols, k * width : (k + 1) * width] = total[
                k * cols : (k + 1) * cols
            ]


def lanes_of(count):
    return -(-(count + 2 * TILE) // 128) * 128


def net_kernel(plan, *refs):
    rows, cols, basis_count, layers = plan
    field, table, owner, encoder_weight, base, weights, cotangent = refs[:7]
    state_out, latent_grad = refs[7:9]
    results = refs[9 : 10 + layers]
    rest = list(refs[10 + layers :])
    bands, ext, spread, errs, features, preact, filtered, latent_in = rest[:8]
    input_halo = InputHalo(rest[8:17])
    rest = rest[17:]
    halos = []
    for _ in range(2 * layers):
        halos.append(Halo(rest[:6]))
        rest = rest[6:]
    sums = []
    for index in range(layers + 1):
        sums.append(GradSum(results[index], rest[:11]))
        rest = rest[11:]
    channels = ext.shape[1]
    progress = [0] * (layers + 1)

    def advance(index):
        getattr(sums[index], STAGES[progress[index]])()
        progress[index] += 1

    greet()
    rows_in = owner.shape[0]
    cols_in = field.shape[0] // rows_in
    input_halo.start(field, table, owner, rows_in, cols_in)
    make_bands(base, bands, rows, cols, basis_count)
    finish_encode(input_halo, field, table, owner, filtered, latent_in, plan, rows_in, cols_in)
    state = jnp.dot(latent_in[...], encoder_weight[...], preferred_element_type=F32)
    state = state.astype(BF16).astype(F32)
    for layer in range(layers):
        send_state(halos[layer], state, rows, cols)
        halos[layer].settle()
        extend(halos[layer], state, ext, rows, cols)
        stencil(bands, ext, features.at[layer], rows, cols, basis_count)
        pre = jnp.dot(features[layer], weights[layer], preferred_element_type=F32)
        preact[layer] = pre
        state = (state + pre / (1.0 + jnp.exp(-pre))).astype(BF16).astype(F32)
    state_out[...] = state.astype(BF16)

    gradient = cotangent[...].astype(F32)
    for layer in reversed(range(layers)):
        pre = preact[layer]
        sigma = 1.0 / (1.0 + jnp.exp(-pre))
        act_grad = (gradient * sigma * (1.0 + pre * (1.0 - sigma))).astype(BF16)
        for k in range(basis_count):
            block = weights[layer, k * channels : (k + 1) * channels, :]
            out = lax.dot_general(
                act_grad, block, (((1,), (1,)), ((), ())), preferred_element_type=F32
            ).astype(BF16)
            for row in range(rows):
                start = (row * basis_count + k) * cols
                errs[start : start + cols, :] = out[row * cols : (row + 1) * cols]
        adjoint(bands, errs, spread, rows, cols, basis_count)
        halo = halos[layers + layer]
        send_spread(halo, spread, rows, cols)
        sums[layer].source[...] = rows_product(features[layer], act_grad).astype(BF16)
        for other in range(layers - 1, layer - 1, -1):
            advance(other)
        halo.settle()
        for other in range(layers - 1, layer - 1, -1):
            advance(other)
        lines = take_spread(halo, spread, gradient, rows, cols)
        gradient = jnp.concatenate(lines, axis=0).astype(BF16).astype(F32)
    latent_grad[...] = gradient.astype(BF16)
    sums[layers].source[...] = rows_product(latent_in[...], gradient.astype(BF16)).astype(BF16)
    advance(layers)
    while min(progress) < len(STAGES):
        for index in [layers] + list(range(layers))[::-1]:
            if progress[index] < len(STAGES):
                advance(index)


def run_net(plan, sizes, field_in, table, owner, encoder_weight, base, weights, cotangent):
    rows, cols, basis_count, layers = plan
    cells, channels = rows * cols, weights.shape[2]
    features = basis_count * channels
    span = cols + 2 * REACH
    rows_in = owner.shape[0]
    in_features = encoder_weight.shape[0]
    heights = [features] * layers + [in_features]
    scratch = [
        pltpu.VMEM((rows * basis_count * cols, base.shape[1]), BF16),
        pltpu.VMEM(((rows + 2) * span, channels), BF16),
        pltpu.VMEM(((rows + 2) * span, channels), F32),
        pltpu.VMEM((rows * basis_count * cols, channels), BF16),
        pltpu.VMEM((layers, cells, features), BF16),
        pltpu.VMEM((layers, cells, channels), F32),
        pltpu.VMEM(((rows_in + 2) * basis_count * cols, field_in.shape[1]), BF16),
        pltpu.VMEM((cells, in_features), BF16),
    ]
    scratch += InputHalo.scratch(
        rows_in, field_in.shape[0] // rows_in, field_in.shape[1], table.shape[0] // rows_in, table.shape[1]
    )
    for index in range(2 * layers):
        scratch += Halo.scratch(rows, cols, channels, 2 if index < layers else 4)
    for height in heights:
        scratch += GradSum.scratch(sizes, height, channels)
    vmem = pl.BlockSpec(memory_space=pltpu.VMEM)
    field = jax.ShapeDtypeStruct((cells, channels), BF16)
    grads = [jax.ShapeDtypeStruct((height, channels // 2), BF16) for height in heights]
    return pl.pallas_call(
        functools.partial(net_kernel, plan),
        out_shape=[field, field] + grads,
        in_specs=[vmem, vmem, pl.BlockSpec(memory_space=pltpu.SMEM)] + [vmem] * 4,
        out_specs=[vmem] * (3 + layers),
        scratch_shapes=scratch,
        compiler_params=pltpu.CompilerParams(
            collective_id=0, has_side_effects=True, vmem_limit_bytes=56 << 20
        ),
    )(field_in, table, owner, encoder_weight, base, weights, cotangent)


def per_device(
    input_field,
    encoder_filter,
    row_owner,
    encoder_weight,
    disco_basis,
    row_widths,
    block_weights,
    cotangent,
):
    if fits_chunks(
        cotangent.shape[0],
        input_field.shape[1],
        cotangent.shape[1],
        block_weights.shape[0],
        [block_weights.shape[1]] * block_weights.shape[0] + [encoder_weight.shape[0]],
    ):
        return per_device_chunks(
            input_field,
            encoder_filter,
            row_owner,
            encoder_weight,
            disco_basis,
            row_widths,
            block_weights,
            cotangent,
        )
    rows_in, cols_in, in_width = input_field.shape
    rows_dev = rows_in // 2
    cols_dev = cols_in // 2
    basis_count = encoder_filter.shape[1]
    tap_count = encoder_filter.shape[2]
    channels = block_weights.shape[2]
    layers = block_weights.shape[0]
    cell_count = rows_dev * cols_dev
    offsets = jnp.abs(jnp.arange(2 * REACH + 1, dtype=jnp.int32) - REACH)
    keep = offsets[None, :] <= row_widths[:, None]
    masked = jnp.where(keep[:, None, None, :], disco_basis, jnp.zeros_like(disco_basis))
    span = cols_dev + 2 * REACH
    table = jnp.pad(masked, ((0, 0), (0, basis_count), (0, 0), (0, span - masked.shape[3])))
    table = table.reshape(rows_dev * 2 * basis_count, 3 * span).astype(jnp.float32)
    lanes = lanes_of(2 * span)
    table = jnp.pad(table, ((0, 0), (0, lanes - 3 * span)))
    taps = jnp.pad(
        encoder_filter.astype(jnp.float32),
        ((0, 0), (0, basis_count), (0, lanes_of(cols_in) - tap_count)),
    ).reshape(rows_in * 2 * basis_count, -1)
    own_width = channels // lax.axis_size("ch")
    sizes = (lax.axis_size("lat"), lax.axis_size("lon"))
    plan = (rows_dev, cols_dev, basis_count, layers)
    outs = run_net(
        plan,
        sizes,
        input_field.reshape(rows_in * cols_in, in_width),
        taps,
        row_owner,
        encoder_weight,
        table,
        block_weights,
        cotangent.reshape(cell_count, channels),
    )
    current, gradient = (field.reshape(rows_dev, cols_dev, channels) for field in outs[:2])
    sums = [value.astype(jnp.float32) for value in outs[2:]]
    block_sum, encoder_sum = jnp.stack(sums[:-1]), sums[-1]
    cells_total = cell_count * lax.axis_size("lon") * lax.axis_size(("lat", "ch"))
    normalizer = 1.0 / math.sqrt(cells_total)
    block_grads = (block_sum * normalizer).reshape(layers, basis_count * channels, own_width)
    encoder_grad = encoder_sum * normalizer
    return (current, gradient, block_grads, encoder_grad)

HALO = 2
DIRECT, ACROSS, WIDE, PAIRED = range(4)
LANES = 128


class Place:
    def __init__(self):
        self.lon, self.ch = lax.axis_size("lon"), lax.axis_size("ch")
        self.bands = lax.axis_size("lat") * self.ch
        self.z = lax.axis_index("lon")
        self.band = lax.axis_index("lat") * self.ch + lax.axis_index("ch")
        self.chunk = self.flip(self.band, self.z)
        self.count = self.bands * self.lon
        self.position = self.band * self.lon + self.chunk

    def flip(self, band, index):
        return index + lax.rem(band, 2) * (self.lon - 1 - 2 * index)

    def offset(self, chunk):
        return (chunk + self.lon - 1) // self.lon + (chunk + 1) // self.lon

    def device(self, band, chunk):
        return {
            "lat": band // self.ch,
            "ch": lax.rem(band, self.ch),
            "lon": self.flip(band, chunk),
        }

    def along_snake(self, step):
        position = lax.rem(self.position + step + self.count, self.count)
        return self.device(position // self.lon, lax.rem(position, self.lon))


def greet_part():
    barrier = pltpu.get_barrier_semaphore()
    count = 0
    for lat in range(lax.axis_size("lat")):
        for ch in range(lax.axis_size("ch")):
            for lon in range(lax.axis_size("lon")):
                if lat or ch or lon:
                    target = {**along("lat", lat), **along("ch", ch), **along("lon", lon)}
                    pl.semaphore_signal(barrier, inc=1, device_id=target, device_id_type=MESH)
                    count += 1
    return lambda: pl.semaphore_wait(barrier, count)


class Regroup(Sender):
    def __init__(self, bufs, rim):
        self.rim = rim
        self.lines, self.rim_ssem, self.rim_rsem, self.own_sem = bufs[0], bufs[3], bufs[4], bufs[5]
        super().__init__(bufs[1:3])

    @staticmethod
    def scratch(lon, rows, cols, width, rim):
        return [
            pltpu.VMEM((rows + 2 + 2 * rim, cols, width), BF16),
            pltpu.SemaphoreType.DMA((lon - 1,)),
            pltpu.SemaphoreType.DMA((lon - 1,)),
            pltpu.SemaphoreType.DMA((2,)),
            pltpu.SemaphoreType.DMA((2 * lon,)),
            pltpu.SemaphoreType.DMA,
        ]

    def start_rims(self, place, source):
        self.place, self.source = place, source
        rows, piece = source.shape[0], source.shape[1]
        self.piece, self.each = piece, rows // place.lon
        self.size = self.each + 2 * self.rim
        self.columns = pl.ds(pl.multiple_of(place.z * piece, piece), piece)
        self.rims = []
        for side, (row, slot, step, chunk) in enumerate(
            ((rows - 1, 0, 1, 0), (0, self.size + 1, -1, place.lon - 1))[: 2 * self.rim]
        ):
            band = lax.rem(place.band + step + place.bands, place.bands)
            copy = pltpu.make_async_remote_copy(
                src_ref=source.at[row],
                dst_ref=self.lines.at[slot, self.columns],
                send_sem=self.rim_ssem.at[side],
                recv_sem=self.rim_rsem.at[side * place.lon + place.z],
                device_id=place.device(band, chunk),
                device_id_type=MESH,
            )
            copy.start()
            self.rims.append(copy)

    def start(self):
        place, source, each, size = self.place, self.source, self.each, self.size
        block = self.lines.at[pl.ds(1, size), self.columns]
        for step in range(1, place.lon):
            peer = along("lon", step)
            chunk = place.flip(place.band, peer["lon"])
            first = chunk * each - self.rim * place.offset(chunk)
            self.send(source.at[pl.ds(first, size)], block, step - 1, peer)
        first = place.chunk * each - self.rim * place.offset(place.chunk)
        self.own = pltpu.make_async_copy(source.at[pl.ds(first, size)], block, self.own_sem)
        self.own.start()

    def finish(self):
        place = self.place
        self.settle()
        self.own.wait()
        ends = ((0, 0), (self.size + 1, place.lon - 1))[: 2 * self.rim]
        for side, (slot, chunk) in enumerate(ends):

            @pl.when(place.chunk == chunk)
            def _():
                for z in range(place.lon):
                    pltpu.make_async_remote_copy(
                        src_ref=self.source.at[0],
                        dst_ref=self.lines.at[slot, pl.ds(z * self.piece, self.piece)],
                        send_sem=self.rim_ssem.at[side],
                        recv_sem=self.rim_rsem.at[side * place.lon + z],
                        device_id=along("lon", 0),
                        device_id_type=MESH,
                    ).wait_recv()

        for copy in self.rims:
            copy.wait_send()

    def row(self, index):
        return self.lines[index + 1 + self.rim * self.place.offset(self.place.chunk)]


class Restore(Sender):
    def __init__(self, bufs):
        self.lines, self.own_sem = bufs[0], bufs[3]
        super().__init__(bufs[1:3])

    @staticmethod
    def scratch(lon, rows, cols, width):
        return [
            pltpu.VMEM((rows, cols, width), BF16),
            pltpu.SemaphoreType.DMA((lon - 1,)),
            pltpu.SemaphoreType.DMA((lon - 1,)),
            pltpu.SemaphoreType.DMA,
        ]

    def start(self, place, result):
        rows, piece = self.lines.shape[0], result.shape[1]
        target = result.at[pl.ds(place.chunk * rows, rows)]
        for step in range(1, place.lon):
            peer = along("lon", step)
            columns = pl.ds(pl.multiple_of(peer["lon"] * piece, piece), piece)
            self.send(self.lines.at[:, columns], target, step - 1, peer)
        columns = pl.ds(pl.multiple_of(place.z * piece, piece), piece)
        self.own = pltpu.make_async_copy(self.lines.at[:, columns], target, self.own_sem)
        self.own.start()

    def finish(self):
        self.settle()
        self.own.wait()


class Swap(Sender):
    def __init__(self, bufs):
        super().__init__(bufs)

    @staticmethod
    def scratch():
        return [pltpu.SemaphoreType.DMA((2,)), pltpu.SemaphoreType.DMA((2,))]

    def start(self, place, buffer, slot_rows, own, halo):
        def part(first):
            return buffer.at[pl.ds(first * slot_rows, halo * slot_rows)]

        self.send(part(own), part(0), 0, place.along_snake(1))
        self.send(part(halo), part(halo + own), 1, place.along_snake(-1))


class ChipSum(Sender):
    def __init__(self, result, source, first, direct, bufs):
        super().__init__(bufs[-2:])
        self.result, self.source, self.first = result, source, first
        self.rec_ch, self.part, self.rec_lat, self.strip, self.rec, self.piece = bufs[:6]
        self.rec_pair, self.half, self.rec_far, self.whole = bufs[6:10]
        self.rows, self.width = self.part.shape
        self.lat, self.lon = lax.axis_size("lat"), lax.axis_size("lon")
        self.height, self.span = self.strip.shape[0], self.piece.shape[0]
        self.side = lax.rem(lax.axis_index("lon"), 2)
        self.direct = direct
        self.stages = [self.start_ch]
        if direct == DIRECT:
            self.stages += [self.scatter_all, self.gather_all]
        elif direct == ACROSS:
            self.stages += [self.scatter_lat, self.scatter_lon, self.gather_lon, self.gather_lat]
        elif direct == WIDE:
            self.stages += [self.scatter_lat, self.scatter_lon, self.gather_all]
        else:
            self.stages += [self.scatter_lat, self.scatter_pair, self.trade_far]
            self.stages += [self.gather_pair, self.gather_lat]
        self.stages.append(self.settle)

    @staticmethod
    def scratch(sizes, rows, columns):
        lat, lon = sizes
        width, height, span = columns // 2, rows // lat, rows // (lat * lon)
        count = 1 + 2 * (lat - 1) + 2 * (lat * lon - 1)
        return [
            pltpu.VMEM((rows, width), BF16),
            pltpu.VMEM((rows, width), BF16),
            pltpu.VMEM((lat - 1, height, width), BF16),
            pltpu.VMEM((height, width), BF16),
            pltpu.VMEM((lat * lon - 1, span, width), BF16),
            pltpu.VMEM((span, width), BF16),
            pltpu.VMEM((height // 2, width), BF16),
            pltpu.VMEM((height // 2, width), BF16),
            pltpu.VMEM((max(lon // 2 - 1, 1), height // 2, width), BF16),
            pltpu.VMEM((height // 2, width), BF16),
            pltpu.SemaphoreType.DMA((count,)),
            pltpu.SemaphoreType.DMA((count,)),
        ]

    def advance(self):
        self.stages.pop(0)()

    def columns(self, half):
        return pl.ds(pl.multiple_of(half * self.width, self.width), self.width)

    def own_columns(self):
        return self.source[self.first : self.first + self.rows, self.columns(lax.axis_index("ch"))]

    def others(self):
        for lat in range(self.lat):
            for lon in range(self.lon):
                if lat or lon:
                    yield lat * self.lon + lon - 1, {**along("lat", lat), **along("lon", lon)}

    def mine(self):
        return lax.axis_index("lat") * self.lon + lax.axis_index("lon")

    def place(self, index, size):
        return pl.ds(pl.multiple_of(index * size, size), size)

    def target(self, index, size):
        return pl.ds(pl.multiple_of(self.first + index * size, size), size)

    def start_ch(self):
        other = 1 - lax.axis_index("ch")
        rows = pl.ds(self.first, self.rows)
        self.send(self.source.at[rows, self.columns(other)], self.rec_ch, 0, {"ch": other})

    def add_ch(self):
        self.settle()
        total = self.own_columns().astype(F32) + self.rec_ch[...].astype(F32)
        self.part[...] = total.astype(BF16)

    def scatter_all(self):
        self.add_ch()
        for slot, peer in self.others():
            rows = self.place(peer["lat"] * self.lon + peer["lon"], self.span)
            self.send(self.part.at[rows], self.rec.at[slot], 1 + slot, peer)

    def scatter_lat(self):
        self.add_ch()
        self.slot = self.lat * self.lon
        for step in range(1, self.lat):
            peer = along("lat", step)
            rows = self.place(peer["lat"], self.height)
            self.send(self.part.at[rows], self.rec_lat.at[step - 1], self.slot, peer)
            self.slot += 1

    def add_lat(self):
        self.settle()
        total = self.part[self.place(lax.axis_index("lat"), self.height), :].astype(F32)
        for step in range(1, self.lat):
            total = total + self.rec_lat[step - 1].astype(F32)
        self.strip[...] = total.astype(BF16)

    def scatter_pair(self):
        self.add_lat()
        rows = self.place(1 - self.side, self.height // 2)
        self.send(self.strip.at[rows], self.rec_pair, 1, along("lon", 1 - 2 * self.side))

    def trade_far(self):
        self.settle()
        total = self.strip[self.place(self.side, self.height // 2), :].astype(F32)
        self.half[...] = (total + self.rec_pair[...].astype(F32)).astype(BF16)
        for step in range(1, self.lon // 2):
            self.send(self.half, self.rec_far.at[step - 1], 1 + step, along("lon", 2 * step))

    def gather_pair(self):
        self.settle()
        total = self.half[...].astype(F32)
        for step in range(1, self.lon // 2):
            total = total + self.rec_far[step - 1].astype(F32)
        self.whole[...] = total.astype(BF16)
        rows = self.target(2 * lax.axis_index("lat") + self.side, self.height // 2)
        self.result[rows, :] = self.whole[...]
        base = self.lat * self.lon + self.lat - 1
        self.send(self.whole, self.result.at[rows], base, along("lon", 1 - 2 * self.side))

    def scatter_lon(self):
        self.add_lat()
        for step in range(1, self.lon):
            peer = along("lon", step)
            rows = self.place(peer["lon"], self.span)
            self.send(self.strip.at[rows], self.rec.at[step - 1], step, peer)

    def add_rest(self):
        self.settle()
        if self.direct == DIRECT:
            total, count = self.part[self.place(self.mine(), self.span), :], self.lat * self.lon
        else:
            total, count = self.strip[self.place(lax.axis_index("lon"), self.span), :], self.lon
        total = total.astype(F32)
        for step in range(1, count):
            total = total + self.rec[step - 1].astype(F32)
        self.piece[...] = total.astype(BF16)
        rows = self.target(self.mine(), self.span)
        self.result[rows, :] = self.piece[...]
        return self.result.at[rows], self.lat * self.lon + self.lat - 1

    def gather_all(self):
        target, base = self.add_rest()
        for slot, peer in self.others():
            self.send(self.piece, target, base + slot, peer)

    def gather_lon(self):
        target, base = self.add_rest()
        for step in range(1, self.lon):
            self.send(self.piece, target, base + step - 1, along("lon", step))

    def gather_lat(self):
        self.settle()
        rows = self.target(lax.axis_index("lat"), self.height)
        base = 2 * self.lat * self.lon + self.lat - 2
        for step in range(1, self.lat):
            self.send(self.result.at[rows], self.result.at[rows], base + step - 1, along("lat", step))


def zero_outside(place, buffer, first, last, size):
    @pl.when(place.position == 0)
    def _():
        buffer[first : first + size, :] = jnp.zeros((size, buffer.shape[1]), buffer.dtype)

    @pl.when(place.position == place.count - 1)
    def _():
        buffer[last : last + size, :] = jnp.zeros((size, buffer.shape[1]), buffer.dtype)


def circulant(line, rows, stride):
    return pltpu.roll(jnp.broadcast_to(line, (rows, LANES)), 0, 1, stride=stride, stride_axis=0)


def silu_slope(pre):
    sigma = 1.0 / (1.0 + jnp.exp(-pre))
    return sigma * (1.0 + pre * (1.0 - sigma))


def chunk_kernel(plan, *refs):
    rows, cols, basis_count, layers = plan
    field, taps, owner, encoder_source, base, widths, weights_source, cotangent = refs[:8]
    state_out, latent_grad = refs[8:10]
    results = refs[10 : 11 + layers]
    rest = list(refs[11 + layers :])
    table, flat, lines, rims, bands, turned, latent_in, state, features, preact, steps, errs = rest[:12]
    encoder_weight, weights, load_sems = rest[12:15]
    rest = rest[15:]
    inputs, arriving = Regroup(rest[:6], 1), Regroup(rest[6:12], 0)
    leaving = [Restore(rest[12:16]), Restore(rest[16:20])]
    swaps = [Swap(rest[20 + 2 * n : 22 + 2 * n]) for n in range(5)]
    rest = rest[30:]
    sources, rest = rest[: layers + 1], rest[layers + 1 :]
    sums = []
    for index, first, size, direct in stretches([source.shape[0] for source in sources]):
        sums.append(ChipSum(results[index], sources[index], first, direct, rest[:12]))
        rest = rest[12:]
    channels = state.shape[1]
    width = field.shape[2]
    block = basis_count * cols
    ext = rows + 2 * HALO
    early, upper, lower, encoder = sums

    loads = [
        pltpu.make_async_copy(source, target, load_sems.at[index])
        for index, (source, target) in enumerate(
            ((encoder_source, encoder_weight), (weights_source, weights))
        )
    ]
    entered = greet_part()
    for load in loads:
        load.start()
    place = Place()
    first = place.position * rows
    rows_in = 2 * rows
    start_in = place.chunk * rows_in
    high, tall = table.shape[0] // ext, rims.shape[1]
    make_table(place, base, widths, table, rows, cols, basis_count, high)
    make_lines(taps, flat, lines, start_in, rows_in, basis_count)
    sides = (
        (0, jnp.where(owner[start_in] == first - 1, 1.0, 0.0)),
        (rows_in - 1, jnp.where(owner[start_in + rows_in - 1] == first + rows, 1.0, 0.0)),
    )
    for side, (row, feeds) in enumerate(sides):
        for k in range(basis_count):
            rims[side, k : k + 1, :] = lines[k * rows_in + row : k * rows_in + row + 1, :] * feeds
    entered()
    inputs.start_rims(place, field)
    swaps[0].start(place, table, high, rows, HALO)
    swaps[1].send(rims.at[1], rims.at[2], 0, place.along_snake(1))
    swaps[1].send(rims.at[0], rims.at[3], 1, place.along_snake(-1))
    inputs.start()

    lane = lax.broadcasted_iota(jnp.int32, (cols, LANES), 1)

    def make_band(row, carry):
        values = table[aligned(row, high), :]
        for k in range(basis_count):
            parts = [
                circulant(values[r * basis_count + k][None, :], cols, 1) for r in range(3)
            ]
            start = pl.multiple_of(row * block + k * cols, cols)
            bands[pl.ds(start, cols), :LANES] = jnp.where(lane < cols, parts[0], parts[1]).astype(BF16)
            bands[pl.ds(start, cols), LANES:] = parts[2].astype(BF16)
        other = bands[aligned(row, block), :].T
        for r in range(3):
            turned[aligned(row + r, cols), (2 - r) * block : (3 - r) * block] = other[
                r * cols : (r + 1) * cols
            ]
        return carry

    lax.fori_loop(HALO, HALO + rows, make_band, 0)
    swaps[0].settle()
    lax.fori_loop(0, HALO, make_band, 0)
    lax.fori_loop(HALO + rows, ext, make_band, 0)
    swaps[1].settle()
    inputs.finish()

    def filtered(row):
        if 0 <= row < rows_in:
            values = [lines[k * rows_in + row : k * rows_in + row + 1, :] for k in range(basis_count)]
        else:
            side = 2 if row < 0 else 3
            values = [rims[side, k : k + 1, :] for k in range(basis_count)]
        lhs = jnp.concatenate([circulant(value, cols, 2) for value in values], axis=0).astype(BF16)
        out = jnp.dot(lhs, inputs.row(row), preferred_element_type=F32)
        return out.astype(BF16).astype(F32)

    filters = [filtered(row) for row in range(-1, rows_in + 1)]
    for row in range(rows):
        total = None
        for step in range(-1, 3):
            source = 2 * row + step
            term = filters[source + 1]
            if 0 <= source < rows_in:
                term = term * jnp.where(owner[start_in + source] == first + row, 1.0, 0.0)
            total = term if total is None else total + term
        total = total.astype(BF16)
        for k in range(basis_count):
            latent_in[row * cols : (row + 1) * cols, k * width : (k + 1) * width] = total[
                k * cols : (k + 1) * cols
            ]
    own = pl.ds(HALO * cols, rows * cols)
    loads[0].wait()
    state[own, :] = jnp.dot(
        latent_in[...], encoder_weight[...], preferred_element_type=F32
    ).astype(BF16)
    swaps[2].start(place, state, cols, rows, HALO)
    arriving.start_rims(place, cotangent)
    arriving.start()
    loads[1].wait()
    swaps[2].settle()
    zero_outside(place, state, 0, (HALO + rows) * cols, HALO * cols)

    for layer in range(layers):
        low, top = layer + 1, ext - layer - 1
        for row in range(low, top):
            out = jnp.dot(
                bands[row * block : (row + 1) * block, : 3 * cols],
                state[(row - 1) * cols : (row + 2) * cols, :],
                preferred_element_type=F32,
            ).astype(BF16)
            for k in range(basis_count):
                features[layer, row * cols : (row + 1) * cols, k * channels : (k + 1) * channels] = out[
                    k * cols : (k + 1) * cols
                ]
        span = pl.ds(low * cols, (top - low) * cols)
        pre = jnp.dot(features[layer, span, :], weights[layer], preferred_element_type=F32)
        preact[layer, span, :] = pre
        new = state[span, :].astype(F32) + pre / (1.0 + jnp.exp(-pre))
        state[span, :] = new.astype(BF16)
        if layer < layers - 1:
            zero_outside(place, state, low * cols, (top - 1) * cols, cols)

    arriving.finish()
    last = layers - 1
    gradient = arriving.lines[1 : rows + 1].reshape(rows * cols, channels).astype(F32)
    act = gradient * silu_slope(preact[last, own, :])
    steps[last, own, :] = act.astype(BF16)
    swaps[3].start(place, steps.at[last], cols, rows, HALO)
    swaps[4].start(place, arriving.lines, 1, rows, 1)
    leaving[0].lines[...] = state[own, :].reshape(rows, cols, channels)

    def errors(layer, low, top):
        for k in range(basis_count):
            out = lax.dot_general(
                steps[layer, low * cols : top * cols, :],
                weights[layer, k * channels : (k + 1) * channels, :],
                (((1,), (1,)), ((), ())),
                preferred_element_type=F32,
            ).astype(BF16)
            for row in range(low, top):
                start = row * block + k * cols
                errs[start : start + cols, :] = out[(row - low) * cols : (row - low + 1) * cols]

    def spread(row):
        return jnp.dot(
            turned[(row + 1) * cols : (row + 2) * cols, :],
            errs[(row - 1) * block : (row + 2) * block, :],
            preferred_element_type=F32,
        )

    def weigh(part):
        stretch = slice(part.first, part.first + part.rows)
        left = features[0, own, stretch]
        sources[0][stretch, :] = rows_product(left, steps[0, own, :]).astype(BF16)

    sources[last][...] = rows_product(features[last, own, :], steps[last, own, :]).astype(BF16)
    early.advance()
    errors(last, HALO, HALO + rows)
    early.advance()
    leaving[0].start(place, state_out)
    swaps[3].settle()
    zero_outside(place, steps.at[last], 0, (HALO + rows) * cols, HALO * cols)
    errors(last, 0, HALO)
    errors(last, HALO + rows, ext)
    swaps[4].settle()
    back = [arriving.lines[row - 1].astype(F32) + spread(row) for row in range(1, ext - 1)]
    gradient = jnp.concatenate(back, axis=0).astype(BF16).astype(F32)
    span = pl.ds(cols, (ext - 2) * cols)
    steps[0, span, :] = (gradient * silu_slope(preact[0, span, :])).astype(BF16)
    zero_outside(place, steps.at[0], cols, (ext - 2) * cols, cols)
    weigh(upper)
    upper.advance()
    weigh(lower)
    lower.advance()
    early.advance()
    errors(0, 1, ext - 1)
    upper.advance()
    lower.advance()
    back = [
        gradient[(row - 1) * cols : row * cols] + spread(row) for row in range(HALO, HALO + rows)
    ]
    final = jnp.concatenate(back, axis=0).astype(BF16)
    leaving[1].lines[...] = final.reshape(rows, cols, channels)
    sources[layers][...] = rows_product(latent_in[...], final).astype(BF16)
    encoder.advance()
    encoder.advance()
    upper.advance()
    lower.advance()
    early.advance()
    encoder.advance()
    upper.advance()
    lower.advance()
    early.advance()
    upper.advance()
    lower.advance()
    encoder.advance()
    leaving[1].start(place, latent_grad)
    for part in sums:
        while part.stages:
            part.advance()
    for part in leaving:
        part.finish()


def make_table(place, base, widths, table, rows, cols, basis_count, high):
    own = pl.ds(HALO * high, rows * high)
    table[own, :] = jnp.zeros((rows * high, LANES), F32)
    size = base.shape[3]
    reach = size // 2
    distance = jnp.abs(lax.broadcasted_iota(jnp.int32, (basis_count, size), 1) - reach)
    for row in range(rows):
        source = place.chunk * rows + row
        values = base[source].astype(F32)
        for r in range(3):
            start = (HALO + row) * high + r * basis_count
            table[start : start + basis_count, :size] = jnp.where(
                distance <= widths[source], values[r], 0.0
            )
    moved = pltpu.roll(table[own, :], LANES - reach, 1)
    table[own, :] = moved + pltpu.roll(moved, cols, 1)


def make_lines(taps, flat, lines, start_in, rows_in, basis_count):
    flat[...] = jnp.zeros_like(flat)
    count, _, held = taps.shape
    for k in range(basis_count):
        for t in range(count):
            row = 8 * k + t
            flat[row : row + 1, :held] = taps[t, k : k + 1, :].astype(F32)
    flat[...] = flat[...].T
    values = flat[aligned(start_in // rows_in, rows_in), :]
    lane = lax.broadcasted_iota(jnp.int32, values.shape, 1)
    for k in range(basis_count):
        moved = pltpu.roll(values, LANES - 8 * k, 1) if k else values
        kept = jnp.where(lane < count, moved, 0.0)
        lines[k * rows_in : (k + 1) * rows_in, :] = pltpu.roll(kept, LANES - count // 2, 1)


def stretches(heights):
    half = heights[0] // 2
    return [
        (len(heights) - 2, 0, heights[-2], ACROSS),
        (0, 0, half, ACROSS),
        (0, half, half, ACROSS),
        (len(heights) - 1, 0, heights[-1], WIDE),
    ]


def run_chunks(
    plan, sizes, field_in, taps, owner, encoder_weight, base, widths, weights, cotangent
):
    rows, cols, basis_count, layers = plan
    lat, lon = sizes
    channels = weights.shape[2]
    features = basis_count * channels
    in_features = encoder_weight.shape[0]
    ext = rows + 2 * HALO
    heights = [features] * layers + [in_features]
    block = basis_count * cols
    high = -(-3 * basis_count // 8) * 8
    tall = -(-basis_count // 8) * 8
    scratch = [
        pltpu.VMEM((ext * high, LANES), F32),
        pltpu.VMEM((LANES, LANES), F32),
        pltpu.VMEM((basis_count * 2 * rows, LANES), F32),
        pltpu.VMEM((4, tall, LANES), F32),
        pltpu.VMEM((ext * block, 2 * LANES), BF16),
        pltpu.VMEM(((ext + 2) * cols, 3 * block), BF16),
        pltpu.VMEM((rows * cols, in_features), BF16),
        pltpu.VMEM((ext * cols, channels), BF16),
        pltpu.VMEM((layers, ext * cols, features), BF16),
        pltpu.VMEM((layers, ext * cols, channels), F32),
        pltpu.VMEM((layers, ext * cols, channels), BF16),
        pltpu.VMEM((ext * block, channels), BF16),
        pltpu.VMEM(encoder_weight.shape, BF16),
        pltpu.VMEM(weights.shape, BF16),
        pltpu.SemaphoreType.DMA((2,)),
    ]
    scratch += Regroup.scratch(lon, 2 * rows, field_in.shape[1] * lon, field_in.shape[2], 1)
    scratch += Regroup.scratch(lon, rows, cols, channels, 0)
    for _ in range(2):
        scratch += Restore.scratch(lon, rows, cols, channels)
    for _ in range(5):
        scratch += Swap.scratch()
    scratch += [pltpu.VMEM((height, channels), BF16) for height in heights]
    for _, _, size, _ in stretches(heights):
        scratch += ChipSum.scratch(sizes, size, channels)
    vmem = pl.BlockSpec(memory_space=pltpu.VMEM)
    smem = pl.BlockSpec(memory_space=pltpu.SMEM)
    hbm = pl.BlockSpec(memory_space=pltpu.HBM)
    out = jax.ShapeDtypeStruct(cotangent.shape, BF16)
    grads = [jax.ShapeDtypeStruct((height, channels // 2), BF16) for height in heights]
    return pl.pallas_call(
        functools.partial(chunk_kernel, plan),
        out_shape=[out, out] + grads,
        in_specs=[hbm, vmem, smem, hbm, vmem, smem, hbm, hbm],
        out_specs=[hbm, hbm] + [vmem] * (1 + layers),
        scratch_shapes=scratch,
        compiler_params=pltpu.CompilerParams(
            collective_id=1, has_side_effects=True, vmem_limit_bytes=56 << 20
        ),
    )(field_in, taps, owner, encoder_weight, base, widths, weights, cotangent)


def finish_body(normalizer, field_count, sum_count, refs):
    fields, sums = refs[:field_count], refs[field_count : field_count + sum_count]
    fields_out = refs[field_count + sum_count : 2 * field_count + sum_count]
    block_grads, encoder_grad = refs[2 * field_count + sum_count :][:2]
    rest = refs[2 * field_count + sum_count + 2 :]
    held, wide = rest[:sum_count], rest[sum_count : 2 * sum_count]
    kept = rest[2 * sum_count : 2 * sum_count + field_count]
    in_sems, out_sems = rest[2 * sum_count + field_count :]
    sources = list(zip(list(sums) + list(fields), list(held) + list(kept)))
    targets = [block_grads.at[n] for n in range(sum_count - 1)] + [encoder_grad] + list(fields_out)
    ready = list(wide) + list(kept)
    loads = [
        pltpu.make_async_copy(source, target, in_sems.at[n])
        for n, (source, target) in enumerate(sources)
    ]
    stores = [
        pltpu.make_async_copy(source, target, out_sems.at[n])
        for n, (source, target) in enumerate(zip(ready, targets))
    ]
    for load in loads:
        load.start()
    for n, (load, store) in enumerate(zip(loads, stores)):
        load.wait()
        if n < sum_count:
            wide[n][...] = held[n][...].astype(F32) * normalizer
        store.start()
    for store in stores:
        store.wait()


def finish_outputs(normalizer, outs):
    hbm = pl.BlockSpec(memory_space=pltpu.HBM)
    fields, sums = outs[:2], outs[2:]
    shapes = [jax.ShapeDtypeStruct(field.shape, field.dtype) for field in fields]
    shapes.append(jax.ShapeDtypeStruct((len(sums) - 1,) + sums[0].shape, F32))
    shapes.append(jax.ShapeDtypeStruct(sums[-1].shape, F32))

    def kernel(*refs):
        finish_body(normalizer, len(fields), len(sums), refs)

    return pl.pallas_call(
        kernel,
        out_shape=shapes,
        in_specs=[hbm] * len(outs),
        out_specs=[hbm] * len(shapes),
        scratch_shapes=[pltpu.VMEM(value.shape, BF16) for value in sums]
        + [pltpu.VMEM(value.shape, F32) for value in sums]
        + [pltpu.VMEM(value.shape, BF16) for value in fields]
        + [pltpu.SemaphoreType.DMA((len(outs),)) for _ in range(2)],
        compiler_params=pltpu.CompilerParams(vmem_limit_bytes=60 << 20),
    )(*outs)


def fits_chunks(rows_dev, cols_in, cols_dev, layers, heights):
    lon = lax.axis_size("lon")
    count = lax.axis_size("lat") * lon
    heights_fit = all(size % (count * TILE) == 0 for _, _, size, _ in stretches(heights))
    return (
        layers == HALO
        and rows_dev % lon == 0
        and heights_fit
        and rows_dev // lon >= HALO
        and lon % 2 == 0
        and cols_in * lon == LANES
        and 2 * cols_dev * lon == LANES
    )


def per_device_chunks(
    input_field,
    encoder_filter,
    row_owner,
    encoder_weight,
    disco_basis,
    row_widths,
    block_weights,
    cotangent,
):
    rows_in, cols_in, _ = input_field.shape
    lat, lon = lax.axis_size("lat"), lax.axis_size("lon")
    rows_dev, cols = rows_in // 2, cols_in // 2 * lon
    plan = (rows_dev // lon, cols, encoder_filter.shape[1], block_weights.shape[0])
    outs = run_chunks(
        plan,
        (lat, lon),
        input_field,
        encoder_filter.transpose(2, 1, 0),
        row_owner,
        encoder_weight,
        disco_basis.transpose(0, 2, 1, 3),
        row_widths,
        block_weights,
        cotangent,
    )
    cells_total = rows_dev * lax.axis_size(("lat", "ch")) * cols
    return tuple(finish_outputs(1.0 / math.sqrt(cells_total), outs))


def solution(mesh):
    placed = (
        P(("ens", "lat", "ch"), "lon", None),
        P(("lat", "ch"), None, None),
        P(("ens", "lat", "ch")),
        P(),
        P(("lat", "ch"), None, None, None),
        P(("lat", "ch")),
        P(),
        P(("ens", "lat", "ch"), "lon", None),
    )
    return jax.shard_map(
        per_device,
        mesh=mesh,
        in_specs=placed,
        out_specs=(
            P(("ens", "lat", "ch"), "lon", None),
            P(("ens", "lat", "ch"), "lon", None),
            P("ens", None, "ch"),
            P("ens", "ch"),
        ),
        check_vma=False,
    )
```

```python
import functools
import math

import jax
import jax.numpy as jnp
from jax import lax
from jax.experimental import pallas as pl
from jax.experimental.pallas import tpu as pltpu
from jax.sharding import PartitionSpec as P

REACH = 8
TAP_REACH = 2
TILE = 16
MESH = pl.DeviceIdType.MESH
BF16 = jnp.bfloat16
F32 = jnp.float32


def along(axis, steps):
    count = lax.axis_size(axis)
    return {axis: lax.rem(lax.axis_index(axis) + steps + count, count)}


def neighbour(row_step, col_step):
    ch_count = lax.axis_size("ch")
    bands = lax.axis_size("lat") * ch_count
    band = lax.axis_index("lat") * ch_count + lax.axis_index("ch")
    band = lax.rem(band + row_step + bands, bands)
    target = {}
    if row_step:
        target = {"lat": band // ch_count, "ch": lax.rem(band, ch_count)}
    if col_step:
        target.update(along("lon", col_step))
    return target


AROUND = [(r, c) for r in (-1, 0, 1) for c in (-1, 0, 1) if r or c]


def greet():
    targets = [neighbour(r, c) for r, c in AROUND]
    for axis in ("ch", "lat", "lon"):
        targets += [along(axis, step) for step in range(1, lax.axis_size(axis))]
    barrier = pltpu.get_barrier_semaphore()
    for target in targets:
        pl.semaphore_signal(barrier, inc=1, device_id=target, device_id_type=MESH)
    pl.semaphore_wait(barrier, len(targets))


class Sender:
    def __init__(self, sems):
        self.ssem, self.rsem = sems
        self.pending = []

    def send(self, source, target, slot, device):
        copy = pltpu.make_async_remote_copy(
            src_ref=source,
            dst_ref=target,
            send_sem=self.ssem.at[slot],
            recv_sem=self.rsem.at[slot],
            device_id=device,
            device_id_type=MESH,
        )
        copy.start()
        self.pending.append(copy)

    def settle(self):
        for copy in self.pending:
            copy.wait()
        self.pending = []


class GradSum(Sender):
    def __init__(self, result, bufs):
        super().__init__(bufs[-2:])
        self.result = result
        self.source, self.rec_ch, self.part, self.rec_lat, self.strip, self.rec_pair, self.half, self.rec_far, self.piece = bufs[:-2]
        self.width = self.part.shape[1]
        self.lat, self.lon = lax.axis_size("lat"), lax.axis_size("lon")
        self.height = self.strip.shape[0]
        self.span = self.piece.shape[0]
        self.pair = self.height // self.span
        self.far = self.lon // self.pair
        self.side = lax.rem(lax.axis_index("lon"), self.pair)

    @staticmethod
    def scratch(sizes, rows, columns):
        lat, lon = sizes
        width = columns // 2
        height = rows // lat
        pair = 2 if lon % 2 == 0 and height % (2 * TILE) == 0 else 1
        span, far = height // pair, lon // pair
        count = 1 + 2 * (lat - 1) + 2 * (pair - 1) + far - 1
        return [
            pltpu.VMEM((rows, columns), BF16),
            pltpu.VMEM((rows, width), BF16),
            pltpu.VMEM((rows, width), BF16),
            pltpu.VMEM((lat - 1, height, width), BF16),
            pltpu.VMEM((height, width), BF16),
            pltpu.VMEM((span, width), BF16),
            pltpu.VMEM((span, width), BF16),
            pltpu.VMEM((far - 1, span, width), BF16),
            pltpu.VMEM((span, width), BF16),
            pltpu.SemaphoreType.DMA((count,)),
            pltpu.SemaphoreType.DMA((count,)),
        ]

    def columns(self, half):
        return pl.ds(pl.multiple_of(half * self.width, self.width), self.width)

    @staticmethod
    def stretch(owner, size):
        return pl.ds(pl.multiple_of(owner * size, size), size)

    def start_ch(self):
        other = 1 - lax.axis_index("ch")
        self.send(self.source.at[:, self.columns(other)], self.rec_ch, 0, {"ch": other})

    def start_lat(self):
        self.settle()
        own = self.source[:, self.columns(lax.axis_index("ch"))].astype(F32)
        self.part[...] = (own + self.rec_ch[...].astype(F32)).astype(BF16)
        for step in range(1, self.lat):
            peer = along("lat", step)
            rows = self.stretch(peer["lat"], self.height)
            self.send(self.part.at[rows], self.rec_lat.at[step - 1], step, peer)

    def start_lon(self):
        self.settle()
        total = self.part[self.stretch(lax.axis_index("lat"), self.height), :].astype(F32)
        for step in range(1, self.lat):
            total = total + self.rec_lat[step - 1].astype(F32)
        self.strip[...] = total.astype(BF16)
        if self.pair > 1:
            rows = self.stretch(1 - self.side, self.span)
            self.send(self.strip.at[rows], self.rec_pair, self.lat, along("lon", 1 - 2 * self.side))

    def start_far(self):
        self.settle()
        total = self.strip[self.stretch(self.side, self.span), :].astype(F32)
        if self.pair > 1:
            total = total + self.rec_pair[...].astype(F32)
        self.half[...] = total.astype(BF16)
        for step in range(1, self.far):
            self.send(
                self.half, self.rec_far.at[step - 1], self.lat + step, along("lon", self.pair * step)
            )

    def gather_lon(self):
        self.settle()
        total = self.half[...].astype(F32)
        for step in range(1, self.far):
            total = total + self.rec_far[step - 1].astype(F32)
        self.piece[...] = total.astype(BF16)
        offset = lax.axis_index("lat") * self.height + self.side * self.span
        rows = pl.ds(pl.multiple_of(offset, TILE), self.span)
        self.result[rows, :] = self.piece[...]
        if self.pair > 1:
            slot = self.lat + self.far
            self.send(self.piece, self.result.at[rows], slot, along("lon", 1 - 2 * self.side))

    def gather_lat(self):
        self.settle()
        rows = self.stretch(lax.axis_index("lat"), self.height)
        for step in range(1, self.lat):
            slot = self.lat + self.far + self.pair - 2 + step
            self.send(self.result.at[rows], self.result.at[rows], slot, along("lat", step))

    def finish(self):
        self.settle()


STAGES = ("start_ch", "start_lat", "start_lon", "start_far", "gather_lon", "gather_lat", "finish")


class Halo(Sender):
    def __init__(self, bufs):
        super().__init__(bufs[-2:])
        self.out_side, self.out_row, self.in_side, self.in_row = bufs[:-2]

    @staticmethod
    def scratch(rows, cols, width, row_blocks):
        return [
            pltpu.VMEM((2, rows * REACH, width), BF16),
            pltpu.VMEM((row_blocks, cols, width), BF16),
            pltpu.VMEM((2, rows * REACH, width), BF16),
            pltpu.VMEM((6, cols, width), BF16),
            pltpu.SemaphoreType.DMA((8,)),
            pltpu.SemaphoreType.DMA((8,)),
        ]

    def start(self, row_block_of):
        self.send(self.out_side.at[0], self.in_side.at[1], 0, neighbour(0, -1))
        self.send(self.out_side.at[1], self.in_side.at[0], 1, neighbour(0, 1))
        slot = 2
        for row_step in (-1, 1):
            for col_step in (-1, 0, 1):
                place = (0 if row_step == 1 else 3) + 1 - col_step
                self.send(
                    self.out_row.at[row_block_of(row_step, col_step)],
                    self.in_row.at[place],
                    slot,
                    neighbour(row_step, col_step),
                )
                slot += 1


def edge_flags():
    ch_count = lax.axis_size("ch")
    bands = lax.axis_size("lat") * ch_count
    band = lax.axis_index("lat") * ch_count + lax.axis_index("ch")
    return band > 0, band < bands - 1


def extend(halo, state, ext, rows, cols):
    span = cols + 2 * REACH
    west, east = halo.in_side[0].astype(F32), halo.in_side[1].astype(F32)
    for row in range(rows):
        low, high = row * REACH, (row + 1) * REACH
        line = jnp.concatenate(
            [west[low:high], state[row * cols : (row + 1) * cols], east[low:high]], axis=0
        )
        ext[(row + 1) * span : (row + 2) * span, :] = line.astype(BF16)
    for first, row, flag in zip((0, 3), (0, rows + 1), edge_flags()):
        line = jnp.concatenate(
            [
                halo.in_row[first].astype(F32)[cols - REACH :],
                halo.in_row[first + 1].astype(F32),
                halo.in_row[first + 2].astype(F32)[:REACH],
            ],
            axis=0,
        )
        ext[row * span : (row + 1) * span, :] = jnp.where(flag, line, 0.0).astype(BF16)


def send_state(halo, state, rows, cols):
    pieces = [
        [state[r * cols : r * cols + REACH] for r in range(rows)],
        [state[(r + 1) * cols - REACH : (r + 1) * cols] for r in range(rows)],
    ]
    for side in range(2):
        halo.out_side[side] = jnp.concatenate(pieces[side], axis=0).astype(BF16)
    halo.out_row[0] = state[:cols].astype(BF16)
    halo.out_row[1] = state[(rows - 1) * cols :].astype(BF16)
    halo.start(lambda row_step, col_step: 0 if row_step == -1 else 1)


def send_spread(halo, spread, rows, cols):
    span = cols + 2 * REACH
    west = [spread[(r + 1) * span : (r + 1) * span + REACH, :] for r in range(rows)]
    east = [spread[(r + 2) * span - REACH : (r + 2) * span, :] for r in range(rows)]
    halo.out_side[0] = jnp.concatenate(west, axis=0).astype(BF16)
    halo.out_side[1] = jnp.concatenate(east, axis=0).astype(BF16)
    for block, row in enumerate((0, rows + 1)):
        base = row * span
        halo.out_row[2 * block] = spread[base + REACH : base + REACH + cols, :].astype(BF16)
        corners = [spread[base : base + REACH, :], spread[base + span - REACH : base + span, :]]
        if cols > 2 * REACH:
            corners.insert(1, jnp.zeros((cols - 2 * REACH, spread.shape[1]), F32))
        halo.out_row[2 * block + 1] = jnp.concatenate(corners, axis=0).astype(BF16)
    halo.start(
        lambda row_step, col_step: (0 if row_step == -1 else 2) + (1 if col_step else 0)
    )


def take_spread(halo, spread, gradient, rows, cols):
    span = cols + 2 * REACH
    west, east = halo.in_side[0].astype(F32), halo.in_side[1].astype(F32)
    outer = {}
    for first, row, flag in zip((0, 3), (0, rows - 1), edge_flags()):
        line = halo.in_row[first + 1].astype(F32)
        rim_west = halo.in_row[first].astype(F32)[cols - REACH :]
        rim_east = halo.in_row[first + 2].astype(F32)[:REACH]
        rims = [rim_west, rim_east]
        if cols > 2 * REACH:
            rims.insert(1, jnp.zeros((cols - 2 * REACH, line.shape[1]), F32))
        outer[row] = jnp.where(flag, line + jnp.concatenate(rims, axis=0), 0.0)
    result = []
    for row in range(rows):
        low, high = row * REACH, (row + 1) * REACH
        rims = [west[low:high], east[low:high]]
        if cols > 2 * REACH:
            rims.insert(1, jnp.zeros((cols - 2 * REACH, west.shape[1]), F32))
        base = (row + 1) * span + REACH
        line = spread[base : base + cols, :] + jnp.concatenate(rims, axis=0)
        if row in outer:
            line = line + outer[row]
        result.append(gradient[row * cols : (row + 1) * cols].astype(F32) + line)
    return result


def aligned(index, size):
    return pl.ds(pl.multiple_of(index * size, size), size)


GROUP = 16


def over_rows(rows, body):
    group = GROUP if rows % GROUP == 0 else 1

    def step(index, carry):
        for inner in range(group):
            body(index * group + inner)
        return carry

    lax.fori_loop(0, rows // group, step, 0)


def make_bands(base, bands, rows, cols, basis_count):
    width = base.shape[1]

    def one(row):
        table = base[aligned(row, 2 * basis_count), :]
        for k in range(basis_count):
            line = jnp.broadcast_to(table[k : k + 1], (cols, width))
            moved = pltpu.roll(line, 0, 1, stride=1, stride_axis=0)
            start = pl.multiple_of((row * basis_count + k) * cols, cols)
            bands[pl.ds(start, cols), :] = moved.astype(BF16)

    over_rows(rows, one)


def stencil(bands, ext, features, rows, cols, basis_count):
    span = cols + 2 * REACH
    channels = ext.shape[1]

    def one(row):
        lhs = bands[aligned(row, basis_count * cols), :][:, : 3 * span]
        rhs = ext[pl.ds(pl.multiple_of(row * span, span), 3 * span), :]
        out = jnp.dot(lhs, rhs, preferred_element_type=F32).astype(BF16)
        for k in range(basis_count):
            features[aligned(row, cols), k * channels : (k + 1) * channels] = out[
                k * cols : (k + 1) * cols
            ]

    over_rows(rows, one)


def adjoint(bands, errs, spread, rows, cols, basis_count):
    span = cols + 2 * REACH
    spread[...] = jnp.zeros_like(spread)

    def one(row):
        lhs = bands[aligned(row, basis_count * cols), :][:, : 3 * span]
        rhs = errs[aligned(row, basis_count * cols), :]
        out = lax.dot_general(lhs, rhs, (((0,), (0,)), ((), ())), preferred_element_type=F32)
        place = pl.ds(pl.multiple_of(row * span, span), 3 * span)
        spread[place, :] = spread[place, :] + out

    over_rows(rows, one)


def rows_product(left, right):
    return lax.dot_general(left, right, (((0,), (0,)), ((), ())), preferred_element_type=F32)
TAPS_LEFT = TAP_REACH


class InputHalo(Sender):
    def __init__(self, bufs):
        super().__init__(bufs[-2:])
        (
            self.edges,
            self.out_cols,
            self.out_table,
            self.in_cols,
            self.in_row,
            self.in_table,
            self.in_tile,
        ) = bufs[:-2]

    @staticmethod
    def scratch(rows_in, cols_in, width, table_rows, lanes):
        return [
            pltpu.VMEM((3, rows_in, width), F32),
            pltpu.VMEM((3, rows_in, width), BF16),
            pltpu.VMEM((2, table_rows, lanes), F32),
            pltpu.VMEM((3, rows_in, width), BF16),
            pltpu.VMEM((2, cols_in, width), BF16),
            pltpu.VMEM((2, table_rows, lanes), F32),
            pltpu.VMEM((4, TILE, width), BF16),
            pltpu.SemaphoreType.DMA((10,)),
            pltpu.SemaphoreType.DMA((10,)),
        ]

    def start(self, field, table, owner, rows_in, cols_in):
        first = own_first_row(rows_in // 2)
        table_rows = self.out_table.shape[1]
        for block, row, target in ((0, 0, first - 1), (1, rows_in - 1, first + rows_in // 2)):
            feeds = jnp.where(owner[row] == target, 1.0, 0.0)
            self.out_table[block] = table[row * table_rows : (row + 1) * table_rows, :] * feeds
        last = (rows_in - 1) * cols_in
        lines = (field.at[pl.ds(0, cols_in)], field.at[pl.ds(last, cols_in)])
        slot = 0
        for block, row_step in ((0, -1), (1, 1)):
            self.send(lines[block], self.in_row.at[1 - block], slot, neighbour(row_step, 0))
            base = block * last
            west = field.at[pl.ds(base, TILE)]
            east = field.at[pl.ds(base + cols_in - TILE, TILE)]
            place = 2 * (1 - block)
            self.send(west, self.in_tile.at[place + 1], slot + 1, neighbour(row_step, -1))
            self.send(east, self.in_tile.at[place], slot + 2, neighbour(row_step, 1))
            slot += 3

        def one(row):
            low = field[pl.ds(pl.multiple_of(row * cols_in, TILE), TILE), :].astype(F32)
            start = pl.multiple_of(row * cols_in + cols_in - TILE, TILE)
            high = field[pl.ds(start, TILE), :].astype(F32)
            self.edges[0, pl.ds(row, 1), :] = high[TILE - 2 : TILE - 1]
            self.edges[1, pl.ds(row, 1), :] = high[TILE - 1 : TILE]
            self.edges[2, pl.ds(row, 1), :] = low[0:1]

        over_rows(rows_in, one)
        self.out_cols[...] = self.edges[...].astype(BF16)
        self.send(self.out_cols.at[pl.ds(0, 2)], self.in_cols.at[pl.ds(0, 2)], 6, neighbour(0, 1))
        self.send(self.out_cols.at[2], self.in_cols.at[2], 7, neighbour(0, -1))
        self.send(self.out_table.at[0], self.in_table.at[1], 8, neighbour(-1, 0))
        self.send(self.out_table.at[1], self.in_table.at[0], 9, neighbour(1, 0))


def own_first_row(rows):
    return (lax.axis_index("lat") * lax.axis_size("ch") + lax.axis_index("ch")) * rows


def tap_matrix(table, basis_count, cols, cols_in):
    lanes = table.shape[1]
    blocks = []
    for k in range(basis_count):
        line = jnp.broadcast_to(table[k : k + 1], (cols, lanes))
        moved = pltpu.roll(line, 0, 1, stride=2, stride_axis=0)
        wrapped = pltpu.roll(moved, cols_in + TILE - TAPS_LEFT, 1)
        moved = pltpu.roll(moved, lanes - TAPS_LEFT, 1)
        lane = lax.broadcasted_iota(jnp.int32, (cols, lanes), 1)
        at_end = (lane >= cols_in + TILE - TAPS_LEFT) & (lane < cols_in + TILE)
        blocks.append(jnp.where(at_end, wrapped, moved))
    return jnp.concatenate(blocks, axis=0)[:, : cols_in + TILE].astype(BF16)


def filtered_row(table, line, left_two, left_one, right, basis_count, cols, cols_in):
    width = line.shape[1]
    place = lax.broadcasted_iota(jnp.int32, (TILE, width), 0)
    tile = jnp.where(place == 0, jnp.broadcast_to(right, (TILE, width)), 0.0)
    tile = jnp.where(place == TILE - 2, jnp.broadcast_to(left_two, (TILE, width)), tile)
    tile = jnp.where(place == TILE - 1, jnp.broadcast_to(left_one, (TILE, width)), tile)
    rhs = jnp.concatenate([line, tile.astype(BF16)], axis=0)
    lhs = tap_matrix(table, basis_count, cols, cols_in)
    return jnp.dot(lhs, rhs, preferred_element_type=F32).astype(BF16)


def finish_encode(halo, field, table, owner, filtered, latent_in, plan, rows_in, cols_in):
    rows, cols, basis_count, _ = plan
    table_rows = halo.out_table.shape[1]
    block = basis_count * cols
    width = field.shape[1]
    halo.settle()
    halo.edges[...] = halo.in_cols[...].astype(F32)

    def one(row):
        sides = [halo.edges[index, pl.ds(row, 1), :] for index in range(3)]
        line = field[aligned(row, cols_in), :]
        taps = table[aligned(row, table_rows), :]
        filtered[aligned(row + 1, block), :] = filtered_row(
            taps, line, *sides, basis_count, cols, cols_in
        )

    over_rows(rows_in, one)
    for side, row in ((0, 0), (1, rows_in + 1)):
        west = halo.in_tile[2 * side].astype(F32)
        east = halo.in_tile[2 * side + 1].astype(F32)
        filtered[row * block : (row + 1) * block, :] = filtered_row(
            halo.in_table[side],
            halo.in_row[side],
            west[TILE - 2 : TILE - 1],
            west[TILE - 1 : TILE],
            east[0:1],
            basis_count,
            cols,
            cols_in,
        )
    first = own_first_row(rows)
    for row in range(rows):
        total = None
        for offset in range(-1, 3):
            source = 2 * row + offset
            term = filtered[(source + 1) * block : (source + 2) * block, :].astype(F32)
            if 0 <= source < rows_in:
                term = term * jnp.where(owner[source] == first + row, 1.0, 0.0)
            total = term if total is None else total + term
        total = total.astype(BF16)
        for k in range(basis_count):
            latent_in[row * cols : (row + 1) * cols, k * width : (k + 1) * width] = total[
                k * cols : (k + 1) * cols
            ]


def lanes_of(count):
    return -(-(count + 2 * TILE) // 128) * 128


def net_kernel(plan, *refs):
    rows, cols, basis_count, layers = plan
    field, table, owner, encoder_weight, base, weights, cotangent = refs[:7]
    state_out, latent_grad = refs[7:9]
    results = refs[9 : 10 + layers]
    rest = list(refs[10 + layers :])
    bands, ext, spread, errs, features, preact, filtered, latent_in = rest[:8]
    input_halo = InputHalo(rest[8:17])
    rest = rest[17:]
    halos = []
    for _ in range(2 * layers):
        halos.append(Halo(rest[:6]))
        rest = rest[6:]
    sums = []
    for index in range(layers + 1):
        sums.append(GradSum(results[index], rest[:11]))
        rest = rest[11:]
    channels = ext.shape[1]
    progress = [0] * (layers + 1)

    def advance(index):
        getattr(sums[index], STAGES[progress[index]])()
        progress[index] += 1

    greet()
    rows_in = owner.shape[0]
    cols_in = field.shape[0] // rows_in
    input_halo.start(field, table, owner, rows_in, cols_in)
    make_bands(base, bands, rows, cols, basis_count)
    finish_encode(input_halo, field, table, owner, filtered, latent_in, plan, rows_in, cols_in)
    state = jnp.dot(latent_in[...], encoder_weight[...], preferred_element_type=F32)
    state = state.astype(BF16).astype(F32)
    for layer in range(layers):
        send_state(halos[layer], state, rows, cols)
        halos[layer].settle()
        extend(halos[layer], state, ext, rows, cols)
        stencil(bands, ext, features.at[layer], rows, cols, basis_count)
        pre = jnp.dot(features[layer], weights[layer], preferred_element_type=F32)
        preact[layer] = pre
        state = (state + pre / (1.0 + jnp.exp(-pre))).astype(BF16).astype(F32)
    state_out[...] = state.astype(BF16)

    gradient = cotangent[...].astype(F32)
    for layer in reversed(range(layers)):
        pre = preact[layer]
        sigma = 1.0 / (1.0 + jnp.exp(-pre))
        act_grad = (gradient * sigma * (1.0 + pre * (1.0 - sigma))).astype(BF16)
        for k in range(basis_count):
            block = weights[layer, k * channels : (k + 1) * channels, :]
            out = lax.dot_general(
                act_grad, block, (((1,), (1,)), ((), ())), preferred_element_type=F32
            ).astype(BF16)
            for row in range(rows):
                start = (row * basis_count + k) * cols
                errs[start : start + cols, :] = out[row * cols : (row + 1) * cols]
        adjoint(bands, errs, spread, rows, cols, basis_count)
        halo = halos[layers + layer]
        send_spread(halo, spread, rows, cols)
        sums[layer].source[...] = rows_product(features[layer], act_grad).astype(BF16)
        for other in range(layers - 1, layer - 1, -1):
            advance(other)
        halo.settle()
        for other in range(layers - 1, layer - 1, -1):
            advance(other)
        lines = take_spread(halo, spread, gradient, rows, cols)
        gradient = jnp.concatenate(lines, axis=0).astype(BF16).astype(F32)
    latent_grad[...] = gradient.astype(BF16)
    sums[layers].source[...] = rows_product(latent_in[...], gradient.astype(BF16)).astype(BF16)
    advance(layers)
    while min(progress) < len(STAGES):
        for index in [layers] + list(range(layers))[::-1]:
            if progress[index] < len(STAGES):
                advance(index)


def run_net(plan, sizes, field_in, table, owner, encoder_weight, base, weights, cotangent):
    rows, cols, basis_count, layers = plan
    cells, channels = rows * cols, weights.shape[2]
    features = basis_count * channels
    span = cols + 2 * REACH
    rows_in = owner.shape[0]
    in_features = encoder_weight.shape[0]
    heights = [features] * layers + [in_features]
    scratch = [
        pltpu.VMEM((rows * basis_count * cols, base.shape[1]), BF16),
        pltpu.VMEM(((rows + 2) * span, channels), BF16),
        pltpu.VMEM(((rows + 2) * span, channels), F32),
        pltpu.VMEM((rows * basis_count * cols, channels), BF16),
        pltpu.VMEM((layers, cells, features), BF16),
        pltpu.VMEM((layers, cells, channels), F32),
        pltpu.VMEM(((rows_in + 2) * basis_count * cols, field_in.shape[1]), BF16),
        pltpu.VMEM((cells, in_features), BF16),
    ]
    scratch += InputHalo.scratch(
        rows_in, field_in.shape[0] // rows_in, field_in.shape[1], table.shape[0] // rows_in, table.shape[1]
    )
    for index in range(2 * layers):
        scratch += Halo.scratch(rows, cols, channels, 2 if index < layers else 4)
    for height in heights:
        scratch += GradSum.scratch(sizes, height, channels)
    vmem = pl.BlockSpec(memory_space=pltpu.VMEM)
    field = jax.ShapeDtypeStruct((cells, channels), BF16)
    grads = [jax.ShapeDtypeStruct((height, channels // 2), BF16) for height in heights]
    return pl.pallas_call(
        functools.partial(net_kernel, plan),
        out_shape=[field, field] + grads,
        in_specs=[vmem, vmem, pl.BlockSpec(memory_space=pltpu.SMEM)] + [vmem] * 4,
        out_specs=[vmem] * (3 + layers),
        scratch_shapes=scratch,
        compiler_params=pltpu.CompilerParams(
            collective_id=0, has_side_effects=True, vmem_limit_bytes=56 << 20
        ),
    )(field_in, table, owner, encoder_weight, base, weights, cotangent)


def per_device(
    input_field,
    encoder_filter,
    row_owner,
    encoder_weight,
    disco_basis,
    row_widths,
    block_weights,
    cotangent,
):
    if fits_chunks(
        cotangent.shape[0],
        input_field.shape[1],
        cotangent.shape[1],
        block_weights.shape[0],
        [block_weights.shape[1]] * block_weights.shape[0] + [encoder_weight.shape[0]],
    ):
        return per_device_chunks(
            input_field,
            encoder_filter,
            row_owner,
            encoder_weight,
            disco_basis,
            row_widths,
            block_weights,
            cotangent,
        )
    rows_in, cols_in, in_width = input_field.shape
    rows_dev = rows_in // 2
    cols_dev = cols_in // 2
    basis_count = encoder_filter.shape[1]
    tap_count = encoder_filter.shape[2]
    channels = block_weights.shape[2]
    layers = block_weights.shape[0]
    cell_count = rows_dev * cols_dev
    offsets = jnp.abs(jnp.arange(2 * REACH + 1, dtype=jnp.int32) - REACH)
    keep = offsets[None, :] <= row_widths[:, None]
    masked = jnp.where(keep[:, None, None, :], disco_basis, jnp.zeros_like(disco_basis))
    span = cols_dev + 2 * REACH
    table = jnp.pad(masked, ((0, 0), (0, basis_count), (0, 0), (0, span - masked.shape[3])))
    table = table.reshape(rows_dev * 2 * basis_count, 3 * span).astype(jnp.float32)
    lanes = lanes_of(2 * span)
    table = jnp.pad(table, ((0, 0), (0, lanes - 3 * span)))
    taps = jnp.pad(
        encoder_filter.astype(jnp.float32),
        ((0, 0), (0, basis_count), (0, lanes_of(cols_in) - tap_count)),
    ).reshape(rows_in * 2 * basis_count, -1)
    own_width = channels // lax.axis_size("ch")
    sizes = (lax.axis_size("lat"), lax.axis_size("lon"))
    plan = (rows_dev, cols_dev, basis_count, layers)
    outs = run_net(
        plan,
        sizes,
        input_field.reshape(rows_in * cols_in, in_width),
        taps,
        row_owner,
        encoder_weight,
        table,
        block_weights,
        cotangent.reshape(cell_count, channels),
    )
    current, gradient = (field.reshape(rows_dev, cols_dev, channels) for field in outs[:2])
    sums = [value.astype(jnp.float32) for value in outs[2:]]
    block_sum, encoder_sum = jnp.stack(sums[:-1]), sums[-1]
    cells_total = cell_count * lax.axis_size("lon") * lax.axis_size(("lat", "ch"))
    normalizer = 1.0 / math.sqrt(cells_total)
    block_grads = (block_sum * normalizer).reshape(layers, basis_count * channels, own_width)
    encoder_grad = encoder_sum * normalizer
    return (current, gradient, block_grads, encoder_grad)

HALO = 2
DIRECT, ACROSS, WIDE, PAIRED = range(4)
LANES = 128


class Place:
    def __init__(self):
        self.lon, self.ch = lax.axis_size("lon"), lax.axis_size("ch")
        self.bands = lax.axis_size("lat") * self.ch
        self.z = lax.axis_index("lon")
        self.band = lax.axis_index("lat") * self.ch + lax.axis_index("ch")
        self.chunk = self.flip(self.band, self.z)
        self.count = self.bands * self.lon
        self.position = self.band * self.lon + self.chunk

    def flip(self, band, index):
        return index + lax.rem(band, 2) * (self.lon - 1 - 2 * index)

    def offset(self, chunk):
        return (chunk + self.lon - 1) // self.lon + (chunk + 1) // self.lon

    def device(self, band, chunk):
        return {
            "lat": band // self.ch,
            "ch": lax.rem(band, self.ch),
            "lon": self.flip(band, chunk),
        }

    def along_snake(self, step):
        position = lax.rem(self.position + step + self.count, self.count)
        return self.device(position // self.lon, lax.rem(position, self.lon))


def greet_part():
    barrier = pltpu.get_barrier_semaphore()
    count = 0
    for lat in range(lax.axis_size("lat")):
        for ch in range(lax.axis_size("ch")):
            for lon in range(lax.axis_size("lon")):
                if lat or ch or lon:
                    target = {**along("lat", lat), **along("ch", ch), **along("lon", lon)}
                    pl.semaphore_signal(barrier, inc=1, device_id=target, device_id_type=MESH)
                    count += 1
    return lambda: pl.semaphore_wait(barrier, count)


class Regroup(Sender):
    def __init__(self, bufs, rim):
        self.rim = rim
        self.lines, self.rim_ssem, self.rim_rsem, self.own_sem = bufs[0], bufs[3], bufs[4], bufs[5]
        super().__init__(bufs[1:3])

    @staticmethod
    def scratch(lon, rows, cols, width, rim):
        return [
            pltpu.VMEM((rows + 2 + 2 * rim, cols, width), BF16),
            pltpu.SemaphoreType.DMA((lon - 1,)),
            pltpu.SemaphoreType.DMA((lon - 1,)),
            pltpu.SemaphoreType.DMA((2,)),
            pltpu.SemaphoreType.DMA((2 * lon,)),
            pltpu.SemaphoreType.DMA,
        ]

    def start_rims(self, place, source):
        self.place, self.source = place, source
        rows, piece = source.shape[0], source.shape[1]
        self.piece, self.each = piece, rows // place.lon
        self.size = self.each + 2 * self.rim
        self.columns = pl.ds(pl.multiple_of(place.z * piece, piece), piece)
        self.rims = []
        for side, (row, slot, step, chunk) in enumerate(
            ((rows - 1, 0, 1, 0), (0, self.size + 1, -1, place.lon - 1))[: 2 * self.rim]
        ):
            band = lax.rem(place.band + step + place.bands, place.bands)
            copy = pltpu.make_async_remote_copy(
                src_ref=source.at[row],
                dst_ref=self.lines.at[slot, self.columns],
                send_sem=self.rim_ssem.at[side],
                recv_sem=self.rim_rsem.at[side * place.lon + place.z],
                device_id=place.device(band, chunk),
                device_id_type=MESH,
            )
            copy.start()
            self.rims.append(copy)

    def start(self):
        place, source, each, size = self.place, self.source, self.each, self.size
        block = self.lines.at[pl.ds(1, size), self.columns]
        for step in range(1, place.lon):
            peer = along("lon", step)
            chunk = place.flip(place.band, peer["lon"])
            first = chunk * each - self.rim * place.offset(chunk)
            self.send(source.at[pl.ds(first, size)], block, step - 1, peer)
        first = place.chunk * each - self.rim * place.offset(place.chunk)
        self.own = pltpu.make_async_copy(source.at[pl.ds(first, size)], block, self.own_sem)
        self.own.start()

    def finish(self):
        place = self.place
        self.settle()
        self.own.wait()
        ends = ((0, 0), (self.size + 1, place.lon - 1))[: 2 * self.rim]
        for side, (slot, chunk) in enumerate(ends):

            @pl.when(place.chunk == chunk)
            def _():
                for z in range(place.lon):
                    pltpu.make_async_remote_copy(
                        src_ref=self.source.at[0],
                        dst_ref=self.lines.at[slot, pl.ds(z * self.piece, self.piece)],
                        send_sem=self.rim_ssem.at[side],
                        recv_sem=self.rim_rsem.at[side * place.lon + z],
                        device_id=along("lon", 0),
                        device_id_type=MESH,
                    ).wait_recv()

        for copy in self.rims:
            copy.wait_send()

    def row(self, index):
        return self.lines[index + 1 + self.rim * self.place.offset(self.place.chunk)]


class Restore(Sender):
    def __init__(self, bufs):
        self.lines, self.own_sem = bufs[0], bufs[3]
        super().__init__(bufs[1:3])

    @staticmethod
    def scratch(lon, rows, cols, width):
        return [
            pltpu.VMEM((rows, cols, width), BF16),
            pltpu.SemaphoreType.DMA((lon - 1,)),
            pltpu.SemaphoreType.DMA((lon - 1,)),
            pltpu.SemaphoreType.DMA,
        ]

    def start(self, place, result):
        rows, piece = self.lines.shape[0], result.shape[1]
        target = result.at[pl.ds(place.chunk * rows, rows)]
        for step in range(1, place.lon):
            peer = along("lon", step)
            columns = pl.ds(pl.multiple_of(peer["lon"] * piece, piece), piece)
            self.send(self.lines.at[:, columns], target, step - 1, peer)
        columns = pl.ds(pl.multiple_of(place.z * piece, piece), piece)
        self.own = pltpu.make_async_copy(self.lines.at[:, columns], target, self.own_sem)
        self.own.start()

    def finish(self):
        self.settle()
        self.own.wait()


class Swap(Sender):
    def __init__(self, bufs):
        super().__init__(bufs)

    @staticmethod
    def scratch():
        return [pltpu.SemaphoreType.DMA((2,)), pltpu.SemaphoreType.DMA((2,))]

    def start(self, place, buffer, slot_rows, own, halo):
        def part(first):
            return buffer.at[pl.ds(first * slot_rows, halo * slot_rows)]

        self.send(part(own), part(0), 0, place.along_snake(1))
        self.send(part(halo), part(halo + own), 1, place.along_snake(-1))


class ChipSum(Sender):
    def __init__(self, result, source, first, direct, bufs):
        super().__init__(bufs[-2:])
        self.result, self.source, self.first = result, source, first
        self.rec_ch, self.part, self.rec_lat, self.strip, self.rec, self.piece = bufs[:6]
        self.rec_pair, self.half, self.rec_far, self.whole = bufs[6:10]
        self.rows, self.width = self.part.shape
        self.lat, self.lon = lax.axis_size("lat"), lax.axis_size("lon")
        self.height, self.span = self.strip.shape[0], self.piece.shape[0]
        self.side = lax.rem(lax.axis_index("lon"), 2)
        self.direct = direct
        self.stages = [self.start_ch]
        if direct == DIRECT:
            self.stages += [self.scatter_all, self.gather_all]
        elif direct == ACROSS:
            self.stages += [self.scatter_lat, self.scatter_lon, self.gather_lon, self.gather_lat]
        elif direct == WIDE:
            self.stages += [self.scatter_lat, self.scatter_lon, self.gather_all]
        else:
            self.stages += [self.scatter_lat, self.scatter_pair, self.trade_far]
            self.stages += [self.gather_pair, self.gather_lat]
        self.stages.append(self.settle)

    @staticmethod
    def scratch(sizes, rows, columns):
        lat, lon = sizes
        width, height, span = columns // 2, rows // lat, rows // (lat * lon)
        count = 1 + 2 * (lat - 1) + 2 * (lat * lon - 1)
        return [
            pltpu.VMEM((rows, width), BF16),
            pltpu.VMEM((rows, width), BF16),
            pltpu.VMEM((lat - 1, height, width), BF16),
            pltpu.VMEM((height, width), BF16),
            pltpu.VMEM((lat * lon - 1, span, width), BF16),
            pltpu.VMEM((span, width), BF16),
            pltpu.VMEM((height // 2, width), BF16),
            pltpu.VMEM((height // 2, width), BF16),
            pltpu.VMEM((max(lon // 2 - 1, 1), height // 2, width), BF16),
            pltpu.VMEM((height // 2, width), BF16),
            pltpu.SemaphoreType.DMA((count,)),
            pltpu.SemaphoreType.DMA((count,)),
        ]

    def advance(self):
        self.stages.pop(0)()

    def columns(self, half):
        return pl.ds(pl.multiple_of(half * self.width, self.width), self.width)

    def own_columns(self):
        return self.source[self.first : self.first + self.rows, self.columns(lax.axis_index("ch"))]

    def others(self):
        for lat in range(self.lat):
            for lon in range(self.lon):
                if lat or lon:
                    yield lat * self.lon + lon - 1, {**along("lat", lat), **along("lon", lon)}

    def mine(self):
        return lax.axis_index("lat") * self.lon + lax.axis_index("lon")

    def place(self, index, size):
        return pl.ds(pl.multiple_of(index * size, size), size)

    def target(self, index, size):
        return pl.ds(pl.multiple_of(self.first + index * size, size), size)

    def start_ch(self):
        other = 1 - lax.axis_index("ch")
        rows = pl.ds(self.first, self.rows)
        self.send(self.source.at[rows, self.columns(other)], self.rec_ch, 0, {"ch": other})

    def add_ch(self):
        self.settle()
        total = self.own_columns().astype(F32) + self.rec_ch[...].astype(F32)
        self.part[...] = total.astype(BF16)

    def scatter_all(self):
        self.add_ch()
        for slot, peer in self.others():
            rows = self.place(peer["lat"] * self.lon + peer["lon"], self.span)
            self.send(self.part.at[rows], self.rec.at[slot], 1 + slot, peer)

    def scatter_lat(self):
        self.add_ch()
        self.slot = self.lat * self.lon
        for step in range(1, self.lat):
            peer = along("lat", step)
            rows = self.place(peer["lat"], self.height)
            self.send(self.part.at[rows], self.rec_lat.at[step - 1], self.slot, peer)
            self.slot += 1

    def add_lat(self):
        self.settle()
        total = self.part[self.place(lax.axis_index("lat"), self.height), :].astype(F32)
        for step in range(1, self.lat):
            total = total + self.rec_lat[step - 1].astype(F32)
        self.strip[...] = total.astype(BF16)

    def scatter_pair(self):
        self.add_lat()
        rows = self.place(1 - self.side, self.height // 2)
        self.send(self.strip.at[rows], self.rec_pair, 1, along("lon", 1 - 2 * self.side))

    def trade_far(self):
        self.settle()
        total = self.strip[self.place(self.side, self.height // 2), :].astype(F32)
        self.half[...] = (total + self.rec_pair[...].astype(F32)).astype(BF16)
        for step in range(1, self.lon // 2):
            self.send(self.half, self.rec_far.at[step - 1], 1 + step, along("lon", 2 * step))

    def gather_pair(self):
        self.settle()
        total = self.half[...].astype(F32)
        for step in range(1, self.lon // 2):
            total = total + self.rec_far[step - 1].astype(F32)
        self.whole[...] = total.astype(BF16)
        rows = self.target(2 * lax.axis_index("lat") + self.side, self.height // 2)
        self.result[rows, :] = self.whole[...]
        base = self.lat * self.lon + self.lat - 1
        self.send(self.whole, self.result.at[rows], base, along("lon", 1 - 2 * self.side))

    def scatter_lon(self):
        self.add_lat()
        for step in range(1, self.lon):
            peer = along("lon", step)
            rows = self.place(peer["lon"], self.span)
            self.send(self.strip.at[rows], self.rec.at[step - 1], step, peer)

    def add_rest(self):
        self.settle()
        if self.direct == DIRECT:
            total, count = self.part[self.place(self.mine(), self.span), :], self.lat * self.lon
        else:
            total, count = self.strip[self.place(lax.axis_index("lon"), self.span), :], self.lon
        total = total.astype(F32)
        for step in range(1, count):
            total = total + self.rec[step - 1].astype(F32)
        self.piece[...] = total.astype(BF16)
        rows = self.target(self.mine(), self.span)
        self.result[rows, :] = self.piece[...]
        return self.result.at[rows], self.lat * self.lon + self.lat - 1

    def gather_all(self):
        target, base = self.add_rest()
        for slot, peer in self.others():
            self.send(self.piece, target, base + slot, peer)

    def gather_lon(self):
        target, base = self.add_rest()
        for step in range(1, self.lon):
            self.send(self.piece, target, base + step - 1, along("lon", step))

    def gather_lat(self):
        self.settle()
        rows = self.target(lax.axis_index("lat"), self.height)
        base = 2 * self.lat * self.lon + self.lat - 2
        for step in range(1, self.lat):
            self.send(self.result.at[rows], self.result.at[rows], base + step - 1, along("lat", step))


def zero_outside(place, buffer, first, last, size):
    @pl.when(place.position == 0)
    def _():
        buffer[first : first + size, :] = jnp.zeros((size, buffer.shape[1]), buffer.dtype)

    @pl.when(place.position == place.count - 1)
    def _():
        buffer[last : last + size, :] = jnp.zeros((size, buffer.shape[1]), buffer.dtype)


def circulant(line, rows, stride):
    return pltpu.roll(jnp.broadcast_to(line, (rows, LANES)), 0, 1, stride=stride, stride_axis=0)


def silu_slope(pre):
    sigma = 1.0 / (1.0 + jnp.exp(-pre))
    return sigma * (1.0 + pre * (1.0 - sigma))


def chunk_kernel(plan, *refs):
    rows, cols, basis_count, layers = plan
    field, taps, owner, encoder_source, base, widths, weights_source, cotangent = refs[:8]
    state_out, latent_grad = refs[8:10]
    results = refs[10 : 11 + layers]
    rest = list(refs[11 + layers :])
    table, flat, lines, rims, bands, turned, latent_in, state, features, preact, steps, errs = rest[:12]
    encoder_weight, weights, load_sems = rest[12:15]
    rest = rest[15:]
    inputs, arriving = Regroup(rest[:6], 1), Regroup(rest[6:12], 0)
    leaving = [Restore(rest[12:16]), Restore(rest[16:20])]
    swaps = [Swap(rest[20 + 2 * n : 22 + 2 * n]) for n in range(5)]
    rest = rest[30:]
    sources, rest = rest[: layers + 1], rest[layers + 1 :]
    sums = []
    for index, first, size, direct in stretches([source.shape[0] for source in sources]):
        sums.append(ChipSum(results[index], sources[index], first, direct, rest[:12]))
        rest = rest[12:]
    channels = state.shape[1]
    width = field.shape[2]
    block = basis_count * cols
    ext = rows + 2 * HALO
    early, upper, lower, encoder = sums

    loads = [
        pltpu.make_async_copy(source, target, load_sems.at[index])
        for index, (source, target) in enumerate(
            ((encoder_source, encoder_weight), (weights_source, weights))
        )
    ]
    entered = greet_part()
    for load in loads:
        load.start()
    place = Place()
    first = place.position * rows
    rows_in = 2 * rows
    start_in = place.chunk * rows_in
    high, tall = table.shape[0] // ext, rims.shape[1]
    make_table(place, base, widths, table, rows, cols, basis_count, high)
    make_lines(taps, flat, lines, start_in, rows_in, basis_count)
    sides = (
        (0, jnp.where(owner[start_in] == first - 1, 1.0, 0.0)),
        (rows_in - 1, jnp.where(owner[start_in + rows_in - 1] == first + rows, 1.0, 0.0)),
    )
    for side, (row, feeds) in enumerate(sides):
        for k in range(basis_count):
            rims[side, k : k + 1, :] = lines[k * rows_in + row : k * rows_in + row + 1, :] * feeds
    entered()
    inputs.start_rims(place, field)
    swaps[0].start(place, table, high, rows, HALO)
    swaps[1].send(rims.at[1], rims.at[2], 0, place.along_snake(1))
    swaps[1].send(rims.at[0], rims.at[3], 1, place.along_snake(-1))
    inputs.start()

    lane = lax.broadcasted_iota(jnp.int32, (cols, LANES), 1)

    def make_band(row, carry):
        values = table[aligned(row, high), :]
        for k in range(basis_count):
            parts = [
                circulant(values[r * basis_count + k][None, :], cols, 1) for r in range(3)
            ]
            start = pl.multiple_of(row * block + k * cols, cols)
            bands[pl.ds(start, cols), :LANES] = jnp.where(lane < cols, parts[0], parts[1]).astype(BF16)
            bands[pl.ds(start, cols), LANES:] = parts[2].astype(BF16)
        other = bands[aligned(row, block), :].T
        for r in range(3):
            turned[aligned(row + r, cols), (2 - r) * block : (3 - r) * block] = other[
                r * cols : (r + 1) * cols
            ]
        return carry

    lax.fori_loop(HALO, HALO + rows, make_band, 0)
    swaps[0].settle()
    lax.fori_loop(0, HALO, make_band, 0)
    lax.fori_loop(HALO + rows, ext, make_band, 0)
    swaps[1].settle()
    inputs.finish()

    def filtered(row):
        if 0 <= row < rows_in:
            values = [lines[k * rows_in + row : k * rows_in + row + 1, :] for k in range(basis_count)]
        else:
            side = 2 if row < 0 else 3
            values = [rims[side, k : k + 1, :] for k in range(basis_count)]
        lhs = jnp.concatenate([circulant(value, cols, 2) for value in values], axis=0).astype(BF16)
        out = jnp.dot(lhs, inputs.row(row), preferred_element_type=F32)
        return out.astype(BF16).astype(F32)

    filters = [filtered(row) for row in range(-1, rows_in + 1)]
    for row in range(rows):
        total = None
        for step in range(-1, 3):
            source = 2 * row + step
            term = filters[source + 1]
            if 0 <= source < rows_in:
                term = term * jnp.where(owner[start_in + source] == first + row, 1.0, 0.0)
            total = term if total is None else total + term
        total = total.astype(BF16)
        for k in range(basis_count):
            latent_in[row * cols : (row + 1) * cols, k * width : (k + 1) * width] = total[
                k * cols : (k + 1) * cols
            ]
    own = pl.ds(HALO * cols, rows * cols)
    loads[0].wait()
    state[own, :] = jnp.dot(
        latent_in[...], encoder_weight[...], preferred_element_type=F32
    ).astype(BF16)
    swaps[2].start(place, state, cols, rows, HALO)
    arriving.start_rims(place, cotangent)
    arriving.start()
    loads[1].wait()
    swaps[2].settle()
    zero_outside(place, state, 0, (HALO + rows) * cols, HALO * cols)

    for layer in range(layers):
        low, top = layer + 1, ext - layer - 1
        for row in range(low, top):
            out = jnp.dot(
                bands[row * block : (row + 1) * block, : 3 * cols],
                state[(row - 1) * cols : (row + 2) * cols, :],
                preferred_element_type=F32,
            ).astype(BF16)
            for k in range(basis_count):
                features[layer, row * cols : (row + 1) * cols, k * channels : (k + 1) * channels] = out[
                    k * cols : (k + 1) * cols
                ]
        span = pl.ds(low * cols, (top - low) * cols)
        pre = jnp.dot(features[layer, span, :], weights[layer], preferred_element_type=F32)
        preact[layer, span, :] = pre
        new = state[span, :].astype(F32) + pre / (1.0 + jnp.exp(-pre))
        state[span, :] = new.astype(BF16)
        if layer < layers - 1:
            zero_outside(place, state, low * cols, (top - 1) * cols, cols)

    arriving.finish()
    last = layers - 1
    gradient = arriving.lines[1 : rows + 1].reshape(rows * cols, channels).astype(F32)
    act = gradient * silu_slope(preact[last, own, :])
    steps[last, own, :] = act.astype(BF16)
    swaps[3].start(place, steps.at[last], cols, rows, HALO)
    swaps[4].start(place, arriving.lines, 1, rows, 1)
    leaving[0].lines[...] = state[own, :].reshape(rows, cols, channels)

    def errors(layer, low, top):
        for k in range(basis_count):
            out = lax.dot_general(
                steps[layer, low * cols : top * cols, :],
                weights[layer, k * channels : (k + 1) * channels, :],
                (((1,), (1,)), ((), ())),
                preferred_element_type=F32,
            ).astype(BF16)
            for row in range(low, top):
                start = row * block + k * cols
                errs[start : start + cols, :] = out[(row - low) * cols : (row - low + 1) * cols]

    def spread(row):
        return jnp.dot(
            turned[(row + 1) * cols : (row + 2) * cols, :],
            errs[(row - 1) * block : (row + 2) * block, :],
            preferred_element_type=F32,
        )

    def weigh(part):
        stretch = slice(part.first, part.first + part.rows)
        left = features[0, own, stretch]
        sources[0][stretch, :] = rows_product(left, steps[0, own, :]).astype(BF16)

    sources[last][...] = rows_product(features[last, own, :], steps[last, own, :]).astype(BF16)
    early.advance()
    errors(last, HALO, HALO + rows)
    early.advance()
    leaving[0].start(place, state_out)
    swaps[3].settle()
    zero_outside(place, steps.at[last], 0, (HALO + rows) * cols, HALO * cols)
    errors(last, 0, HALO)
    errors(last, HALO + rows, ext)
    swaps[4].settle()
    back = [arriving.lines[row - 1].astype(F32) + spread(row) for row in range(1, ext - 1)]
    gradient = jnp.concatenate(back, axis=0).astype(BF16).astype(F32)
    span = pl.ds(cols, (ext - 2) * cols)
    steps[0, span, :] = (gradient * silu_slope(preact[0, span, :])).astype(BF16)
    zero_outside(place, steps.at[0], cols, (ext - 2) * cols, cols)
    weigh(upper)
    upper.advance()
    weigh(lower)
    lower.advance()
    early.advance()
    errors(0, 1, ext - 1)
    upper.advance()
    lower.advance()
    back = [
        gradient[(row - 1) * cols : row * cols] + spread(row) for row in range(HALO, HALO + rows)
    ]
    final = jnp.concatenate(back, axis=0).astype(BF16)
    leaving[1].lines[...] = final.reshape(rows, cols, channels)
    sources[layers][...] = rows_product(latent_in[...], final).astype(BF16)
    encoder.advance()
    encoder.advance()
    upper.advance()
    lower.advance()
    early.advance()
    encoder.advance()
    upper.advance()
    lower.advance()
    early.advance()
    upper.advance()
    lower.advance()
    encoder.advance()
    leaving[1].start(place, latent_grad)
    for part in sums:
        while part.stages:
            part.advance()
    for part in leaving:
        part.finish()


def make_table(place, base, widths, table, rows, cols, basis_count, high):
    own = pl.ds(HALO * high, rows * high)
    table[own, :] = jnp.zeros((rows * high, LANES), F32)
    size = base.shape[3]
    reach = size // 2
    distance = jnp.abs(lax.broadcasted_iota(jnp.int32, (basis_count, size), 1) - reach)
    for row in range(rows):
        source = place.chunk * rows + row
        values = base[source].astype(F32)
        for r in range(3):
            start = (HALO + row) * high + r * basis_count
            table[start : start + basis_count, :size] = jnp.where(
                distance <= widths[source], values[r], 0.0
            )
    moved = pltpu.roll(table[own, :], LANES - reach, 1)
    table[own, :] = moved + pltpu.roll(moved, cols, 1)


def make_lines(taps, flat, lines, start_in, rows_in, basis_count):
    flat[...] = jnp.zeros_like(flat)
    count, _, held = taps.shape
    for k in range(basis_count):
        for t in range(count):
            row = 8 * k + t
            flat[row : row + 1, :held] = taps[t, k : k + 1, :].astype(F32)
    flat[...] = flat[...].T
    values = flat[aligned(start_in // rows_in, rows_in), :]
    lane = lax.broadcasted_iota(jnp.int32, values.shape, 1)
    for k in range(basis_count):
        moved = pltpu.roll(values, LANES - 8 * k, 1) if k else values
        kept = jnp.where(lane < count, moved, 0.0)
        lines[k * rows_in : (k + 1) * rows_in, :] = pltpu.roll(kept, LANES - count // 2, 1)


def stretches(heights):
    half = heights[0] // 2
    return [
        (len(heights) - 2, 0, heights[-2], ACROSS),
        (0, 0, half, ACROSS),
        (0, half, half, ACROSS),
        (len(heights) - 1, 0, heights[-1], WIDE),
    ]


def run_chunks(
    plan, sizes, field_in, taps, owner, encoder_weight, base, widths, weights, cotangent
):
    rows, cols, basis_count, layers = plan
    lat, lon = sizes
    channels = weights.shape[2]
    features = basis_count * channels
    in_features = encoder_weight.shape[0]
    ext = rows + 2 * HALO
    heights = [features] * layers + [in_features]
    block = basis_count * cols
    high = -(-3 * basis_count // 8) * 8
    tall = -(-basis_count // 8) * 8
    scratch = [
        pltpu.VMEM((ext * high, LANES), F32),
        pltpu.VMEM((LANES, LANES), F32),
        pltpu.VMEM((basis_count * 2 * rows, LANES), F32),
        pltpu.VMEM((4, tall, LANES), F32),
        pltpu.VMEM((ext * block, 2 * LANES), BF16),
        pltpu.VMEM(((ext + 2) * cols, 3 * block), BF16),
        pltpu.VMEM((rows * cols, in_features), BF16),
        pltpu.VMEM((ext * cols, channels), BF16),
        pltpu.VMEM((layers, ext * cols, features), BF16),
        pltpu.VMEM((layers, ext * cols, channels), F32),
        pltpu.VMEM((layers, ext * cols, channels), BF16),
        pltpu.VMEM((ext * block, channels), BF16),
        pltpu.VMEM(encoder_weight.shape, BF16),
        pltpu.VMEM(weights.shape, BF16),
        pltpu.SemaphoreType.DMA((2,)),
    ]
    scratch += Regroup.scratch(lon, 2 * rows, field_in.shape[1] * lon, field_in.shape[2], 1)
    scratch += Regroup.scratch(lon, rows, cols, channels, 0)
    for _ in range(2):
        scratch += Restore.scratch(lon, rows, cols, channels)
    for _ in range(5):
        scratch += Swap.scratch()
    scratch += [pltpu.VMEM((height, channels), BF16) for height in heights]
    for _, _, size, _ in stretches(heights):
        scratch += ChipSum.scratch(sizes, size, channels)
    vmem = pl.BlockSpec(memory_space=pltpu.VMEM)
    smem = pl.BlockSpec(memory_space=pltpu.SMEM)
    hbm = pl.BlockSpec(memory_space=pltpu.HBM)
    out = pltpu.VMEM(cotangent.shape, BF16)
    grads = [pltpu.VMEM((height, channels // 2), BF16) for height in heights]
    return pl.pallas_call(
        functools.partial(chunk_kernel, plan),
        out_shape=[out, out] + grads,
        in_specs=[hbm, vmem, smem, hbm, vmem, smem, hbm, hbm],
        out_specs=[vmem, vmem] + [vmem] * (1 + layers),
        scratch_shapes=scratch,
        compiler_params=pltpu.CompilerParams(
            collective_id=1, has_side_effects=True, vmem_limit_bytes=56 << 20
        ),
    )(field_in, taps, owner, encoder_weight, base, widths, weights, cotangent)


def finish_body(normalizer, field_count, sum_count, refs):
    fields, sums = refs[:field_count], refs[field_count : field_count + sum_count]
    fields_out = refs[field_count + sum_count : 2 * field_count + sum_count]
    block_grads, encoder_grad = refs[2 * field_count + sum_count :][:2]
    rest = refs[2 * field_count + sum_count + 2 :]
    wide, out_sems = rest[:sum_count], rest[sum_count]
    targets = list(fields_out) + [block_grads.at[n] for n in range(sum_count - 1)] + [encoder_grad]
    stores = [
        pltpu.make_async_copy(source, target, out_sems.at[n])
        for n, (source, target) in enumerate(zip(list(fields) + list(wide), targets))
    ]
    for n, store in enumerate(stores):
        if n >= field_count:
            wide[n - field_count][...] = sums[n - field_count][...].astype(F32) * normalizer
        store.start()
    for store in stores:
        store.wait()


def finish_outputs(normalizer, outs):
    hbm = pl.BlockSpec(memory_space=pltpu.HBM)
    fields, sums = outs[:2], outs[2:]
    shapes = [jax.ShapeDtypeStruct(field.shape, field.dtype) for field in fields]
    shapes.append(jax.ShapeDtypeStruct((len(sums) - 1,) + sums[0].shape, F32))
    shapes.append(jax.ShapeDtypeStruct(sums[-1].shape, F32))

    def kernel(*refs):
        finish_body(normalizer, len(fields), len(sums), refs)

    return pl.pallas_call(
        kernel,
        out_shape=shapes,
        in_specs=[pl.BlockSpec(memory_space=pltpu.VMEM)] * len(outs),
        out_specs=[hbm] * len(shapes),
        scratch_shapes=[pltpu.VMEM(value.shape, F32) for value in sums]
        + [pltpu.SemaphoreType.DMA((len(outs),))],
        compiler_params=pltpu.CompilerParams(vmem_limit_bytes=16 << 20),
    )(*outs)


def fits_chunks(rows_dev, cols_in, cols_dev, layers, heights):
    lon = lax.axis_size("lon")
    count = lax.axis_size("lat") * lon
    heights_fit = all(size % (count * TILE) == 0 for _, _, size, _ in stretches(heights))
    return (
        layers == HALO
        and rows_dev % lon == 0
        and heights_fit
        and rows_dev // lon >= HALO
        and lon % 2 == 0
        and cols_in * lon == LANES
        and 2 * cols_dev * lon == LANES
    )


def per_device_chunks(
    input_field,
    encoder_filter,
    row_owner,
    encoder_weight,
    disco_basis,
    row_widths,
    block_weights,
    cotangent,
):
    rows_in, cols_in, _ = input_field.shape
    lat, lon = lax.axis_size("lat"), lax.axis_size("lon")
    rows_dev, cols = rows_in // 2, cols_in // 2 * lon
    plan = (rows_dev // lon, cols, encoder_filter.shape[1], block_weights.shape[0])
    outs = run_chunks(
        plan,
        (lat, lon),
        input_field,
        encoder_filter.transpose(2, 1, 0),
        row_owner,
        encoder_weight,
        disco_basis.transpose(0, 2, 1, 3),
        row_widths,
        block_weights,
        cotangent,
    )
    cells_total = rows_dev * lax.axis_size(("lat", "ch")) * cols
    return tuple(finish_outputs(1.0 / math.sqrt(cells_total), outs))


def solution(mesh):
    placed = (
        P(("ens", "lat", "ch"), "lon", None),
        P(("lat", "ch"), None, None),
        P(("ens", "lat", "ch")),
        P(),
        P(("lat", "ch"), None, None, None),
        P(("lat", "ch")),
        P(),
        P(("ens", "lat", "ch"), "lon", None),
    )
    return jax.shard_map(
        per_device,
        mesh=mesh,
        in_specs=placed,
        out_specs=(
            P(("ens", "lat", "ch"), "lon", None),
            P(("ens", "lat", "ch"), "lon", None),
            P("ens", None, "ch"),
            P("ens", "ch"),
        ),
        check_vma=False,
    )
```

```python
import functools
import math

import jax
import jax.numpy as jnp
from jax import lax
from jax.experimental import pallas as pl
from jax.experimental.pallas import tpu as pltpu
from jax.sharding import PartitionSpec as P

REACH = 8
TAP_REACH = 2
TILE = 16
MESH = pl.DeviceIdType.MESH
BF16 = jnp.bfloat16
F32 = jnp.float32


def along(axis, steps):
    count = lax.axis_size(axis)
    return {axis: lax.rem(lax.axis_index(axis) + steps + count, count)}


def neighbour(row_step, col_step):
    ch_count = lax.axis_size("ch")
    bands = lax.axis_size("lat") * ch_count
    band = lax.axis_index("lat") * ch_count + lax.axis_index("ch")
    band = lax.rem(band + row_step + bands, bands)
    target = {}
    if row_step:
        target = {"lat": band // ch_count, "ch": lax.rem(band, ch_count)}
    if col_step:
        target.update(along("lon", col_step))
    return target


AROUND = [(r, c) for r in (-1, 0, 1) for c in (-1, 0, 1) if r or c]


def greet():
    targets = [neighbour(r, c) for r, c in AROUND]
    for axis in ("ch", "lat", "lon"):
        targets += [along(axis, step) for step in range(1, lax.axis_size(axis))]
    barrier = pltpu.get_barrier_semaphore()
    for target in targets:
        pl.semaphore_signal(barrier, inc=1, device_id=target, device_id_type=MESH)
    pl.semaphore_wait(barrier, len(targets))


class Sender:
    def __init__(self, sems):
        self.ssem, self.rsem = sems
        self.pending = []

    def send(self, source, target, slot, device):
        copy = pltpu.make_async_remote_copy(
            src_ref=source,
            dst_ref=target,
            send_sem=self.ssem.at[slot],
            recv_sem=self.rsem.at[slot],
            device_id=device,
            device_id_type=MESH,
        )
        copy.start()
        self.pending.append(copy)

    def settle(self):
        for copy in self.pending:
            copy.wait()
        self.pending = []


class GradSum(Sender):
    def __init__(self, result, bufs):
        super().__init__(bufs[-2:])
        self.result = result
        self.source, self.rec_ch, self.part, self.rec_lat, self.strip, self.rec_pair, self.half, self.rec_far, self.piece = bufs[:-2]
        self.width = self.part.shape[1]
        self.lat, self.lon = lax.axis_size("lat"), lax.axis_size("lon")
        self.height = self.strip.shape[0]
        self.span = self.piece.shape[0]
        self.pair = self.height // self.span
        self.far = self.lon // self.pair
        self.side = lax.rem(lax.axis_index("lon"), self.pair)

    @staticmethod
    def scratch(sizes, rows, columns):
        lat, lon = sizes
        width = columns // 2
        height = rows // lat
        pair = 2 if lon % 2 == 0 and height % (2 * TILE) == 0 else 1
        span, far = height // pair, lon // pair
        count = 1 + 2 * (lat - 1) + 2 * (pair - 1) + far - 1
        return [
            pltpu.VMEM((rows, columns), BF16),
            pltpu.VMEM((rows, width), BF16),
            pltpu.VMEM((rows, width), BF16),
            pltpu.VMEM((lat - 1, height, width), BF16),
            pltpu.VMEM((height, width), BF16),
            pltpu.VMEM((span, width), BF16),
            pltpu.VMEM((span, width), BF16),
            pltpu.VMEM((far - 1, span, width), BF16),
            pltpu.VMEM((span, width), BF16),
            pltpu.SemaphoreType.DMA((count,)),
            pltpu.SemaphoreType.DMA((count,)),
        ]

    def columns(self, half):
        return pl.ds(pl.multiple_of(half * self.width, self.width), self.width)

    @staticmethod
    def stretch(owner, size):
        return pl.ds(pl.multiple_of(owner * size, size), size)

    def start_ch(self):
        other = 1 - lax.axis_index("ch")
        self.send(self.source.at[:, self.columns(other)], self.rec_ch, 0, {"ch": other})

    def start_lat(self):
        self.settle()
        own = self.source[:, self.columns(lax.axis_index("ch"))].astype(F32)
        self.part[...] = (own + self.rec_ch[...].astype(F32)).astype(BF16)
        for step in range(1, self.lat):
            peer = along("lat", step)
            rows = self.stretch(peer["lat"], self.height)
            self.send(self.part.at[rows], self.rec_lat.at[step - 1], step, peer)

    def start_lon(self):
        self.settle()
        total = self.part[self.stretch(lax.axis_index("lat"), self.height), :].astype(F32)
        for step in range(1, self.lat):
            total = total + self.rec_lat[step - 1].astype(F32)
        self.strip[...] = total.astype(BF16)
        if self.pair > 1:
            rows = self.stretch(1 - self.side, self.span)
            self.send(self.strip.at[rows], self.rec_pair, self.lat, along("lon", 1 - 2 * self.side))

    def start_far(self):
        self.settle()
        total = self.strip[self.stretch(self.side, self.span), :].astype(F32)
        if self.pair > 1:
            total = total + self.rec_pair[...].astype(F32)
        self.half[...] = total.astype(BF16)
        for step in range(1, self.far):
            self.send(
                self.half, self.rec_far.at[step - 1], self.lat + step, along("lon", self.pair * step)
            )

    def gather_lon(self):
        self.settle()
        total = self.half[...].astype(F32)
        for step in range(1, self.far):
            total = total + self.rec_far[step - 1].astype(F32)
        self.piece[...] = total.astype(BF16)
        offset = lax.axis_index("lat") * self.height + self.side * self.span
        rows = pl.ds(pl.multiple_of(offset, TILE), self.span)
        self.result[rows, :] = self.piece[...]
        if self.pair > 1:
            slot = self.lat + self.far
            self.send(self.piece, self.result.at[rows], slot, along("lon", 1 - 2 * self.side))

    def gather_lat(self):
        self.settle()
        rows = self.stretch(lax.axis_index("lat"), self.height)
        for step in range(1, self.lat):
            slot = self.lat + self.far + self.pair - 2 + step
            self.send(self.result.at[rows], self.result.at[rows], slot, along("lat", step))

    def finish(self):
        self.settle()


STAGES = ("start_ch", "start_lat", "start_lon", "start_far", "gather_lon", "gather_lat", "finish")


class Halo(Sender):
    def __init__(self, bufs):
        super().__init__(bufs[-2:])
        self.out_side, self.out_row, self.in_side, self.in_row = bufs[:-2]

    @staticmethod
    def scratch(rows, cols, width, row_blocks):
        return [
            pltpu.VMEM((2, rows * REACH, width), BF16),
            pltpu.VMEM((row_blocks, cols, width), BF16),
            pltpu.VMEM((2, rows * REACH, width), BF16),
            pltpu.VMEM((6, cols, width), BF16),
            pltpu.SemaphoreType.DMA((8,)),
            pltpu.SemaphoreType.DMA((8,)),
        ]

    def start(self, row_block_of):
        self.send(self.out_side.at[0], self.in_side.at[1], 0, neighbour(0, -1))
        self.send(self.out_side.at[1], self.in_side.at[0], 1, neighbour(0, 1))
        slot = 2
        for row_step in (-1, 1):
            for col_step in (-1, 0, 1):
                place = (0 if row_step == 1 else 3) + 1 - col_step
                self.send(
                    self.out_row.at[row_block_of(row_step, col_step)],
                    self.in_row.at[place],
                    slot,
                    neighbour(row_step, col_step),
                )
                slot += 1


def edge_flags():
    ch_count = lax.axis_size("ch")
    bands = lax.axis_size("lat") * ch_count
    band = lax.axis_index("lat") * ch_count + lax.axis_index("ch")
    return band > 0, band < bands - 1


def extend(halo, state, ext, rows, cols):
    span = cols + 2 * REACH
    west, east = halo.in_side[0].astype(F32), halo.in_side[1].astype(F32)
    for row in range(rows):
        low, high = row * REACH, (row + 1) * REACH
        line = jnp.concatenate(
            [west[low:high], state[row * cols : (row + 1) * cols], east[low:high]], axis=0
        )
        ext[(row + 1) * span : (row + 2) * span, :] = line.astype(BF16)
    for first, row, flag in zip((0, 3), (0, rows + 1), edge_flags()):
        line = jnp.concatenate(
            [
                halo.in_row[first].astype(F32)[cols - REACH :],
                halo.in_row[first + 1].astype(F32),
                halo.in_row[first + 2].astype(F32)[:REACH],
            ],
            axis=0,
        )
        ext[row * span : (row + 1) * span, :] = jnp.where(flag, line, 0.0).astype(BF16)


def send_state(halo, state, rows, cols):
    pieces = [
        [state[r * cols : r * cols + REACH] for r in range(rows)],
        [state[(r + 1) * cols - REACH : (r + 1) * cols] for r in range(rows)],
    ]
    for side in range(2):
        halo.out_side[side] = jnp.concatenate(pieces[side], axis=0).astype(BF16)
    halo.out_row[0] = state[:cols].astype(BF16)
    halo.out_row[1] = state[(rows - 1) * cols :].astype(BF16)
    halo.start(lambda row_step, col_step: 0 if row_step == -1 else 1)


def send_spread(halo, spread, rows, cols):
    span = cols + 2 * REACH
    west = [spread[(r + 1) * span : (r + 1) * span + REACH, :] for r in range(rows)]
    east = [spread[(r + 2) * span - REACH : (r + 2) * span, :] for r in range(rows)]
    halo.out_side[0] = jnp.concatenate(west, axis=0).astype(BF16)
    halo.out_side[1] = jnp.concatenate(east, axis=0).astype(BF16)
    for block, row in enumerate((0, rows + 1)):
        base = row * span
        halo.out_row[2 * block] = spread[base + REACH : base + REACH + cols, :].astype(BF16)
        corners = [spread[base : base + REACH, :], spread[base + span - REACH : base + span, :]]
        if cols > 2 * REACH:
            corners.insert(1, jnp.zeros((cols - 2 * REACH, spread.shape[1]), F32))
        halo.out_row[2 * block + 1] = jnp.concatenate(corners, axis=0).astype(BF16)
    halo.start(
        lambda row_step, col_step: (0 if row_step == -1 else 2) + (1 if col_step else 0)
    )


def take_spread(halo, spread, gradient, rows, cols):
    span = cols + 2 * REACH
    west, east = halo.in_side[0].astype(F32), halo.in_side[1].astype(F32)
    outer = {}
    for first, row, flag in zip((0, 3), (0, rows - 1), edge_flags()):
        line = halo.in_row[first + 1].astype(F32)
        rim_west = halo.in_row[first].astype(F32)[cols - REACH :]
        rim_east = halo.in_row[first + 2].astype(F32)[:REACH]
        rims = [rim_west, rim_east]
        if cols > 2 * REACH:
            rims.insert(1, jnp.zeros((cols - 2 * REACH, line.shape[1]), F32))
        outer[row] = jnp.where(flag, line + jnp.concatenate(rims, axis=0), 0.0)
    result = []
    for row in range(rows):
        low, high = row * REACH, (row + 1) * REACH
        rims = [west[low:high], east[low:high]]
        if cols > 2 * REACH:
            rims.insert(1, jnp.zeros((cols - 2 * REACH, west.shape[1]), F32))
        base = (row + 1) * span + REACH
        line = spread[base : base + cols, :] + jnp.concatenate(rims, axis=0)
        if row in outer:
            line = line + outer[row]
        result.append(gradient[row * cols : (row + 1) * cols].astype(F32) + line)
    return result


def aligned(index, size):
    return pl.ds(pl.multiple_of(index * size, size), size)


GROUP = 16


def over_rows(rows, body):
    group = GROUP if rows % GROUP == 0 else 1

    def step(index, carry):
        for inner in range(group):
            body(index * group + inner)
        return carry

    lax.fori_loop(0, rows // group, step, 0)


def make_bands(base, bands, rows, cols, basis_count):
    width = base.shape[1]

    def one(row):
        table = base[aligned(row, 2 * basis_count), :]
        for k in range(basis_count):
            line = jnp.broadcast_to(table[k : k + 1], (cols, width))
            moved = pltpu.roll(line, 0, 1, stride=1, stride_axis=0)
            start = pl.multiple_of((row * basis_count + k) * cols, cols)
            bands[pl.ds(start, cols), :] = moved.astype(BF16)

    over_rows(rows, one)


def stencil(bands, ext, features, rows, cols, basis_count):
    span = cols + 2 * REACH
    channels = ext.shape[1]

    def one(row):
        lhs = bands[aligned(row, basis_count * cols), :][:, : 3 * span]
        rhs = ext[pl.ds(pl.multiple_of(row * span, span), 3 * span), :]
        out = jnp.dot(lhs, rhs, preferred_element_type=F32).astype(BF16)
        for k in range(basis_count):
            features[aligned(row, cols), k * channels : (k + 1) * channels] = out[
                k * cols : (k + 1) * cols
            ]

    over_rows(rows, one)


def adjoint(bands, errs, spread, rows, cols, basis_count):
    span = cols + 2 * REACH
    spread[...] = jnp.zeros_like(spread)

    def one(row):
        lhs = bands[aligned(row, basis_count * cols), :][:, : 3 * span]
        rhs = errs[aligned(row, basis_count * cols), :]
        out = lax.dot_general(lhs, rhs, (((0,), (0,)), ((), ())), preferred_element_type=F32)
        place = pl.ds(pl.multiple_of(row * span, span), 3 * span)
        spread[place, :] = spread[place, :] + out

    over_rows(rows, one)


def rows_product(left, right):
    return lax.dot_general(left, right, (((0,), (0,)), ((), ())), preferred_element_type=F32)
TAPS_LEFT = TAP_REACH


class InputHalo(Sender):
    def __init__(self, bufs):
        super().__init__(bufs[-2:])
        (
            self.edges,
            self.out_cols,
            self.out_table,
            self.in_cols,
            self.in_row,
            self.in_table,
            self.in_tile,
        ) = bufs[:-2]

    @staticmethod
    def scratch(rows_in, cols_in, width, table_rows, lanes):
        return [
            pltpu.VMEM((3, rows_in, width), F32),
            pltpu.VMEM((3, rows_in, width), BF16),
            pltpu.VMEM((2, table_rows, lanes), F32),
            pltpu.VMEM((3, rows_in, width), BF16),
            pltpu.VMEM((2, cols_in, width), BF16),
            pltpu.VMEM((2, table_rows, lanes), F32),
            pltpu.VMEM((4, TILE, width), BF16),
            pltpu.SemaphoreType.DMA((10,)),
            pltpu.SemaphoreType.DMA((10,)),
        ]

    def start(self, field, table, owner, rows_in, cols_in):
        first = own_first_row(rows_in // 2)
        table_rows = self.out_table.shape[1]
        for block, row, target in ((0, 0, first - 1), (1, rows_in - 1, first + rows_in // 2)):
            feeds = jnp.where(owner[row] == target, 1.0, 0.0)
            self.out_table[block] = table[row * table_rows : (row + 1) * table_rows, :] * feeds
        last = (rows_in - 1) * cols_in
        lines = (field.at[pl.ds(0, cols_in)], field.at[pl.ds(last, cols_in)])
        slot = 0
        for block, row_step in ((0, -1), (1, 1)):
            self.send(lines[block], self.in_row.at[1 - block], slot, neighbour(row_step, 0))
            base = block * last
            west = field.at[pl.ds(base, TILE)]
            east = field.at[pl.ds(base + cols_in - TILE, TILE)]
            place = 2 * (1 - block)
            self.send(west, self.in_tile.at[place + 1], slot + 1, neighbour(row_step, -1))
            self.send(east, self.in_tile.at[place], slot + 2, neighbour(row_step, 1))
            slot += 3

        def one(row):
            low = field[pl.ds(pl.multiple_of(row * cols_in, TILE), TILE), :].astype(F32)
            start = pl.multiple_of(row * cols_in + cols_in - TILE, TILE)
            high = field[pl.ds(start, TILE), :].astype(F32)
            self.edges[0, pl.ds(row, 1), :] = high[TILE - 2 : TILE - 1]
            self.edges[1, pl.ds(row, 1), :] = high[TILE - 1 : TILE]
            self.edges[2, pl.ds(row, 1), :] = low[0:1]

        over_rows(rows_in, one)
        self.out_cols[...] = self.edges[...].astype(BF16)
        self.send(self.out_cols.at[pl.ds(0, 2)], self.in_cols.at[pl.ds(0, 2)], 6, neighbour(0, 1))
        self.send(self.out_cols.at[2], self.in_cols.at[2], 7, neighbour(0, -1))
        self.send(self.out_table.at[0], self.in_table.at[1], 8, neighbour(-1, 0))
        self.send(self.out_table.at[1], self.in_table.at[0], 9, neighbour(1, 0))


def own_first_row(rows):
    return (lax.axis_index("lat") * lax.axis_size("ch") + lax.axis_index("ch")) * rows


def tap_matrix(table, basis_count, cols, cols_in):
    lanes = table.shape[1]
    blocks = []
    for k in range(basis_count):
        line = jnp.broadcast_to(table[k : k + 1], (cols, lanes))
        moved = pltpu.roll(line, 0, 1, stride=2, stride_axis=0)
        wrapped = pltpu.roll(moved, cols_in + TILE - TAPS_LEFT, 1)
        moved = pltpu.roll(moved, lanes - TAPS_LEFT, 1)
        lane = lax.broadcasted_iota(jnp.int32, (cols, lanes), 1)
        at_end = (lane >= cols_in + TILE - TAPS_LEFT) & (lane < cols_in + TILE)
        blocks.append(jnp.where(at_end, wrapped, moved))
    return jnp.concatenate(blocks, axis=0)[:, : cols_in + TILE].astype(BF16)


def filtered_row(table, line, left_two, left_one, right, basis_count, cols, cols_in):
    width = line.shape[1]
    place = lax.broadcasted_iota(jnp.int32, (TILE, width), 0)
    tile = jnp.where(place == 0, jnp.broadcast_to(right, (TILE, width)), 0.0)
    tile = jnp.where(place == TILE - 2, jnp.broadcast_to(left_two, (TILE, width)), tile)
    tile = jnp.where(place == TILE - 1, jnp.broadcast_to(left_one, (TILE, width)), tile)
    rhs = jnp.concatenate([line, tile.astype(BF16)], axis=0)
    lhs = tap_matrix(table, basis_count, cols, cols_in)
    return jnp.dot(lhs, rhs, preferred_element_type=F32).astype(BF16)


def finish_encode(halo, field, table, owner, filtered, latent_in, plan, rows_in, cols_in):
    rows, cols, basis_count, _ = plan
    table_rows = halo.out_table.shape[1]
    block = basis_count * cols
    width = field.shape[1]
    halo.settle()
    halo.edges[...] = halo.in_cols[...].astype(F32)

    def one(row):
        sides = [halo.edges[index, pl.ds(row, 1), :] for index in range(3)]
        line = field[aligned(row, cols_in), :]
        taps = table[aligned(row, table_rows), :]
        filtered[aligned(row + 1, block), :] = filtered_row(
            taps, line, *sides, basis_count, cols, cols_in
        )

    over_rows(rows_in, one)
    for side, row in ((0, 0), (1, rows_in + 1)):
        west = halo.in_tile[2 * side].astype(F32)
        east = halo.in_tile[2 * side + 1].astype(F32)
        filtered[row * block : (row + 1) * block, :] = filtered_row(
            halo.in_table[side],
            halo.in_row[side],
            west[TILE - 2 : TILE - 1],
            west[TILE - 1 : TILE],
            east[0:1],
            basis_count,
            cols,
            cols_in,
        )
    first = own_first_row(rows)
    for row in range(rows):
        total = None
        for offset in range(-1, 3):
            source = 2 * row + offset
            term = filtered[(source + 1) * block : (source + 2) * block, :].astype(F32)
            if 0 <= source < rows_in:
                term = term * jnp.where(owner[source] == first + row, 1.0, 0.0)
            total = term if total is None else total + term
        total = total.astype(BF16)
        for k in range(basis_count):
            latent_in[row * cols : (row + 1) * cols, k * width : (k + 1) * width] = total[
                k * cols : (k + 1) * cols
            ]


def lanes_of(count):
    return -(-(count + 2 * TILE) // 128) * 128


def net_kernel(plan, *refs):
    rows, cols, basis_count, layers = plan
    field, table, owner, encoder_weight, base, weights, cotangent = refs[:7]
    state_out, latent_grad = refs[7:9]
    results = refs[9 : 10 + layers]
    rest = list(refs[10 + layers :])
    bands, ext, spread, errs, features, preact, filtered, latent_in = rest[:8]
    input_halo = InputHalo(rest[8:17])
    rest = rest[17:]
    halos = []
    for _ in range(2 * layers):
        halos.append(Halo(rest[:6]))
        rest = rest[6:]
    sums = []
    for index in range(layers + 1):
        sums.append(GradSum(results[index], rest[:11]))
        rest = rest[11:]
    channels = ext.shape[1]
    progress = [0] * (layers + 1)

    def advance(index):
        getattr(sums[index], STAGES[progress[index]])()
        progress[index] += 1

    greet()
    rows_in = owner.shape[0]
    cols_in = field.shape[0] // rows_in
    input_halo.start(field, table, owner, rows_in, cols_in)
    make_bands(base, bands, rows, cols, basis_count)
    finish_encode(input_halo, field, table, owner, filtered, latent_in, plan, rows_in, cols_in)
    state = jnp.dot(latent_in[...], encoder_weight[...], preferred_element_type=F32)
    state = state.astype(BF16).astype(F32)
    for layer in range(layers):
        send_state(halos[layer], state, rows, cols)
        halos[layer].settle()
        extend(halos[layer], state, ext, rows, cols)
        stencil(bands, ext, features.at[layer], rows, cols, basis_count)
        pre = jnp.dot(features[layer], weights[layer], preferred_element_type=F32)
        preact[layer] = pre
        state = (state + pre / (1.0 + jnp.exp(-pre))).astype(BF16).astype(F32)
    state_out[...] = state.astype(BF16)

    gradient = cotangent[...].astype(F32)
    for layer in reversed(range(layers)):
        pre = preact[layer]
        sigma = 1.0 / (1.0 + jnp.exp(-pre))
        act_grad = (gradient * sigma * (1.0 + pre * (1.0 - sigma))).astype(BF16)
        for k in range(basis_count):
            block = weights[layer, k * channels : (k + 1) * channels, :]
            out = lax.dot_general(
                act_grad, block, (((1,), (1,)), ((), ())), preferred_element_type=F32
            ).astype(BF16)
            for row in range(rows):
                start = (row * basis_count + k) * cols
                errs[start : start + cols, :] = out[row * cols : (row + 1) * cols]
        adjoint(bands, errs, spread, rows, cols, basis_count)
        halo = halos[layers + layer]
        send_spread(halo, spread, rows, cols)
        sums[layer].source[...] = rows_product(features[layer], act_grad).astype(BF16)
        for other in range(layers - 1, layer - 1, -1):
            advance(other)
        halo.settle()
        for other in range(layers - 1, layer - 1, -1):
            advance(other)
        lines = take_spread(halo, spread, gradient, rows, cols)
        gradient = jnp.concatenate(lines, axis=0).astype(BF16).astype(F32)
    latent_grad[...] = gradient.astype(BF16)
    sums[layers].source[...] = rows_product(latent_in[...], gradient.astype(BF16)).astype(BF16)
    advance(layers)
    while min(progress) < len(STAGES):
        for index in [layers] + list(range(layers))[::-1]:
            if progress[index] < len(STAGES):
                advance(index)


def run_net(plan, sizes, field_in, table, owner, encoder_weight, base, weights, cotangent):
    rows, cols, basis_count, layers = plan
    cells, channels = rows * cols, weights.shape[2]
    features = basis_count * channels
    span = cols + 2 * REACH
    rows_in = owner.shape[0]
    in_features = encoder_weight.shape[0]
    heights = [features] * layers + [in_features]
    scratch = [
        pltpu.VMEM((rows * basis_count * cols, base.shape[1]), BF16),
        pltpu.VMEM(((rows + 2) * span, channels), BF16),
        pltpu.VMEM(((rows + 2) * span, channels), F32),
        pltpu.VMEM((rows * basis_count * cols, channels), BF16),
        pltpu.VMEM((layers, cells, features), BF16),
        pltpu.VMEM((layers, cells, channels), F32),
        pltpu.VMEM(((rows_in + 2) * basis_count * cols, field_in.shape[1]), BF16),
        pltpu.VMEM((cells, in_features), BF16),
    ]
    scratch += InputHalo.scratch(
        rows_in, field_in.shape[0] // rows_in, field_in.shape[1], table.shape[0] // rows_in, table.shape[1]
    )
    for index in range(2 * layers):
        scratch += Halo.scratch(rows, cols, channels, 2 if index < layers else 4)
    for height in heights:
        scratch += GradSum.scratch(sizes, height, channels)
    vmem = pl.BlockSpec(memory_space=pltpu.VMEM)
    field = jax.ShapeDtypeStruct((cells, channels), BF16)
    grads = [jax.ShapeDtypeStruct((height, channels // 2), BF16) for height in heights]
    return pl.pallas_call(
        functools.partial(net_kernel, plan),
        out_shape=[field, field] + grads,
        in_specs=[vmem, vmem, pl.BlockSpec(memory_space=pltpu.SMEM)] + [vmem] * 4,
        out_specs=[vmem] * (3 + layers),
        scratch_shapes=scratch,
        compiler_params=pltpu.CompilerParams(
            collective_id=0, has_side_effects=True, vmem_limit_bytes=56 << 20
        ),
    )(field_in, table, owner, encoder_weight, base, weights, cotangent)


def per_device(
    input_field,
    encoder_filter,
    row_owner,
    encoder_weight,
    disco_basis,
    row_widths,
    block_weights,
    cotangent,
):
    if fits_chunks(
        cotangent.shape[0],
        input_field.shape[1],
        cotangent.shape[1],
        block_weights.shape[0],
        [block_weights.shape[1]] * block_weights.shape[0] + [encoder_weight.shape[0]],
    ):
        return per_device_chunks(
            input_field,
            encoder_filter,
            row_owner,
            encoder_weight,
            disco_basis,
            row_widths,
            block_weights,
            cotangent,
        )
    rows_in, cols_in, in_width = input_field.shape
    rows_dev = rows_in // 2
    cols_dev = cols_in // 2
    basis_count = encoder_filter.shape[1]
    tap_count = encoder_filter.shape[2]
    channels = block_weights.shape[2]
    layers = block_weights.shape[0]
    cell_count = rows_dev * cols_dev
    offsets = jnp.abs(jnp.arange(2 * REACH + 1, dtype=jnp.int32) - REACH)
    keep = offsets[None, :] <= row_widths[:, None]
    masked = jnp.where(keep[:, None, None, :], disco_basis, jnp.zeros_like(disco_basis))
    span = cols_dev + 2 * REACH
    table = jnp.pad(masked, ((0, 0), (0, basis_count), (0, 0), (0, span - masked.shape[3])))
    table = table.reshape(rows_dev * 2 * basis_count, 3 * span).astype(jnp.float32)
    lanes = lanes_of(2 * span)
    table = jnp.pad(table, ((0, 0), (0, lanes - 3 * span)))
    taps = jnp.pad(
        encoder_filter.astype(jnp.float32),
        ((0, 0), (0, basis_count), (0, lanes_of(cols_in) - tap_count)),
    ).reshape(rows_in * 2 * basis_count, -1)
    own_width = channels // lax.axis_size("ch")
    sizes = (lax.axis_size("lat"), lax.axis_size("lon"))
    plan = (rows_dev, cols_dev, basis_count, layers)
    outs = run_net(
        plan,
        sizes,
        input_field.reshape(rows_in * cols_in, in_width),
        taps,
        row_owner,
        encoder_weight,
        table,
        block_weights,
        cotangent.reshape(cell_count, channels),
    )
    current, gradient = (field.reshape(rows_dev, cols_dev, channels) for field in outs[:2])
    sums = [value.astype(jnp.float32) for value in outs[2:]]
    block_sum, encoder_sum = jnp.stack(sums[:-1]), sums[-1]
    cells_total = cell_count * lax.axis_size("lon") * lax.axis_size(("lat", "ch"))
    normalizer = 1.0 / math.sqrt(cells_total)
    block_grads = (block_sum * normalizer).reshape(layers, basis_count * channels, own_width)
    encoder_grad = encoder_sum * normalizer
    return (current, gradient, block_grads, encoder_grad)

HALO = 2
DIRECT, ACROSS, WIDE, PAIRED = range(4)
LANES = 128


class Place:
    def __init__(self):
        self.lon, self.ch = lax.axis_size("lon"), lax.axis_size("ch")
        self.bands = lax.axis_size("lat") * self.ch
        self.z = lax.axis_index("lon")
        self.band = lax.axis_index("lat") * self.ch + lax.axis_index("ch")
        self.chunk = self.flip(self.band, self.z)
        self.count = self.bands * self.lon
        self.position = self.band * self.lon + self.chunk

    def flip(self, band, index):
        return index + lax.rem(band, 2) * (self.lon - 1 - 2 * index)

    def offset(self, chunk):
        return (chunk + self.lon - 1) // self.lon + (chunk + 1) // self.lon

    def device(self, band, chunk):
        return {
            "lat": band // self.ch,
            "ch": lax.rem(band, self.ch),
            "lon": self.flip(band, chunk),
        }

    def along_snake(self, step):
        position = lax.rem(self.position + step + self.count, self.count)
        return self.device(position // self.lon, lax.rem(position, self.lon))


def greet_part():
    barrier = pltpu.get_barrier_semaphore()
    count = 0
    for lat in range(lax.axis_size("lat")):
        for ch in range(lax.axis_size("ch")):
            for lon in range(lax.axis_size("lon")):
                if lat or ch or lon:
                    target = {**along("lat", lat), **along("ch", ch), **along("lon", lon)}
                    pl.semaphore_signal(barrier, inc=1, device_id=target, device_id_type=MESH)
                    count += 1
    return lambda: pl.semaphore_wait(barrier, count)


class Regroup(Sender):
    def __init__(self, bufs, rim):
        self.rim = rim
        self.lines, self.rim_ssem, self.rim_rsem, self.own_sem = bufs[0], bufs[3], bufs[4], bufs[5]
        super().__init__(bufs[1:3])

    @staticmethod
    def scratch(lon, rows, cols, width, rim):
        return [
            pltpu.VMEM((rows + 2 + 2 * rim, cols, width), BF16),
            pltpu.SemaphoreType.DMA((lon - 1,)),
            pltpu.SemaphoreType.DMA((lon - 1,)),
            pltpu.SemaphoreType.DMA((2,)),
            pltpu.SemaphoreType.DMA((2 * lon,)),
            pltpu.SemaphoreType.DMA,
        ]

    def start_rims(self, place, source):
        self.place, self.source = place, source
        rows, piece = source.shape[0], source.shape[1]
        self.piece, self.each = piece, rows // place.lon
        self.size = self.each + 2 * self.rim
        self.columns = pl.ds(pl.multiple_of(place.z * piece, piece), piece)
        self.rims = []
        for side, (row, slot, step, chunk) in enumerate(
            ((rows - 1, 0, 1, 0), (0, self.size + 1, -1, place.lon - 1))[: 2 * self.rim]
        ):
            band = lax.rem(place.band + step + place.bands, place.bands)
            copy = pltpu.make_async_remote_copy(
                src_ref=source.at[row],
                dst_ref=self.lines.at[slot, self.columns],
                send_sem=self.rim_ssem.at[side],
                recv_sem=self.rim_rsem.at[side * place.lon + place.z],
                device_id=place.device(band, chunk),
                device_id_type=MESH,
            )
            copy.start()
            self.rims.append(copy)

    def start(self):
        place, source, each, size = self.place, self.source, self.each, self.size
        block = self.lines.at[pl.ds(1, size), self.columns]
        for step in range(1, place.lon):
            peer = along("lon", step)
            chunk = place.flip(place.band, peer["lon"])
            first = chunk * each - self.rim * place.offset(chunk)
            self.send(source.at[pl.ds(first, size)], block, step - 1, peer)
        first = place.chunk * each - self.rim * place.offset(place.chunk)
        self.own = pltpu.make_async_copy(source.at[pl.ds(first, size)], block, self.own_sem)
        self.own.start()

    def finish(self):
        place = self.place
        self.settle()
        self.own.wait()
        ends = ((0, 0), (self.size + 1, place.lon - 1))[: 2 * self.rim]
        for side, (slot, chunk) in enumerate(ends):

            @pl.when(place.chunk == chunk)
            def _():
                for z in range(place.lon):
                    pltpu.make_async_remote_copy(
                        src_ref=self.source.at[0],
                        dst_ref=self.lines.at[slot, pl.ds(z * self.piece, self.piece)],
                        send_sem=self.rim_ssem.at[side],
                        recv_sem=self.rim_rsem.at[side * place.lon + z],
                        device_id=along("lon", 0),
                        device_id_type=MESH,
                    ).wait_recv()

        for copy in self.rims:
            copy.wait_send()

    def row(self, index):
        return self.lines[index + 1 + self.rim * self.place.offset(self.place.chunk)]


class Restore(Sender):
    def __init__(self, bufs):
        self.lines, self.own_sem = bufs[0], bufs[3]
        super().__init__(bufs[1:3])

    @staticmethod
    def scratch(lon, rows, cols, width):
        return [
            pltpu.VMEM((rows, cols, width), BF16),
            pltpu.SemaphoreType.DMA((lon - 1,)),
            pltpu.SemaphoreType.DMA((lon - 1,)),
            pltpu.SemaphoreType.DMA,
        ]

    def start(self, place, result):
        rows, piece = self.lines.shape[0], result.shape[1]
        target = result.at[pl.ds(place.chunk * rows, rows)]
        for step in range(1, place.lon):
            peer = along("lon", step)
            columns = pl.ds(pl.multiple_of(peer["lon"] * piece, piece), piece)
            self.send(self.lines.at[:, columns], target, step - 1, peer)
        columns = pl.ds(pl.multiple_of(place.z * piece, piece), piece)
        self.own = pltpu.make_async_copy(self.lines.at[:, columns], target, self.own_sem)
        self.own.start()

    def finish(self):
        self.settle()
        self.own.wait()


class Swap(Sender):
    def __init__(self, bufs):
        super().__init__(bufs)

    @staticmethod
    def scratch():
        return [pltpu.SemaphoreType.DMA((2,)), pltpu.SemaphoreType.DMA((2,))]

    def start(self, place, buffer, slot_rows, own, halo):
        def part(first):
            return buffer.at[pl.ds(first * slot_rows, halo * slot_rows)]

        self.send(part(own), part(0), 0, place.along_snake(1))
        self.send(part(halo), part(halo + own), 1, place.along_snake(-1))


class ChipSum(Sender):
    def __init__(self, result, source, first, direct, bufs):
        super().__init__(bufs[-2:])
        self.result, self.source, self.first = result, source, first
        self.rec_ch, self.part, self.rec_lat, self.strip, self.rec, self.piece = bufs[:6]
        self.rec_pair, self.half, self.rec_far, self.whole = bufs[6:10]
        self.rows, self.width = self.part.shape
        self.lat, self.lon = lax.axis_size("lat"), lax.axis_size("lon")
        self.height, self.span = self.strip.shape[0], self.piece.shape[0]
        self.side = lax.rem(lax.axis_index("lon"), 2)
        self.direct = direct
        self.stages = [self.start_ch]
        if direct == DIRECT:
            self.stages += [self.scatter_all, self.gather_all]
        elif direct == ACROSS:
            self.stages += [self.scatter_lat, self.scatter_lon, self.gather_lon, self.gather_lat]
        elif direct == WIDE:
            self.stages += [self.scatter_lat, self.scatter_lon, self.gather_all]
        else:
            self.stages += [self.scatter_lat, self.scatter_pair, self.trade_far]
            self.stages += [self.gather_pair, self.gather_lat]
        self.stages.append(self.settle)

    @staticmethod
    def scratch(sizes, rows, columns):
        lat, lon = sizes
        width, height, span = columns // 2, rows // lat, rows // (lat * lon)
        count = 1 + 2 * (lat - 1) + 2 * (lat * lon - 1)
        return [
            pltpu.VMEM((rows, width), BF16),
            pltpu.VMEM((rows, width), BF16),
            pltpu.VMEM((lat - 1, height, width), BF16),
            pltpu.VMEM((height, width), BF16),
            pltpu.VMEM((lat * lon - 1, span, width), BF16),
            pltpu.VMEM((span, width), BF16),
            pltpu.VMEM((height // 2, width), BF16),
            pltpu.VMEM((height // 2, width), BF16),
            pltpu.VMEM((max(lon // 2 - 1, 1), height // 2, width), BF16),
            pltpu.VMEM((height // 2, width), BF16),
            pltpu.SemaphoreType.DMA((count,)),
            pltpu.SemaphoreType.DMA((count,)),
        ]

    def advance(self):
        self.stages.pop(0)()

    def columns(self, half):
        return pl.ds(pl.multiple_of(half * self.width, self.width), self.width)

    def own_columns(self):
        return self.source[self.first : self.first + self.rows, self.columns(lax.axis_index("ch"))]

    def others(self):
        for lat in range(self.lat):
            for lon in range(self.lon):
                if lat or lon:
                    yield lat * self.lon + lon - 1, {**along("lat", lat), **along("lon", lon)}

    def mine(self):
        return lax.axis_index("lat") * self.lon + lax.axis_index("lon")

    def place(self, index, size):
        return pl.ds(pl.multiple_of(index * size, size), size)

    def target(self, index, size):
        return pl.ds(pl.multiple_of(self.first + index * size, size), size)

    def start_ch(self):
        other = 1 - lax.axis_index("ch")
        rows = pl.ds(self.first, self.rows)
        self.send(self.source.at[rows, self.columns(other)], self.rec_ch, 0, {"ch": other})

    def add_ch(self):
        self.settle()
        total = self.own_columns().astype(F32) + self.rec_ch[...].astype(F32)
        self.part[...] = total.astype(BF16)

    def scatter_all(self):
        self.add_ch()
        for slot, peer in self.others():
            rows = self.place(peer["lat"] * self.lon + peer["lon"], self.span)
            self.send(self.part.at[rows], self.rec.at[slot], 1 + slot, peer)

    def scatter_lat(self):
        self.add_ch()
        self.slot = self.lat * self.lon
        for step in range(1, self.lat):
            peer = along("lat", step)
            rows = self.place(peer["lat"], self.height)
            self.send(self.part.at[rows], self.rec_lat.at[step - 1], self.slot, peer)
            self.slot += 1

    def add_lat(self):
        self.settle()
        total = self.part[self.place(lax.axis_index("lat"), self.height), :].astype(F32)
        for step in range(1, self.lat):
            total = total + self.rec_lat[step - 1].astype(F32)
        self.strip[...] = total.astype(BF16)

    def scatter_pair(self):
        self.add_lat()
        rows = self.place(1 - self.side, self.height // 2)
        self.send(self.strip.at[rows], self.rec_pair, 1, along("lon", 1 - 2 * self.side))

    def trade_far(self):
        self.settle()
        total = self.strip[self.place(self.side, self.height // 2), :].astype(F32)
        self.half[...] = (total + self.rec_pair[...].astype(F32)).astype(BF16)
        for step in range(1, self.lon // 2):
            self.send(self.half, self.rec_far.at[step - 1], 1 + step, along("lon", 2 * step))

    def gather_pair(self):
        self.settle()
        total = self.half[...].astype(F32)
        for step in range(1, self.lon // 2):
            total = total + self.rec_far[step - 1].astype(F32)
        self.whole[...] = total.astype(BF16)
        rows = self.target(2 * lax.axis_index("lat") + self.side, self.height // 2)
        self.result[rows, :] = self.whole[...]
        base = self.lat * self.lon + self.lat - 1
        self.send(self.whole, self.result.at[rows], base, along("lon", 1 - 2 * self.side))

    def scatter_lon(self):
        self.add_lat()
        for step in range(1, self.lon):
            peer = along("lon", step)
            rows = self.place(peer["lon"], self.span)
            self.send(self.strip.at[rows], self.rec.at[step - 1], step, peer)

    def add_rest(self):
        self.settle()
        if self.direct == DIRECT:
            total, count = self.part[self.place(self.mine(), self.span), :], self.lat * self.lon
        else:
            total, count = self.strip[self.place(lax.axis_index("lon"), self.span), :], self.lon
        total = total.astype(F32)
        for step in range(1, count):
            total = total + self.rec[step - 1].astype(F32)
        self.piece[...] = total.astype(BF16)
        rows = self.target(self.mine(), self.span)
        self.result[rows, :] = self.piece[...]
        return self.result.at[rows], self.lat * self.lon + self.lat - 1

    def gather_all(self):
        target, base = self.add_rest()
        for slot, peer in self.others():
            self.send(self.piece, target, base + slot, peer)

    def gather_lon(self):
        target, base = self.add_rest()
        for step in range(1, self.lon):
            self.send(self.piece, target, base + step - 1, along("lon", step))

    def gather_lat(self):
        self.settle()
        rows = self.target(lax.axis_index("lat"), self.height)
        base = 2 * self.lat * self.lon + self.lat - 2
        for step in range(1, self.lat):
            self.send(self.result.at[rows], self.result.at[rows], base + step - 1, along("lat", step))


def zero_outside(place, buffer, first, last, size):
    @pl.when(place.position == 0)
    def _():
        buffer[first : first + size, :] = jnp.zeros((size, buffer.shape[1]), buffer.dtype)

    @pl.when(place.position == place.count - 1)
    def _():
        buffer[last : last + size, :] = jnp.zeros((size, buffer.shape[1]), buffer.dtype)


def circulant(line, rows, stride):
    return pltpu.roll(jnp.broadcast_to(line, (rows, LANES)), 0, 1, stride=stride, stride_axis=0)


def silu_slope(pre):
    sigma = 1.0 / (1.0 + jnp.exp(-pre))
    return sigma * (1.0 + pre * (1.0 - sigma))


def chunk_kernel(plan, *refs):
    rows, cols, basis_count, layers = plan
    field, taps, owner, encoder_source, base, widths, weights_source, cotangent = refs[:8]
    state_out, latent_grad = refs[8:10]
    results = refs[10 : 11 + layers]
    rest = list(refs[11 + layers :])
    table, flat, lines, rims, bands, turned, latent_in, state, features, preact, steps, errs = rest[:12]
    encoder_weight, weights, load_sems = rest[12:15]
    rest = rest[15:]
    inputs, arriving = Regroup(rest[:6], 1), Regroup(rest[6:12], 0)
    leaving = [Restore(rest[12:16]), Restore(rest[16:20])]
    swaps = [Swap(rest[20 + 2 * n : 22 + 2 * n]) for n in range(5)]
    rest = rest[30:]
    sources, rest = rest[: layers + 1], rest[layers + 1 :]
    sums = []
    for index, first, size, direct in stretches([source.shape[0] for source in sources]):
        sums.append(ChipSum(results[index], sources[index], first, direct, rest[:12]))
        rest = rest[12:]
    channels = state.shape[1]
    width = field.shape[2]
    block = basis_count * cols
    ext = rows + 2 * HALO
    early, upper, lower, encoder = sums

    loads = [
        pltpu.make_async_copy(source, target, load_sems.at[index])
        for index, (source, target) in enumerate(
            ((encoder_source, encoder_weight), (weights_source, weights))
        )
    ]
    entered = greet_part()
    for load in loads:
        load.start()
    place = Place()
    first = place.position * rows
    rows_in = 2 * rows
    start_in = place.chunk * rows_in
    high, tall = table.shape[0] // ext, rims.shape[1]
    make_table(place, base, widths, table, rows, cols, basis_count, high)
    make_lines(taps, flat, lines, start_in, rows_in, basis_count)
    sides = (
        (0, jnp.where(owner[start_in] == first - 1, 1.0, 0.0)),
        (rows_in - 1, jnp.where(owner[start_in + rows_in - 1] == first + rows, 1.0, 0.0)),
    )
    for side, (row, feeds) in enumerate(sides):
        for k in range(basis_count):
            rims[side, k : k + 1, :] = lines[k * rows_in + row : k * rows_in + row + 1, :] * feeds
    entered()
    inputs.start_rims(place, field)
    swaps[0].start(place, table, high, rows, HALO)
    swaps[1].send(rims.at[1], rims.at[2], 0, place.along_snake(1))
    swaps[1].send(rims.at[0], rims.at[3], 1, place.along_snake(-1))
    inputs.start()

    lane = lax.broadcasted_iota(jnp.int32, (cols, LANES), 1)

    def make_band(row, carry):
        values = table[aligned(row, high), :]
        for k in range(basis_count):
            parts = [
                circulant(values[r * basis_count + k][None, :], cols, 1) for r in range(3)
            ]
            start = pl.multiple_of(row * block + k * cols, cols)
            bands[pl.ds(start, cols), :LANES] = jnp.where(lane < cols, parts[0], parts[1]).astype(BF16)
            bands[pl.ds(start, cols), LANES:] = parts[2].astype(BF16)
        other = bands[aligned(row, block), :].T
        for r in range(3):
            turned[aligned(row + r, cols), (2 - r) * block : (3 - r) * block] = other[
                r * cols : (r + 1) * cols
            ]
        return carry

    lax.fori_loop(HALO, HALO + rows, make_band, 0)
    swaps[0].settle()
    lax.fori_loop(0, HALO, make_band, 0)
    lax.fori_loop(HALO + rows, ext, make_band, 0)
    swaps[1].settle()
    inputs.finish()

    def filtered(row):
        if 0 <= row < rows_in:
            values = [lines[k * rows_in + row : k * rows_in + row + 1, :] for k in range(basis_count)]
        else:
            side = 2 if row < 0 else 3
            values = [rims[side, k : k + 1, :] for k in range(basis_count)]
        lhs = jnp.concatenate([circulant(value, cols, 2) for value in values], axis=0).astype(BF16)
        out = jnp.dot(lhs, inputs.row(row), preferred_element_type=F32)
        return out.astype(BF16).astype(F32)

    filters = [filtered(row) for row in range(-1, rows_in + 1)]
    for row in range(rows):
        total = None
        for step in range(-1, 3):
            source = 2 * row + step
            term = filters[source + 1]
            if 0 <= source < rows_in:
                term = term * jnp.where(owner[start_in + source] == first + row, 1.0, 0.0)
            total = term if total is None else total + term
        total = total.astype(BF16)
        for k in range(basis_count):
            latent_in[row * cols : (row + 1) * cols, k * width : (k + 1) * width] = total[
                k * cols : (k + 1) * cols
            ]
    own = pl.ds(HALO * cols, rows * cols)
    loads[0].wait()
    state[own, :] = jnp.dot(
        latent_in[...], encoder_weight[...], preferred_element_type=F32
    ).astype(BF16)
    swaps[2].start(place, state, cols, rows, HALO)
    arriving.start_rims(place, cotangent)
    arriving.start()
    loads[1].wait()
    swaps[2].settle()
    zero_outside(place, state, 0, (HALO + rows) * cols, HALO * cols)

    for layer in range(layers):
        low, top = layer + 1, ext - layer - 1
        for row in range(low, top):
            out = jnp.dot(
                bands[row * block : (row + 1) * block, : 3 * cols],
                state[(row - 1) * cols : (row + 2) * cols, :],
                preferred_element_type=F32,
            ).astype(BF16)
            for k in range(basis_count):
                features[layer, row * cols : (row + 1) * cols, k * channels : (k + 1) * channels] = out[
                    k * cols : (k + 1) * cols
                ]
        span = pl.ds(low * cols, (top - low) * cols)
        pre = jnp.dot(features[layer, span, :], weights[layer], preferred_element_type=F32)
        preact[layer, span, :] = pre
        new = state[span, :].astype(F32) + pre / (1.0 + jnp.exp(-pre))
        state[span, :] = new.astype(BF16)
        if layer < layers - 1:
            zero_outside(place, state, low * cols, (top - 1) * cols, cols)

    arriving.finish()
    last = layers - 1
    gradient = arriving.lines[1 : rows + 1].reshape(rows * cols, channels).astype(F32)
    act = gradient * silu_slope(preact[last, own, :])
    steps[last, own, :] = act.astype(BF16)
    swaps[3].start(place, steps.at[last], cols, rows, HALO)
    swaps[4].start(place, arriving.lines, 1, rows, 1)
    leaving[0].lines[...] = state[own, :].reshape(rows, cols, channels)

    def errors(layer, low, top):
        for k in range(basis_count):
            out = lax.dot_general(
                steps[layer, low * cols : top * cols, :],
                weights[layer, k * channels : (k + 1) * channels, :],
                (((1,), (1,)), ((), ())),
                preferred_element_type=F32,
            ).astype(BF16)
            for row in range(low, top):
                start = row * block + k * cols
                errs[start : start + cols, :] = out[(row - low) * cols : (row - low + 1) * cols]

    def spread(row):
        return jnp.dot(
            turned[(row + 1) * cols : (row + 2) * cols, :],
            errs[(row - 1) * block : (row + 2) * block, :],
            preferred_element_type=F32,
        )

    def weigh(part):
        stretch = slice(part.first, part.first + part.rows)
        left = features[0, own, stretch]
        sources[0][stretch, :] = rows_product(left, steps[0, own, :]).astype(BF16)

    sources[last][...] = rows_product(features[last, own, :], steps[last, own, :]).astype(BF16)
    early.advance()
    errors(last, HALO, HALO + rows)
    early.advance()
    leaving[0].start(place, state_out)
    swaps[3].settle()
    zero_outside(place, steps.at[last], 0, (HALO + rows) * cols, HALO * cols)
    errors(last, 0, HALO)
    errors(last, HALO + rows, ext)
    swaps[4].settle()
    back = [arriving.lines[row - 1].astype(F32) + spread(row) for row in range(1, ext - 1)]
    gradient = jnp.concatenate(back, axis=0).astype(BF16).astype(F32)
    span = pl.ds(cols, (ext - 2) * cols)
    steps[0, span, :] = (gradient * silu_slope(preact[0, span, :])).astype(BF16)
    zero_outside(place, steps.at[0], cols, (ext - 2) * cols, cols)
    weigh(upper)
    upper.advance()
    weigh(lower)
    lower.advance()
    early.advance()
    upper.advance()
    errors(0, 1, ext - 1)
    lower.advance()
    back = [
        gradient[(row - 1) * cols : row * cols] + spread(row) for row in range(HALO, HALO + rows)
    ]
    final = jnp.concatenate(back, axis=0).astype(BF16)
    leaving[1].lines[...] = final.reshape(rows, cols, channels)
    sources[layers][...] = rows_product(latent_in[...], final).astype(BF16)
    encoder.advance()
    encoder.advance()
    upper.advance()
    early.advance()
    lower.advance()
    encoder.advance()
    upper.advance()
    lower.advance()
    encoder.advance()
    early.advance()
    upper.advance()
    lower.advance()
    leaving[1].start(place, latent_grad)
    for part in sums:
        while part.stages:
            part.advance()
    for part in leaving:
        part.finish()


def make_table(place, base, widths, table, rows, cols, basis_count, high):
    own = pl.ds(HALO * high, rows * high)
    table[own, :] = jnp.zeros((rows * high, LANES), F32)
    size = base.shape[3]
    reach = size // 2
    distance = jnp.abs(lax.broadcasted_iota(jnp.int32, (basis_count, size), 1) - reach)
    for row in range(rows):
        source = place.chunk * rows + row
        values = base[source].astype(F32)
        for r in range(3):
            start = (HALO + row) * high + r * basis_count
            table[start : start + basis_count, :size] = jnp.where(
                distance <= widths[source], values[r], 0.0
            )
    moved = pltpu.roll(table[own, :], LANES - reach, 1)
    table[own, :] = moved + pltpu.roll(moved, cols, 1)


def make_lines(taps, flat, lines, start_in, rows_in, basis_count):
    flat[...] = jnp.zeros_like(flat)
    count, _, held = taps.shape
    for k in range(basis_count):
        for t in range(count):
            row = 8 * k + t
            flat[row : row + 1, :held] = taps[t, k : k + 1, :].astype(F32)
    flat[...] = flat[...].T
    values = flat[aligned(start_in // rows_in, rows_in), :]
    lane = lax.broadcasted_iota(jnp.int32, values.shape, 1)
    for k in range(basis_count):
        moved = pltpu.roll(values, LANES - 8 * k, 1) if k else values
        kept = jnp.where(lane < count, moved, 0.0)
        lines[k * rows_in : (k + 1) * rows_in, :] = pltpu.roll(kept, LANES - count // 2, 1)


def stretches(heights):
    half = heights[0] // 2
    return [
        (len(heights) - 2, 0, heights[-2], ACROSS),
        (0, 0, half, ACROSS),
        (0, half, half, ACROSS),
        (len(heights) - 1, 0, heights[-1], WIDE),
    ]


def run_chunks(
    plan, sizes, field_in, taps, owner, encoder_weight, base, widths, weights, cotangent
):
    rows, cols, basis_count, layers = plan
    lat, lon = sizes
    channels = weights.shape[2]
    features = basis_count * channels
    in_features = encoder_weight.shape[0]
    ext = rows + 2 * HALO
    heights = [features] * layers + [in_features]
    block = basis_count * cols
    high = -(-3 * basis_count // 8) * 8
    tall = -(-basis_count // 8) * 8
    scratch = [
        pltpu.VMEM((ext * high, LANES), F32),
        pltpu.VMEM((LANES, LANES), F32),
        pltpu.VMEM((basis_count * 2 * rows, LANES), F32),
        pltpu.VMEM((4, tall, LANES), F32),
        pltpu.VMEM((ext * block, 2 * LANES), BF16),
        pltpu.VMEM(((ext + 2) * cols, 3 * block), BF16),
        pltpu.VMEM((rows * cols, in_features), BF16),
        pltpu.VMEM((ext * cols, channels), BF16),
        pltpu.VMEM((layers, ext * cols, features), BF16),
        pltpu.VMEM((layers, ext * cols, channels), F32),
        pltpu.VMEM((layers, ext * cols, channels), BF16),
        pltpu.VMEM((ext * block, channels), BF16),
        pltpu.VMEM(encoder_weight.shape, BF16),
        pltpu.VMEM(weights.shape, BF16),
        pltpu.SemaphoreType.DMA((2,)),
    ]
    scratch += Regroup.scratch(lon, 2 * rows, field_in.shape[1] * lon, field_in.shape[2], 1)
    scratch += Regroup.scratch(lon, rows, cols, channels, 0)
    for _ in range(2):
        scratch += Restore.scratch(lon, rows, cols, channels)
    for _ in range(5):
        scratch += Swap.scratch()
    scratch += [pltpu.VMEM((height, channels), BF16) for height in heights]
    for _, _, size, _ in stretches(heights):
        scratch += ChipSum.scratch(sizes, size, channels)
    vmem = pl.BlockSpec(memory_space=pltpu.VMEM)
    smem = pl.BlockSpec(memory_space=pltpu.SMEM)
    hbm = pl.BlockSpec(memory_space=pltpu.HBM)
    out = pltpu.VMEM(cotangent.shape, BF16)
    grads = [pltpu.VMEM((height, channels // 2), BF16) for height in heights]
    return pl.pallas_call(
        functools.partial(chunk_kernel, plan),
        out_shape=[out, out] + grads,
        in_specs=[hbm, vmem, smem, hbm, vmem, smem, hbm, hbm],
        out_specs=[vmem, vmem] + [vmem] * (1 + layers),
        scratch_shapes=scratch,
        compiler_params=pltpu.CompilerParams(
            collective_id=1, has_side_effects=True, vmem_limit_bytes=56 << 20
        ),
    )(field_in, taps, owner, encoder_weight, base, widths, weights, cotangent)


def finish_body(normalizer, field_count, sum_count, refs):
    fields, sums = refs[:field_count], refs[field_count : field_count + sum_count]
    fields_out = refs[field_count + sum_count : 2 * field_count + sum_count]
    block_grads, encoder_grad = refs[2 * field_count + sum_count :][:2]
    rest = refs[2 * field_count + sum_count + 2 :]
    wide, out_sems = rest[:sum_count], rest[sum_count]
    targets = list(fields_out) + [block_grads.at[n] for n in range(sum_count - 1)] + [encoder_grad]
    stores = [
        pltpu.make_async_copy(source, target, out_sems.at[n])
        for n, (source, target) in enumerate(zip(list(fields) + list(wide), targets))
    ]
    for n, store in enumerate(stores):
        if n >= field_count:
            wide[n - field_count][...] = sums[n - field_count][...].astype(F32) * normalizer
        store.start()
    for store in stores:
        store.wait()


def finish_outputs(normalizer, outs):
    hbm = pl.BlockSpec(memory_space=pltpu.HBM)
    fields, sums = outs[:2], outs[2:]
    shapes = [jax.ShapeDtypeStruct(field.shape, field.dtype) for field in fields]
    shapes.append(jax.ShapeDtypeStruct((len(sums) - 1,) + sums[0].shape, F32))
    shapes.append(jax.ShapeDtypeStruct(sums[-1].shape, F32))

    def kernel(*refs):
        finish_body(normalizer, len(fields), len(sums), refs)

    return pl.pallas_call(
        kernel,
        out_shape=shapes,
        in_specs=[pl.BlockSpec(memory_space=pltpu.VMEM)] * len(outs),
        out_specs=[hbm] * len(shapes),
        scratch_shapes=[pltpu.VMEM(value.shape, F32) for value in sums]
        + [pltpu.SemaphoreType.DMA((len(outs),))],
        compiler_params=pltpu.CompilerParams(vmem_limit_bytes=16 << 20),
    )(*outs)


def fits_chunks(rows_dev, cols_in, cols_dev, layers, heights):
    lon = lax.axis_size("lon")
    count = lax.axis_size("lat") * lon
    heights_fit = all(size % (count * TILE) == 0 for _, _, size, _ in stretches(heights))
    return (
        layers == HALO
        and rows_dev % lon == 0
        and heights_fit
        and rows_dev // lon >= HALO
        and lon % 2 == 0
        and cols_in * lon == LANES
        and 2 * cols_dev * lon == LANES
    )


def per_device_chunks(
    input_field,
    encoder_filter,
    row_owner,
    encoder_weight,
    disco_basis,
    row_widths,
    block_weights,
    cotangent,
):
    rows_in, cols_in, _ = input_field.shape
    lat, lon = lax.axis_size("lat"), lax.axis_size("lon")
    rows_dev, cols = rows_in // 2, cols_in // 2 * lon
    plan = (rows_dev // lon, cols, encoder_filter.shape[1], block_weights.shape[0])
    outs = run_chunks(
        plan,
        (lat, lon),
        input_field,
        encoder_filter.transpose(2, 1, 0),
        row_owner,
        encoder_weight,
        disco_basis.transpose(0, 2, 1, 3),
        row_widths,
        block_weights,
        cotangent,
    )
    cells_total = rows_dev * lax.axis_size(("lat", "ch")) * cols
    return tuple(finish_outputs(1.0 / math.sqrt(cells_total), outs))


def solution(mesh):
    placed = (
        P(("ens", "lat", "ch"), "lon", None),
        P(("lat", "ch"), None, None),
        P(("ens", "lat", "ch")),
        P(),
        P(("lat", "ch"), None, None, None),
        P(("lat", "ch")),
        P(),
        P(("ens", "lat", "ch"), "lon", None),
    )
    return jax.shard_map(
        per_device,
        mesh=mesh,
        in_specs=placed,
        out_specs=(
            P(("ens", "lat", "ch"), "lon", None),
            P(("ens", "lat", "ch"), "lon", None),
            P("ens", None, "ch"),
            P("ens", "ch"),
        ),
        check_vma=False,
    )
```

```python
import functools
import math

import jax
import jax.numpy as jnp
from jax import lax
from jax.experimental import pallas as pl
from jax.experimental.pallas import tpu as pltpu
from jax.sharding import PartitionSpec as P

REACH = 8
TAP_REACH = 2
TILE = 16
MESH = pl.DeviceIdType.MESH
BF16 = jnp.bfloat16
F32 = jnp.float32


def along(axis, steps):
    count = lax.axis_size(axis)
    return {axis: lax.rem(lax.axis_index(axis) + steps + count, count)}


def neighbour(row_step, col_step):
    ch_count = lax.axis_size("ch")
    bands = lax.axis_size("lat") * ch_count
    band = lax.axis_index("lat") * ch_count + lax.axis_index("ch")
    band = lax.rem(band + row_step + bands, bands)
    target = {}
    if row_step:
        target = {"lat": band // ch_count, "ch": lax.rem(band, ch_count)}
    if col_step:
        target.update(along("lon", col_step))
    return target


AROUND = [(r, c) for r in (-1, 0, 1) for c in (-1, 0, 1) if r or c]


def greet():
    targets = [neighbour(r, c) for r, c in AROUND]
    for axis in ("ch", "lat", "lon"):
        targets += [along(axis, step) for step in range(1, lax.axis_size(axis))]
    barrier = pltpu.get_barrier_semaphore()
    for target in targets:
        pl.semaphore_signal(barrier, inc=1, device_id=target, device_id_type=MESH)
    pl.semaphore_wait(barrier, len(targets))


class Sender:
    def __init__(self, sems):
        self.ssem, self.rsem = sems
        self.pending = []

    def send(self, source, target, slot, device):
        copy = pltpu.make_async_remote_copy(
            src_ref=source,
            dst_ref=target,
            send_sem=self.ssem.at[slot],
            recv_sem=self.rsem.at[slot],
            device_id=device,
            device_id_type=MESH,
        )
        copy.start()
        self.pending.append(copy)

    def settle(self):
        for copy in self.pending:
            copy.wait()
        self.pending = []


class GradSum(Sender):
    def __init__(self, result, bufs):
        super().__init__(bufs[-2:])
        self.result = result
        self.source, self.rec_ch, self.part, self.rec_lat, self.strip, self.rec_pair, self.half, self.rec_far, self.piece = bufs[:-2]
        self.width = self.part.shape[1]
        self.lat, self.lon = lax.axis_size("lat"), lax.axis_size("lon")
        self.height = self.strip.shape[0]
        self.span = self.piece.shape[0]
        self.pair = self.height // self.span
        self.far = self.lon // self.pair
        self.side = lax.rem(lax.axis_index("lon"), self.pair)

    @staticmethod
    def scratch(sizes, rows, columns):
        lat, lon = sizes
        width = columns // 2
        height = rows // lat
        pair = 2 if lon % 2 == 0 and height % (2 * TILE) == 0 else 1
        span, far = height // pair, lon // pair
        count = 1 + 2 * (lat - 1) + 2 * (pair - 1) + far - 1
        return [
            pltpu.VMEM((rows, columns), BF16),
            pltpu.VMEM((rows, width), BF16),
            pltpu.VMEM((rows, width), BF16),
            pltpu.VMEM((lat - 1, height, width), BF16),
            pltpu.VMEM((height, width), BF16),
            pltpu.VMEM((span, width), BF16),
            pltpu.VMEM((span, width), BF16),
            pltpu.VMEM((far - 1, span, width), BF16),
            pltpu.VMEM((span, width), BF16),
            pltpu.SemaphoreType.DMA((count,)),
            pltpu.SemaphoreType.DMA((count,)),
        ]

    def columns(self, half):
        return pl.ds(pl.multiple_of(half * self.width, self.width), self.width)

    @staticmethod
    def stretch(owner, size):
        return pl.ds(pl.multiple_of(owner * size, size), size)

    def start_ch(self):
        other = 1 - lax.axis_index("ch")
        self.send(self.source.at[:, self.columns(other)], self.rec_ch, 0, {"ch": other})

    def start_lat(self):
        self.settle()
        own = self.source[:, self.columns(lax.axis_index("ch"))].astype(F32)
        self.part[...] = (own + self.rec_ch[...].astype(F32)).astype(BF16)
        for step in range(1, self.lat):
            peer = along("lat", step)
            rows = self.stretch(peer["lat"], self.height)
            self.send(self.part.at[rows], self.rec_lat.at[step - 1], step, peer)

    def start_lon(self):
        self.settle()
        total = self.part[self.stretch(lax.axis_index("lat"), self.height), :].astype(F32)
        for step in range(1, self.lat):
            total = total + self.rec_lat[step - 1].astype(F32)
        self.strip[...] = total.astype(BF16)
        if self.pair > 1:
            rows = self.stretch(1 - self.side, self.span)
            self.send(self.strip.at[rows], self.rec_pair, self.lat, along("lon", 1 - 2 * self.side))

    def start_far(self):
        self.settle()
        total = self.strip[self.stretch(self.side, self.span), :].astype(F32)
        if self.pair > 1:
            total = total + self.rec_pair[...].astype(F32)
        self.half[...] = total.astype(BF16)
        for step in range(1, self.far):
            self.send(
                self.half, self.rec_far.at[step - 1], self.lat + step, along("lon", self.pair * step)
            )

    def gather_lon(self):
        self.settle()
        total = self.half[...].astype(F32)
        for step in range(1, self.far):
            total = total + self.rec_far[step - 1].astype(F32)
        self.piece[...] = total.astype(BF16)
        offset = lax.axis_index("lat") * self.height + self.side * self.span
        rows = pl.ds(pl.multiple_of(offset, TILE), self.span)
        self.result[rows, :] = self.piece[...]
        if self.pair > 1:
            slot = self.lat + self.far
            self.send(self.piece, self.result.at[rows], slot, along("lon", 1 - 2 * self.side))

    def gather_lat(self):
        self.settle()
        rows = self.stretch(lax.axis_index("lat"), self.height)
        for step in range(1, self.lat):
            slot = self.lat + self.far + self.pair - 2 + step
            self.send(self.result.at[rows], self.result.at[rows], slot, along("lat", step))

    def finish(self):
        self.settle()


STAGES = ("start_ch", "start_lat", "start_lon", "start_far", "gather_lon", "gather_lat", "finish")


class Halo(Sender):
    def __init__(self, bufs):
        super().__init__(bufs[-2:])
        self.out_side, self.out_row, self.in_side, self.in_row = bufs[:-2]

    @staticmethod
    def scratch(rows, cols, width, row_blocks):
        return [
            pltpu.VMEM((2, rows * REACH, width), BF16),
            pltpu.VMEM((row_blocks, cols, width), BF16),
            pltpu.VMEM((2, rows * REACH, width), BF16),
            pltpu.VMEM((6, cols, width), BF16),
            pltpu.SemaphoreType.DMA((8,)),
            pltpu.SemaphoreType.DMA((8,)),
        ]

    def start(self, row_block_of):
        self.send(self.out_side.at[0], self.in_side.at[1], 0, neighbour(0, -1))
        self.send(self.out_side.at[1], self.in_side.at[0], 1, neighbour(0, 1))
        slot = 2
        for row_step in (-1, 1):
            for col_step in (-1, 0, 1):
                place = (0 if row_step == 1 else 3) + 1 - col_step
                self.send(
                    self.out_row.at[row_block_of(row_step, col_step)],
                    self.in_row.at[place],
                    slot,
                    neighbour(row_step, col_step),
                )
                slot += 1


def edge_flags():
    ch_count = lax.axis_size("ch")
    bands = lax.axis_size("lat") * ch_count
    band = lax.axis_index("lat") * ch_count + lax.axis_index("ch")
    return band > 0, band < bands - 1


def extend(halo, state, ext, rows, cols):
    span = cols + 2 * REACH
    west, east = halo.in_side[0].astype(F32), halo.in_side[1].astype(F32)
    for row in range(rows):
        low, high = row * REACH, (row + 1) * REACH
        line = jnp.concatenate(
            [west[low:high], state[row * cols : (row + 1) * cols], east[low:high]], axis=0
        )
        ext[(row + 1) * span : (row + 2) * span, :] = line.astype(BF16)
    for first, row, flag in zip((0, 3), (0, rows + 1), edge_flags()):
        line = jnp.concatenate(
            [
                halo.in_row[first].astype(F32)[cols - REACH :],
                halo.in_row[first + 1].astype(F32),
                halo.in_row[first + 2].astype(F32)[:REACH],
            ],
            axis=0,
        )
        ext[row * span : (row + 1) * span, :] = jnp.where(flag, line, 0.0).astype(BF16)


def send_state(halo, state, rows, cols):
    pieces = [
        [state[r * cols : r * cols + REACH] for r in range(rows)],
        [state[(r + 1) * cols - REACH : (r + 1) * cols] for r in range(rows)],
    ]
    for side in range(2):
        halo.out_side[side] = jnp.concatenate(pieces[side], axis=0).astype(BF16)
    halo.out_row[0] = state[:cols].astype(BF16)
    halo.out_row[1] = state[(rows - 1) * cols :].astype(BF16)
    halo.start(lambda row_step, col_step: 0 if row_step == -1 else 1)


def send_spread(halo, spread, rows, cols):
    span = cols + 2 * REACH
    west = [spread[(r + 1) * span : (r + 1) * span + REACH, :] for r in range(rows)]
    east = [spread[(r + 2) * span - REACH : (r + 2) * span, :] for r in range(rows)]
    halo.out_side[0] = jnp.concatenate(west, axis=0).astype(BF16)
    halo.out_side[1] = jnp.concatenate(east, axis=0).astype(BF16)
    for block, row in enumerate((0, rows + 1)):
        base = row * span
        halo.out_row[2 * block] = spread[base + REACH : base + REACH + cols, :].astype(BF16)
        corners = [spread[base : base + REACH, :], spread[base + span - REACH : base + span, :]]
        if cols > 2 * REACH:
            corners.insert(1, jnp.zeros((cols - 2 * REACH, spread.shape[1]), F32))
        halo.out_row[2 * block + 1] = jnp.concatenate(corners, axis=0).astype(BF16)
    halo.start(
        lambda row_step, col_step: (0 if row_step == -1 else 2) + (1 if col_step else 0)
    )


def take_spread(halo, spread, gradient, rows, cols):
    span = cols + 2 * REACH
    west, east = halo.in_side[0].astype(F32), halo.in_side[1].astype(F32)
    outer = {}
    for first, row, flag in zip((0, 3), (0, rows - 1), edge_flags()):
        line = halo.in_row[first + 1].astype(F32)
        rim_west = halo.in_row[first].astype(F32)[cols - REACH :]
        rim_east = halo.in_row[first + 2].astype(F32)[:REACH]
        rims = [rim_west, rim_east]
        if cols > 2 * REACH:
            rims.insert(1, jnp.zeros((cols - 2 * REACH, line.shape[1]), F32))
        outer[row] = jnp.where(flag, line + jnp.concatenate(rims, axis=0), 0.0)
    result = []
    for row in range(rows):
        low, high = row * REACH, (row + 1) * REACH
        rims = [west[low:high], east[low:high]]
        if cols > 2 * REACH:
            rims.insert(1, jnp.zeros((cols - 2 * REACH, west.shape[1]), F32))
        base = (row + 1) * span + REACH
        line = spread[base : base + cols, :] + jnp.concatenate(rims, axis=0)
        if row in outer:
            line = line + outer[row]
        result.append(gradient[row * cols : (row + 1) * cols].astype(F32) + line)
    return result


def aligned(index, size):
    return pl.ds(pl.multiple_of(index * size, size), size)


GROUP = 16


def over_rows(rows, body):
    group = GROUP if rows % GROUP == 0 else 1

    def step(index, carry):
        for inner in range(group):
            body(index * group + inner)
        return carry

    lax.fori_loop(0, rows // group, step, 0)


def make_bands(base, bands, rows, cols, basis_count):
    width = base.shape[1]

    def one(row):
        table = base[aligned(row, 2 * basis_count), :]
        for k in range(basis_count):
            line = jnp.broadcast_to(table[k : k + 1], (cols, width))
            moved = pltpu.roll(line, 0, 1, stride=1, stride_axis=0)
            start = pl.multiple_of((row * basis_count + k) * cols, cols)
            bands[pl.ds(start, cols), :] = moved.astype(BF16)

    over_rows(rows, one)


def stencil(bands, ext, features, rows, cols, basis_count):
    span = cols + 2 * REACH
    channels = ext.shape[1]

    def one(row):
        lhs = bands[aligned(row, basis_count * cols), :][:, : 3 * span]
        rhs = ext[pl.ds(pl.multiple_of(row * span, span), 3 * span), :]
        out = jnp.dot(lhs, rhs, preferred_element_type=F32).astype(BF16)
        for k in range(basis_count):
            features[aligned(row, cols), k * channels : (k + 1) * channels] = out[
                k * cols : (k + 1) * cols
            ]

    over_rows(rows, one)


def adjoint(bands, errs, spread, rows, cols, basis_count):
    span = cols + 2 * REACH
    spread[...] = jnp.zeros_like(spread)

    def one(row):
        lhs = bands[aligned(row, basis_count * cols), :][:, : 3 * span]
        rhs = errs[aligned(row, basis_count * cols), :]
        out = lax.dot_general(lhs, rhs, (((0,), (0,)), ((), ())), preferred_element_type=F32)
        place = pl.ds(pl.multiple_of(row * span, span), 3 * span)
        spread[place, :] = spread[place, :] + out

    over_rows(rows, one)


def rows_product(left, right):
    return lax.dot_general(left, right, (((0,), (0,)), ((), ())), preferred_element_type=F32)
TAPS_LEFT = TAP_REACH


class InputHalo(Sender):
    def __init__(self, bufs):
        super().__init__(bufs[-2:])
        (
            self.edges,
            self.out_cols,
            self.out_table,
            self.in_cols,
            self.in_row,
            self.in_table,
            self.in_tile,
        ) = bufs[:-2]

    @staticmethod
    def scratch(rows_in, cols_in, width, table_rows, lanes):
        return [
            pltpu.VMEM((3, rows_in, width), F32),
            pltpu.VMEM((3, rows_in, width), BF16),
            pltpu.VMEM((2, table_rows, lanes), F32),
            pltpu.VMEM((3, rows_in, width), BF16),
            pltpu.VMEM((2, cols_in, width), BF16),
            pltpu.VMEM((2, table_rows, lanes), F32),
            pltpu.VMEM((4, TILE, width), BF16),
            pltpu.SemaphoreType.DMA((10,)),
            pltpu.SemaphoreType.DMA((10,)),
        ]

    def start(self, field, table, owner, rows_in, cols_in):
        first = own_first_row(rows_in // 2)
        table_rows = self.out_table.shape[1]
        for block, row, target in ((0, 0, first - 1), (1, rows_in - 1, first + rows_in // 2)):
            feeds = jnp.where(owner[row] == target, 1.0, 0.0)
            self.out_table[block] = table[row * table_rows : (row + 1) * table_rows, :] * feeds
        last = (rows_in - 1) * cols_in
        lines = (field.at[pl.ds(0, cols_in)], field.at[pl.ds(last, cols_in)])
        slot = 0
        for block, row_step in ((0, -1), (1, 1)):
            self.send(lines[block], self.in_row.at[1 - block], slot, neighbour(row_step, 0))
            base = block * last
            west = field.at[pl.ds(base, TILE)]
            east = field.at[pl.ds(base + cols_in - TILE, TILE)]
            place = 2 * (1 - block)
            self.send(west, self.in_tile.at[place + 1], slot + 1, neighbour(row_step, -1))
            self.send(east, self.in_tile.at[place], slot + 2, neighbour(row_step, 1))
            slot += 3

        def one(row):
            low = field[pl.ds(pl.multiple_of(row * cols_in, TILE), TILE), :].astype(F32)
            start = pl.multiple_of(row * cols_in + cols_in - TILE, TILE)
            high = field[pl.ds(start, TILE), :].astype(F32)
            self.edges[0, pl.ds(row, 1), :] = high[TILE - 2 : TILE - 1]
            self.edges[1, pl.ds(row, 1), :] = high[TILE - 1 : TILE]
            self.edges[2, pl.ds(row, 1), :] = low[0:1]

        over_rows(rows_in, one)
        self.out_cols[...] = self.edges[...].astype(BF16)
        self.send(self.out_cols.at[pl.ds(0, 2)], self.in_cols.at[pl.ds(0, 2)], 6, neighbour(0, 1))
        self.send(self.out_cols.at[2], self.in_cols.at[2], 7, neighbour(0, -1))
        self.send(self.out_table.at[0], self.in_table.at[1], 8, neighbour(-1, 0))
        self.send(self.out_table.at[1], self.in_table.at[0], 9, neighbour(1, 0))


def own_first_row(rows):
    return (lax.axis_index("lat") * lax.axis_size("ch") + lax.axis_index("ch")) * rows


def tap_matrix(table, basis_count, cols, cols_in):
    lanes = table.shape[1]
    blocks = []
    for k in range(basis_count):
        line = jnp.broadcast_to(table[k : k + 1], (cols, lanes))
        moved = pltpu.roll(line, 0, 1, stride=2, stride_axis=0)
        wrapped = pltpu.roll(moved, cols_in + TILE - TAPS_LEFT, 1)
        moved = pltpu.roll(moved, lanes - TAPS_LEFT, 1)
        lane = lax.broadcasted_iota(jnp.int32, (cols, lanes), 1)
        at_end = (lane >= cols_in + TILE - TAPS_LEFT) & (lane < cols_in + TILE)
        blocks.append(jnp.where(at_end, wrapped, moved))
    return jnp.concatenate(blocks, axis=0)[:, : cols_in + TILE].astype(BF16)


def filtered_row(table, line, left_two, left_one, right, basis_count, cols, cols_in):
    width = line.shape[1]
    place = lax.broadcasted_iota(jnp.int32, (TILE, width), 0)
    tile = jnp.where(place == 0, jnp.broadcast_to(right, (TILE, width)), 0.0)
    tile = jnp.where(place == TILE - 2, jnp.broadcast_to(left_two, (TILE, width)), tile)
    tile = jnp.where(place == TILE - 1, jnp.broadcast_to(left_one, (TILE, width)), tile)
    rhs = jnp.concatenate([line, tile.astype(BF16)], axis=0)
    lhs = tap_matrix(table, basis_count, cols, cols_in)
    return jnp.dot(lhs, rhs, preferred_element_type=F32).astype(BF16)


def finish_encode(halo, field, table, owner, filtered, latent_in, plan, rows_in, cols_in):
    rows, cols, basis_count, _ = plan
    table_rows = halo.out_table.shape[1]
    block = basis_count * cols
    width = field.shape[1]
    halo.settle()
    halo.edges[...] = halo.in_cols[...].astype(F32)

    def one(row):
        sides = [halo.edges[index, pl.ds(row, 1), :] for index in range(3)]
        line = field[aligned(row, cols_in), :]
        taps = table[aligned(row, table_rows), :]
        filtered[aligned(row + 1, block), :] = filtered_row(
            taps, line, *sides, basis_count, cols, cols_in
        )

    over_rows(rows_in, one)
    for side, row in ((0, 0), (1, rows_in + 1)):
        west = halo.in_tile[2 * side].astype(F32)
        east = halo.in_tile[2 * side + 1].astype(F32)
        filtered[row * block : (row + 1) * block, :] = filtered_row(
            halo.in_table[side],
            halo.in_row[side],
            west[TILE - 2 : TILE - 1],
            west[TILE - 1 : TILE],
            east[0:1],
            basis_count,
            cols,
            cols_in,
        )
    first = own_first_row(rows)
    for row in range(rows):
        total = None
        for offset in range(-1, 3):
            source = 2 * row + offset
            term = filtered[(source + 1) * block : (source + 2) * block, :].astype(F32)
            if 0 <= source < rows_in:
                term = term * jnp.where(owner[source] == first + row, 1.0, 0.0)
            total = term if total is None else total + term
        total = total.astype(BF16)
        for k in range(basis_count):
            latent_in[row * cols : (row + 1) * cols, k * width : (k + 1) * width] = total[
                k * cols : (k + 1) * cols
            ]


def lanes_of(count):
    return -(-(count + 2 * TILE) // 128) * 128


def net_kernel(plan, *refs):
    rows, cols, basis_count, layers = plan
    field, table, owner, encoder_weight, base, weights, cotangent = refs[:7]
    state_out, latent_grad = refs[7:9]
    results = refs[9 : 10 + layers]
    rest = list(refs[10 + layers :])
    bands, ext, spread, errs, features, preact, filtered, latent_in = rest[:8]
    input_halo = InputHalo(rest[8:17])
    rest = rest[17:]
    halos = []
    for _ in range(2 * layers):
        halos.append(Halo(rest[:6]))
        rest = rest[6:]
    sums = []
    for index in range(layers + 1):
        sums.append(GradSum(results[index], rest[:11]))
        rest = rest[11:]
    channels = ext.shape[1]
    progress = [0] * (layers + 1)

    def advance(index):
        getattr(sums[index], STAGES[progress[index]])()
        progress[index] += 1

    greet()
    rows_in = owner.shape[0]
    cols_in = field.shape[0] // rows_in
    input_halo.start(field, table, owner, rows_in, cols_in)
    make_bands(base, bands, rows, cols, basis_count)
    finish_encode(input_halo, field, table, owner, filtered, latent_in, plan, rows_in, cols_in)
    state = jnp.dot(latent_in[...], encoder_weight[...], preferred_element_type=F32)
    state = state.astype(BF16).astype(F32)
    for layer in range(layers):
        send_state(halos[layer], state, rows, cols)
        halos[layer].settle()
        extend(halos[layer], state, ext, rows, cols)
        stencil(bands, ext, features.at[layer], rows, cols, basis_count)
        pre = jnp.dot(features[layer], weights[layer], preferred_element_type=F32)
        preact[layer] = pre
        state = (state + pre / (1.0 + jnp.exp(-pre))).astype(BF16).astype(F32)
    state_out[...] = state.astype(BF16)

    gradient = cotangent[...].astype(F32)
    for layer in reversed(range(layers)):
        pre = preact[layer]
        sigma = 1.0 / (1.0 + jnp.exp(-pre))
        act_grad = (gradient * sigma * (1.0 + pre * (1.0 - sigma))).astype(BF16)
        for k in range(basis_count):
            block = weights[layer, k * channels : (k + 1) * channels, :]
            out = lax.dot_general(
                act_grad, block, (((1,), (1,)), ((), ())), preferred_element_type=F32
            ).astype(BF16)
            for row in range(rows):
                start = (row * basis_count + k) * cols
                errs[start : start + cols, :] = out[row * cols : (row + 1) * cols]
        adjoint(bands, errs, spread, rows, cols, basis_count)
        halo = halos[layers + layer]
        send_spread(halo, spread, rows, cols)
        sums[layer].source[...] = rows_product(features[layer], act_grad).astype(BF16)
        for other in range(layers - 1, layer - 1, -1):
            advance(other)
        halo.settle()
        for other in range(layers - 1, layer - 1, -1):
            advance(other)
        lines = take_spread(halo, spread, gradient, rows, cols)
        gradient = jnp.concatenate(lines, axis=0).astype(BF16).astype(F32)
    latent_grad[...] = gradient.astype(BF16)
    sums[layers].source[...] = rows_product(latent_in[...], gradient.astype(BF16)).astype(BF16)
    advance(layers)
    while min(progress) < len(STAGES):
        for index in [layers] + list(range(layers))[::-1]:
            if progress[index] < len(STAGES):
                advance(index)


def run_net(plan, sizes, field_in, table, owner, encoder_weight, base, weights, cotangent):
    rows, cols, basis_count, layers = plan
    cells, channels = rows * cols, weights.shape[2]
    features = basis_count * channels
    span = cols + 2 * REACH
    rows_in = owner.shape[0]
    in_features = encoder_weight.shape[0]
    heights = [features] * layers + [in_features]
    scratch = [
        pltpu.VMEM((rows * basis_count * cols, base.shape[1]), BF16),
        pltpu.VMEM(((rows + 2) * span, channels), BF16),
        pltpu.VMEM(((rows + 2) * span, channels), F32),
        pltpu.VMEM((rows * basis_count * cols, channels), BF16),
        pltpu.VMEM((layers, cells, features), BF16),
        pltpu.VMEM((layers, cells, channels), F32),
        pltpu.VMEM(((rows_in + 2) * basis_count * cols, field_in.shape[1]), BF16),
        pltpu.VMEM((cells, in_features), BF16),
    ]
    scratch += InputHalo.scratch(
        rows_in, field_in.shape[0] // rows_in, field_in.shape[1], table.shape[0] // rows_in, table.shape[1]
    )
    for index in range(2 * layers):
        scratch += Halo.scratch(rows, cols, channels, 2 if index < layers else 4)
    for height in heights:
        scratch += GradSum.scratch(sizes, height, channels)
    vmem = pl.BlockSpec(memory_space=pltpu.VMEM)
    field = jax.ShapeDtypeStruct((cells, channels), BF16)
    grads = [jax.ShapeDtypeStruct((height, channels // 2), BF16) for height in heights]
    return pl.pallas_call(
        functools.partial(net_kernel, plan),
        out_shape=[field, field] + grads,
        in_specs=[vmem, vmem, pl.BlockSpec(memory_space=pltpu.SMEM)] + [vmem] * 4,
        out_specs=[vmem] * (3 + layers),
        scratch_shapes=scratch,
        compiler_params=pltpu.CompilerParams(
            collective_id=0, has_side_effects=True, vmem_limit_bytes=56 << 20
        ),
    )(field_in, table, owner, encoder_weight, base, weights, cotangent)


def per_device(
    input_field,
    encoder_filter,
    row_owner,
    encoder_weight,
    disco_basis,
    row_widths,
    block_weights,
    cotangent,
):
    if fits_chunks(
        cotangent.shape[0],
        input_field.shape[1],
        cotangent.shape[1],
        block_weights.shape[0],
        [block_weights.shape[1]] * block_weights.shape[0] + [encoder_weight.shape[0]],
    ):
        return per_device_chunks(
            input_field,
            encoder_filter,
            row_owner,
            encoder_weight,
            disco_basis,
            row_widths,
            block_weights,
            cotangent,
        )
    rows_in, cols_in, in_width = input_field.shape
    rows_dev = rows_in // 2
    cols_dev = cols_in // 2
    basis_count = encoder_filter.shape[1]
    tap_count = encoder_filter.shape[2]
    channels = block_weights.shape[2]
    layers = block_weights.shape[0]
    cell_count = rows_dev * cols_dev
    offsets = jnp.abs(jnp.arange(2 * REACH + 1, dtype=jnp.int32) - REACH)
    keep = offsets[None, :] <= row_widths[:, None]
    masked = jnp.where(keep[:, None, None, :], disco_basis, jnp.zeros_like(disco_basis))
    span = cols_dev + 2 * REACH
    table = jnp.pad(masked, ((0, 0), (0, basis_count), (0, 0), (0, span - masked.shape[3])))
    table = table.reshape(rows_dev * 2 * basis_count, 3 * span).astype(jnp.float32)
    lanes = lanes_of(2 * span)
    table = jnp.pad(table, ((0, 0), (0, lanes - 3 * span)))
    taps = jnp.pad(
        encoder_filter.astype(jnp.float32),
        ((0, 0), (0, basis_count), (0, lanes_of(cols_in) - tap_count)),
    ).reshape(rows_in * 2 * basis_count, -1)
    own_width = channels // lax.axis_size("ch")
    sizes = (lax.axis_size("lat"), lax.axis_size("lon"))
    plan = (rows_dev, cols_dev, basis_count, layers)
    outs = run_net(
        plan,
        sizes,
        input_field.reshape(rows_in * cols_in, in_width),
        taps,
        row_owner,
        encoder_weight,
        table,
        block_weights,
        cotangent.reshape(cell_count, channels),
    )
    current, gradient = (field.reshape(rows_dev, cols_dev, channels) for field in outs[:2])
    sums = [value.astype(jnp.float32) for value in outs[2:]]
    block_sum, encoder_sum = jnp.stack(sums[:-1]), sums[-1]
    cells_total = cell_count * lax.axis_size("lon") * lax.axis_size(("lat", "ch"))
    normalizer = 1.0 / math.sqrt(cells_total)
    block_grads = (block_sum * normalizer).reshape(layers, basis_count * channels, own_width)
    encoder_grad = encoder_sum * normalizer
    return (current, gradient, block_grads, encoder_grad)

HALO = 2
DIRECT, ACROSS, WIDE, PAIRED = range(4)
LANES = 128


class Place:
    def __init__(self):
        self.lon, self.ch = lax.axis_size("lon"), lax.axis_size("ch")
        self.bands = lax.axis_size("lat") * self.ch
        self.z = lax.axis_index("lon")
        self.band = lax.axis_index("lat") * self.ch + lax.axis_index("ch")
        self.chunk = self.flip(self.band, self.z)
        self.count = self.bands * self.lon
        self.position = self.band * self.lon + self.chunk

    def flip(self, band, index):
        return index + lax.rem(band, 2) * (self.lon - 1 - 2 * index)

    def offset(self, chunk):
        return (chunk + self.lon - 1) // self.lon + (chunk + 1) // self.lon

    def device(self, band, chunk):
        return {
            "lat": band // self.ch,
            "ch": lax.rem(band, self.ch),
            "lon": self.flip(band, chunk),
        }

    def along_snake(self, step):
        position = lax.rem(self.position + step + self.count, self.count)
        return self.device(position // self.lon, lax.rem(position, self.lon))


def greet_part():
    barrier = pltpu.get_barrier_semaphore()
    count = 0
    for lat in range(lax.axis_size("lat")):
        for ch in range(lax.axis_size("ch")):
            for lon in range(lax.axis_size("lon")):
                if lat or ch or lon:
                    target = {**along("lat", lat), **along("ch", ch), **along("lon", lon)}
                    pl.semaphore_signal(barrier, inc=1, device_id=target, device_id_type=MESH)
                    count += 1
    return lambda: pl.semaphore_wait(barrier, count)


class Regroup(Sender):
    def __init__(self, bufs, rim):
        self.rim = rim
        self.lines, self.rim_ssem, self.rim_rsem, self.own_sem = bufs[0], bufs[3], bufs[4], bufs[5]
        super().__init__(bufs[1:3])

    @staticmethod
    def scratch(lon, rows, cols, width, rim):
        return [
            pltpu.VMEM((rows + 2 + 2 * rim, cols, width), BF16),
            pltpu.SemaphoreType.DMA((lon - 1,)),
            pltpu.SemaphoreType.DMA((lon - 1,)),
            pltpu.SemaphoreType.DMA((2,)),
            pltpu.SemaphoreType.DMA((2 * lon,)),
            pltpu.SemaphoreType.DMA,
        ]

    def start_rims(self, place, source):
        self.place, self.source = place, source
        rows, piece = source.shape[0], source.shape[1]
        self.piece, self.each = piece, rows // place.lon
        self.size = self.each + 2 * self.rim
        self.columns = pl.ds(pl.multiple_of(place.z * piece, piece), piece)
        self.rims = []
        for side, (row, slot, step, chunk) in enumerate(
            ((rows - 1, 0, 1, 0), (0, self.size + 1, -1, place.lon - 1))[: 2 * self.rim]
        ):
            band = lax.rem(place.band + step + place.bands, place.bands)
            copy = pltpu.make_async_remote_copy(
                src_ref=source.at[row],
                dst_ref=self.lines.at[slot, self.columns],
                send_sem=self.rim_ssem.at[side],
                recv_sem=self.rim_rsem.at[side * place.lon + place.z],
                device_id=place.device(band, chunk),
                device_id_type=MESH,
            )
            copy.start()
            self.rims.append(copy)

    def start(self):
        place, source, each, size = self.place, self.source, self.each, self.size
        block = self.lines.at[pl.ds(1, size), self.columns]
        for step in range(1, place.lon):
            peer = along("lon", step)
            chunk = place.flip(place.band, peer["lon"])
            first = chunk * each - self.rim * place.offset(chunk)
            self.send(source.at[pl.ds(first, size)], block, step - 1, peer)
        first = place.chunk * each - self.rim * place.offset(place.chunk)
        self.own = pltpu.make_async_copy(source.at[pl.ds(first, size)], block, self.own_sem)
        self.own.start()

    def finish(self):
        place = self.place
        self.settle()
        self.own.wait()
        ends = ((0, 0), (self.size + 1, place.lon - 1))[: 2 * self.rim]
        for side, (slot, chunk) in enumerate(ends):

            @pl.when(place.chunk == chunk)
            def _():
                for z in range(place.lon):
                    pltpu.make_async_remote_copy(
                        src_ref=self.source.at[0],
                        dst_ref=self.lines.at[slot, pl.ds(z * self.piece, self.piece)],
                        send_sem=self.rim_ssem.at[side],
                        recv_sem=self.rim_rsem.at[side * place.lon + z],
                        device_id=along("lon", 0),
                        device_id_type=MESH,
                    ).wait_recv()

        for copy in self.rims:
            copy.wait_send()

    def row(self, index):
        return self.lines[index + 1 + self.rim * self.place.offset(self.place.chunk)]


class Restore(Sender):
    def __init__(self, bufs):
        self.lines, self.own_sem = bufs[0], bufs[3]
        super().__init__(bufs[1:3])

    @staticmethod
    def scratch(lon, rows, cols, width):
        return [
            pltpu.VMEM((rows, cols, width), BF16),
            pltpu.SemaphoreType.DMA((lon - 1,)),
            pltpu.SemaphoreType.DMA((lon - 1,)),
            pltpu.SemaphoreType.DMA,
        ]

    def start(self, place, result):
        rows, piece = self.lines.shape[0], result.shape[1]
        target = result.at[pl.ds(place.chunk * rows, rows)]
        for step in range(1, place.lon):
            peer = along("lon", step)
            columns = pl.ds(pl.multiple_of(peer["lon"] * piece, piece), piece)
            self.send(self.lines.at[:, columns], target, step - 1, peer)
        columns = pl.ds(pl.multiple_of(place.z * piece, piece), piece)
        self.own = pltpu.make_async_copy(self.lines.at[:, columns], target, self.own_sem)
        self.own.start()

    def finish(self):
        self.settle()
        self.own.wait()


class Swap(Sender):
    def __init__(self, bufs):
        super().__init__(bufs)

    @staticmethod
    def scratch():
        return [pltpu.SemaphoreType.DMA((2,)), pltpu.SemaphoreType.DMA((2,))]

    def start(self, place, buffer, slot_rows, own, halo):
        def part(first):
            return buffer.at[pl.ds(first * slot_rows, halo * slot_rows)]

        self.send(part(own), part(0), 0, place.along_snake(1))
        self.send(part(halo), part(halo + own), 1, place.along_snake(-1))


class ChipSum(Sender):
    def __init__(self, result, source, first, direct, bufs):
        super().__init__(bufs[-2:])
        self.result, self.source, self.first = result, source, first
        self.rec_ch, self.part, self.rec_lat, self.strip, self.rec, self.piece = bufs[:6]
        self.rec_pair, self.half, self.rec_far, self.whole = bufs[6:10]
        self.rows, self.width = self.part.shape
        self.lat, self.lon = lax.axis_size("lat"), lax.axis_size("lon")
        self.height, self.span = self.strip.shape[0], self.piece.shape[0]
        self.side = lax.rem(lax.axis_index("lon"), 2)
        self.direct = direct
        self.stages = [self.start_ch]
        if direct == DIRECT:
            self.stages += [self.scatter_all, self.gather_all]
        elif direct == ACROSS:
            self.stages += [self.scatter_lat, self.scatter_lon, self.gather_lon, self.gather_lat]
        elif direct == WIDE:
            self.stages += [self.scatter_lat, self.scatter_lon, self.gather_all]
        else:
            self.stages += [self.scatter_lat, self.scatter_pair, self.trade_far]
            self.stages += [self.gather_pair, self.gather_lat]
        self.stages.append(self.settle)

    @staticmethod
    def scratch(sizes, rows, columns):
        lat, lon = sizes
        width, height, span = columns // 2, rows // lat, rows // (lat * lon)
        count = 1 + 2 * (lat - 1) + 2 * (lat * lon - 1)
        return [
            pltpu.VMEM((rows, width), BF16),
            pltpu.VMEM((rows, width), BF16),
            pltpu.VMEM((lat - 1, height, width), BF16),
            pltpu.VMEM((height, width), BF16),
            pltpu.VMEM((lat * lon - 1, span, width), BF16),
            pltpu.VMEM((span, width), BF16),
            pltpu.VMEM((height // 2, width), BF16),
            pltpu.VMEM((height // 2, width), BF16),
            pltpu.VMEM((max(lon // 2 - 1, 1), height // 2, width), BF16),
            pltpu.VMEM((height // 2, width), BF16),
            pltpu.SemaphoreType.DMA((count,)),
            pltpu.SemaphoreType.DMA((count,)),
        ]

    def advance(self):
        self.stages.pop(0)()

    def columns(self, half):
        return pl.ds(pl.multiple_of(half * self.width, self.width), self.width)

    def own_columns(self):
        return self.source[self.first : self.first + self.rows, self.columns(lax.axis_index("ch"))]

    def others(self):
        for lat in range(self.lat):
            for lon in range(self.lon):
                if lat or lon:
                    yield lat * self.lon + lon - 1, {**along("lat", lat), **along("lon", lon)}

    def mine(self):
        return lax.axis_index("lat") * self.lon + lax.axis_index("lon")

    def place(self, index, size):
        return pl.ds(pl.multiple_of(index * size, size), size)

    def target(self, index, size):
        return pl.ds(pl.multiple_of(self.first + index * size, size), size)

    def start_ch(self):
        other = 1 - lax.axis_index("ch")
        rows = pl.ds(self.first, self.rows)
        self.send(self.source.at[rows, self.columns(other)], self.rec_ch, 0, {"ch": other})

    def add_ch(self):
        self.settle()
        total = self.own_columns().astype(F32) + self.rec_ch[...].astype(F32)
        self.part[...] = total.astype(BF16)

    def scatter_all(self):
        self.add_ch()
        for slot, peer in self.others():
            rows = self.place(peer["lat"] * self.lon + peer["lon"], self.span)
            self.send(self.part.at[rows], self.rec.at[slot], 1 + slot, peer)

    def scatter_lat(self):
        self.add_ch()
        self.slot = self.lat * self.lon
        for step in range(1, self.lat):
            peer = along("lat", step)
            rows = self.place(peer["lat"], self.height)
            self.send(self.part.at[rows], self.rec_lat.at[step - 1], self.slot, peer)
            self.slot += 1

    def add_lat(self):
        self.settle()
        total = self.part[self.place(lax.axis_index("lat"), self.height), :].astype(F32)
        for step in range(1, self.lat):
            total = total + self.rec_lat[step - 1].astype(F32)
        self.strip[...] = total.astype(BF16)

    def scatter_pair(self):
        self.add_lat()
        rows = self.place(1 - self.side, self.height // 2)
        self.send(self.strip.at[rows], self.rec_pair, 1, along("lon", 1 - 2 * self.side))

    def trade_far(self):
        self.settle()
        total = self.strip[self.place(self.side, self.height // 2), :].astype(F32)
        self.half[...] = (total + self.rec_pair[...].astype(F32)).astype(BF16)
        for step in range(1, self.lon // 2):
            self.send(self.half, self.rec_far.at[step - 1], 1 + step, along("lon", 2 * step))

    def gather_pair(self):
        self.settle()
        total = self.half[...].astype(F32)
        for step in range(1, self.lon // 2):
            total = total + self.rec_far[step - 1].astype(F32)
        self.whole[...] = total.astype(BF16)
        rows = self.target(2 * lax.axis_index("lat") + self.side, self.height // 2)
        self.result[rows, :] = self.whole[...]
        base = self.lat * self.lon + self.lat - 1
        self.send(self.whole, self.result.at[rows], base, along("lon", 1 - 2 * self.side))

    def scatter_lon(self):
        self.add_lat()
        for step in range(1, self.lon):
            peer = along("lon", step)
            rows = self.place(peer["lon"], self.span)
            self.send(self.strip.at[rows], self.rec.at[step - 1], step, peer)

    def add_rest(self):
        self.settle()
        if self.direct == DIRECT:
            total, count = self.part[self.place(self.mine(), self.span), :], self.lat * self.lon
        else:
            total, count = self.strip[self.place(lax.axis_index("lon"), self.span), :], self.lon
        total = total.astype(F32)
        for step in range(1, count):
            total = total + self.rec[step - 1].astype(F32)
        self.piece[...] = total.astype(BF16)
        rows = self.target(self.mine(), self.span)
        self.result[rows, :] = self.piece[...]
        return self.result.at[rows], self.lat * self.lon + self.lat - 1

    def gather_all(self):
        target, base = self.add_rest()
        for slot, peer in self.others():
            self.send(self.piece, target, base + slot, peer)

    def gather_lon(self):
        target, base = self.add_rest()
        for step in range(1, self.lon):
            self.send(self.piece, target, base + step - 1, along("lon", step))

    def gather_lat(self):
        self.settle()
        rows = self.target(lax.axis_index("lat"), self.height)
        base = 2 * self.lat * self.lon + self.lat - 2
        for step in range(1, self.lat):
            self.send(self.result.at[rows], self.result.at[rows], base + step - 1, along("lat", step))


def zero_outside(place, buffer, first, last, size):
    @pl.when(place.position == 0)
    def _():
        buffer[first : first + size, :] = jnp.zeros((size, buffer.shape[1]), buffer.dtype)

    @pl.when(place.position == place.count - 1)
    def _():
        buffer[last : last + size, :] = jnp.zeros((size, buffer.shape[1]), buffer.dtype)


def circulant(line, rows, stride):
    return pltpu.roll(jnp.broadcast_to(line, (rows, LANES)), 0, 1, stride=stride, stride_axis=0)


def silu_slope(pre):
    sigma = 1.0 / (1.0 + jnp.exp(-pre))
    return sigma * (1.0 + pre * (1.0 - sigma))


def chunk_kernel(plan, *refs):
    rows, cols, basis_count, layers = plan
    field, taps, owner, encoder_source, base, widths, weights_source, cotangent = refs[:8]
    state_out, latent_grad = refs[8:10]
    results = refs[10 : 11 + layers]
    rest = list(refs[11 + layers :])
    table, flat, lines, rims, bands, turned, latent_in, state, features, preact, steps, errs = rest[:12]
    encoder_weight, weights, load_sems = rest[12:15]
    rest = rest[15:]
    inputs, arriving = Regroup(rest[:6], 1), Regroup(rest[6:12], 0)
    leaving = [Restore(rest[12:16]), Restore(rest[16:20])]
    swaps = [Swap(rest[20 + 2 * n : 22 + 2 * n]) for n in range(5)]
    rest = rest[30:]
    sources, rest = rest[: layers + 1], rest[layers + 1 :]
    sums = []
    for index, first, size, direct in stretches([source.shape[0] for source in sources]):
        sums.append(ChipSum(results[index], sources[index], first, direct, rest[:12]))
        rest = rest[12:]
    channels = state.shape[1]
    width = field.shape[2]
    block = basis_count * cols
    ext = rows + 2 * HALO
    early, upper, lower, encoder = sums

    loads = [
        pltpu.make_async_copy(source, target, load_sems.at[index])
        for index, (source, target) in enumerate(
            ((encoder_source, encoder_weight), (weights_source, weights))
        )
    ]
    entered = greet_part()
    for load in loads:
        load.start()
    place = Place()
    first = place.position * rows
    rows_in = 2 * rows
    start_in = place.chunk * rows_in
    high, tall = table.shape[0] // ext, rims.shape[1]
    make_table(place, base, widths, table, rows, cols, basis_count, high)
    make_lines(taps, flat, lines, start_in, rows_in, basis_count)
    sides = (
        (0, jnp.where(owner[start_in] == first - 1, 1.0, 0.0)),
        (rows_in - 1, jnp.where(owner[start_in + rows_in - 1] == first + rows, 1.0, 0.0)),
    )
    for side, (row, feeds) in enumerate(sides):
        for k in range(basis_count):
            rims[side, k : k + 1, :] = lines[k * rows_in + row : k * rows_in + row + 1, :] * feeds
    entered()
    inputs.start_rims(place, field)
    swaps[0].start(place, table, high, rows, HALO)
    swaps[1].send(rims.at[1], rims.at[2], 0, place.along_snake(1))
    swaps[1].send(rims.at[0], rims.at[3], 1, place.along_snake(-1))
    inputs.start()

    lane = lax.broadcasted_iota(jnp.int32, (cols, LANES), 1)

    def make_band(row, carry):
        values = table[aligned(row, high), :]
        for k in range(basis_count):
            parts = [
                circulant(values[r * basis_count + k][None, :], cols, 1) for r in range(3)
            ]
            start = pl.multiple_of(row * block + k * cols, cols)
            bands[pl.ds(start, cols), :LANES] = jnp.where(lane < cols, parts[0], parts[1]).astype(BF16)
            bands[pl.ds(start, cols), LANES:] = parts[2].astype(BF16)
        other = bands[aligned(row, block), :].T
        for r in range(3):
            turned[aligned(row + r, cols), (2 - r) * block : (3 - r) * block] = other[
                r * cols : (r + 1) * cols
            ]
        return carry

    lax.fori_loop(HALO, HALO + rows, make_band, 0)
    swaps[0].settle()
    lax.fori_loop(0, HALO, make_band, 0)
    lax.fori_loop(HALO + rows, ext, make_band, 0)
    swaps[1].settle()
    inputs.finish()

    def filtered(row):
        if 0 <= row < rows_in:
            values = [lines[k * rows_in + row : k * rows_in + row + 1, :] for k in range(basis_count)]
        else:
            side = 2 if row < 0 else 3
            values = [rims[side, k : k + 1, :] for k in range(basis_count)]
        lhs = jnp.concatenate([circulant(value, cols, 2) for value in values], axis=0).astype(BF16)
        out = jnp.dot(lhs, inputs.row(row), preferred_element_type=F32)
        return out.astype(BF16).astype(F32)

    filters = [filtered(row) for row in range(-1, rows_in + 1)]
    for row in range(rows):
        total = None
        for step in range(-1, 3):
            source = 2 * row + step
            term = filters[source + 1]
            if 0 <= source < rows_in:
                term = term * jnp.where(owner[start_in + source] == first + row, 1.0, 0.0)
            total = term if total is None else total + term
        total = total.astype(BF16)
        for k in range(basis_count):
            latent_in[row * cols : (row + 1) * cols, k * width : (k + 1) * width] = total[
                k * cols : (k + 1) * cols
            ]
    own = pl.ds(HALO * cols, rows * cols)
    loads[0].wait()
    state[own, :] = jnp.dot(
        latent_in[...], encoder_weight[...], preferred_element_type=F32
    ).astype(BF16)
    swaps[2].start(place, state, cols, rows, HALO)
    arriving.start_rims(place, cotangent)
    arriving.start()
    loads[1].wait()
    swaps[2].settle()
    zero_outside(place, state, 0, (HALO + rows) * cols, HALO * cols)

    for layer in range(layers):
        low, top = layer + 1, ext - layer - 1
        for row in range(low, top):
            out = jnp.dot(
                bands[row * block : (row + 1) * block, : 3 * cols],
                state[(row - 1) * cols : (row + 2) * cols, :],
                preferred_element_type=F32,
            ).astype(BF16)
            for k in range(basis_count):
                features[layer, row * cols : (row + 1) * cols, k * channels : (k + 1) * channels] = out[
                    k * cols : (k + 1) * cols
                ]
        span = pl.ds(low * cols, (top - low) * cols)
        pre = jnp.dot(features[layer, span, :], weights[layer], preferred_element_type=F32)
        preact[layer, span, :] = pre
        new = state[span, :].astype(F32) + pre / (1.0 + jnp.exp(-pre))
        state[span, :] = new.astype(BF16)
        if layer < layers - 1:
            zero_outside(place, state, low * cols, (top - 1) * cols, cols)

    arriving.finish()
    last = layers - 1
    gradient = arriving.lines[1 : rows + 1].reshape(rows * cols, channels).astype(F32)
    act = gradient * silu_slope(preact[last, own, :])
    steps[last, own, :] = act.astype(BF16)
    swaps[3].start(place, steps.at[last], cols, rows, HALO)
    swaps[4].start(place, arriving.lines, 1, rows, 1)
    leaving[0].lines[...] = state[own, :].reshape(rows, cols, channels)

    def errors(layer, low, top):
        for k in range(basis_count):
            out = lax.dot_general(
                steps[layer, low * cols : top * cols, :],
                weights[layer, k * channels : (k + 1) * channels, :],
                (((1,), (1,)), ((), ())),
                preferred_element_type=F32,
            ).astype(BF16)
            for row in range(low, top):
                start = row * block + k * cols
                errs[start : start + cols, :] = out[(row - low) * cols : (row - low + 1) * cols]

    def spread(row):
        return jnp.dot(
            turned[(row + 1) * cols : (row + 2) * cols, :],
            errs[(row - 1) * block : (row + 2) * block, :],
            preferred_element_type=F32,
        )

    def weigh(part):
        stretch = slice(part.first, part.first + part.rows)
        left = features[0, own, stretch]
        sources[0][stretch, :] = rows_product(left, steps[0, own, :]).astype(BF16)

    sources[last][...] = rows_product(features[last, own, :], steps[last, own, :]).astype(BF16)
    early.advance()
    errors(last, HALO, HALO + rows)
    early.advance()
    leaving[0].start(place, state_out)
    swaps[3].settle()
    zero_outside(place, steps.at[last], 0, (HALO + rows) * cols, HALO * cols)
    errors(last, 0, HALO)
    errors(last, HALO + rows, ext)
    swaps[4].settle()
    back = [arriving.lines[row - 1].astype(F32) + spread(row) for row in range(1, ext - 1)]
    gradient = jnp.concatenate(back, axis=0).astype(BF16).astype(F32)
    span = pl.ds(cols, (ext - 2) * cols)
    steps[0, span, :] = (gradient * silu_slope(preact[0, span, :])).astype(BF16)
    zero_outside(place, steps.at[0], cols, (ext - 2) * cols, cols)
    weigh(upper)
    upper.advance()
    weigh(lower)
    lower.advance()
    early.advance()
    upper.advance()
    errors(0, 1, ext - 1)
    lower.advance()
    back = [
        gradient[(row - 1) * cols : row * cols] + spread(row) for row in range(HALO, HALO + rows)
    ]
    final = jnp.concatenate(back, axis=0).astype(BF16)
    leaving[1].lines[...] = final.reshape(rows, cols, channels)
    sources[layers][...] = rows_product(latent_in[...], final).astype(BF16)
    encoder.advance()
    encoder.advance()
    upper.advance()
    early.advance()
    lower.advance()
    encoder.advance()
    upper.advance()
    lower.advance()
    early.advance()
    encoder.advance()
    upper.advance()
    lower.advance()
    leaving[1].start(place, latent_grad)
    for part in sums:
        while part.stages:
            part.advance()
    for part in leaving:
        part.finish()


def make_table(place, base, widths, table, rows, cols, basis_count, high):
    own = pl.ds(HALO * high, rows * high)
    table[own, :] = jnp.zeros((rows * high, LANES), F32)
    size = base.shape[3]
    reach = size // 2
    distance = jnp.abs(lax.broadcasted_iota(jnp.int32, (basis_count, size), 1) - reach)
    for row in range(rows):
        source = place.chunk * rows + row
        values = base[source].astype(F32)
        for r in range(3):
            start = (HALO + row) * high + r * basis_count
            table[start : start + basis_count, :size] = jnp.where(
                distance <= widths[source], values[r], 0.0
            )
    moved = pltpu.roll(table[own, :], LANES - reach, 1)
    table[own, :] = moved + pltpu.roll(moved, cols, 1)


def make_lines(taps, flat, lines, start_in, rows_in, basis_count):
    flat[...] = jnp.zeros_like(flat)
    count, _, held = taps.shape
    for k in range(basis_count):
        for t in range(count):
            row = 8 * k + t
            flat[row : row + 1, :held] = taps[t, k : k + 1, :].astype(F32)
    flat[...] = flat[...].T
    values = flat[aligned(start_in // rows_in, rows_in), :]
    lane = lax.broadcasted_iota(jnp.int32, values.shape, 1)
    for k in range(basis_count):
        moved = pltpu.roll(values, LANES - 8 * k, 1) if k else values
        kept = jnp.where(lane < count, moved, 0.0)
        lines[k * rows_in : (k + 1) * rows_in, :] = pltpu.roll(kept, LANES - count // 2, 1)


def stretches(heights):
    half = heights[0] // 2
    return [
        (len(heights) - 2, 0, heights[-2], ACROSS),
        (0, 0, half, ACROSS),
        (0, half, half, ACROSS),
        (len(heights) - 1, 0, heights[-1], WIDE),
    ]


def run_chunks(
    plan, sizes, field_in, taps, owner, encoder_weight, base, widths, weights, cotangent
):
    rows, cols, basis_count, layers = plan
    lat, lon = sizes
    channels = weights.shape[2]
    features = basis_count * channels
    in_features = encoder_weight.shape[0]
    ext = rows + 2 * HALO
    heights = [features] * layers + [in_features]
    block = basis_count * cols
    high = -(-3 * basis_count // 8) * 8
    tall = -(-basis_count // 8) * 8
    scratch = [
        pltpu.VMEM((ext * high, LANES), F32),
        pltpu.VMEM((LANES, LANES), F32),
        pltpu.VMEM((basis_count * 2 * rows, LANES), F32),
        pltpu.VMEM((4, tall, LANES), F32),
        pltpu.VMEM((ext * block, 2 * LANES), BF16),
        pltpu.VMEM(((ext + 2) * cols, 3 * block), BF16),
        pltpu.VMEM((rows * cols, in_features), BF16),
        pltpu.VMEM((ext * cols, channels), BF16),
        pltpu.VMEM((layers, ext * cols, features), BF16),
        pltpu.VMEM((layers, ext * cols, channels), F32),
        pltpu.VMEM((layers, ext * cols, channels), BF16),
        pltpu.VMEM((ext * block, channels), BF16),
        pltpu.VMEM(encoder_weight.shape, BF16),
        pltpu.VMEM(weights.shape, BF16),
        pltpu.SemaphoreType.DMA((2,)),
    ]
    scratch += Regroup.scratch(lon, 2 * rows, field_in.shape[1] * lon, field_in.shape[2], 1)
    scratch += Regroup.scratch(lon, rows, cols, channels, 0)
    for _ in range(2):
        scratch += Restore.scratch(lon, rows, cols, channels)
    for _ in range(5):
        scratch += Swap.scratch()
    scratch += [pltpu.VMEM((height, channels), BF16) for height in heights]
    for _, _, size, _ in stretches(heights):
        scratch += ChipSum.scratch(sizes, size, channels)
    vmem = pl.BlockSpec(memory_space=pltpu.VMEM)
    smem = pl.BlockSpec(memory_space=pltpu.SMEM)
    hbm = pl.BlockSpec(memory_space=pltpu.HBM)
    out = pltpu.VMEM(cotangent.shape, BF16)
    grads = [pltpu.VMEM((height, channels // 2), BF16) for height in heights]
    return pl.pallas_call(
        functools.partial(chunk_kernel, plan),
        out_shape=[out, out] + grads,
        in_specs=[hbm, vmem, smem, hbm, vmem, smem, hbm, hbm],
        out_specs=[vmem, vmem] + [vmem] * (1 + layers),
        scratch_shapes=scratch,
        compiler_params=pltpu.CompilerParams(
            collective_id=1, has_side_effects=True, vmem_limit_bytes=56 << 20
        ),
    )(field_in, taps, owner, encoder_weight, base, widths, weights, cotangent)


def finish_body(normalizer, field_count, sum_count, refs):
    fields, sums = refs[:field_count], refs[field_count : field_count + sum_count]
    fields_out = refs[field_count + sum_count : 2 * field_count + sum_count]
    block_grads, encoder_grad = refs[2 * field_count + sum_count :][:2]
    rest = refs[2 * field_count + sum_count + 2 :]
    wide, out_sems = rest[:sum_count], rest[sum_count]
    targets = list(fields_out) + [block_grads.at[n] for n in range(sum_count - 1)] + [encoder_grad]
    stores = [
        pltpu.make_async_copy(source, target, out_sems.at[n])
        for n, (source, target) in enumerate(zip(list(fields) + list(wide), targets))
    ]
    for n, store in enumerate(stores):
        if n >= field_count:
            wide[n - field_count][...] = sums[n - field_count][...].astype(F32) * normalizer
        store.start()
    for store in stores:
        store.wait()


def finish_outputs(normalizer, outs):
    hbm = pl.BlockSpec(memory_space=pltpu.HBM)
    fields, sums = outs[:2], outs[2:]
    shapes = [jax.ShapeDtypeStruct(field.shape, field.dtype) for field in fields]
    shapes.append(jax.ShapeDtypeStruct((len(sums) - 1,) + sums[0].shape, F32))
    shapes.append(jax.ShapeDtypeStruct(sums[-1].shape, F32))

    def kernel(*refs):
        finish_body(normalizer, len(fields), len(sums), refs)

    return pl.pallas_call(
        kernel,
        out_shape=shapes,
        in_specs=[pl.BlockSpec(memory_space=pltpu.VMEM)] * len(outs),
        out_specs=[hbm] * len(shapes),
        scratch_shapes=[pltpu.VMEM(value.shape, F32) for value in sums]
        + [pltpu.SemaphoreType.DMA((len(outs),))],
        compiler_params=pltpu.CompilerParams(vmem_limit_bytes=16 << 20),
    )(*outs)


def fits_chunks(rows_dev, cols_in, cols_dev, layers, heights):
    lon = lax.axis_size("lon")
    count = lax.axis_size("lat") * lon
    heights_fit = all(size % (count * TILE) == 0 for _, _, size, _ in stretches(heights))
    return (
        layers == HALO
        and rows_dev % lon == 0
        and heights_fit
        and rows_dev // lon >= HALO
        and lon % 2 == 0
        and cols_in * lon == LANES
        and 2 * cols_dev * lon == LANES
    )


def per_device_chunks(
    input_field,
    encoder_filter,
    row_owner,
    encoder_weight,
    disco_basis,
    row_widths,
    block_weights,
    cotangent,
):
    rows_in, cols_in, _ = input_field.shape
    lat, lon = lax.axis_size("lat"), lax.axis_size("lon")
    rows_dev, cols = rows_in // 2, cols_in // 2 * lon
    plan = (rows_dev // lon, cols, encoder_filter.shape[1], block_weights.shape[0])
    outs = run_chunks(
        plan,
        (lat, lon),
        input_field,
        encoder_filter.transpose(2, 1, 0),
        row_owner,
        encoder_weight,
        disco_basis.transpose(0, 2, 1, 3),
        row_widths,
        block_weights,
        cotangent,
    )
    cells_total = rows_dev * lax.axis_size(("lat", "ch")) * cols
    return tuple(finish_outputs(1.0 / math.sqrt(cells_total), outs))


def solution(mesh):
    placed = (
        P(("ens", "lat", "ch"), "lon", None),
        P(("lat", "ch"), None, None),
        P(("ens", "lat", "ch")),
        P(),
        P(("lat", "ch"), None, None, None),
        P(("lat", "ch")),
        P(),
        P(("ens", "lat", "ch"), "lon", None),
    )
    return jax.shard_map(
        per_device,
        mesh=mesh,
        in_specs=placed,
        out_specs=(
            P(("ens", "lat", "ch"), "lon", None),
            P(("ens", "lat", "ch"), "lon", None),
            P("ens", None, "ch"),
            P("ens", "ch"),
        ),
        check_vma=False,
    )
```
